32 devices in a mesh: ctx: 4 (over z), fsdp: 8 (over y, x, core).
Axes of the slice: x: 2, y: 2, z: 4, core: 2. Of those that a mesh axis runs over, the one named last changes fastest.
Arguments:
- earlier: bfloat16 [8, 16, 2, 512, 1024], P(None, 'fsdp', None, 'ctx'), may hold values from -6 to 6
- mix_in: float32 [4, 8, 16, 2, 512], P(None, None, 'fsdp', None, 'ctx'), may hold values from -0.6 to 0.6
- segment_ids: int32 [16, 2, 512], P('fsdp'), may hold values from 0 to 1, as said below
- attn_qkv: bfloat16 [1024, 3072], P('fsdp'), may hold values from -0.1875 to 0.1875
- attn_out: bfloat16 [1024, 1024], P('fsdp'), may hold values from -1.5 to 1.5
- mlp_in: bfloat16 [1024, 4096], P('fsdp'), may hold values from -0.1875 to 0.1875
- mlp_out: bfloat16 [4096, 1024], P('fsdp'), may hold values from -0.09375 to 0.09375
- norm_gain: float32 [4, 1024], replicated, may hold values from 0.25 to 1.75
- norm_bias: float32 [4, 1024], replicated, may hold values from -1.2 to 1.2
- mix_w1: bfloat16 [36, 1024], replicated, may hold values from -0.1875 to 0.1875
- mix_w2: bfloat16 [36, 36], replicated, may hold values from -1 to 1
- mix_bias: float32 [36], replicated, may hold values from -3 to 3
- out_grad: bfloat16 [16, 2, 512, 1024], P('fsdp', None, 'ctx'), may hold values from -6 to 6
- coef_grad: float32 [4, 9, 16, 2, 512], P(None, None, 'fsdp', None, 'ctx'), may hold values from -6 to 6
Outputs:
- layer_out: bfloat16 [16, 2, 512, 1024], P('fsdp', None, 'ctx')
- coefficients: float32 [4, 9, 16, 2, 512], P(None, None, 'fsdp', None, 'ctx')
- earlier_grad: bfloat16 [8, 16, 2, 512, 1024], P(None, 'fsdp', None, 'ctx')
- mix_grad: float32 [4, 8, 16, 2, 512], P(None, None, 'fsdp', None, 'ctx')
- attn_qkv_grad: float32 [1024, 3072], P('fsdp')
- attn_out_grad: float32 [1024, 1024], P('fsdp')
- mlp_in_grad: float32 [1024, 4096], P('fsdp')
- mlp_out_grad: float32 [4096, 1024], P('fsdp')
- norm_gain_grad: float32 [4, 1024], replicated
- norm_bias_grad: float32 [4, 1024], replicated
- mix_w1_grad: float32 [36, 1024], replicated
- mix_w2_grad: float32 [36, 36], replicated
- mix_bias_grad: float32 [36], replicated
The draws below stay inside these ranges and needn't reach their ends.
Inputs may be any that keep to these rules, and one draw needn't show every extreme that they name: `segment_ids`: in each sequence, taken in order of place, the ids begin at 0, rise by 0 or 1 from one position to the next, and reach the largest value.
All inputs are finite; a program needn't handle non-finite values.
Results may differ from the reference program's by a relative error of at most 0.019.
Values may be sent and summed in bfloat16 or wider, within the bound.
A program may use at most 512 MiB of HBM per device.

```python
import math
import jax
import jax.numpy as jnp
from jax import lax

D = 1024
HEADS = 16
HD = 64
FF = 4096
ROT = 16
NIN = 8
MIXH = 36
COEF = 36
SEQ_LEN = 1024
BLK = 128
HALF = 512
SEQS = 16
N_CTX = 4


def draw_segment_ids(key, part):
    documents = max(SEQ_LEN // 512, 2)
    top_score = 2 ** 31 // SEQ_LEN - 1
    raw_scores = jax.random.randint(key, (SEQS, SEQ_LEN - 1), 0, top_score, dtype=jnp.int32)
    scores = raw_scores * SEQ_LEN + jnp.arange(SEQ_LEN - 1, dtype=jnp.int32)[None, :]
    picked = lax.top_k(scores, documents - 1)[1].astype(jnp.int32) + 1
    positions = jnp.arange(SEQ_LEN, dtype=jnp.int32)
    marks = jnp.sum(jnp.where(positions[None, :, None] == picked[:, None, :], 1, 0), axis=2).astype(jnp.int32)
    ordered = jnp.cumsum(marks, axis=1).astype(jnp.int32)
    column = jnp.arange(HALF, dtype=jnp.int32)
    later = SEQ_LEN - BLK * (column // BLK + 1) + column % BLK
    table = jnp.stack([column, later], axis=0)
    return ordered[:, table].astype(jnp.int32)


def levels(stream_key, extent, cuts, low, high):
    factor_of, own = 1.0, jax.random.fold_in(stream_key, 6)
    for position, parts in cuts:
        steps = jnp.exp(jax.random.uniform(jax.random.fold_in(own, position), (parts,), jnp.float32, low / len(cuts), high / len(cuts)))
        factor_of = factor_of * jnp.repeat(steps, extent[position] // parts).reshape([-1 if axis == position else 1 for axis in range(len(extent))])
    return factor_of


def noise(rng, extent, scale, most, pieces=(), kind=jnp.bfloat16):
    drawn = jax.random.normal(rng, extent, jnp.float32) * scale
    if len(pieces) > 0:
        drawn = levels(rng, extent, pieces, -0.22, 0.18) * drawn
    return jnp.clip(drawn, min=-most, max=most).astype(kind)


def setup_inputs(seed: int = 0) -> dict:
    key_of = jax.random.split(jax.random.key(seed), 15)
    return {
        "earlier": noise(key_of[0], (NIN, SEQS, 2, HALF, D), 1.0, 6.0, ((1, 8), (3, 4))),
        "mix_in": jnp.clip(jax.random.uniform(key_of[1], (4, NIN, SEQS, 2, HALF), jnp.float32, -0.6, 0.6) * levels(key_of[1], (4, NIN, SEQS, 2, HALF), ((2, 8), (4, 4)), -0.4, 0.0), -0.6, 0.6),
        "segment_ids": draw_segment_ids(jax.random.fold_in(key_of[14], 71), 0),
        "attn_qkv": noise(key_of[3], (D, 3 * D), D ** -0.5, 0.1875, ((0, 8),)),
        "attn_out": noise(key_of[4], (D, D), (max(D // 64, 4)) ** -0.5, 1.5, ((0, 8),)),
        "mlp_in": noise(key_of[5], (D, FF), D ** -0.5, 0.1875, ((0, 8),)),
        "mlp_out": noise(key_of[6], (FF, D), FF ** -0.5, 0.09375, ((0, 8),)),
        "norm_gain": jnp.clip(1.0 + 0.15 * jax.random.normal(key_of[7], (4, D), jnp.float32), 0.25, 1.75),
        "norm_bias": noise(key_of[8], (4, D), 0.2, 1.2, (), jnp.float32),
        "mix_w1": noise(key_of[9], (MIXH, D), D ** -0.5, 0.1875),
        "mix_w2": noise(key_of[10], (MIXH, COEF), MIXH ** -0.5, 1.0),
        "mix_bias": noise(key_of[11], (COEF,), 0.5, 3.0, (), jnp.float32),
        "out_grad": noise(key_of[12], (SEQS, 2, HALF, D), 1.0, 6.0, ((0, 8), (2, 4))),
        "coef_grad": noise(key_of[13], (4, NIN + 1, SEQS, 2, HALF), 1.0, 6.0, ((2, 8), (4, 4)), jnp.float32),
    }


EPSILON = 1e-05
TOP_PRECISION = lax.Precision.HIGHEST
MASKED = -1e+30

@jax.custom_vjp
def low(v):
    return lax.optimization_barrier(v.astype(jnp.bfloat16)).astype(jnp.float32)

@jax.custom_vjp
def low_back(v):
    return v

def low_keep(v):
    return (low(v), None)

def low_pass(kept, grad):
    return (grad,)

def back_keep(v):
    return (v, None)

def back_low(kept, grad):
    return (low(grad),)
low.defvjp(low_keep, low_pass)
low_back.defvjp(back_keep, back_low)

def layer_norm(values, gain, shift):
    center = values - lax.optimization_barrier(jnp.mean(values, axis=-1, keepdims=True))
    spread = lax.optimization_barrier(jnp.mean(center * center, axis=-1, keepdims=True))
    return center * lax.rsqrt(spread + EPSILON) * gain + shift

def rotate(values, places):
    half_width = ROT // 2
    frequency = 10000.0 ** (-(jnp.arange(half_width, dtype=jnp.float32) * 2.0 / ROT))
    angles = places[:, None] * frequency[None, :]
    cosine = jnp.cos(angles)[:, None, :]
    sine_part = jnp.sin(angles)[:, None, :]
    first = values[..., :half_width]
    second = values[..., half_width:ROT]
    return jnp.concatenate([first * cosine - second * sine_part, second * cosine + first * sine_part, values[..., ROT:]], axis=-1)

def coefficient_head(layer_sum, first_weight, second_weight, head_shift):
    factor = lax.rsqrt(lax.optimization_barrier(jnp.mean(layer_sum * layer_sum, axis=-1, keepdims=True)) + 1e-06)
    middle = jax.nn.gelu(jnp.dot(layer_sum * factor, first_weight.T, precision=TOP_PRECISION), approximate=False)
    return jnp.dot(middle, second_weight, precision=TOP_PRECISION) + head_shift

def to_order(array, axis):
    moved = jnp.moveaxis(array, (axis, axis + 1), (0, 1))
    rest = moved.shape[2:]
    second = jnp.flip(moved[1].reshape((N_CTX, BLK) + rest), axis=0).reshape((HALF,) + rest)
    return jnp.moveaxis(jnp.concatenate([moved[0], second], axis=0), 0, axis)

def from_order(array, axis):
    moved = jnp.moveaxis(array, axis, 0)
    rest = moved.shape[1:]
    second = jnp.flip(moved[HALF:].reshape((N_CTX, BLK) + rest), axis=0).reshape((HALF,) + rest)
    return jnp.moveaxis(jnp.stack([moved[:HALF], second], axis=0), (0, 1), (axis, axis + 1))

def attention(queries, keys, values, segments, positions):
    block = math.gcd(SEQ_LEN, 512)

    def one_block(index):
        begin = index * block
        query_block = lax.dynamic_slice_in_dim(queries, begin, block, 0)
        query_segments = lax.dynamic_slice_in_dim(segments, begin, block, 0)
        query_places = lax.dynamic_slice_in_dim(positions, begin, block, 0)
        raw = low_back(jnp.einsum('qhd,khd->hqk', query_block, keys, precision=TOP_PRECISION))
        scaled = raw * HD ** (-0.5)
        allowed = (query_segments[:, None] == segments[None, :]) & (positions[None, :] <= query_places[:, None])
        scaled = jnp.where(allowed[None], scaled, MASKED)
        peak = lax.optimization_barrier(jnp.max(scaled, axis=-1, keepdims=True))
        raised = jnp.exp(scaled - peak)
        probs = low(raised / lax.optimization_barrier(jnp.sum(raised, axis=-1, keepdims=True)))
        return jnp.einsum('hqk,khd->qhd', probs, values, precision=TOP_PRECISION)
    blocks = lax.map(jax.checkpoint(one_block), jnp.arange(SEQ_LEN // block, dtype=jnp.int32))
    return blocks.reshape(SEQ_LEN, HEADS * HD)

def forward(input_rows, mixing_weights, segments, qkv, proj, w_in, w_out, gain, shift, head_first, second_head_half, head_shift):
    positions = jnp.arange(SEQ_LEN, dtype=jnp.int32)
    residual_streams = jnp.einsum('icw,cwy->iwy', mixing_weights, input_rows, precision=TOP_PRECISION)
    normed = low(layer_norm(residual_streams[:3], gain[:3, None, :], shift[:3, None, :]))
    raw_q = low_back(jnp.dot(normed[0], qkv[:, :D], precision=TOP_PRECISION))
    raw_k = low_back(jnp.dot(normed[1], qkv[:, D:2 * D], precision=TOP_PRECISION))
    values = low_back(low(jnp.dot(normed[2], qkv[:, 2 * D:], precision=TOP_PRECISION)))
    angle = positions.astype(jnp.float32)
    queries = low(rotate(raw_q.reshape(SEQ_LEN, HEADS, HD), angle))
    keys = low(rotate(raw_k.reshape(SEQ_LEN, HEADS, HD), angle))
    context = low_back(low(attention(queries, keys, values.reshape(SEQ_LEN, HEADS, HD), segments, positions)))
    hidden = residual_streams[3] + low_back(jnp.dot(context, proj, precision=TOP_PRECISION))
    normed_mlp = low(layer_norm(hidden, gain[3], shift[3]))
    upward = low_back(jnp.dot(normed_mlp, w_in, precision=TOP_PRECISION))
    active = low(jax.nn.gelu(upward, approximate=False))
    layer_sum = hidden + low_back(jnp.dot(active, w_out, precision=TOP_PRECISION))
    coefs_rows = coefficient_head(layer_sum, head_first, second_head_half, head_shift)
    return (layer_sum, coefs_rows.reshape(SEQ_LEN, 4, NIN + 1).transpose(1, 2, 0))

def reference(earlier, mix_in, segment_ids, attn_qkv, attn_out, mlp_in, mlp_out, norm_gain, norm_bias, mix_w1, mix_w2, mix_bias, out_grad, coef_grad):
    params = (attn_qkv.astype(jnp.float32), attn_out.astype(jnp.float32), mlp_in.astype(jnp.float32), mlp_out.astype(jnp.float32), norm_gain.astype(jnp.float32), norm_bias.astype(jnp.float32), mix_w1.astype(jnp.float32), mix_w2.astype(jnp.float32), mix_bias.astype(jnp.float32))

    def step(sums, items):
        inputs_store, mixing_store, segments_store, out_store, coef_store = items
        input_rows = to_order(inputs_store.astype(jnp.float32), 1)
        mixing_weights = to_order(mixing_store, 2)
        segments = to_order(segments_store, 0)
        cotangent = to_order(out_store.astype(jnp.float32), 0)
        coef_cotangent = to_order(coef_store, 2)

        def run(inputs_now, mixing_now, *weights):
            return forward(inputs_now, mixing_now, segments, *weights)
        (layer_sum, coefs_now), pull = jax.vjp(run, input_rows, mixing_weights, *params)
        gradients = pull((cotangent, coef_cotangent))
        sums = tuple((total + grad for total, grad in zip(sums, gradients[2:])))
        results = (from_order(layer_sum.astype(jnp.bfloat16), 0), from_order(coefs_now, 2), from_order(gradients[0].astype(jnp.bfloat16), 1), from_order(gradients[1], 2))
        return (sums, results)
    start = tuple((jnp.zeros(param.shape, jnp.float32) for param in params))
    items = (jnp.moveaxis(earlier, 1, 0), jnp.moveaxis(mix_in, 2, 0), segment_ids, out_grad, jnp.moveaxis(coef_grad, 2, 0))
    sums, results = lax.scan(step, start, items)
    layer_out = results[0]
    coefficients = jnp.moveaxis(results[1], 0, 2)
    earlier_grad = jnp.moveaxis(results[2], 0, 1)
    mix_grad = jnp.moveaxis(results[3], 0, 2)
    return (layer_out, coefficients, earlier_grad, mix_grad, sums[0], sums[1], sums[2], sums[3], sums[4], sums[5], sums[6], sums[7], sums[8])
```

```python
import functools
import math

import jax
import jax.numpy as jnp
import numpy as np
from jax import lax
from jax.experimental import pallas as pl
from jax.experimental.pallas import tpu as pltpu
from jax.sharding import PartitionSpec as P

HD = 64
ROT = 16
LANES = 128
EPSILON = 1e-05
RMS_EPSILON = 1e-06
MASKED = -1e30
F32 = jnp.float32
BF16 = jnp.bfloat16
MESH = pl.DeviceIdType.MESH
MIB = 1024 * 1024

NN = (((1,), (0,)), ((), ()))
NT = (((1,), (1,)), ((), ()))
TN = (((0,), (0,)), ((), ()))

ERFC_RATE = 0.4
ERFC = (
    0.22567586600780487,
    0.22566929459571838,
    0.20784726738929749,
    0.16851142048835754,
    0.1415392905473709,
    -0.005822250619530678,
    0.16932761669158936,
    -0.18304575979709625,
    0.05029737576842308,
)


def dot(a, b, dims=NN):
    return lax.dot_general(a, b, dims, preferred_element_type=F32)


def gelu_and_slope(v):
    z = jnp.abs(v) * math.sqrt(0.5)
    bell = jnp.exp(-0.5 * v * v)
    t = 1.0 / (1.0 + ERFC_RATE * z)
    poly = jnp.full_like(t, ERFC[-1])
    for coefficient in ERFC[-2::-1]:
        poly = poly * t + coefficient
    tail = 0.5 * poly * t * bell
    phi = jnp.where(v >= 0.0, 1.0 - tail, tail)
    return v * phi, phi + v * bell * (1.0 / math.sqrt(2.0 * math.pi))


def params(limit_mib, **more):
    return pltpu.CompilerParams(vmem_limit_bytes=limit_mib * MIB, **more)


def once(shape, index):
    return pl.BlockSpec(shape, index, pipeline_mode=pl.Buffered(1))


def front_kernel(e_ref, m_ref, g_ref, b_ref, n_ref, r_ref, s_ref, *, strip):
    tile = e_ref.shape[1]
    width = e_ref.shape[2]
    count = e_ref.shape[0]
    chunk = 256
    mixes = m_ref[...].T

    for strip_index in range(tile // strip):
        rows = slice(strip_index * strip, (strip_index + 1) * strip)
        mix = mixes[rows]
        for c in range(width // chunk):
            cols = slice(c * chunk, (c + 1) * chunk)
            parts = [e_ref[j, rows, cols].astype(F32) for j in range(count)]
            for s in range(4):
                total = parts[0] * mix[:, s * count : s * count + 1]
                for j in range(1, count):
                    total = total + parts[j] * mix[:, s * count + j : s * count + j + 1]
                if s < 3:
                    s_ref[s, :, cols] = total
                else:
                    r_ref[rows, cols] = total
        for s in range(3):
            v = s_ref[s]
            center = v - jnp.mean(v, axis=-1, keepdims=True)
            spread = jnp.mean(center * center, axis=-1, keepdims=True)
            out = center * lax.rsqrt(spread + EPSILON) * g_ref[s : s + 1] + b_ref[s : s + 1]
            n_ref[s, rows] = out.astype(BF16)


def front(e, mix, gain, bias):
    count, tokens, width = e.shape
    tile = 128
    strip = 16
    return pl.pallas_call(
        functools.partial(front_kernel, strip=strip),
        grid=(tokens // tile,),
        in_specs=[
            pl.BlockSpec((count, tile, width), lambda i: (0, i, 0)),
            pl.BlockSpec((4 * count, tile), lambda i: (0, i)),
            pl.BlockSpec((4, width), lambda i: (0, 0)),
            pl.BlockSpec((4, width), lambda i: (0, 0)),
        ],
        out_specs=[
            pl.BlockSpec((3, tile, width), lambda i: (0, i, 0)),
            pl.BlockSpec((tile, width), lambda i: (i, 0)),
        ],
        out_shape=[
            jax.ShapeDtypeStruct((3, tokens, width), BF16),
            jax.ShapeDtypeStruct((tokens, width), F32),
        ],
        scratch_shapes=[pltpu.VMEM((3, strip, width), F32)],
        compiler_params=params(32),
        cost_estimate=pl.CostEstimate(
            flops=64 * tokens * width, bytes_accessed=26 * tokens * width, transcendentals=0
        ),
        name="front",
    )(e, mix, gain, bias)


def turn_tables(length):
    half = ROT // 2
    frequency = 10000.0 ** (-(np.arange(half) * 2.0 / ROT))
    angle = np.arange(length)[:, None] * frequency[None, :]
    lane = np.arange(LANES) % HD
    cosine = np.ones((length, LANES), np.float32)
    sine = np.zeros((length, LANES), np.float32)
    for k in range(LANES):
        if lane[k] < ROT:
            cosine[:, k] = np.cos(angle[:, lane[k] % half])
            sign = -1.0 if lane[k] < half else 1.0
            sine[:, k] = sign * np.sin(angle[:, lane[k] % half])
    return cosine, sine


def turned(x, cosine, sine):
    half = ROT // 2
    lane = lax.broadcasted_iota(jnp.int32, x.shape, 1) % HD
    other = jnp.where(
        lane < half, pltpu.roll(x, LANES - half, axis=1), pltpu.roll(x, half, axis=1)
    )
    return x * cosine + other * sine


def qkv_kernel(n_ref, w_ref, c_ref, s_ref, out_ref, x_ref):
    which = pl.program_id(0)
    tokens = n_ref.shape[1]
    width = w_ref.shape[1]
    group = out_ref.shape[3]
    seq_rows = c_ref.shape[0]
    x_ref[...] = dot(n_ref[0], w_ref[...])

    @pl.when(which < 2)
    def _():
        cosine = c_ref[...]
        sine = s_ref[...]
        for s in range(tokens // seq_rows):
            rows = slice(s * seq_rows, (s + 1) * seq_rows)
            for c in range(width // LANES):
                cols = slice(c * LANES, (c + 1) * LANES)
                y = turned(x_ref[rows, cols], cosine, sine).astype(BF16)
                to = c * LANES % group
                out_ref[0, c * LANES // group, rows, to : to + LANES] = y

    @pl.when(which == 2)
    def _():
        for g in range(width // group):
            out_ref[0, g] = x_ref[:, g * group : (g + 1) * group].astype(BF16)


def project(normed, w, cosine, sine, groups):
    _, tokens, width = normed.shape
    group = width // groups
    cut = max(group, 512)
    inner = width // cut
    return pl.pallas_call(
        qkv_kernel,
        grid=(3, inner),
        in_specs=[
            pl.BlockSpec((1, tokens, width), lambda i, j: (i, 0, 0)),
            pl.BlockSpec((width, cut), lambda i, j: (0, i * inner + j)),
            pl.BlockSpec(cosine.shape, lambda i, j: (0, 0)),
            pl.BlockSpec(sine.shape, lambda i, j: (0, 0)),
        ],
        out_specs=pl.BlockSpec((1, cut // group, tokens, group), lambda i, j: (i, j, 0, 0)),
        out_shape=jax.ShapeDtypeStruct((3, groups, tokens, group), BF16),
        scratch_shapes=[pltpu.VMEM((tokens, cut), F32)],
        compiler_params=params(32),
        cost_estimate=pl.CostEstimate(
            flops=6 * tokens * width * width,
            bytes_accessed=6 * width * width + 12 * tokens * width,
            transcendentals=0,
        ),
        name="project",
    )(normed, w, cosine, sine)


def greet(n):
    me = lax.axis_index("ctx")
    barrier = pltpu.get_barrier_semaphore()
    for k in range(1, n):
        pl.semaphore_signal(
            barrier, inc=1, device_id={"ctx": lax.rem(me + k, n)}, device_id_type=MESH
        )
    pl.semaphore_wait(barrier, n - 1)


def to_heads_kernel(n, x_ref, o_ref, send, recv, own):
    me = lax.axis_index("ctx")
    spots = (me, 2 * n - 1 - me)
    kept = []
    for h in range(2):
        copy = pltpu.make_async_copy(x_ref.at[:, me, :, h], o_ref.at[:, :, spots[h]], own.at[h])
        copy.start()
        kept.append(copy)
    greet(n)
    sent = []
    for k in range(1, n):
        to = lax.rem(me + k, n)
        for h in range(2):
            slot = 2 * (k - 1) + h
            copy = pltpu.make_async_remote_copy(
                src_ref=x_ref.at[:, to, :, h],
                dst_ref=o_ref.at[:, :, spots[h]],
                send_sem=send.at[slot],
                recv_sem=recv.at[slot],
                device_id={"ctx": to},
                device_id_type=MESH,
            )
            copy.start()
            sent.append(copy)
    for copy in kept + sent:
        copy.wait()


def to_heads(x, n, seqs, block, collective):
    kinds, _, _, cols = x.shape
    view = x.reshape(kinds, n, seqs, 2, block, cols)
    out = pl.pallas_call(
        functools.partial(to_heads_kernel, n),
        in_specs=[pl.BlockSpec(memory_space=pltpu.HBM)],
        out_specs=pl.BlockSpec(memory_space=pltpu.HBM),
        out_shape=jax.ShapeDtypeStruct((kinds, seqs, 2 * n, block, cols), BF16),
        scratch_shapes=[
            pltpu.SemaphoreType.DMA((2 * n - 2,)),
            pltpu.SemaphoreType.DMA((2 * n - 2,)),
            pltpu.SemaphoreType.DMA((2,)),
        ],
        compiler_params=params(1, collective_id=collective, has_side_effects=True),
        name="to_heads",
    )(view)
    return out.reshape(kinds, seqs, 2 * n * block, cols)


def to_tokens_kernel(n, x_ref, o_ref, send, recv, own):
    me = lax.axis_index("ctx")
    cols = x_ref.shape[4]
    mine = pl.ds(pl.multiple_of(me * cols, LANES), cols)
    kept = []
    for h in range(2):
        spot = me if h == 0 else 2 * n - 1 - me
        copy = pltpu.make_async_copy(
            x_ref.at[:, :, spot], o_ref.at[:, :, h, :, mine], own.at[h]
        )
        copy.start()
        kept.append(copy)
    greet(n)
    sent = []
    for k in range(1, n):
        to = lax.rem(me + k, n)
        for h in range(2):
            spot = to if h == 0 else 2 * n - 1 - to
            slot = 2 * (k - 1) + h
            copy = pltpu.make_async_remote_copy(
                src_ref=x_ref.at[:, :, spot],
                dst_ref=o_ref.at[:, :, h, :, mine],
                send_sem=send.at[slot],
                recv_sem=recv.at[slot],
                device_id={"ctx": to},
                device_id_type=MESH,
            )
            copy.start()
            sent.append(copy)
    for copy in kept + sent:
        copy.wait()


def to_tokens(x, n, block, collective):
    kinds, seqs, length, cols = x.shape
    view = x.reshape(kinds, seqs, 2 * n, block, cols)
    out = pl.pallas_call(
        functools.partial(to_tokens_kernel, n),
        in_specs=[pl.BlockSpec(memory_space=pltpu.HBM)],
        out_specs=pl.BlockSpec(memory_space=pltpu.HBM),
        out_shape=jax.ShapeDtypeStruct((kinds, seqs, 2, block, n * cols), BF16),
        scratch_shapes=[
            pltpu.SemaphoreType.DMA((2 * n - 2,)),
            pltpu.SemaphoreType.DMA((2 * n - 2,)),
            pltpu.SemaphoreType.DMA((2,)),
        ],
        compiler_params=params(1, collective_id=collective, has_side_effects=True),
        name="to_tokens",
    )(view)
    return out.reshape(kinds, seqs * 2 * block, n * cols)


def row_tile(length):
    return min(256, length)


def head_lanes(shape, h):
    lane = lax.broadcasted_iota(jnp.int32, shape, 1)
    return (lane >= h * HD) & (lane < (h + 1) * HD)


def only(x, h):
    return jnp.where(head_lanes(x.shape, h), x, jnp.zeros_like(x))


def allowed_here(column_ref, row_ref, first, rows):
    until = first + rows
    shape = (rows, until)
    query = first + lax.broadcasted_iota(jnp.int32, shape, 0)
    key = lax.broadcasted_iota(jnp.int32, shape, 1)
    same = column_ref[0, first:until, 0:1] == row_ref[0, 0:1, 0:until]
    return same & (key <= query)


def attend_kernel(q_ref, k_ref, v_ref, column_ref, row_ref, o_ref):
    length = q_ref.shape[2]
    rows = row_tile(length)
    for i in range(length // rows):
        first, until = i * rows, (i + 1) * rows
        allowed = allowed_here(column_ref, row_ref, first, rows)
        q = q_ref[0, 0, first:until] * BF16(HD**-0.5)
        k = k_ref[0, 0, 0:until]
        v = v_ref[0, 0, 0:until]
        total = None
        for h in range(LANES // HD):
            scores = jnp.where(allowed, dot(only(q, h), k, NT), MASKED)
            peak = jnp.max(scores, axis=-1, keepdims=True)
            raised = jnp.exp(scores - peak)
            mass = jnp.sum(raised, axis=-1, keepdims=True)
            probs = (raised * (1.0 / mass)).astype(BF16)
            part = dot(probs, v)
            part = jnp.where(head_lanes(part.shape, h), part, 0.0)
            total = part if total is None else total + part
        o_ref[0, 0, first:until] = total.astype(BF16)


def attend(qkv, column, row):
    _, seqs, length, cols = qkv.shape
    pairs = cols // LANES

    def spec(kind):
        return pl.BlockSpec((1, 1, length, LANES), lambda s, p: (kind, s, 0, p))

    return pl.pallas_call(
        attend_kernel,
        grid=(seqs, pairs),
        in_specs=[
            spec(0),
            spec(1),
            spec(2),
            pl.BlockSpec((1, length, 1), lambda s, p: (s, 0, 0)),
            pl.BlockSpec((1, 1, length), lambda s, p: (s, 0, 0)),
        ],
        out_specs=spec(0),
        out_shape=jax.ShapeDtypeStruct((1, seqs, length, cols), BF16),
        compiler_params=params(32),
        cost_estimate=pl.CostEstimate(
            flops=4 * seqs * length * length * cols,
            bytes_accessed=8 * seqs * length * cols,
            transcendentals=seqs * length * length * cols // 128,
        ),
        name="attend",
    )(qkv, qkv, qkv, column, row)


def attend_back_kernel(
    q_ref, k_ref, v_ref, g_ref, column_ref, row_ref, c_ref, s_ref, o_ref, dk_ref, dv_ref
):
    length = q_ref.shape[2]
    rows = row_tile(length)
    factor = HD**-0.5
    for i in range(length // rows):
        here = slice(i * rows, (i + 1) * rows)
        dk_ref[here] = jnp.zeros((rows, LANES), F32)
        dv_ref[here] = jnp.zeros((rows, LANES), F32)
    for i in range(length // rows):
        first, until = i * rows, (i + 1) * rows
        allowed = allowed_here(column_ref, row_ref, first, rows)
        q = q_ref[0, 0, first:until] * BF16(factor)
        g = g_ref[0, 0, first:until]
        k = k_ref[0, 0, 0:until]
        v = v_ref[0, 0, 0:until]
        total = None
        for h in range(LANES // HD):
            q_h = only(q, h)
            g_h = only(g, h)
            scores = jnp.where(allowed, dot(q_h, k, NT), MASKED)
            peak = jnp.max(scores, axis=-1, keepdims=True)
            raised = jnp.exp(scores - peak)
            mass = jnp.sum(raised, axis=-1, keepdims=True)
            probs = raised * (1.0 / mass)
            dots = dot(g_h, v, NT)
            center = jnp.sum(probs * dots, axis=-1, keepdims=True)
            slope = (probs * (dots - center)).astype(BF16)
            part = dot(slope, k)
            part = jnp.where(head_lanes(part.shape, h), part, 0.0)
            total = part if total is None else total + part
            dk_ref[0:until] += dot(slope, q_h, TN)
            dv_ref[0:until] += dot(probs.astype(BF16), g_h, TN)
        cosine, sine = c_ref[first:until], s_ref[first:until]
        o_ref[0, 0, first:until] = turned(total * factor, cosine, -sine).astype(BF16)
    for i in range(length // rows):
        here = slice(i * rows, (i + 1) * rows)
        o_ref[1, 0, here] = turned(dk_ref[here], c_ref[here], -s_ref[here]).astype(BF16)
        o_ref[2, 0, here] = dv_ref[here].astype(BF16)


def attend_back(qkv, grad, column, row, cosine, sine):
    _, seqs, length, cols = qkv.shape
    pairs = cols // LANES

    def spec(kind):
        return pl.BlockSpec((1, 1, length, LANES), lambda s, p: (kind, s, 0, p))

    return pl.pallas_call(
        attend_back_kernel,
        grid=(seqs, pairs),
        in_specs=[
            spec(0),
            spec(1),
            spec(2),
            spec(0),
            pl.BlockSpec((1, length, 1), lambda s, p: (s, 0, 0)),
            pl.BlockSpec((1, 1, length), lambda s, p: (s, 0, 0)),
            pl.BlockSpec((length, LANES), lambda s, p: (0, 0)),
            pl.BlockSpec((length, LANES), lambda s, p: (0, 0)),
        ],
        out_specs=pl.BlockSpec((3, 1, length, LANES), lambda s, p: (0, s, 0, p)),
        out_shape=jax.ShapeDtypeStruct((3, seqs, length, cols), BF16),
        scratch_shapes=[pltpu.VMEM((length, LANES), F32), pltpu.VMEM((length, LANES), F32)],
        compiler_params=params(40),
        cost_estimate=pl.CostEstimate(
            flops=10 * seqs * length * length * cols,
            bytes_accessed=14 * seqs * length * cols,
            transcendentals=seqs * length * length * cols // 128,
        ),
        name="attend_back",
    )(qkv, qkv, qkv, grad, column, row, cosine, sine)


def feed_kernel(
    res_ref,
    ctx_ref,
    wo_ref,
    win_ref,
    wout_ref,
    g_ref,
    b_ref,
    w1_ref,
    w2_ref,
    mb_ref,
    og_ref,
    cg_ref,
    out_ref,
    coef_ref,
    dwin_ref,
    dwout_ref,
    dwo_ref,
    cgrad_ref,
    hgrad_ref,
    dgain_ref,
    dbias_ref,
    dw1_ref,
    dw2_ref,
    dmb_ref,
    hidden,
    normed,
    total,
    active,
    slope,
    branch,
    *,
    tiles,
    strip,
):
    step = pl.program_id(0)
    tokens, width = res_ref.shape
    cut = win_ref.shape[1]
    inv = 1.0 / width

    @pl.when(step == 0)
    def _():
        hidden[...] = dot(ctx_ref[...], wo_ref[...])

        @pl.loop(0, tokens // strip)
        def _(i):
            rows = pl.ds(pl.multiple_of(i * strip, strip), strip)
            v = hidden[rows] + res_ref[rows]
            hidden[rows] = v
            center = v - jnp.sum(v, axis=-1, keepdims=True) * inv
            spread = jnp.sum(center * center, axis=-1, keepdims=True) * inv
            hat = center * lax.rsqrt(spread + EPSILON)
            normed[rows] = (hat * g_ref[3:4] + b_ref[3:4]).astype(BF16)
            total[rows] = v

    @pl.when(step < tiles)
    def _():
        half = tokens // 2
        for part in range(2):
            rows = slice(part * half, (part + 1) * half)
            up = dot(normed[rows], win_ref[...])
            value, rate = gelu_and_slope(up)
            low = value.astype(BF16)
            active[step, rows] = low
            slope[step, rows] = rate
            total[rows] += dot(low, wout_ref[...])

    @pl.when(step == tiles - 1)
    def _():
        w1 = w1_ref[...]
        w2 = w2_ref[...]
        out_ref[...] = total[...].astype(BF16)
        dw1_ref[...] = jnp.zeros_like(dw1_ref)
        dw2_ref[...] = jnp.zeros_like(dw2_ref)
        dmb_ref[...] = jnp.zeros_like(dmb_ref)

        for i in range(tokens // LANES):
            rows = slice(i * LANES, (i + 1) * LANES)
            v = total[rows]
            scale = lax.rsqrt(jnp.sum(v * v, axis=-1, keepdims=True) * inv + RMS_EPSILON)
            r = v * scale
            r_high = r.astype(BF16)
            r_rest = (r - r_high.astype(F32)).astype(BF16)
            z = dot(w1, r_high, NT) + dot(w1, r_rest, NT)
            value, rate = gelu_and_slope(z)
            v_high = value.astype(BF16)
            v_rest = (value - v_high.astype(F32)).astype(BF16)
            coef_ref[:, rows] = dot(w2, v_high, TN) + dot(w2, v_rest, TN) + mb_ref[...]
            cg = cg_ref[:, rows]
            c_high = cg.astype(BF16)
            c_rest = (cg - c_high.astype(F32)).astype(BF16)
            dmb_ref[...] += jnp.sum(cg, axis=-1, keepdims=True)
            dw2_ref[...] += dot(v_high, c_high, NT) + dot(v_rest, c_high, NT) + dot(v_high, c_rest, NT)
            dz = (dot(w2, c_high) + dot(w2, c_rest)) * rate
            z_high = dz.astype(BF16)
            z_rest = (dz - z_high.astype(F32)).astype(BF16)
            dw1_ref[...] += dot(z_high, r_high) + dot(z_high, r_rest) + dot(z_rest, r_high)
            dr = dot(z_high, w1, TN) + dot(z_rest, w1, TN)
            mean = jnp.sum(dr * r, axis=-1, keepdims=True) * inv
            grad = scale * (dr - r * mean) + og_ref[rows].astype(F32)
            hgrad_ref[rows] = grad
            branch[rows] = grad.astype(BF16)
            total[rows] = jnp.zeros_like(v)

    @pl.when(step >= tiles)
    def _():
        j = step - tiles
        half = tokens // 2
        for part in range(2):
            rows = slice(part * half, (part + 1) * half)
            back = dot(branch[rows], wout_ref[...], NT)
            low = (back * slope[j, rows]).astype(BF16)
            total[rows] += dot(low, win_ref[...], NT)
            slope[j, rows] = low.astype(F32)
        dwout_ref[...] = dot(active[j], branch[...], TN).astype(BF16)
        dwin_ref[...] = dot(normed[...], slope[j].astype(BF16), TN).astype(BF16)

    @pl.when(step == 2 * tiles - 1)
    def _():
        dgain_ref[...] = jnp.zeros_like(dgain_ref)
        dbias_ref[...] = jnp.zeros_like(dbias_ref)

        @pl.loop(0, tokens // strip)
        def _(i):
            rows = pl.ds(pl.multiple_of(i * strip, strip), strip)
            v = hidden[rows]
            dy = total[rows]
            center = v - jnp.sum(v, axis=-1, keepdims=True) * inv
            spread = jnp.sum(center * center, axis=-1, keepdims=True) * inv
            scale = lax.rsqrt(spread + EPSILON)
            hat = center * scale
            dgain_ref[...] += jnp.sum(dy * hat, axis=0, keepdims=True)
            dbias_ref[...] += jnp.sum(dy, axis=0, keepdims=True)
            dh = dy * g_ref[3:4]
            first = jnp.sum(dh, axis=-1, keepdims=True) * inv
            second = jnp.sum(dh * hat, axis=-1, keepdims=True) * inv
            grad = hgrad_ref[rows] + scale * (dh - first - hat * second)
            hgrad_ref[rows] = grad
            branch[rows] = grad.astype(BF16)

        dwo_ref[...] = dot(ctx_ref[...], branch[...], TN).astype(BF16)
        cgrad_ref[...] = dot(branch[...], wo_ref[...], NT).astype(BF16)


def feed(res, ctx, wo, win, wout, gain, bias, w1, w2, mb, og, cg):
    tokens, width = res.shape
    hidden_units = win.shape[1]
    cut = 512
    tiles = hidden_units // cut
    small, coefs = w1.shape[0], w2.shape[1]

    def whole(x):
        zeros = (0,) * x.ndim
        return once(x.shape, lambda i: zeros)

    def result(shape, dtype=F32):
        zeros = (0,) * len(shape)
        return once(shape, lambda i: zeros), jax.ShapeDtypeStruct(shape, dtype)

    def back(i):
        return jnp.maximum(i - tiles, 0)

    outs = [
        result((tokens, width), BF16),
        result((coefs, tokens)),
        (
            pl.BlockSpec((width, cut), lambda i: (0, back(i))),
            jax.ShapeDtypeStruct((width, hidden_units), BF16),
        ),
        (
            pl.BlockSpec((cut, width), lambda i: (back(i), 0)),
            jax.ShapeDtypeStruct((hidden_units, width), BF16),
        ),
        result((width, width), BF16),
        result((tokens, width), BF16),
        result((tokens, width)),
        result((1, width)),
        result((1, width)),
        result((small, width)),
        result((small, coefs)),
        result((coefs, 1)),
    ]
    return pl.pallas_call(
        functools.partial(feed_kernel, tiles=tiles, strip=32),
        grid=(2 * tiles,),
        in_specs=[
            whole(res),
            whole(ctx),
            whole(wo),
            pl.BlockSpec((width, cut), lambda i: (0, lax.rem(i, tiles))),
            pl.BlockSpec((cut, width), lambda i: (lax.rem(i, tiles), 0)),
            whole(gain),
            whole(bias),
            whole(w1),
            whole(w2),
            whole(mb),
            whole(og),
            whole(cg),
        ],
        out_specs=[spec for spec, _ in outs],
        out_shape=[shape for _, shape in outs],
        scratch_shapes=[
            pltpu.VMEM((tokens, width), F32),
            pltpu.VMEM((tokens, width), BF16),
            pltpu.VMEM((tokens, width), F32),
            pltpu.VMEM((tiles, tokens, cut), BF16),
            pltpu.VMEM((tiles, tokens, cut), F32),
            pltpu.VMEM((tokens, width), BF16),
        ],
        compiler_params=params(58),
        cost_estimate=pl.CostEstimate(
            flops=12 * tokens * width * hidden_units + 6 * tokens * width * width,
            bytes_accessed=12 * width * hidden_units + 4 * width * width + 20 * tokens * width,
            transcendentals=2 * tokens * hidden_units,
        ),
        name="feed",
    )(res, ctx, wo, win, wout, gain, bias, w1, w2, mb, og, cg)


def weight_kernel(n_ref, g_ref, o_ref):
    o_ref[...] = dot(n_ref[0], g_ref[0], TN).astype(BF16)


def project_weight_grad(normed, grads):
    _, tokens, width = normed.shape
    return pl.pallas_call(
        weight_kernel,
        grid=(3,),
        in_specs=[pl.BlockSpec((1, tokens, width), lambda i: (i, 0, 0))] * 2,
        out_specs=pl.BlockSpec((width, width), lambda i: (0, i)),
        out_shape=jax.ShapeDtypeStruct((width, 3 * width), BF16),
        compiler_params=params(32),
        cost_estimate=pl.CostEstimate(
            flops=6 * tokens * width * width,
            bytes_accessed=6 * width * width + 12 * tokens * width,
            transcendentals=0,
        ),
        name="project_weight_grad",
    )(normed, grads)


def front_back_kernel(
    e_ref,
    m_ref,
    gr_ref,
    w_ref,
    h_ref,
    g_ref,
    eg_ref,
    mg_ref,
    dgain_ref,
    dbias_ref,
    ng,
    st,
    *,
    strip,
):
    step = pl.program_id(0)
    count, tile, width = e_ref.shape
    chunk = 256
    inv = 1.0 / width
    mixes = m_ref[...].T

    @pl.when(step == 0)
    def _():
        dgain_ref[...] = jnp.zeros_like(dgain_ref)
        dbias_ref[...] = jnp.zeros_like(dbias_ref)

    for s in range(3):
        ng[s] = dot(gr_ref[s], w_ref[:, s * width : (s + 1) * width], NT)

    lane = lax.broadcasted_iota(jnp.int32, (strip, 4 * count), 1)
    collected = []
    for index in range(tile // strip):
        rows = slice(index * strip, (index + 1) * strip)
        mix = mixes[rows]
        for c in range(width // chunk):
            cols = slice(c * chunk, (c + 1) * chunk)
            parts = [e_ref[j, rows, cols].astype(F32) for j in range(count)]
            for s in range(3):
                total = parts[0] * mix[:, s * count : s * count + 1]
                for j in range(1, count):
                    total = total + parts[j] * mix[:, s * count + j : s * count + j + 1]
                st[s, :, cols] = total
        for s in range(3):
            v = st[s]
            dy = ng[s, rows]
            center = v - jnp.sum(v, axis=-1, keepdims=True) * inv
            spread = jnp.sum(center * center, axis=-1, keepdims=True) * inv
            scale = lax.rsqrt(spread + EPSILON)
            hat = center * scale
            dgain_ref[s : s + 1] += jnp.sum(dy * hat, axis=0, keepdims=True)
            dbias_ref[s : s + 1] += jnp.sum(dy, axis=0, keepdims=True)
            dh = dy * g_ref[s : s + 1]
            first = jnp.sum(dh, axis=-1, keepdims=True) * inv
            second = jnp.sum(dh * hat, axis=-1, keepdims=True) * inv
            st[s] = scale * (dh - first - hat * second)
        st[3] = h_ref[rows]
        sums = [[None] * count for _ in range(4)]
        for c in range(width // chunk):
            cols = slice(c * chunk, (c + 1) * chunk)
            grads = [st[s, :, cols] for s in range(4)]
            for j in range(count):
                e = e_ref[j, rows, cols].astype(F32)
                total = grads[0] * mix[:, j : j + 1]
                for s in range(1, 4):
                    total = total + grads[s] * mix[:, s * count + j : s * count + j + 1]
                eg_ref[j, rows, cols] = total.astype(BF16)
                for s in range(4):
                    product = e * grads[s]
                    product = product[:, :LANES] + product[:, LANES:]
                    sums[s][j] = product if sums[s][j] is None else sums[s][j] + product
        out = jnp.zeros((strip, 4 * count), F32)
        for s in range(4):
            for j in range(count):
                one = jnp.sum(sums[s][j], axis=-1, keepdims=True)
                out = jnp.where(lane == s * count + j, one, out)
        collected.append(out)
    mg_ref[...] = jnp.concatenate(collected, axis=0).T


def front_back(e, mix, grads, w, hgrad, gain):
    count, tokens, width = e.shape
    tile = 128
    strip = 16
    return pl.pallas_call(
        functools.partial(front_back_kernel, strip=strip),
        grid=(tokens // tile,),
        in_specs=[
            pl.BlockSpec((count, tile, width), lambda i: (0, i, 0)),
            pl.BlockSpec((4 * count, tile), lambda i: (0, i)),
            pl.BlockSpec((3, tile, width), lambda i: (0, i, 0)),
            once(w.shape, lambda i: (0, 0)),
            pl.BlockSpec((tile, width), lambda i: (i, 0)),
            pl.BlockSpec((4, width), lambda i: (0, 0)),
        ],
        out_specs=[
            pl.BlockSpec((count, tile, width), lambda i: (0, i, 0)),
            pl.BlockSpec((4 * count, tile), lambda i: (0, i)),
            pl.BlockSpec((3, width), lambda i: (0, 0)),
            pl.BlockSpec((3, width), lambda i: (0, 0)),
        ],
        out_shape=[
            jax.ShapeDtypeStruct((count, tokens, width), BF16),
            jax.ShapeDtypeStruct((4 * count, tokens), F32),
            jax.ShapeDtypeStruct((3, width), F32),
            jax.ShapeDtypeStruct((3, width), F32),
        ],
        scratch_shapes=[
            pltpu.VMEM((3, tile, width), F32),
            pltpu.VMEM((4, strip, width), F32),
        ],
        compiler_params=params(48),
        cost_estimate=pl.CostEstimate(
            flops=6 * tokens * width * width + 200 * tokens * width,
            bytes_accessed=6 * width * width + 42 * tokens * width,
            transcendentals=0,
        ),
        name="front_back",
    )(e, mix, grads, w, hgrad, gain)


def body(
    earlier,
    mix_in,
    segment_ids,
    attn_qkv,
    attn_out,
    mlp_in,
    mlp_out,
    norm_gain,
    norm_bias,
    mix_w1,
    mix_w2,
    mix_bias,
    out_grad,
    coef_grad,
):
    count, seqs, _, block, width = earlier.shape
    n = lax.axis_size("ctx")
    tokens = seqs * 2 * block
    length = 2 * n * block
    me = lax.axis_index("ctx")

    e = earlier.reshape(count, tokens, width)
    mix = mix_in.reshape(4 * count, tokens)
    og = out_grad.reshape(tokens, width)
    cg = coef_grad.reshape(-1, tokens)

    late = segment_ids[:, 1].reshape(seqs, n, block)[:, ::-1].reshape(seqs, n * block)
    placed = jnp.concatenate([segment_ids[:, 0], late], axis=1)
    column = placed[:, :, None]
    row = placed[:, None, :]

    cosine, sine = (jnp.asarray(table) for table in turn_tables(length))

    def own_rows(table):
        return jnp.concatenate(
            [
                lax.dynamic_slice_in_dim(table, me * block, block, 0),
                lax.dynamic_slice_in_dim(table, (2 * n - 1 - me) * block, block, 0),
            ],
            axis=0,
        )

    w_qkv = lax.all_gather(attn_qkv, "fsdp", axis=0, tiled=True)
    w_o = lax.all_gather(attn_out, "fsdp", axis=0, tiled=True)
    w_in = lax.all_gather(mlp_in, "fsdp", axis=0, tiled=True)
    w_out = lax.all_gather(mlp_out, "fsdp", axis=0, tiled=True)

    normed, residual = front(e, mix, norm_gain, norm_bias)
    shares = project(normed, w_qkv, own_rows(cosine), own_rows(sine), n)
    qkv = to_heads(shares, n, seqs, block, 0)
    heads = attend(qkv, column, row)
    context = to_tokens(heads, n, block, 1)[0]
    (
        layer_out,
        coefs,
        d_in,
        d_out,
        d_o,
        context_grad,
        hidden_grad,
        d_gain,
        d_bias,
        d_w1,
        d_w2,
        d_mb,
    ) = feed(
        residual,
        context,
        w_o,
        w_in,
        w_out,
        norm_gain,
        norm_bias,
        mix_w1,
        mix_w2,
        mix_bias[:, None],
        og,
        cg,
    )
    groups = context_grad.reshape(tokens, n, width // n).transpose(1, 0, 2)[None]
    grad_heads = to_heads(groups, n, seqs, block, 2)
    turned_back = attend_back(qkv, grad_heads, column, row, cosine, sine)
    grads = to_tokens(turned_back, n, block, 3)
    d_qkv = project_weight_grad(normed, grads)
    e_grad, m_grad, f_gain, f_bias = front_back(e, mix, grads, w_qkv, hidden_grad, norm_gain)

    owned = []
    for grad in (d_qkv, d_o, d_in, d_out):
        own = lax.psum_scatter(grad, "fsdp", scatter_dimension=0, tiled=True)
        owned.append(own)
    owned = [v.astype(F32) for v in lax.psum(tuple(owned), "ctx")]
    gain_grad = jnp.concatenate([f_gain, d_gain], axis=0)
    bias_grad = jnp.concatenate([f_bias, d_bias], axis=0)
    small = lax.psum((gain_grad, bias_grad, d_w1, d_w2, d_mb[:, 0]), ("ctx", "fsdp"))

    return (
        layer_out.reshape(seqs, 2, block, width),
        coefs.reshape(4, -1, seqs, 2, block),
        e_grad.reshape(count, seqs, 2, block, width),
        m_grad.reshape(4, count, seqs, 2, block),
        owned[0],
        owned[1],
        owned[2],
        owned[3],
        small[0],
        small[1],
        small[2],
        small[3],
        small[4],
    )


def solution(mesh):
    in_specs = (
        P(None, "fsdp", None, "ctx", None),
        P(None, None, "fsdp", None, "ctx"),
        P("fsdp", None, None),
        P("fsdp", None),
        P("fsdp", None),
        P("fsdp", None),
        P("fsdp", None),
        P(),
        P(),
        P(),
        P(),
        P(),
        P("fsdp", None, "ctx", None),
        P(None, None, "fsdp", None, "ctx"),
    )
    out_specs = (
        P("fsdp", None, "ctx", None),
        P(None, None, "fsdp", None, "ctx"),
        P(None, "fsdp", None, "ctx", None),
        P(None, None, "fsdp", None, "ctx"),
        P("fsdp", None),
        P("fsdp", None),
        P("fsdp", None),
        P("fsdp", None),
        P(),
        P(),
        P(),
        P(),
        P(),
    )
    return jax.shard_map(body, mesh=mesh, in_specs=in_specs, out_specs=out_specs, check_vma=False)
```

```python
import functools
import math

import jax
import jax.numpy as jnp
import numpy as np
from jax import lax
from jax.experimental import pallas as pl
from jax.experimental.pallas import tpu as pltpu
from jax.sharding import PartitionSpec as P

HD = 64
ROT = 16
LANES = 128
EPSILON = 1e-05
RMS_EPSILON = 1e-06
MASKED = -1e30
F32 = jnp.float32
BF16 = jnp.bfloat16
MESH = pl.DeviceIdType.MESH
MIB = 1024 * 1024

NN = (((1,), (0,)), ((), ()))
NT = (((1,), (1,)), ((), ()))
TN = (((0,), (0,)), ((), ()))

ERFC_RATE = 0.4
ERFC = (
    0.22567586600780487,
    0.22566929459571838,
    0.20784726738929749,
    0.16851142048835754,
    0.1415392905473709,
    -0.005822250619530678,
    0.16932761669158936,
    -0.18304575979709625,
    0.05029737576842308,
)


def dot(a, b, dims=NN):
    return lax.dot_general(a, b, dims, preferred_element_type=F32)


def gelu_and_slope(v):
    z = jnp.abs(v) * math.sqrt(0.5)
    bell = jnp.exp(-0.5 * v * v)
    t = 1.0 / (1.0 + ERFC_RATE * z)
    poly = jnp.full_like(t, ERFC[-1])
    for coefficient in ERFC[-2::-1]:
        poly = poly * t + coefficient
    tail = 0.5 * poly * t * bell
    phi = jnp.where(v >= 0.0, 1.0 - tail, tail)
    return v * phi, phi + v * bell * (1.0 / math.sqrt(2.0 * math.pi))


def params(limit_mib, **more):
    return pltpu.CompilerParams(vmem_limit_bytes=limit_mib * MIB, **more)


def once(shape, index):
    return pl.BlockSpec(shape, index, pipeline_mode=pl.Buffered(1))


def front_kernel(e_ref, m_ref, g_ref, b_ref, n_ref, r_ref, s_ref, *, strip):
    tile = e_ref.shape[1]
    width = e_ref.shape[2]
    count = e_ref.shape[0]
    chunk = 256
    mixes = m_ref[...].T

    for strip_index in range(tile // strip):
        rows = slice(strip_index * strip, (strip_index + 1) * strip)
        mix = mixes[rows]
        for c in range(width // chunk):
            cols = slice(c * chunk, (c + 1) * chunk)
            parts = [e_ref[j, rows, cols].astype(F32) for j in range(count)]
            for s in range(4):
                total = parts[0] * mix[:, s * count : s * count + 1]
                for j in range(1, count):
                    total = total + parts[j] * mix[:, s * count + j : s * count + j + 1]
                if s < 3:
                    s_ref[s, :, cols] = total
                else:
                    r_ref[rows, cols] = total
        for s in range(3):
            v = s_ref[s]
            center = v - jnp.mean(v, axis=-1, keepdims=True)
            spread = jnp.mean(center * center, axis=-1, keepdims=True)
            out = center * lax.rsqrt(spread + EPSILON) * g_ref[s : s + 1] + b_ref[s : s + 1]
            n_ref[s, rows] = out.astype(BF16)


def front(e, mix, gain, bias):
    count, tokens, width = e.shape
    tile = 128
    strip = 16
    return pl.pallas_call(
        functools.partial(front_kernel, strip=strip),
        grid=(tokens // tile,),
        in_specs=[
            pl.BlockSpec((count, tile, width), lambda i: (0, i, 0)),
            pl.BlockSpec((4 * count, tile), lambda i: (0, i)),
            pl.BlockSpec((4, width), lambda i: (0, 0)),
            pl.BlockSpec((4, width), lambda i: (0, 0)),
        ],
        out_specs=[
            pl.BlockSpec((3, tile, width), lambda i: (0, i, 0)),
            pl.BlockSpec((tile, width), lambda i: (i, 0)),
        ],
        out_shape=[
            jax.ShapeDtypeStruct((3, tokens, width), BF16),
            jax.ShapeDtypeStruct((tokens, width), F32),
        ],
        scratch_shapes=[pltpu.VMEM((3, strip, width), F32)],
        compiler_params=params(32),
        cost_estimate=pl.CostEstimate(
            flops=64 * tokens * width, bytes_accessed=26 * tokens * width, transcendentals=0
        ),
        name="front",
    )(e, mix, gain, bias)


def turn_tables(length):
    half = ROT // 2
    frequency = 10000.0 ** (-(np.arange(half) * 2.0 / ROT))
    angle = np.arange(length)[:, None] * frequency[None, :]
    lane = np.arange(LANES) % HD
    cosine = np.ones((length, LANES), np.float32)
    sine = np.zeros((length, LANES), np.float32)
    for k in range(LANES):
        if lane[k] < ROT:
            cosine[:, k] = np.cos(angle[:, lane[k] % half])
            sign = -1.0 if lane[k] < half else 1.0
            sine[:, k] = sign * np.sin(angle[:, lane[k] % half])
    return cosine, sine


def turned(x, cosine, sine):
    half = ROT // 2
    lane = lax.broadcasted_iota(jnp.int32, x.shape, 1) % HD
    other = jnp.where(
        lane < half, pltpu.roll(x, LANES - half, axis=1), pltpu.roll(x, half, axis=1)
    )
    return x * cosine + other * sine


def qkv_kernel(n_ref, w_ref, c_ref, s_ref, out_ref, x_ref):
    which = pl.program_id(0)
    tokens = n_ref.shape[1]
    width = w_ref.shape[1]
    group = out_ref.shape[3]
    seq_rows = c_ref.shape[0]
    x_ref[...] = dot(n_ref[0], w_ref[...])

    @pl.when(which < 2)
    def _():
        cosine = c_ref[...]
        sine = s_ref[...]
        for s in range(tokens // seq_rows):
            rows = slice(s * seq_rows, (s + 1) * seq_rows)
            for c in range(width // LANES):
                cols = slice(c * LANES, (c + 1) * LANES)
                y = turned(x_ref[rows, cols], cosine, sine).astype(BF16)
                to = c * LANES % group
                out_ref[0, c * LANES // group, rows, to : to + LANES] = y

    @pl.when(which == 2)
    def _():
        for g in range(width // group):
            out_ref[0, g] = x_ref[:, g * group : (g + 1) * group].astype(BF16)


def project(normed, w, cosine, sine, groups):
    _, tokens, width = normed.shape
    group = width // groups
    cut = max(group, 512)
    inner = width // cut
    return pl.pallas_call(
        qkv_kernel,
        grid=(3, inner),
        in_specs=[
            pl.BlockSpec((1, tokens, width), lambda i, j: (i, 0, 0)),
            pl.BlockSpec((width, cut), lambda i, j: (0, i * inner + j)),
            pl.BlockSpec(cosine.shape, lambda i, j: (0, 0)),
            pl.BlockSpec(sine.shape, lambda i, j: (0, 0)),
        ],
        out_specs=pl.BlockSpec((1, cut // group, tokens, group), lambda i, j: (i, j, 0, 0)),
        out_shape=jax.ShapeDtypeStruct((3, groups, tokens, group), BF16),
        scratch_shapes=[pltpu.VMEM((tokens, cut), F32)],
        compiler_params=params(32),
        cost_estimate=pl.CostEstimate(
            flops=6 * tokens * width * width,
            bytes_accessed=6 * width * width + 12 * tokens * width,
            transcendentals=0,
        ),
        name="project",
    )(normed, w, cosine, sine)


def greet(n):
    me = lax.axis_index("ctx")
    barrier = pltpu.get_barrier_semaphore()
    for k in range(1, n):
        pl.semaphore_signal(
            barrier, inc=1, device_id={"ctx": lax.rem(me + k, n)}, device_id_type=MESH
        )
    pl.semaphore_wait(barrier, n - 1)


def to_heads_kernel(n, x_ref, o_ref, send, recv, own):
    me = lax.axis_index("ctx")
    spots = (me, 2 * n - 1 - me)
    kept = []
    for h in range(2):
        copy = pltpu.make_async_copy(x_ref.at[:, me, :, h], o_ref.at[:, :, spots[h]], own.at[h])
        copy.start()
        kept.append(copy)
    greet(n)
    sent = []
    for k in range(1, n):
        to = lax.rem(me + k, n)
        for h in range(2):
            slot = 2 * (k - 1) + h
            copy = pltpu.make_async_remote_copy(
                src_ref=x_ref.at[:, to, :, h],
                dst_ref=o_ref.at[:, :, spots[h]],
                send_sem=send.at[slot],
                recv_sem=recv.at[slot],
                device_id={"ctx": to},
                device_id_type=MESH,
            )
            copy.start()
            sent.append(copy)
    for copy in kept + sent:
        copy.wait()


def to_heads(x, n, seqs, block, collective):
    kinds, _, _, cols = x.shape
    view = x.reshape(kinds, n, seqs, 2, block, cols)
    out = pl.pallas_call(
        functools.partial(to_heads_kernel, n),
        in_specs=[pl.BlockSpec(memory_space=pltpu.HBM)],
        out_specs=pl.BlockSpec(memory_space=pltpu.HBM),
        out_shape=jax.ShapeDtypeStruct((kinds, seqs, 2 * n, block, cols), BF16),
        scratch_shapes=[
            pltpu.SemaphoreType.DMA((2 * n - 2,)),
            pltpu.SemaphoreType.DMA((2 * n - 2,)),
            pltpu.SemaphoreType.DMA((2,)),
        ],
        compiler_params=params(1, collective_id=collective, has_side_effects=True),
        name="to_heads",
    )(view)
    return out.reshape(kinds, seqs, 2 * n * block, cols)


def to_tokens_kernel(n, x_ref, o_ref, send, recv, own):
    me = lax.axis_index("ctx")
    cols = x_ref.shape[4]
    mine = pl.ds(pl.multiple_of(me * cols, LANES), cols)
    kept = []
    for h in range(2):
        spot = me if h == 0 else 2 * n - 1 - me
        copy = pltpu.make_async_copy(
            x_ref.at[:, :, spot], o_ref.at[:, :, h, :, mine], own.at[h]
        )
        copy.start()
        kept.append(copy)
    greet(n)
    sent = []
    for k in range(1, n):
        to = lax.rem(me + k, n)
        for h in range(2):
            spot = to if h == 0 else 2 * n - 1 - to
            slot = 2 * (k - 1) + h
            copy = pltpu.make_async_remote_copy(
                src_ref=x_ref.at[:, :, spot],
                dst_ref=o_ref.at[:, :, h, :, mine],
                send_sem=send.at[slot],
                recv_sem=recv.at[slot],
                device_id={"ctx": to},
                device_id_type=MESH,
            )
            copy.start()
            sent.append(copy)
    for copy in kept + sent:
        copy.wait()


def to_tokens(x, n, block, collective):
    kinds, seqs, length, cols = x.shape
    view = x.reshape(kinds, seqs, 2 * n, block, cols)
    out = pl.pallas_call(
        functools.partial(to_tokens_kernel, n),
        in_specs=[pl.BlockSpec(memory_space=pltpu.HBM)],
        out_specs=pl.BlockSpec(memory_space=pltpu.HBM),
        out_shape=jax.ShapeDtypeStruct((kinds, seqs, 2, block, n * cols), BF16),
        scratch_shapes=[
            pltpu.SemaphoreType.DMA((2 * n - 2,)),
            pltpu.SemaphoreType.DMA((2 * n - 2,)),
            pltpu.SemaphoreType.DMA((2,)),
        ],
        compiler_params=params(1, collective_id=collective, has_side_effects=True),
        name="to_tokens",
    )(view)
    return out.reshape(kinds, seqs * 2 * block, n * cols)


def row_tile(length):
    return min(256, length)


def head_lanes(shape, h):
    lane = lax.broadcasted_iota(jnp.int32, shape, 1)
    return (lane >= h * HD) & (lane < (h + 1) * HD)


def only(x, h):
    return jnp.where(head_lanes(x.shape, h), x, jnp.zeros_like(x))


def allowed_here(column_ref, row_ref, first, rows):
    until = first + rows
    shape = (rows, until)
    query = first + lax.broadcasted_iota(jnp.int32, shape, 0)
    key = lax.broadcasted_iota(jnp.int32, shape, 1)
    same = column_ref[0, first:until, 0:1] == row_ref[0, 0:1, 0:until]
    return same & (key <= query)


def attend_kernel(q_ref, k_ref, v_ref, column_ref, row_ref, o_ref):
    length = q_ref.shape[2]
    rows = row_tile(length)
    for i in range(length // rows):
        first, until = i * rows, (i + 1) * rows
        allowed = allowed_here(column_ref, row_ref, first, rows)
        q = q_ref[0, 0, first:until] * BF16(HD**-0.5)
        k = k_ref[0, 0, 0:until]
        v = v_ref[0, 0, 0:until]
        total = None
        for h in range(LANES // HD):
            scores = jnp.where(allowed, dot(only(q, h), k, NT), MASKED)
            peak = jnp.max(scores, axis=-1, keepdims=True)
            raised = jnp.exp(scores - peak)
            mass = jnp.sum(raised, axis=-1, keepdims=True)
            probs = (raised * (1.0 / mass)).astype(BF16)
            part = dot(probs, v)
            part = jnp.where(head_lanes(part.shape, h), part, 0.0)
            total = part if total is None else total + part
        o_ref[0, 0, first:until] = total.astype(BF16)


def attend(qkv, column, row):
    _, seqs, length, cols = qkv.shape
    pairs = cols // LANES

    def spec(kind):
        return pl.BlockSpec((1, 1, length, LANES), lambda s, p: (kind, s, 0, p))

    return pl.pallas_call(
        attend_kernel,
        grid=(seqs, pairs),
        in_specs=[
            spec(0),
            spec(1),
            spec(2),
            pl.BlockSpec((1, length, 1), lambda s, p: (s, 0, 0)),
            pl.BlockSpec((1, 1, length), lambda s, p: (s, 0, 0)),
        ],
        out_specs=spec(0),
        out_shape=jax.ShapeDtypeStruct((1, seqs, length, cols), BF16),
        compiler_params=params(32),
        cost_estimate=pl.CostEstimate(
            flops=4 * seqs * length * length * cols,
            bytes_accessed=8 * seqs * length * cols,
            transcendentals=seqs * length * length * cols // 128,
        ),
        name="attend",
    )(qkv, qkv, qkv, column, row)


def attend_back_kernel(
    q_ref, k_ref, v_ref, g_ref, column_ref, row_ref, c_ref, s_ref, o_ref, dk_ref, dv_ref
):
    length = q_ref.shape[2]
    rows = row_tile(length)
    factor = HD**-0.5
    for i in range(length // rows):
        here = slice(i * rows, (i + 1) * rows)
        dk_ref[here] = jnp.zeros((rows, LANES), F32)
        dv_ref[here] = jnp.zeros((rows, LANES), F32)
    for i in range(length // rows):
        first, until = i * rows, (i + 1) * rows
        allowed = allowed_here(column_ref, row_ref, first, rows)
        q = q_ref[0, 0, first:until] * BF16(factor)
        g = g_ref[0, 0, first:until]
        k = k_ref[0, 0, 0:until]
        v = v_ref[0, 0, 0:until]
        total = None
        for h in range(LANES // HD):
            q_h = only(q, h)
            g_h = only(g, h)
            scores = jnp.where(allowed, dot(q_h, k, NT), MASKED)
            peak = jnp.max(scores, axis=-1, keepdims=True)
            raised = jnp.exp(scores - peak)
            mass = jnp.sum(raised, axis=-1, keepdims=True)
            probs = raised * (1.0 / mass)
            dots = dot(g_h, v, NT)
            center = jnp.sum(probs * dots, axis=-1, keepdims=True)
            slope = (probs * (dots - center)).astype(BF16)
            part = dot(slope, k)
            part = jnp.where(head_lanes(part.shape, h), part, 0.0)
            total = part if total is None else total + part
            dk_ref[0:until] += dot(slope, q_h, TN)
            dv_ref[0:until] += dot(probs.astype(BF16), g_h, TN)
        cosine, sine = c_ref[first:until], s_ref[first:until]
        o_ref[0, 0, first:until] = turned(total * factor, cosine, -sine).astype(BF16)
    for i in range(length // rows):
        here = slice(i * rows, (i + 1) * rows)
        o_ref[1, 0, here] = turned(dk_ref[here], c_ref[here], -s_ref[here]).astype(BF16)
        o_ref[2, 0, here] = dv_ref[here].astype(BF16)


def attend_back(qkv, grad, column, row, cosine, sine):
    _, seqs, length, cols = qkv.shape
    pairs = cols // LANES

    def spec(kind):
        return pl.BlockSpec((1, 1, length, LANES), lambda s, p: (kind, s, 0, p))

    return pl.pallas_call(
        attend_back_kernel,
        grid=(seqs, pairs),
        in_specs=[
            spec(0),
            spec(1),
            spec(2),
            spec(0),
            pl.BlockSpec((1, length, 1), lambda s, p: (s, 0, 0)),
            pl.BlockSpec((1, 1, length), lambda s, p: (s, 0, 0)),
            pl.BlockSpec((length, LANES), lambda s, p: (0, 0)),
            pl.BlockSpec((length, LANES), lambda s, p: (0, 0)),
        ],
        out_specs=pl.BlockSpec((3, 1, length, LANES), lambda s, p: (0, s, 0, p)),
        out_shape=jax.ShapeDtypeStruct((3, seqs, length, cols), BF16),
        scratch_shapes=[pltpu.VMEM((length, LANES), F32), pltpu.VMEM((length, LANES), F32)],
        compiler_params=params(40),
        cost_estimate=pl.CostEstimate(
            flops=10 * seqs * length * length * cols,
            bytes_accessed=14 * seqs * length * cols,
            transcendentals=seqs * length * length * cols // 128,
        ),
        name="attend_back",
    )(qkv, qkv, qkv, grad, column, row, cosine, sine)


def feed_kernel(
    res_ref,
    ctx_ref,
    wo_ref,
    win_ref,
    wout_ref,
    g_ref,
    b_ref,
    w1_ref,
    w2_ref,
    mb_ref,
    og_ref,
    cg_ref,
    out_ref,
    coef_ref,
    dwin_ref,
    dwout_ref,
    dwo_ref,
    cgrad_ref,
    hgrad_ref,
    dgain_ref,
    dbias_ref,
    dw1_ref,
    dw2_ref,
    dmb_ref,
    hidden,
    normed,
    total,
    active,
    slope,
    branch,
    *,
    tiles,
    strip,
):
    step = pl.program_id(0)
    tokens, width = res_ref.shape
    cut = win_ref.shape[1]
    inv = 1.0 / width

    @pl.when(step == 0)
    def _():
        hidden[...] = dot(ctx_ref[...], wo_ref[...])

        @pl.loop(0, tokens // strip)
        def _(i):
            rows = pl.ds(pl.multiple_of(i * strip, strip), strip)
            v = hidden[rows] + res_ref[rows]
            hidden[rows] = v
            center = v - jnp.sum(v, axis=-1, keepdims=True) * inv
            spread = jnp.sum(center * center, axis=-1, keepdims=True) * inv
            hat = center * lax.rsqrt(spread + EPSILON)
            normed[rows] = (hat * g_ref[3:4] + b_ref[3:4]).astype(BF16)
            total[rows] = v

    @pl.when(step < tiles)
    def _():
        half = tokens // 2
        for part in range(2):
            rows = slice(part * half, (part + 1) * half)
            up = dot(normed[rows], win_ref[...])
            value, rate = gelu_and_slope(up)
            low = value.astype(BF16)
            active[step, rows] = low
            slope[step, rows] = rate
            total[rows] += dot(low, wout_ref[...])

    @pl.when(step == tiles - 1)
    def _():
        w1 = w1_ref[...]
        w2 = w2_ref[...]
        out_ref[...] = total[...].astype(BF16)
        dw1_ref[...] = jnp.zeros_like(dw1_ref)
        dw2_ref[...] = jnp.zeros_like(dw2_ref)
        dmb_ref[...] = jnp.zeros_like(dmb_ref)

        for i in range(tokens // LANES):
            rows = slice(i * LANES, (i + 1) * LANES)
            v = total[rows]
            scale = lax.rsqrt(jnp.sum(v * v, axis=-1, keepdims=True) * inv + RMS_EPSILON)
            r = v * scale
            r_high = r.astype(BF16)
            r_rest = (r - r_high.astype(F32)).astype(BF16)
            z = dot(w1, r_high, NT) + dot(w1, r_rest, NT)
            value, rate = gelu_and_slope(z)
            v_high = value.astype(BF16)
            v_rest = (value - v_high.astype(F32)).astype(BF16)
            coef_ref[:, rows] = dot(w2, v_high, TN) + dot(w2, v_rest, TN) + mb_ref[...]
            cg = cg_ref[:, rows]
            c_high = cg.astype(BF16)
            c_rest = (cg - c_high.astype(F32)).astype(BF16)
            dmb_ref[...] += jnp.sum(cg, axis=-1, keepdims=True)
            dw2_ref[...] += dot(v_high, c_high, NT) + dot(v_rest, c_high, NT) + dot(v_high, c_rest, NT)
            dz = (dot(w2, c_high) + dot(w2, c_rest)) * rate
            z_high = dz.astype(BF16)
            z_rest = (dz - z_high.astype(F32)).astype(BF16)
            dw1_ref[...] += dot(z_high, r_high) + dot(z_high, r_rest) + dot(z_rest, r_high)
            dr = dot(z_high, w1, TN) + dot(z_rest, w1, TN)
            mean = jnp.sum(dr * r, axis=-1, keepdims=True) * inv
            grad = scale * (dr - r * mean) + og_ref[rows].astype(F32)
            hgrad_ref[rows] = grad
            branch[rows] = grad.astype(BF16)
            total[rows] = jnp.zeros_like(v)

    @pl.when(step >= tiles)
    def _():
        j = step - tiles
        half = tokens // 2
        for part in range(2):
            rows = slice(part * half, (part + 1) * half)
            back = dot(branch[rows], wout_ref[...], NT)
            low = (back * slope[j, rows]).astype(BF16)
            total[rows] += dot(low, win_ref[...], NT)
            slope[j, rows] = low.astype(F32)
        dwout_ref[...] = dot(active[j], branch[...], TN).astype(BF16)
        dwin_ref[...] = dot(normed[...], slope[j].astype(BF16), TN).astype(BF16)

    @pl.when(step == 2 * tiles - 1)
    def _():
        dgain_ref[...] = jnp.zeros_like(dgain_ref)
        dbias_ref[...] = jnp.zeros_like(dbias_ref)

        @pl.loop(0, tokens // strip)
        def _(i):
            rows = pl.ds(pl.multiple_of(i * strip, strip), strip)
            v = hidden[rows]
            dy = total[rows]
            center = v - jnp.sum(v, axis=-1, keepdims=True) * inv
            spread = jnp.sum(center * center, axis=-1, keepdims=True) * inv
            scale = lax.rsqrt(spread + EPSILON)
            hat = center * scale
            dgain_ref[...] += jnp.sum(dy * hat, axis=0, keepdims=True)
            dbias_ref[...] += jnp.sum(dy, axis=0, keepdims=True)
            dh = dy * g_ref[3:4]
            first = jnp.sum(dh, axis=-1, keepdims=True) * inv
            second = jnp.sum(dh * hat, axis=-1, keepdims=True) * inv
            grad = hgrad_ref[rows] + scale * (dh - first - hat * second)
            hgrad_ref[rows] = grad
            branch[rows] = grad.astype(BF16)

        dwo_ref[...] = dot(ctx_ref[...], branch[...], TN).astype(BF16)
        groups, _, group = cgrad_ref.shape
        for i in range(groups):
            rows = slice(i * group, (i + 1) * group)
            cgrad_ref[i] = dot(branch[...], wo_ref[rows], NT).astype(BF16)


def feed(res, ctx, wo, win, wout, gain, bias, w1, w2, mb, og, cg, groups):
    tokens, width = res.shape
    hidden_units = win.shape[1]
    cut = 512
    tiles = hidden_units // cut
    small, coefs = w1.shape[0], w2.shape[1]

    def whole(x):
        zeros = (0,) * x.ndim
        return once(x.shape, lambda i: zeros)

    def result(shape, dtype=F32):
        zeros = (0,) * len(shape)
        return once(shape, lambda i: zeros), jax.ShapeDtypeStruct(shape, dtype)

    def back(i):
        return jnp.maximum(i - tiles, 0)

    outs = [
        result((tokens, width), BF16),
        result((coefs, tokens)),
        (
            pl.BlockSpec((width, cut), lambda i: (0, back(i))),
            jax.ShapeDtypeStruct((width, hidden_units), BF16),
        ),
        (
            pl.BlockSpec((cut, width), lambda i: (back(i), 0)),
            jax.ShapeDtypeStruct((hidden_units, width), BF16),
        ),
        result((width, width), BF16),
        result((groups, tokens, width // groups), BF16),
        result((tokens, width)),
        result((1, width)),
        result((1, width)),
        result((small, width)),
        result((small, coefs)),
        result((coefs, 1)),
    ]
    return pl.pallas_call(
        functools.partial(feed_kernel, tiles=tiles, strip=32),
        grid=(2 * tiles,),
        in_specs=[
            whole(res),
            whole(ctx),
            whole(wo),
            pl.BlockSpec((width, cut), lambda i: (0, lax.rem(i, tiles))),
            pl.BlockSpec((cut, width), lambda i: (lax.rem(i, tiles), 0)),
            whole(gain),
            whole(bias),
            whole(w1),
            whole(w2),
            whole(mb),
            whole(og),
            whole(cg),
        ],
        out_specs=[spec for spec, _ in outs],
        out_shape=[shape for _, shape in outs],
        scratch_shapes=[
            pltpu.VMEM((tokens, width), F32),
            pltpu.VMEM((tokens, width), BF16),
            pltpu.VMEM((tokens, width), F32),
            pltpu.VMEM((tiles, tokens, cut), BF16),
            pltpu.VMEM((tiles, tokens, cut), F32),
            pltpu.VMEM((tokens, width), BF16),
        ],
        compiler_params=params(58),
        cost_estimate=pl.CostEstimate(
            flops=12 * tokens * width * hidden_units + 6 * tokens * width * width,
            bytes_accessed=12 * width * hidden_units + 4 * width * width + 20 * tokens * width,
            transcendentals=2 * tokens * hidden_units,
        ),
        name="feed",
    )(res, ctx, wo, win, wout, gain, bias, w1, w2, mb, og, cg)


def weight_kernel(n_ref, g_ref, o_ref):
    o_ref[...] = dot(n_ref[0], g_ref[0], TN).astype(BF16)


def project_weight_grad(normed, grads):
    _, tokens, width = normed.shape
    return pl.pallas_call(
        weight_kernel,
        grid=(3,),
        in_specs=[pl.BlockSpec((1, tokens, width), lambda i: (i, 0, 0))] * 2,
        out_specs=pl.BlockSpec((width, width), lambda i: (0, i)),
        out_shape=jax.ShapeDtypeStruct((width, 3 * width), BF16),
        compiler_params=params(32),
        cost_estimate=pl.CostEstimate(
            flops=6 * tokens * width * width,
            bytes_accessed=6 * width * width + 12 * tokens * width,
            transcendentals=0,
        ),
        name="project_weight_grad",
    )(normed, grads)


def front_back_kernel(
    e_ref,
    m_ref,
    gr_ref,
    w_ref,
    h_ref,
    g_ref,
    eg_ref,
    mg_ref,
    dgain_ref,
    dbias_ref,
    ng,
    st,
    *,
    strip,
):
    step = pl.program_id(0)
    count, tile, width = e_ref.shape
    chunk = 256
    inv = 1.0 / width
    mixes = m_ref[...].T

    @pl.when(step == 0)
    def _():
        dgain_ref[...] = jnp.zeros_like(dgain_ref)
        dbias_ref[...] = jnp.zeros_like(dbias_ref)

    for s in range(3):
        ng[s] = dot(gr_ref[s], w_ref[:, s * width : (s + 1) * width], NT)

    lane = lax.broadcasted_iota(jnp.int32, (strip, 4 * count), 1)
    collected = []
    for index in range(tile // strip):
        rows = slice(index * strip, (index + 1) * strip)
        mix = mixes[rows]
        for c in range(width // chunk):
            cols = slice(c * chunk, (c + 1) * chunk)
            parts = [e_ref[j, rows, cols].astype(F32) for j in range(count)]
            for s in range(3):
                total = parts[0] * mix[:, s * count : s * count + 1]
                for j in range(1, count):
                    total = total + parts[j] * mix[:, s * count + j : s * count + j + 1]
                st[s, :, cols] = total
        for s in range(3):
            v = st[s]
            dy = ng[s, rows]
            center = v - jnp.sum(v, axis=-1, keepdims=True) * inv
            spread = jnp.sum(center * center, axis=-1, keepdims=True) * inv
            scale = lax.rsqrt(spread + EPSILON)
            hat = center * scale
            dgain_ref[s : s + 1] += jnp.sum(dy * hat, axis=0, keepdims=True)
            dbias_ref[s : s + 1] += jnp.sum(dy, axis=0, keepdims=True)
            dh = dy * g_ref[s : s + 1]
            first = jnp.sum(dh, axis=-1, keepdims=True) * inv
            second = jnp.sum(dh * hat, axis=-1, keepdims=True) * inv
            st[s] = scale * (dh - first - hat * second)
        st[3] = h_ref[rows]
        sums = [[None] * count for _ in range(4)]
        for c in range(width // chunk):
            cols = slice(c * chunk, (c + 1) * chunk)
            grads = [st[s, :, cols] for s in range(4)]
            for j in range(count):
                e = e_ref[j, rows, cols].astype(F32)
                total = grads[0] * mix[:, j : j + 1]
                for s in range(1, 4):
                    total = total + grads[s] * mix[:, s * count + j : s * count + j + 1]
                eg_ref[j, rows, cols] = total.astype(BF16)
                for s in range(4):
                    product = e * grads[s]
                    product = product[:, :LANES] + product[:, LANES:]
                    sums[s][j] = product if sums[s][j] is None else sums[s][j] + product
        out = jnp.zeros((strip, 4 * count), F32)
        for s in range(4):
            for j in range(count):
                one = jnp.sum(sums[s][j], axis=-1, keepdims=True)
                out = jnp.where(lane == s * count + j, one, out)
        collected.append(out)
    mg_ref[...] = jnp.concatenate(collected, axis=0).T


def front_back(e, mix, grads, w, hgrad, gain):
    count, tokens, width = e.shape
    tile = 128
    strip = 16
    return pl.pallas_call(
        functools.partial(front_back_kernel, strip=strip),
        grid=(tokens // tile,),
        in_specs=[
            pl.BlockSpec((count, tile, width), lambda i: (0, i, 0)),
            pl.BlockSpec((4 * count, tile), lambda i: (0, i)),
            pl.BlockSpec((3, tile, width), lambda i: (0, i, 0)),
            once(w.shape, lambda i: (0, 0)),
            pl.BlockSpec((tile, width), lambda i: (i, 0)),
            pl.BlockSpec((4, width), lambda i: (0, 0)),
        ],
        out_specs=[
            pl.BlockSpec((count, tile, width), lambda i: (0, i, 0)),
            pl.BlockSpec((4 * count, tile), lambda i: (0, i)),
            pl.BlockSpec((3, width), lambda i: (0, 0)),
            pl.BlockSpec((3, width), lambda i: (0, 0)),
        ],
        out_shape=[
            jax.ShapeDtypeStruct((count, tokens, width), BF16),
            jax.ShapeDtypeStruct((4 * count, tokens), F32),
            jax.ShapeDtypeStruct((3, width), F32),
            jax.ShapeDtypeStruct((3, width), F32),
        ],
        scratch_shapes=[
            pltpu.VMEM((3, tile, width), F32),
            pltpu.VMEM((4, strip, width), F32),
        ],
        compiler_params=params(48),
        cost_estimate=pl.CostEstimate(
            flops=6 * tokens * width * width + 200 * tokens * width,
            bytes_accessed=6 * width * width + 42 * tokens * width,
            transcendentals=0,
        ),
        name="front_back",
    )(e, mix, grads, w, hgrad, gain)


def flipped(v, mask):
    bit = 1
    while bit <= mask:
        if mask & bit:
            v = v + bit - 2 * bit * lax.rem(v // bit, 2)
        bit *= 2
    return v


def added(out_ref, refs, rows, strip=16):
    @pl.loop(0, rows // strip)
    def _(i):
        at = pl.ds(pl.multiple_of(i * strip, strip), strip)
        total = refs[0][at].astype(F32)
        for ref in refs[1:]:
            total = total + ref[at].astype(F32)
        out_ref[at] = total.astype(out_ref.dtype)


class Remote:
    def __init__(self, send, recv):
        self.send, self.recv, self.used = send, recv, 0

    def start(self, src, dst, where):
        copy = pltpu.make_async_remote_copy(
            src_ref=src,
            dst_ref=dst,
            send_sem=self.send.at[self.used],
            recv_sem=self.recv.at[self.used],
            device_id=where,
            device_id_type=MESH,
        )
        self.used += 1
        copy.start()
        return copy


class LineSum:
    def __init__(self, remote, n, work, out, pair, others, steps):
        self.remote, self.n, self.work, self.out = remote, n, work, out
        self.pair, self.others, self.steps = pair, others, steps
        self.me = lax.axis_index("ctx")
        self.half = work.shape[0] // 2
        bit = lax.rem(self.me, 2)
        self.mine = pl.ds(pl.multiple_of(bit * self.half, 16), self.half)
        self.his = pl.ds(pl.multiple_of((1 - bit) * self.half, 16), self.half)
        self.done = []

    def first(self):
        self.copy = self.remote.start(
            self.work.at[self.his], self.pair, {"ctx": flipped(self.me, 1)}
        )

    def second(self):
        self.copy.wait()
        added(self.steps.at[0], [self.work.at[self.mine], self.pair], self.half)
        self.level, self.bit = 0, 2
        self.copy = self.remote.start(
            self.steps.at[0], self.others.at[0], {"ctx": flipped(self.me, 2)}
        )

    def third(self):
        while True:
            self.copy.wait()
            last = self.bit * 2 >= self.n
            to = self.out.at[self.mine] if last else self.steps.at[self.level + 1]
            added(to, [self.steps.at[self.level], self.others.at[self.level]], self.half)
            if last:
                break
            self.level, self.bit = self.level + 1, self.bit * 2
            self.copy = self.remote.start(
                self.steps.at[self.level],
                self.others.at[self.level],
                {"ctx": flipped(self.me, self.bit)},
            )
        self.copy = self.remote.start(
            self.out.at[self.mine], self.out.at[self.mine], {"ctx": flipped(self.me, 1)}
        )

    def end(self):
        self.copy.wait()


def reduce_kernel(
    n,
    nf,
    qkv_ref,
    o_ref,
    in_ref,
    out_ref,
    small_ref,
    big_sum,
    in_sum,
    out_sum,
    small_sum,
    keep,
    got,
    part,
    own,
    big_pair,
    big_others,
    big_steps,
    in_work,
    in_pair,
    in_others,
    in_steps,
    out_work,
    out_pair,
    out_others,
    out_steps,
    small_in,
    small_line,
    send,
    recv,
    local,
):
    f, z = lax.axis_index("fsdp"), lax.axis_index("ctx")
    chip, core = f // 2, lax.rem(f, 2)
    chips = nf // 2
    rows = keep.shape[1]
    wide = qkv_ref.shape[3]
    remote = Remote(send, recv)

    loads = [
        pltpu.make_async_copy(qkv_ref.at[:, core], keep.at[:, :, :wide], local.at[0]),
        pltpu.make_async_copy(o_ref.at[:, core], keep.at[:, :, wide:], local.at[1]),
        pltpu.make_async_copy(in_ref, in_work, local.at[2]),
        pltpu.make_async_copy(out_ref, out_work, local.at[3]),
    ]
    for load in loads:
        load.start()

    barrier = pltpu.get_barrier_semaphore()
    for k in range(1, nf):
        pl.semaphore_signal(
            barrier, inc=1, device_id={"fsdp": lax.rem(f + k, nf)}, device_id_type=MESH
        )
    for k in range(1, n):
        pl.semaphore_signal(
            barrier, inc=1, device_id={"ctx": lax.rem(z + k, n)}, device_id_type=MESH
        )
    pl.semaphore_wait(barrier, nf + n - 2)

    sibling = {"fsdp": flipped(f, 1)}
    cores = [
        remote.start(qkv_ref.at[:, 1 - core], got.at[:, :, :wide], sibling),
        remote.start(o_ref.at[:, 1 - core], got.at[:, :, wide:], sibling),
    ]
    loads[2].wait()
    sum_in = LineSum(remote, n, in_work, in_sum, in_pair, in_others, in_steps)
    sum_in.first()
    loads[3].wait()
    sum_out = LineSum(remote, n, out_work, out_sum, out_pair, out_others, out_steps)
    sum_out.first()

    thin = small_in.shape[1]
    small_in[0] = small_ref[pl.ds(pl.multiple_of(f * thin, thin), thin)]
    slices = []
    for k in range(1, nf):
        to = lax.rem(f + k, nf)
        slices.append(
            remote.start(
                small_ref.at[pl.ds(pl.multiple_of(to * thin, thin), thin)],
                small_in.at[k],
                {"fsdp": to},
            )
        )

    loads[0].wait()
    loads[1].wait()
    for copy in cores:
        copy.wait()
    crossing = []
    for k in range(1, chips):
        to = flipped(chip, k)
        added(keep.at[to], [keep.at[to], got.at[to]], rows)
        crossing.append(remote.start(keep.at[to], part.at[k - 1], {"fsdp": 2 * to + core}))
    added(keep.at[chip], [keep.at[chip], got.at[chip]], rows)

    sum_in.second()

    for copy in slices:
        copy.wait()
    total = small_in[0]
    for k in range(1, nf):
        total = total + small_in[k]
    small_line[z] = total
    lines = []
    for k in range(1, n):
        lines.append(
            remote.start(small_line.at[z], small_line.at[z], {"ctx": lax.rem(z + k, n)})
        )

    sum_out.second()

    for copy in lines:
        copy.wait()
    total = small_line[0]
    for k in range(1, n):
        total = total + small_line[k]
    here = pl.ds(pl.multiple_of(f * thin, thin), thin)
    small_sum[here] = total
    spread = []
    for k in range(1, nf):
        spread.append(
            remote.start(small_sum.at[here], small_sum.at[here], {"fsdp": lax.rem(f + k, nf)})
        )

    sum_in.third()

    for copy in crossing:
        copy.wait()
    added(own, [keep.at[chip]] + [part.at[k] for k in range(chips - 1)], rows)
    sum_big = LineSum(remote, n, own, big_sum, big_pair, big_others, big_steps)
    sum_big.first()
    sum_out.third()
    sum_big.second()
    sum_in.end()
    sum_out.end()
    sum_big.third()
    sum_big.end()
    for copy in spread:
        copy.wait()


def reduce_all(d_qkv, d_o, d_in, d_out, small, n, nf):
    width = d_o.shape[1]
    rows = width // nf
    chips = nf // 2
    wide = d_qkv.shape[1]
    full = wide + width
    levels = max(n.bit_length() - 2, 1)
    qkv_view = d_qkv.reshape(chips, 2, rows, wide)
    o_view = d_o.reshape(chips, 2, rows, width)
    thin = small.shape[0] // nf

    def line(shape):
        half = (shape[0] // 2, shape[1])
        return [
            pltpu.VMEM(half, BF16),
            pltpu.VMEM((levels,) + half, BF16),
            pltpu.VMEM((levels,) + half, BF16),
        ]

    copies = 2 + 3 * (levels + 2) + (chips - 1) + 2 * (nf - 1) + (n - 1)
    vmem = pl.BlockSpec(memory_space=pltpu.VMEM)
    hbm = pl.BlockSpec(memory_space=pltpu.HBM)
    return pl.pallas_call(
        functools.partial(reduce_kernel, n, nf),
        in_specs=[hbm, hbm, hbm, hbm, vmem],
        out_specs=[vmem] * 4,
        out_shape=[
            jax.ShapeDtypeStruct((rows, full), BF16),
            jax.ShapeDtypeStruct(d_in.shape, BF16),
            jax.ShapeDtypeStruct(d_out.shape, BF16),
            jax.ShapeDtypeStruct(small.shape, F32),
        ],
        scratch_shapes=[
            pltpu.VMEM((chips, rows, full), BF16),
            pltpu.VMEM((chips, rows, full), BF16),
            pltpu.VMEM((chips - 1, rows, full), BF16),
            pltpu.VMEM((rows, full), BF16),
            *line((rows, full)),
            pltpu.VMEM(d_in.shape, BF16),
            *line(d_in.shape),
            pltpu.VMEM(d_out.shape, BF16),
            *line(d_out.shape),
            pltpu.VMEM((nf, thin, width), F32),
            pltpu.VMEM((n, thin, width), F32),
            pltpu.SemaphoreType.DMA((copies,)),
            pltpu.SemaphoreType.DMA((copies,)),
            pltpu.SemaphoreType.DMA((4,)),
        ],
        compiler_params=params(48, collective_id=4, has_side_effects=True),
        name="reduce_all",
    )(qkv_view, o_view, d_in, d_out, small)


def body(
    earlier,
    mix_in,
    segment_ids,
    attn_qkv,
    attn_out,
    mlp_in,
    mlp_out,
    norm_gain,
    norm_bias,
    mix_w1,
    mix_w2,
    mix_bias,
    out_grad,
    coef_grad,
):
    count, seqs, _, block, width = earlier.shape
    n = lax.axis_size("ctx")
    tokens = seqs * 2 * block
    length = 2 * n * block
    me = lax.axis_index("ctx")

    e = earlier.reshape(count, tokens, width)
    mix = mix_in.reshape(4 * count, tokens)
    og = out_grad.reshape(tokens, width)
    cg = coef_grad.reshape(-1, tokens)

    late = segment_ids[:, 1].reshape(seqs, n, block)[:, ::-1].reshape(seqs, n * block)
    placed = jnp.concatenate([segment_ids[:, 0], late], axis=1)
    column = placed[:, :, None]
    row = placed[:, None, :]

    cosine, sine = (jnp.asarray(table) for table in turn_tables(length))

    def own_rows(table):
        return jnp.concatenate(
            [
                lax.dynamic_slice_in_dim(table, me * block, block, 0),
                lax.dynamic_slice_in_dim(table, (2 * n - 1 - me) * block, block, 0),
            ],
            axis=0,
        )

    w_qkv = lax.all_gather(attn_qkv, "fsdp", axis=0, tiled=True)
    w_o = lax.all_gather(attn_out, "fsdp", axis=0, tiled=True)
    w_in = lax.all_gather(mlp_in, "fsdp", axis=0, tiled=True)
    w_out = lax.all_gather(mlp_out, "fsdp", axis=0, tiled=True)

    normed, residual = front(e, mix, norm_gain, norm_bias)
    shares = project(normed, w_qkv, own_rows(cosine), own_rows(sine), n)
    qkv = to_heads(shares, n, seqs, block, 0)
    heads = attend(qkv, column, row)
    context = to_tokens(heads, n, block, 1)[0]
    (
        layer_out,
        coefs,
        d_in,
        d_out,
        d_o,
        context_grad,
        hidden_grad,
        d_gain,
        d_bias,
        d_w1,
        d_w2,
        d_mb,
    ) = feed(
        residual,
        context,
        w_o,
        w_in,
        w_out,
        norm_gain,
        norm_bias,
        mix_w1,
        mix_w2,
        mix_bias[:, None],
        og,
        cg,
        n,
    )
    grad_heads = to_heads(context_grad[None], n, seqs, block, 2)
    turned_back = attend_back(qkv, grad_heads, column, row, cosine, sine)
    grads = to_tokens(turned_back, n, block, 3)
    d_qkv = project_weight_grad(normed, grads)
    e_grad, m_grad, f_gain, f_bias = front_back(e, mix, grads, w_qkv, hidden_grad, norm_gain)

    m_in = lax.psum_scatter(d_in, "fsdp", scatter_dimension=0, tiled=True)
    m_out = lax.psum_scatter(d_out, "fsdp", scatter_dimension=0, tiled=True)
    nf = lax.axis_size("fsdp")
    small_count, coef_count = d_w2.shape
    tail = jnp.concatenate([d_w2.reshape(-1), d_mb.reshape(-1)])
    tail_rows = -(-tail.shape[0] // width)
    tail = jnp.pad(tail, (0, tail_rows * width - tail.shape[0])).reshape(tail_rows, width)
    pieces = [f_gain, d_gain, f_bias, d_bias, d_w1, tail]
    filled = sum(piece.shape[0] for piece in pieces)
    step = 8 * nf
    blank = jnp.zeros((-filled % step, width), F32)
    small = jnp.concatenate(pieces + [blank], axis=0)
    big, s_in, s_out, small = reduce_all(d_qkv, d_o, m_in, m_out, small, n, nf)
    end = 8 + small_count
    tail = small[end : end + tail_rows].reshape(-1)
    owned = [
        big[:, : 3 * width].astype(F32),
        big[:, 3 * width :].astype(F32),
        s_in.astype(F32),
        s_out.astype(F32),
    ]
    square = small_count * coef_count
    small = [
        small[0:4],
        small[4:8],
        small[8:end],
        tail[:square].reshape(small_count, coef_count),
        tail[square : square + coef_count],
    ]

    return (
        layer_out.reshape(seqs, 2, block, width),
        coefs.reshape(4, -1, seqs, 2, block),
        e_grad.reshape(count, seqs, 2, block, width),
        m_grad.reshape(4, count, seqs, 2, block),
        owned[0],
        owned[1],
        owned[2],
        owned[3],
        small[0],
        small[1],
        small[2],
        small[3],
        small[4],
    )


def solution(mesh):
    in_specs = (
        P(None, "fsdp", None, "ctx", None),
        P(None, None, "fsdp", None, "ctx"),
        P("fsdp", None, None),
        P("fsdp", None),
        P("fsdp", None),
        P("fsdp", None),
        P("fsdp", None),
        P(),
        P(),
        P(),
        P(),
        P(),
        P("fsdp", None, "ctx", None),
        P(None, None, "fsdp", None, "ctx"),
    )
    out_specs = (
        P("fsdp", None, "ctx", None),
        P(None, None, "fsdp", None, "ctx"),
        P(None, "fsdp", None, "ctx", None),
        P(None, None, "fsdp", None, "ctx"),
        P("fsdp", None),
        P("fsdp", None),
        P("fsdp", None),
        P("fsdp", None),
        P(),
        P(),
        P(),
        P(),
        P(),
    )
    return jax.shard_map(body, mesh=mesh, in_specs=in_specs, out_specs=out_specs, check_vma=False)
```

```python
import functools
import math

import jax
import jax.numpy as jnp
import numpy as np
from jax import lax
from jax.experimental import pallas as pl
from jax.experimental.pallas import tpu as pltpu
from jax.sharding import PartitionSpec as P

HD = 64
ROT = 16
LANES = 128
EPSILON = 1e-05
RMS_EPSILON = 1e-06
MASKED = -1e30
F32 = jnp.float32
BF16 = jnp.bfloat16
MESH = pl.DeviceIdType.MESH
MIB = 1024 * 1024

NN = (((1,), (0,)), ((), ()))
NT = (((1,), (1,)), ((), ()))
TN = (((0,), (0,)), ((), ()))

ERFC_RATE = 0.4
ERFC = (
    0.22567586600780487,
    0.22566929459571838,
    0.20784726738929749,
    0.16851142048835754,
    0.1415392905473709,
    -0.005822250619530678,
    0.16932761669158936,
    -0.18304575979709625,
    0.05029737576842308,
)


def dot(a, b, dims=NN):
    return lax.dot_general(a, b, dims, preferred_element_type=F32)


def gelu_and_slope(v):
    z = jnp.abs(v) * math.sqrt(0.5)
    bell = jnp.exp(-0.5 * v * v)
    t = 1.0 / (1.0 + ERFC_RATE * z)
    poly = jnp.full_like(t, ERFC[-1])
    for coefficient in ERFC[-2::-1]:
        poly = poly * t + coefficient
    tail = 0.5 * poly * t * bell
    phi = jnp.where(v >= 0.0, 1.0 - tail, tail)
    return v * phi, phi + v * bell * (1.0 / math.sqrt(2.0 * math.pi))


def halves(x):
    high = x.astype(BF16)
    return high, (x - high.astype(F32)).astype(BF16)


def params(limit_mib, **more):
    return pltpu.CompilerParams(vmem_limit_bytes=limit_mib * MIB, **more)


def once(shape, index):
    return pl.BlockSpec(shape, index, pipeline_mode=pl.Buffered(1))


def turn_tables(length):
    half = ROT // 2
    frequency = 10000.0 ** (-(np.arange(half) * 2.0 / ROT))
    angle = np.arange(length)[:, None] * frequency[None, :]
    lane = np.arange(LANES) % HD
    cosine = np.ones((length, LANES), np.float32)
    sine = np.zeros((length, LANES), np.float32)
    for k in range(LANES):
        if lane[k] < ROT:
            cosine[:, k] = np.cos(angle[:, lane[k] % half])
            sign = -1.0 if lane[k] < half else 1.0
            sine[:, k] = sign * np.sin(angle[:, lane[k] % half])
    return cosine, sine


def turned(x, cosine, sine):
    half = ROT // 2
    lane = lax.broadcasted_iota(jnp.int32, x.shape, 1) % HD
    other = jnp.where(
        lane < half, pltpu.roll(x, LANES - half, axis=1), pltpu.roll(x, half, axis=1)
    )
    return x * cosine + other * sine


def row_tile(length):
    return min(256, length)


def head_lanes(shape, h):
    lane = lax.broadcasted_iota(jnp.int32, shape, 1)
    return (lane >= h * HD) & (lane < (h + 1) * HD)


def only(x, h):
    return jnp.where(head_lanes(x.shape, h), x, jnp.zeros_like(x))


def coefficient_places(ref):
    outer, inner, seqs, _, block = ref.shape
    for a in range(outer):
        for seq in range(seqs):
            for h in range(2):
                first = (2 * seq + h) * block
                yield a, seq, h, slice(a * inner, (a + 1) * inner), slice(first, first + block)


def feed_kernel(
    res_ref,
    ctx_ref,
    wo_ref,
    win_ref,
    wout_ref,
    g_ref,
    b_ref,
    w1_ref,
    w2_ref,
    mb_ref,
    og_ref,
    cg_ref,
    out_ref,
    coef_ref,
    dwin_ref,
    dwout_ref,
    dwo_ref,
    cgrad_ref,
    hgrad_ref,
    dgain_ref,
    dbias_ref,
    dw1_ref,
    dw2_ref,
    dmb_ref,
    hidden,
    normed,
    total,
    active,
    slope,
    branch,
    r_high,
    r_rest,
    cotangent,
    *,
    tiles,
    strip,
):
    step = pl.program_id(0)
    tokens, width = res_ref.shape
    cut = win_ref.shape[1]
    inv = 1.0 / width

    @pl.when(step == 0)
    def _():
        hidden[...] = dot(ctx_ref[...], wo_ref[...])

        @pl.loop(0, tokens // strip)
        def _(i):
            rows = pl.ds(pl.multiple_of(i * strip, strip), strip)
            v = hidden[rows] + res_ref[rows]
            hidden[rows] = v
            center = v - jnp.sum(v, axis=-1, keepdims=True) * inv
            spread = jnp.sum(center * center, axis=-1, keepdims=True) * inv
            hat = center * lax.rsqrt(spread + EPSILON)
            normed[rows] = (hat * g_ref[3:4] + b_ref[3:4]).astype(BF16)
            total[rows] = v

    @pl.when(step < tiles)
    def _():
        value, rate = gelu_and_slope(dot(normed[...], win_ref[...]))
        low = value.astype(BF16)
        active[step] = low
        slope[step] = rate
        total[...] += dot(low, wout_ref[...])

    @pl.when(step == tiles - 1)
    def _():
        w1 = w1_ref[...]
        w2 = w2_ref[...]

        @pl.loop(0, tokens // strip)
        def _(i):
            rows = pl.ds(pl.multiple_of(i * strip, strip), strip)
            v = total[rows]
            out_ref[rows] = v.astype(BF16)
            scale = lax.rsqrt(jnp.sum(v * v, axis=-1, keepdims=True) * inv + RMS_EPSILON)
            r = v * scale
            high = r.astype(BF16)
            r_high[rows] = high
            r_rest[rows] = (r - high.astype(F32)).astype(BF16)

        high, rest = r_high[...], r_rest[...]
        for a, seq, h, rows, cols in coefficient_places(cg_ref):
            cotangent[rows, cols] = cg_ref[a, :, seq, h, :]
        z = dot(w1, high, NT) + dot(w1, rest, NT)
        value, rate = gelu_and_slope(z)
        v_high, v_rest = halves(value)
        ones = jnp.ones((1, tokens), BF16)
        mb_high, mb_rest = halves(mb_ref[...])
        mb_last = (mb_ref[...] - mb_high.astype(F32) - mb_rest.astype(F32)).astype(BF16)
        shift = dot(mb_high, ones, TN) + dot(mb_rest, ones, TN) + dot(mb_last, ones, TN)
        coefs = dot(w2, v_high, TN) + dot(w2, v_rest, TN) + shift
        for a, seq, h, rows, cols in coefficient_places(coef_ref):
            coef_ref[a, :, seq, h, :] = coefs[rows, cols]
        c_high, c_rest = halves(cotangent[...])
        dmb_ref[...] = dot(ones, c_high, NT) + dot(ones, c_rest, NT)
        dw2_ref[...] = dot(v_high, c_high, NT) + dot(v_rest, c_high, NT) + dot(v_high, c_rest, NT)
        z_high, z_rest = halves((dot(w2, c_high) + dot(w2, c_rest)) * rate)
        dw1_ref[...] = dot(z_high, high) + dot(z_high, rest) + dot(z_rest, high)
        hgrad_ref[...] = dot(z_high, w1, TN) + dot(z_rest, w1, TN)

        @pl.loop(0, tokens // strip)
        def _(i):
            rows = pl.ds(pl.multiple_of(i * strip, strip), strip)
            v = total[rows]
            scale = lax.rsqrt(jnp.sum(v * v, axis=-1, keepdims=True) * inv + RMS_EPSILON)
            dr = hgrad_ref[rows]
            r = v * scale
            mean = jnp.sum(dr * r, axis=-1, keepdims=True) * inv
            grad = scale * (dr - r * mean) + og_ref[rows].astype(F32)
            hgrad_ref[rows] = grad
            branch[rows] = grad.astype(BF16)
            total[rows] = jnp.zeros_like(v)

    @pl.when(step >= tiles)
    def _():
        j = step - tiles
        low = (dot(branch[...], wout_ref[...], NT) * slope[j]).astype(BF16)
        total[...] += dot(low, win_ref[...], NT)
        dwin_ref[...] = dot(normed[...], low, TN).astype(BF16)
        dwout_ref[...] = dot(active[j], branch[...], TN).astype(BF16)

    @pl.when(step == 2 * tiles - 1)
    def _():
        dgain_ref[...] = jnp.zeros_like(dgain_ref)
        dbias_ref[...] = jnp.zeros_like(dbias_ref)

        @pl.loop(0, tokens // strip)
        def _(i):
            rows = pl.ds(pl.multiple_of(i * strip, strip), strip)
            v = hidden[rows]
            dy = total[rows]
            center = v - jnp.sum(v, axis=-1, keepdims=True) * inv
            spread = jnp.sum(center * center, axis=-1, keepdims=True) * inv
            scale = lax.rsqrt(spread + EPSILON)
            hat = center * scale
            dgain_ref[...] += jnp.sum(dy * hat, axis=0, keepdims=True)
            dbias_ref[...] += jnp.sum(dy, axis=0, keepdims=True)
            dh = dy * g_ref[3:4]
            first = jnp.sum(dh, axis=-1, keepdims=True) * inv
            second = jnp.sum(dh * hat, axis=-1, keepdims=True) * inv
            grad = hgrad_ref[rows] + scale * (dh - first - hat * second)
            hgrad_ref[rows] = grad
            branch[rows] = grad.astype(BF16)

        dwo_ref[...] = dot(ctx_ref[...], branch[...], TN).astype(BF16)
        groups, _, group = cgrad_ref.shape
        for i in range(groups):
            rows = slice(i * group, (i + 1) * group)
            cgrad_ref[i] = dot(branch[...], wo_ref[rows], NT).astype(BF16)


def feed(res, ctx, wo, win, wout, gain, bias, w1, w2, mb, og, cg, groups):
    tokens, width = res.shape
    hidden_units = win.shape[1]
    cut = 1024
    tiles = hidden_units // cut
    small, coefs = w1.shape[0], w2.shape[1]

    def whole(x):
        zeros = (0,) * x.ndim
        return once(x.shape, lambda i: zeros)

    def result(shape, dtype=F32):
        zeros = (0,) * len(shape)
        return once(shape, lambda i: zeros), jax.ShapeDtypeStruct(shape, dtype)

    def back(i):
        return jnp.maximum(i - tiles, 0)

    outs = [
        result((tokens, width), BF16),
        result(cg.shape),
        (
            pl.BlockSpec((width, cut), lambda i: (0, back(i))),
            jax.ShapeDtypeStruct((width, hidden_units), BF16),
        ),
        (
            pl.BlockSpec((cut, width), lambda i: (back(i), 0)),
            jax.ShapeDtypeStruct((hidden_units, width), BF16),
        ),
        result((width, width), BF16),
        result((groups, tokens, width // groups), BF16),
        result((tokens, width)),
        result((1, width)),
        result((1, width)),
        result((small, width)),
        result((small, coefs)),
        result((1, coefs)),
    ]
    return pl.pallas_call(
        functools.partial(feed_kernel, tiles=tiles, strip=min(512, tokens)),
        grid=(2 * tiles,),
        in_specs=[
            whole(res),
            whole(ctx),
            whole(wo),
            pl.BlockSpec((width, cut), lambda i: (0, lax.rem(i, tiles))),
            pl.BlockSpec((cut, width), lambda i: (lax.rem(i, tiles), 0)),
            whole(gain),
            whole(bias),
            whole(w1),
            whole(w2),
            whole(mb),
            whole(og),
            whole(cg),
        ],
        out_specs=[spec for spec, _ in outs],
        out_shape=[shape for _, shape in outs],
        scratch_shapes=[
            pltpu.VMEM((tokens, width), F32),
            pltpu.VMEM((tokens, width), BF16),
            pltpu.VMEM((tokens, width), F32),
            pltpu.VMEM((tiles, tokens, cut), BF16),
            pltpu.VMEM((tiles, tokens, cut), F32),
            pltpu.VMEM((tokens, width), BF16),
            pltpu.VMEM((tokens, width), BF16),
            pltpu.VMEM((tokens, width), BF16),
            pltpu.VMEM((coefs, tokens), F32),
        ],
        compiler_params=params(58),
        cost_estimate=pl.CostEstimate(
            flops=12 * tokens * width * hidden_units + 6 * tokens * width * width,
            bytes_accessed=12 * width * hidden_units + 4 * width * width + 20 * tokens * width,
            transcendentals=2 * tokens * hidden_units,
        ),
        name="feed",
    )(res, ctx, wo, win, wout, gain, bias, w1, w2, mb, og, cg)


def flipped(v, mask):
    bit = 1
    while bit <= mask:
        if mask & bit:
            v = v + bit - 2 * bit * lax.rem(v // bit, 2)
        bit *= 2
    return v


def added(out_ref, refs, rows, strip=32):
    strip = min(strip, rows)

    @pl.loop(0, rows // strip)
    def _(i):
        at = pl.ds(pl.multiple_of(i * strip, strip), strip)
        total = refs[0][at].astype(F32)
        for ref in refs[1:]:
            total = total + ref[at].astype(F32)
        out_ref[at] = total.astype(out_ref.dtype)


class Remote:
    def __init__(self, send, recv):
        self.send, self.recv, self.used = send, recv, 0

    def start(self, src, dst, where):
        copy = pltpu.make_async_remote_copy(
            src_ref=src,
            dst_ref=dst,
            send_sem=self.send.at[self.used],
            recv_sem=self.recv.at[self.used],
            device_id=where,
            device_id_type=MESH,
        )
        self.used += 1
        copy.start()
        return copy


class LineSum:
    def __init__(self, remote, n, work, out, pair, others, steps):
        self.remote, self.n, self.work, self.out = remote, n, work, out
        self.pair, self.others, self.steps = pair, others, steps
        self.me = lax.axis_index("ctx")
        self.half = work.shape[0] // 2
        bit = lax.rem(self.me, 2)
        self.mine = pl.ds(pl.multiple_of(bit * self.half, 16), self.half)
        self.his = pl.ds(pl.multiple_of((1 - bit) * self.half, 16), self.half)
        self.done = []

    def first(self):
        self.copy = self.remote.start(
            self.work.at[self.his], self.pair, {"ctx": flipped(self.me, 1)}
        )

    def second(self):
        self.copy.wait()
        added(self.steps.at[0], [self.work.at[self.mine], self.pair], self.half)
        self.level, self.bit = 0, 2
        self.copy = self.remote.start(
            self.steps.at[0], self.others.at[0], {"ctx": flipped(self.me, 2)}
        )

    def third(self):
        while True:
            self.copy.wait()
            last = self.bit * 2 >= self.n
            to = self.out.at[self.mine] if last else self.steps.at[self.level + 1]
            added(to, [self.steps.at[self.level], self.others.at[self.level]], self.half)
            if last:
                break
            self.level, self.bit = self.level + 1, self.bit * 2
            self.copy = self.remote.start(
                self.steps.at[self.level],
                self.others.at[self.level],
                {"ctx": flipped(self.me, self.bit)},
            )
        self.copy = self.remote.start(
            self.out.at[self.mine], self.out.at[self.mine], {"ctx": flipped(self.me, 1)}
        )

    def end(self):
        self.copy.wait()


class ChipSum:
    def __init__(self, remote, nf, terms, keep, got, part):
        self.remote, self.nf, self.terms = remote, nf, terms
        self.keep, self.got, self.part = keep, got, part
        self.f = lax.axis_index("fsdp")
        self.chip, self.core = self.f // 2, lax.rem(self.f, 2)
        self.rows = got.shape[1]
        self.half = self.rows // 2
        bits = []
        bit = 1
        while bit < nf // 2:
            bits.append(bit)
            bit *= 2
        self.orders = (bits, bits[::-1])
        self.level = len(bits) - 1
        self.slots = 0

    def cores(self):
        self.copy = self.remote.start(
            self.terms.at[:, 1 - self.core], self.got, {"fsdp": flipped(self.f, 1)}
        )

    def masks(self, which, level):
        found = [0]
        for bit in self.orders[which][:level]:
            found += [mask + bit for mask in found]
        return found

    def piece(self, which, chip):
        return self.got.at[chip, pl.ds(which * self.half, self.half)]

    def launch(self):
        self.flying = []
        for which in range(2):
            bit = self.orders[which][self.level]
            to = 2 * flipped(self.chip, bit) + self.core
            for mask in self.masks(which, self.level):
                landing = self.part.at[self.slots]
                self.slots += 1
                copy = self.remote.start(
                    self.piece(which, flipped(self.chip, mask + bit)), landing, {"fsdp": to}
                )
                self.flying.append((copy, which, mask, landing))

    def cross(self):
        self.copy.wait()
        for k in range(self.nf // 2):
            added(self.got.at[k], [self.keep.at[k], self.got.at[k]], self.rows)
        self.launch()

    def relay(self):
        while self.level > 0:
            for copy, which, mask, landing in self.flying:
                copy.wait()
                here = self.piece(which, flipped(self.chip, mask))
                added(here, [here, landing], self.half)
            self.level -= 1
            self.launch()

    def total(self, out):
        for copy, which, _, landing in self.flying:
            copy.wait()
            added(
                out.at[pl.ds(which * self.half, self.half)],
                [self.piece(which, self.chip), landing],
                self.half,
            )

    @staticmethod
    def count(nf):
        return 1 + 2 * (nf // 2 - 1)


def chip_scratch(nf, rows, cols):
    chips = nf // 2
    return [
        pltpu.VMEM((chips, rows, cols), BF16),
        pltpu.VMEM((chips, rows, cols), BF16),
        pltpu.VMEM((2 * chips - 2, rows // 2, cols), BF16),
    ]


def greet_all(n, nf):
    z, f = lax.axis_index("ctx"), lax.axis_index("fsdp")
    barrier = pltpu.get_barrier_semaphore()
    for k in range(1, nf):
        pl.semaphore_signal(
            barrier, inc=1, device_id={"fsdp": lax.rem(f + k, nf)}, device_id_type=MESH
        )
    for k in range(1, n):
        pl.semaphore_signal(
            barrier, inc=1, device_id={"ctx": lax.rem(z + k, n)}, device_id_type=MESH
        )
    pl.semaphore_wait(barrier, nf + n - 2)


def place_segments(ids_ref, row, column, block):
    seqs, _, half = ids_ref.shape
    n = half // block
    for s in range(seqs):
        row[s, :, 0:half] = ids_ref[s, 0:1].astype(F32)
        for b in range(n):
            at = slice((n - 1 - b) * block, (n - b) * block)
            to = slice(half + b * block, half + (b + 1) * block)
            row[s, :, to] = ids_ref[s, 1:2, at].astype(F32)
        column[s] = jnp.broadcast_to(row[s], (8, 2 * half)).T


def mix_columns(mix_ref, mixes, t):
    block = mix_ref.shape[4]
    tile = mixes.shape[0]
    per = tile // block
    parts = []
    for i in range(t * per, (t + 1) * per):
        rows = [mix_ref[a, :, i // 2, i % 2, :] for a in range(mix_ref.shape[0])]
        parts.append(jnp.concatenate(rows, axis=0))
    mixes[...] = (parts[0] if per == 1 else jnp.concatenate(parts, axis=1)).T


class PlaneGather:
    def __init__(self, remote, nf, src, out):
        self.remote, self.nf, self.src, self.out = remote, nf, src, out
        self.f = lax.axis_index("fsdp")
        self.half = src.shape[0] // 2
        bits = []
        bit = 2
        while bit < nf:
            bits.append(bit)
            bit *= 2
        self.orders = (bits, bits[::-1])
        self.levels = len(bits)
        self.flying = {}
        self.inner = []

    def masks(self, which, level):
        found = [0]
        for bit in self.orders[which][:level]:
            found += [mask + bit for mask in found]
        return found

    def place(self, which, shard):
        return self.out.at[shard, pl.ds(which * self.half, self.half)]

    def launch(self, which, level, mask):
        shard = flipped(self.f, mask)
        here = self.src.at[pl.ds(which * self.half, self.half)]
        if mask:
            here = self.place(which, shard)
        to = flipped(self.f, self.orders[which][level])
        self.flying[which, level, mask] = self.remote.start(
            here, self.place(which, shard), {"fsdp": to}
        )

    def begin(self, sem):
        for level in range(self.levels):
            for which in range(2):
                self.launch(which, level, 0)
        self.inner.append(
            self.remote.start(self.src, self.out.at[self.f], {"fsdp": flipped(self.f, 1)})
        )
        self.own = pltpu.make_async_copy(self.src, self.out.at[self.f], sem)
        self.own.start()

    def relay(self, level):
        for which in range(2):
            order = self.orders[which]
            for mask in self.masks(which, level):
                self.flying[which, level, mask].wait()
                arrived = mask + order[level]
                for later in range(level + 1, self.levels):
                    self.launch(which, later, arrived)
                place = self.place(which, flipped(self.f, arrived))
                self.inner.append(self.remote.start(place, place, {"fsdp": flipped(self.f, 1)}))

    def end(self):
        self.own.wait()
        for copy in self.inner:
            copy.wait()

    @staticmethod
    def count(nf):
        return 2 * (nf // 2 - 1) + 2 * (nf // 2 - 1) + 1


def front_tile(e, mixes, st, g_ref, b_ref, normed, hats, scales, res, first, strip=16):
    count, tile, width = e.shape
    inv = 1.0 / width

    @pl.loop(0, tile // strip)
    def _(i):
        rows = pl.ds(pl.multiple_of(i * strip, strip), strip)
        mix = mixes[rows]
        for pair in ((0, 1), (2, 3)):
            totals = [None, None]
            for j in range(count):
                part = e[j, rows].astype(F32)
                for slot, s in enumerate(pair):
                    term = part * mix[:, s * count + j : s * count + j + 1]
                    totals[slot] = term if j == 0 else totals[slot] + term
            for slot, s in enumerate(pair):
                st[s, rows] = totals[slot]

    to = slice(first, first + tile)
    lane = lax.broadcasted_iota(jnp.int32, (tile, LANES), 1)
    kept = jnp.zeros((tile, LANES), F32)
    for s in range(3):
        v = st[s]
        center = v - jnp.sum(v, axis=-1, keepdims=True) * inv
        spread = jnp.sum(center * center, axis=-1, keepdims=True) * inv
        scale = lax.rsqrt(spread + EPSILON)
        hat = center * scale
        hats[s, to] = hat.astype(BF16)
        normed[s, to] = (hat * g_ref[s : s + 1] + b_ref[s : s + 1]).astype(BF16)
        kept = jnp.where(lane == s, scale, kept)
    scales[to] = kept
    res[to] = st[3]


def attend_pair(qkv, out, column_ref, row_ref, seq, lanes):
    blocks, block = out.shape[1], out.shape[2]
    length = blocks * block
    rows = row_tile(length)
    per = rows // block

    def load(kind, first, last):
        return qkv[kind, seq, first:last, :, lanes].reshape(-1, LANES)

    for i in range(length // rows):
        first, until = i * rows, (i + 1) * rows
        b0, b1 = i * per, (i + 1) * per
        query = first + lax.broadcasted_iota(jnp.int32, (rows, until), 0)
        key = lax.broadcasted_iota(jnp.int32, (rows, until), 1)
        same = column_ref[seq, first:until, 0:1] == row_ref[seq, 0:1, 0:until]
        allowed = same & (key <= query)
        q = load(0, b0, b1) * BF16(HD**-0.5)
        k = load(1, 0, b1)
        v = load(2, 0, b1)
        total = None
        for h in range(LANES // HD):
            scores = jnp.where(allowed, dot(only(q, h), k, NT), MASKED)
            peak = jnp.max(scores, axis=-1, keepdims=True)
            raised = jnp.exp(scores - peak)
            mass = jnp.sum(raised, axis=-1, keepdims=True)
            probs = (raised * (1.0 / mass)).astype(BF16)
            part = dot(probs, v)
            part = jnp.where(head_lanes(part.shape, h), part, 0.0)
            total = part if total is None else total + part
        out[seq, b0:b1, :, lanes] = total.astype(BF16).reshape(per, block, LANES)


def forward_kernel(
    n,
    nf,
    e_ref,
    wqkv_ref,
    wo_ref,
    win_ref,
    wout_ref,
    mix_ref,
    gain_ref,
    bias_ref,
    c_ref,
    s_ref,
    ids_ref,
    normed_ref,
    hats_ref,
    scales_ref,
    res_ref,
    gqkv_ref,
    go_ref,
    gin_ref,
    gout_ref,
    qkv_ref,
    ctx_ref,
    e,
    mixes,
    st,
    normed,
    hats,
    scales,
    res,
    w,
    raw,
    shares,
    qkv,
    heads,
    row,
    column,
    send,
    recv,
    local,
    e_sem,
):
    f, z = lax.axis_index("fsdp"), lax.axis_index("ctx")
    count, tokens, width = e_ref.shape
    tile = e.shape[2]
    tiles = tokens // tile
    seqs, _, block, cols = heads.shape
    seq_rows = 2 * block
    cut = raw.shape[1]
    remote = Remote(send, recv)
    spots = (z, 2 * n - 1 - z)
    mine = pl.ds(pl.multiple_of(z * cols, LANES), cols)

    def fetch(t):
        return pltpu.make_async_copy(
            e_ref.at[:, t * tile : (t + 1) * tile], e.at[t % 2], e_sem.at[t % 2]
        )

    fetch(0).start()
    greet_all(n, nf)

    def columns(ref, i):
        at = pl.ds(i * width, width)
        return ref.at[:, at] if len(ref.shape) == 2 else ref.at[:, :, at]

    parts = [
        PlaneGather(remote, nf, columns(wqkv_ref, i), columns(w, i)) for i in range(3)
    ]
    others = [
        PlaneGather(remote, nf, win_ref, gin_ref),
        PlaneGather(remote, nf, wout_ref, gout_ref),
        PlaneGather(remote, nf, wo_ref, go_ref),
    ]
    levels = parts[0].levels
    parts[0].begin(local.at[0])
    parts[1].begin(local.at[1])

    def do_tile(t):
        fetch(t).wait()
        if t + 1 < tiles:
            fetch(t + 1).start()
        mix_columns(mix_ref, mixes, t)
        front_tile(
            e.at[t % 2], mixes, st, gain_ref, bias_ref, normed, hats, scales, res, t * tile
        )

    do_tile(0)
    parts[0].relay(0)
    parts[2].begin(local.at[2])
    do_tile(1)
    parts[1].relay(0)
    for t in range(2, tiles - 1):
        do_tile(t)
    parts[2].relay(0)
    for level in range(1, levels):
        parts[0].relay(level)
    if tiles > 2:
        do_tile(tiles - 1)
    others[0].begin(local.at[3])
    own_tables = []
    for table in (c_ref, s_ref):
        early = table[pl.ds(pl.multiple_of(z * block, block), block)]
        late = table[pl.ds(pl.multiple_of((2 * n - 1 - z) * block, block), block)]
        own_tables.append((early, late))

    def project(i):
        @pl.loop(0, width // cut)
        def _(j):
            at = pl.ds(pl.multiple_of(i * width + j * cut, cut), cut)
            raw[...] = dot(normed[i], w[:, :, at].reshape(width, cut))
            for s in range(seqs):
                for h in range(2):
                    first = s * seq_rows + h * block
                    for c in range(cut // LANES):
                        x = raw[first : first + block, c * LANES : (c + 1) * LANES]
                        if i < 2:
                            x = turned(x, own_tables[0][h], own_tables[1][h])
                        to = c * LANES % cols
                        group = j * (cut // cols) + c * LANES // cols
                        shares[i, group, s, h, :, to : to + LANES] = x.astype(BF16)

    pairs = cols // LANES
    units = [(0, None)] + [(s, p) for s in range(1, seqs) for p in range(pairs)]
    arriving = {unit: [] for unit in units}
    kept = []

    def give(kind, unit):
        s, p = unit
        lanes = slice(None) if p is None else slice(p * LANES, (p + 1) * LANES)
        for k in range(1, n):
            to = lax.rem(z + k, n)
            for h in range(2):
                arriving[unit].append(
                    remote.start(
                        shares.at[kind, to, s, h, :, lanes],
                        qkv.at[kind, s, spots[h], :, lanes],
                        {"ctx": to},
                    )
                )

    for i in range(3):
        parts[i].end()
        project(i)
        give(i, units[0])
        if i < 2:
            for level in range(1, levels):
                parts[i + 1].relay(level)
    for h in range(2):
        copy = pltpu.make_async_copy(
            shares.at[:, z, :, h], qkv.at[:, :, spots[h]], local.at[8 + h]
        )
        copy.start()
        kept.append(copy)
    for unit in units[1:]:
        give(slice(None), unit)
    others[1].begin(local.at[4])
    others[2].begin(local.at[5])
    out_copies = [
        pltpu.make_async_copy(w, gqkv_ref, local.at[10]),
        pltpu.make_async_copy(normed, normed_ref, local.at[6]),
        pltpu.make_async_copy(res, res_ref, local.at[7]),
        pltpu.make_async_copy(hats, hats_ref, local.at[12]),
        pltpu.make_async_copy(scales, scales_ref, local.at[13]),
    ]
    for copy in out_copies:
        copy.start()
    place_segments(ids_ref, row, column, block)

    others[0].relay(0)
    for copy in kept:
        copy.wait()
    leaving = []
    stored = 14
    for index, unit in enumerate(units):
        for copy in arriving[unit]:
            copy.wait()
        s, p = unit
        if p is None:

            @pl.loop(0, pairs)
            def _(p):
                lanes = pl.ds(pl.multiple_of(p * LANES, LANES), LANES)
                attend_pair(qkv, heads, column, row, s, lanes)

            there, here = mine, slice(None)
        else:
            here = slice(p * LANES, (p + 1) * LANES)
            attend_pair(qkv, heads, column, row, s, here)
            there = pl.ds(pl.multiple_of(z * cols + p * LANES, LANES), LANES)
        for k in range(1, n):
            to = lax.rem(z + k, n)
            for h in range(2):
                spot = to if h == 0 else 2 * n - 1 - to
                leaving.append(
                    remote.start(
                        heads.at[s, spot, :, here], ctx_ref.at[s, h, :, there], {"ctx": to}
                    )
                )
        for h in range(2):
            copy = pltpu.make_async_copy(
                heads.at[s, spots[h], :, here], ctx_ref.at[s, h, :, there], local.at[stored]
            )
            stored += 1
            copy.start()
            out_copies.append(copy)
        if index == 0:
            others[1].relay(0)
            others[2].relay(0)
            for level in range(1, levels):
                others[0].relay(level)
    copy = pltpu.make_async_copy(qkv, qkv_ref, local.at[11])
    copy.start()
    out_copies.append(copy)
    for level in range(1, levels):
        others[1].relay(level)
        others[2].relay(level)
    for gather in others:
        gather.end()
    for copy in out_copies + leaving:
        copy.wait()


def forward(e, mix, w_qkv, w_o, w_in, w_out, gain, bias, cosine, sine, ids, n, nf):
    count, tokens, width = e.shape
    seqs, block = mix.shape[2], mix.shape[4]
    length = 2 * n * block
    cols = width // n
    spots = 2 * n
    tile = 128
    cut = max(cols, 512)
    rows = width // nf
    units = 1 + (seqs - 1) * (cols // LANES)
    copies = 6 * PlaneGather.count(nf) + (2 + 2 * units) * 2 * (n - 1)
    vmem = pl.BlockSpec(memory_space=pltpu.VMEM)
    hbm = pl.BlockSpec(memory_space=pltpu.HBM)

    def gathered(x):
        return jax.ShapeDtypeStruct((nf,) + x.shape, x.dtype)

    normed, hats, scales, res, g_qkv, g_o, g_in, g_out, qkv, ctx = pl.pallas_call(
        functools.partial(forward_kernel, n, nf),
        in_specs=[hbm] * 5 + [vmem] * 6,
        out_specs=[hbm] * 10,
        out_shape=[
            jax.ShapeDtypeStruct((3, tokens, width), BF16),
            jax.ShapeDtypeStruct((3, tokens, width), BF16),
            jax.ShapeDtypeStruct((tokens, LANES), F32),
            jax.ShapeDtypeStruct((tokens, width), F32),
            gathered(w_qkv),
            gathered(w_o),
            gathered(w_in),
            gathered(w_out),
            jax.ShapeDtypeStruct((3, seqs, spots, block, cols), BF16),
            jax.ShapeDtypeStruct((seqs, 2, block, width), BF16),
        ],
        scratch_shapes=[
            pltpu.VMEM((2, count, tile, width), BF16),
            pltpu.VMEM((tile, 4 * count), F32),
            pltpu.VMEM((4, tile, width), F32),
            pltpu.VMEM((3, tokens, width), BF16),
            pltpu.VMEM((3, tokens, width), BF16),
            pltpu.VMEM((tokens, LANES), F32),
            pltpu.VMEM((tokens, width), F32),
            pltpu.VMEM((nf, rows, 3 * width), BF16),
            pltpu.VMEM((tokens, cut), F32),
            pltpu.VMEM((3, n, seqs, 2, block, cols), BF16),
            pltpu.VMEM((3, seqs, spots, block, cols), BF16),
            pltpu.VMEM((seqs, spots, block, cols), BF16),
            pltpu.VMEM((seqs, 1, length), F32),
            pltpu.VMEM((seqs, length, 8), F32),
            pltpu.SemaphoreType.DMA((copies,)),
            pltpu.SemaphoreType.DMA((copies,)),
            pltpu.SemaphoreType.DMA((14 + 2 * units,)),
            pltpu.SemaphoreType.DMA((2,)),
        ],
        compiler_params=params(58, collective_id=0, has_side_effects=True),
        name="forward",
    )(e, w_qkv, w_o, w_in, w_out, mix, gain, bias, cosine, sine, ids)

    def whole(x):
        return x.reshape(x.shape[0] * x.shape[1], x.shape[2])

    weights = [whole(g) for g in (g_qkv, g_o, g_in, g_out)]
    return normed, hats, scales, res, *weights, qkv, ctx.reshape(tokens, width)


def attend_back_pair(qkv, grad, out, dk, dv, column_ref, row_ref, c_ref, s_ref, seq, lanes):
    blocks, block = grad.shape[1], grad.shape[2]
    length = blocks * block
    rows = row_tile(length)
    per = rows // block
    factor = HD**-0.5

    def load(ref, at, first, last):
        return ref[(*at, slice(first, last), slice(None), lanes)].reshape(-1, LANES)

    for i in range(length // rows):
        here = slice(i * rows, (i + 1) * rows)
        dk[here] = jnp.zeros((rows, LANES), F32)
        dv[here] = jnp.zeros((rows, LANES), F32)
    for i in range(length // rows):
        first, until = i * rows, (i + 1) * rows
        b0, b1 = i * per, (i + 1) * per
        query = first + lax.broadcasted_iota(jnp.int32, (rows, until), 0)
        key = lax.broadcasted_iota(jnp.int32, (rows, until), 1)
        same = column_ref[seq, first:until, 0:1] == row_ref[seq, 0:1, 0:until]
        allowed = same & (key <= query)
        q = load(qkv, (0, seq), b0, b1) * BF16(factor)
        g = load(grad, (seq,), b0, b1)
        k = load(qkv, (1, seq), 0, b1)
        v = load(qkv, (2, seq), 0, b1)
        total = None
        for h in range(LANES // HD):
            q_h = only(q, h)
            g_h = only(g, h)
            scores = jnp.where(allowed, dot(q_h, k, NT), MASKED)
            peak = jnp.max(scores, axis=-1, keepdims=True)
            raised = jnp.exp(scores - peak)
            mass = jnp.sum(raised, axis=-1, keepdims=True)
            probs = raised * (1.0 / mass)
            dots = dot(g_h, v, NT)
            center = jnp.sum(probs * dots, axis=-1, keepdims=True)
            slope = (probs * (dots - center)).astype(BF16)
            part = dot(slope, k)
            part = jnp.where(head_lanes(part.shape, h), part, 0.0)
            total = part if total is None else total + part
            dk[0:until] += dot(slope, q_h, TN)
            dv[0:until] += dot(probs.astype(BF16), g_h, TN)
        cosine, sine = c_ref[first:until], s_ref[first:until]
        low = turned(total * factor, cosine, -sine).astype(BF16)
        out[0, seq, b0:b1, :, lanes] = low.reshape(per, block, LANES)
    for i in range(length // rows):
        here = slice(i * rows, (i + 1) * rows)
        b0, b1 = i * per, (i + 1) * per
        low = turned(dk[here], c_ref[here], -s_ref[here]).astype(BF16)
        out[1, seq, b0:b1, :, lanes] = low.reshape(per, block, LANES)
        out[2, seq, b0:b1, :, lanes] = dv[here].astype(BF16).reshape(per, block, LANES)


def back_kernel(
    n,
    nf,
    cg_ref,
    qkv_ref,
    in_ref,
    out_ref,
    o_ref,
    ids_ref,
    c_ref,
    s_ref,
    grads_ref,
    in_sum,
    out_sum,
    o_sum,
    qkv,
    grad,
    back,
    dk,
    dv,
    in_keep,
    in_got,
    in_part,
    out_keep,
    out_got,
    out_part,
    o_keep,
    o_got,
    o_part,
    row,
    column,
    send,
    recv,
    local,
):
    f, z = lax.axis_index("fsdp"), lax.axis_index("ctx")
    core = lax.rem(f, 2)
    seqs, _, block, cols = grad.shape
    remote = Remote(send, recv)
    sums = [
        ChipSum(remote, nf, in_ref, in_keep, in_got, in_part),
        ChipSum(remote, nf, out_ref, out_keep, out_got, out_part),
        ChipSum(remote, nf, o_ref, o_keep, o_got, o_part),
    ]
    spots = (z, 2 * n - 1 - z)
    mine = pl.ds(pl.multiple_of(z * cols, LANES), cols)

    loads = [pltpu.make_async_copy(qkv_ref, qkv, local.at[0])]
    for i, (ref, keep) in enumerate([(in_ref, in_keep), (out_ref, out_keep), (o_ref, o_keep)]):
        loads.append(pltpu.make_async_copy(ref.at[:, core], keep, local.at[1 + i]))
    for h in range(2):
        loads.append(
            pltpu.make_async_copy(cg_ref.at[z, :, h], grad.at[:, spots[h]], local.at[4 + h])
        )
    for load in loads:
        load.start()

    greet_all(n, nf)

    arriving = []
    for s in range(seqs):
        copies = []
        for k in range(1, n):
            to = lax.rem(z + k, n)
            for h in range(2):
                copies.append(
                    remote.start(cg_ref.at[to, s, h], grad.at[s, spots[h]], {"ctx": to})
                )
        arriving.append(copies)
    for chip_sum in sums:
        chip_sum.cores()
    place_segments(ids_ref, row, column, block)
    for load in loads:
        load.wait()
    sums[0].cross()

    leaving = []
    kept = []
    for s in range(seqs):
        for copy in arriving[s]:
            copy.wait()

        @pl.loop(0, cols // LANES)
        def _(p):
            lanes = pl.ds(pl.multiple_of(p * LANES, LANES), LANES)
            attend_back_pair(qkv, grad, back, dk, dv, column, row, c_ref, s_ref, s, lanes)

        for k in range(1, n):
            to = lax.rem(z + k, n)
            for h in range(2):
                spot = to if h == 0 else 2 * n - 1 - to
                leaving.append(
                    remote.start(
                        back.at[:, s, spot], grads_ref.at[:, s, h, :, mine], {"ctx": to}
                    )
                )
        for h in range(2):
            copy = pltpu.make_async_copy(
                back.at[:, s, spots[h]], grads_ref.at[:, s, h, :, mine], local.at[6 + 2 * s + h]
            )
            copy.start()
            kept.append(copy)
        if s == 0:
            sums[1].cross()
            sums[2].cross()
            sums[0].relay()

    sums[1].relay()
    sums[2].relay()
    for chip_sum, out in zip(sums, (in_sum, out_sum, o_sum)):
        chip_sum.total(out)
    for copy in kept + leaving:
        copy.wait()


def attention_back(context_grad, qkv, d_in, d_out, d_o, ids, cosine, sine, n, nf):
    _, seqs, spots, block, cols = qkv.shape
    length = spots * block
    width = d_o.shape[1]
    chips = nf // 2

    def by_owner(x):
        return x.reshape(chips, 2, x.shape[0] // nf, x.shape[1])

    terms = [by_owner(d_in), by_owner(d_out), by_owner(d_o)]
    copies = seqs * 4 * (n - 1) + 3 * ChipSum.count(nf)
    vmem = pl.BlockSpec(memory_space=pltpu.VMEM)
    hbm = pl.BlockSpec(memory_space=pltpu.HBM)
    scratch = []
    for term in terms:
        scratch += chip_scratch(nf, term.shape[2], term.shape[3])
    grads, *owned = pl.pallas_call(
        functools.partial(back_kernel, n, nf),
        in_specs=[hbm] * 5 + [vmem] * 3,
        out_specs=[hbm, vmem, vmem, vmem],
        out_shape=[jax.ShapeDtypeStruct((3, seqs, 2, block, width), BF16)]
        + [jax.ShapeDtypeStruct(term.shape[2:], BF16) for term in terms],
        scratch_shapes=[
            pltpu.VMEM((3, seqs, spots, block, cols), BF16),
            pltpu.VMEM((seqs, spots, block, cols), BF16),
            pltpu.VMEM((3, seqs, spots, block, cols), BF16),
            pltpu.VMEM((length, LANES), F32),
            pltpu.VMEM((length, LANES), F32),
            *scratch,
            pltpu.VMEM((seqs, 1, length), F32),
            pltpu.VMEM((seqs, length, 8), F32),
            pltpu.SemaphoreType.DMA((copies,)),
            pltpu.SemaphoreType.DMA((copies,)),
            pltpu.SemaphoreType.DMA((6 + 2 * seqs,)),
        ],
        compiler_params=params(56, collective_id=2, has_side_effects=True),
        name="attention_back",
    )(
        context_grad.reshape(n, seqs, 2, block, cols),
        qkv,
        *terms,
        ids,
        cosine,
        sine,
    )
    return grads.reshape(3, seqs * 2 * block, width), owned


def norm_back_tile(hats, scales, ng, st, e, mg, mg_ref, g_ref, h, low, dgain, dbias, selector, t, strip=16):
    count, tile, width = e.shape
    inv = 1.0 / width
    to = slice(t * tile, (t + 1) * tile)
    for s in range(3):
        dy = ng[s]
        hat = hats[s, to].astype(F32)
        scale = scales[to, s : s + 1]
        dgain[s : s + 1] += jnp.sum(dy * hat, axis=0, keepdims=True)
        dbias[s : s + 1] += jnp.sum(dy, axis=0, keepdims=True)
        dh = dy * g_ref[s : s + 1]
        mean = jnp.sum(dh, axis=-1, keepdims=True) * inv
        along = jnp.sum(dh * hat, axis=-1, keepdims=True) * inv
        out = (scale * (dh - mean - hat * along)).astype(BF16)
        low[s, to] = out
        st[s] = out
    st[3] = h[to].astype(BF16)

    shape = (4 * strip, count * strip)
    same = lax.rem(lax.broadcasted_iota(jnp.int32, shape, 0), strip) == lax.rem(
        lax.broadcasted_iota(jnp.int32, shape, 1), strip
    )
    for i in range(tile // strip):
        rows = slice(i * strip, (i + 1) * strip)
        grads = st[:, rows].reshape(4 * strip, width)
        inputs = e[:, rows].reshape(count * strip, width)
        products = jnp.where(same, dot(grads, inputs, NT), 0.0)
        wide = jnp.concatenate(
            [products[s * strip : (s + 1) * strip] for s in range(4)], axis=1
        )
        high, rest = halves(wide)
        mg[rows] = dot(high, selector[...]) + dot(rest, selector[...])
    turned_mg = mg[...].T
    block = mg_ref.shape[4]
    per = tile // block
    for i in range(per):
        place = t * per + i
        for a in range(4):
            mg_ref[a, :, place // 2, place % 2, :] = turned_mg[
                a * count : (a + 1) * count, i * block : (i + 1) * block
            ]


def end_kernel(
    n,
    nf,
    grads_ref,
    normed_ref,
    hats_ref,
    scales_ref,
    e_ref,
    w_ref,
    h_ref,
    gain_ref,
    in_ref,
    out_ref,
    o_ref,
    sgain_ref,
    sbias_ref,
    sw1_ref,
    sw2_ref,
    smb_ref,
    low_ref,
    mg_ref,
    q_sum,
    k_sum,
    v_sum,
    in_sum,
    out_sum,
    o_sum,
    gain_sum,
    bias_sum,
    w1_sum,
    w2_sum,
    mb_sum,
    grads,
    normed,
    hats,
    scales,
    w,
    h,
    e,
    ng,
    st,
    low,
    mg,
    selector,
    dgain,
    dbias,
    small_work,
    small_in,
    small_line,
    small_sum,
    send,
    recv,
    local,
    e_sem,
    *more,
):
    f, z = lax.axis_index("fsdp"), lax.axis_index("ctx")
    core = lax.rem(f, 2)
    count, tokens, width = e_ref.shape
    tile = e.shape[2]
    tiles = tokens // tile
    remote = Remote(send, recv)
    line_sets = [more[3 * i : 3 * i + 3] for i in range(6)]
    chip_sets = [more[18 + 4 * i : 22 + 4 * i] for i in range(3)]
    shard = chip_sets[0][1].shape[1]

    def fetch(t):
        return pltpu.make_async_copy(
            e_ref.at[:, t * tile : (t + 1) * tile], e.at[t % 2], e_sem.at[t % 2]
        )

    loads = [
        pltpu.make_async_copy(src, dst, local.at[i])
        for i, (src, dst) in enumerate(
            [
                (grads_ref, grads),
                (normed_ref, normed),
                (w_ref, w),
                (hats_ref, hats),
                (scales_ref, scales),
                (h_ref, h),
            ]
        )
    ]
    for load in loads:
        load.start()
    fetch(0).start()

    greet_all(n, nf)

    lines = [
        LineSum(remote, n, work, out, *scratch)
        for work, out, scratch in zip(
            (in_ref, out_ref, o_ref), (in_sum, out_sum, o_sum), line_sets
        )
    ]
    for line in lines:
        line.first()

    loads[0].wait()
    loads[1].wait()
    cut = 256
    per = cut // (2 * shard)
    sums = []
    for i in range(3):
        terms, got, part, own = chip_sets[i]
        for c in range(width // cut):
            value = dot(normed[i, :, c * cut : (c + 1) * cut], grads[i], TN).astype(BF16)
            terms[c * per : (c + 1) * per] = value.reshape(per, 2, shard, width)
        chip_sum = ChipSum(remote, nf, terms, terms.at[:, core], got, part)
        chip_sum.cores()
        sums.append(chip_sum)
    dgain[...] = jnp.zeros_like(dgain)
    dbias[...] = jnp.zeros_like(dbias)
    size = selector.shape
    group = lax.broadcasted_iota(jnp.int32, size, 0) // 16
    selector[...] = jnp.where(
        group == lax.broadcasted_iota(jnp.int32, size, 1), 1.0, 0.0
    ).astype(BF16)
    for load in loads[2:]:
        load.wait()

    def do_tile(t):
        fetch(t).wait()
        if t + 1 < tiles:
            fetch(t + 1).start()
        rows = slice(t * tile, (t + 1) * tile)
        for i in range(3):
            ng[i] = dot(grads[i, rows], w[:, i * width : (i + 1) * width], NT)
        norm_back_tile(
            hats, scales, ng, st, e.at[t % 2], mg, mg_ref, gain_ref, h, low, dgain, dbias, selector, t
        )

    todo = list(range(tiles))

    def some():
        if todo:
            do_tile(todo.pop(0))

    for chip_sum in sums:
        chip_sum.cross()
    lines[0].second()
    some()
    lines[1].second()
    some()
    sums[0].relay()
    lines[2].second()
    some()
    sums[1].relay()
    lines[0].third()
    while todo:
        some()
    keep = pltpu.make_async_copy(low, low_ref, local.at[6])
    keep.start()
    sums[2].relay()

    thin = small_in.shape[1]
    hidden_count, coef_count = sw2_ref.shape
    first = 8 + hidden_count
    last = first + hidden_count
    small_work[...] = jnp.zeros_like(small_work)
    small_work[0:3] = dgain[...]
    small_work[3:4] = sgain_ref[...]
    small_work[4:7] = dbias[...]
    small_work[7:8] = sbias_ref[...]
    small_work[8:first] = sw1_ref[...]
    small_work[first:last, 0:coef_count] = sw2_ref[...]
    small_work[last : last + 1, 0:coef_count] = smb_ref[...]
    here = pl.ds(pl.multiple_of(f * thin, thin), thin)
    small_in[0] = small_work[here]
    slices = []
    for k in range(1, nf):
        to = lax.rem(f + k, nf)
        slices.append(
            remote.start(
                small_work.at[pl.ds(pl.multiple_of(to * thin, thin), thin)],
                small_in.at[k],
                {"fsdp": to},
            )
        )

    late = []
    for chip_sum, chip_set, out, scratch in zip(
        sums, chip_sets, (q_sum, k_sum, v_sum), line_sets[3:]
    ):
        chip_sum.total(chip_set[3])
        line = LineSum(remote, n, chip_set[3], out, *scratch)
        line.first()
        late.append(line)

    for copy in slices:
        copy.wait()
    total = small_in[0]
    for k in range(1, nf):
        total = total + small_in[k]
    small_line[z] = total
    across = []
    for k in range(1, n):
        across.append(
            remote.start(small_line.at[z], small_line.at[z], {"ctx": lax.rem(z + k, n)})
        )
    for line in late:
        line.second()
    for copy in across:
        copy.wait()
    total = small_line[0]
    for k in range(1, n):
        total = total + small_line[k]
    small_sum[here] = total
    spread = []
    for k in range(1, nf):
        spread.append(
            remote.start(small_sum.at[here], small_sum.at[here], {"fsdp": lax.rem(f + k, nf)})
        )
    for line in lines[1:] + late:
        line.third()
    for copy in spread:
        copy.wait()
    gain_sum[...] = small_sum[0:4]
    bias_sum[...] = small_sum[4:8]
    w1_sum[...] = small_sum[8:first]
    w2_sum[...] = small_sum[first:last, 0:coef_count]
    mb_sum[...] = small_sum[last : last + 1, 0:coef_count]
    for line in lines + late:
        line.end()
    keep.wait()


def finish(grads, normed, hats, scales, e, w, hgrad, gain, owned, small, mix_shape, n, nf):
    count, tokens, width = e.shape
    tile = 128
    chips = nf // 2
    shard = width // nf
    levels = max(n.bit_length() - 2, 1)
    rows = sum(x.shape[0] for x in small) + 6
    thin = 8 * -(-rows // (8 * nf))

    def line(shape):
        half = (shape[0] // 2, shape[1])
        return [
            pltpu.VMEM(half, BF16),
            pltpu.VMEM((levels,) + half, BF16),
            pltpu.VMEM((levels,) + half, BF16),
        ]

    lines, chip_sums = [], []
    for x in owned:
        lines += line(x.shape)
    for _ in range(3):
        lines += line((shard, width))
        chip_sums += [
            pltpu.VMEM((chips, 2, shard, width), BF16),
            *chip_scratch(nf, shard, width)[1:],
            pltpu.VMEM((shard, width), BF16),
        ]
    copies = 6 * (levels + 2) + 3 * ChipSum.count(nf) + 2 * (nf - 1) + (n - 1)
    vmem = pl.BlockSpec(memory_space=pltpu.VMEM)
    hbm = pl.BlockSpec(memory_space=pltpu.HBM)
    wide = jax.ShapeDtypeStruct((shard, width), BF16)
    s_gain, s_bias, s_w1, s_w2, s_mb = small
    return pl.pallas_call(
        functools.partial(end_kernel, n, nf),
        in_specs=[hbm] * 7 + [vmem] * 9,
        out_specs=[hbm] + [vmem] * 12,
        out_shape=[
            jax.ShapeDtypeStruct((3, tokens, width), BF16),
            jax.ShapeDtypeStruct(mix_shape, F32),
            wide,
            wide,
            wide,
            *[jax.ShapeDtypeStruct(x.shape, BF16) for x in owned],
            jax.ShapeDtypeStruct((4, width), F32),
            jax.ShapeDtypeStruct((4, width), F32),
            jax.ShapeDtypeStruct(s_w1.shape, F32),
            jax.ShapeDtypeStruct(s_w2.shape, F32),
            jax.ShapeDtypeStruct(s_mb.shape, F32),
        ],
        scratch_shapes=[
            pltpu.VMEM(grads.shape, BF16),
            pltpu.VMEM(normed.shape, BF16),
            pltpu.VMEM(hats.shape, BF16),
            pltpu.VMEM(scales.shape, F32),
            pltpu.VMEM(w.shape, BF16),
            pltpu.VMEM(hgrad.shape, F32),
            pltpu.VMEM((2, count, tile, width), BF16),
            pltpu.VMEM((3, tile, width), F32),
            pltpu.VMEM((4, tile, width), BF16),
            pltpu.VMEM((3, tokens, width), BF16),
            pltpu.VMEM((tile, LANES), F32),
            pltpu.VMEM((4 * count * 16, LANES), BF16),
            pltpu.VMEM((3, width), F32),
            pltpu.VMEM((3, width), F32),
            pltpu.VMEM((nf * thin, width), F32),
            pltpu.VMEM((nf, thin, width), F32),
            pltpu.VMEM((n, thin, width), F32),
            pltpu.VMEM((nf * thin, width), F32),
            pltpu.SemaphoreType.DMA((copies,)),
            pltpu.SemaphoreType.DMA((copies,)),
            pltpu.SemaphoreType.DMA((7,)),
            pltpu.SemaphoreType.DMA((2,)),
            *lines,
            *chip_sums,
        ],
        compiler_params=params(60, collective_id=3, has_side_effects=True),
        name="finish",
    )(grads, normed, hats, scales, e, w, hgrad, gain, *owned, *small)


def tail_kernel(
    low_ref,
    h_ref,
    mix_ref,
    q_ref,
    k_ref,
    v_ref,
    in_ref,
    out_ref,
    o_ref,
    eg_ref,
    qkv_ref,
    in32_ref,
    out32_ref,
    o32_ref,
    mixes,
    *,
    strip,
):
    count, tile, width = eg_ref.shape
    chunk = 512
    block = mix_ref.shape[4]
    tiles = mix_ref.shape[2] * 2 * block // tile
    for t in range(tiles):

        @pl.when(pl.program_id(0) == t)
        def _():
            mix_columns(mix_ref, mixes, t)

    for i, ref in enumerate((q_ref, k_ref, v_ref)):
        qkv_ref[:, i * width : (i + 1) * width] = ref[...].astype(F32)
    in32_ref[...] = in_ref[...].astype(F32)
    out32_ref[...] = out_ref[...].astype(F32)
    o32_ref[...] = o_ref[...].astype(F32)

    @pl.loop(0, tile // strip)
    def _(i):
        rows = pl.ds(pl.multiple_of(i * strip, strip), strip)
        mix = mixes[rows]
        for c in range(width // chunk):
            cols = slice(c * chunk, (c + 1) * chunk)
            grads = [low_ref[s, rows, cols].astype(F32) for s in range(3)]
            grads.append(h_ref[rows, cols])
            for j in range(count):
                total = grads[0] * mix[:, j : j + 1]
                for s in range(1, 4):
                    total = total + grads[s] * mix[:, s * count + j : s * count + j + 1]
                eg_ref[j, rows, cols] = total.astype(BF16)


def spread_back(low, hgrad, mix, q, k, v, s_in, s_out, s_o):
    _, tokens, width = low.shape
    count = mix.shape[1]
    tile = 128
    tiles = tokens // tile

    def part(x):
        return pl.BlockSpec((x.shape[0] // tiles, x.shape[1]), lambda i: (i, 0))

    shard = q.shape[0]
    outs = [
        jax.ShapeDtypeStruct((count, tokens, width), BF16),
        jax.ShapeDtypeStruct((shard, 3 * width), F32),
        jax.ShapeDtypeStruct(s_in.shape, F32),
        jax.ShapeDtypeStruct(s_out.shape, F32),
        jax.ShapeDtypeStruct(s_o.shape, F32),
    ]
    zeros = (0,) * mix.ndim
    return pl.pallas_call(
        functools.partial(tail_kernel, strip=16),
        grid=(tiles,),
        in_specs=[
            pl.BlockSpec((3, tile, width), lambda i: (0, i, 0)),
            pl.BlockSpec((tile, width), lambda i: (i, 0)),
            pl.BlockSpec(mix.shape, lambda i: zeros),
            *[part(x) for x in (q, k, v, s_in, s_out, s_o)],
        ],
        out_specs=[pl.BlockSpec((count, tile, width), lambda i: (0, i, 0))]
        + [part(x) for x in outs[1:]],
        out_shape=outs,
        scratch_shapes=[pltpu.VMEM((tile, 4 * count), F32)],
        compiler_params=params(40),
        cost_estimate=pl.CostEstimate(
            flops=64 * tokens * width, bytes_accessed=40 * tokens * width, transcendentals=0
        ),
        name="spread_back",
    )(low, hgrad, mix, q, k, v, s_in, s_out, s_o)


def body(
    earlier,
    mix_in,
    segment_ids,
    attn_qkv,
    attn_out,
    mlp_in,
    mlp_out,
    norm_gain,
    norm_bias,
    mix_w1,
    mix_w2,
    mix_bias,
    out_grad,
    coef_grad,
):
    count, seqs, _, block, width = earlier.shape
    n = lax.axis_size("ctx")
    tokens = seqs * 2 * block
    length = 2 * n * block
    me = lax.axis_index("ctx")

    nf = lax.axis_size("fsdp")
    e = earlier.reshape(count, tokens, width)
    cosine, sine = (jnp.asarray(table) for table in turn_tables(length))
    normed, hats, scales, residual, w_qkv, w_o, w_in, w_out, qkv, context = forward(
        e,
        mix_in,
        attn_qkv,
        attn_out,
        mlp_in,
        mlp_out,
        norm_gain,
        norm_bias,
        cosine,
        sine,
        segment_ids,
        n,
        nf,
    )
    (
        layer_out,
        coefs,
        d_in,
        d_out,
        d_o,
        context_grad,
        hidden_grad,
        d_gain,
        d_bias,
        d_w1,
        d_w2,
        d_mb,
    ) = feed(
        residual,
        context,
        w_o,
        w_in,
        w_out,
        norm_gain,
        norm_bias,
        mix_w1,
        mix_w2,
        mix_bias[None, :],
        out_grad.reshape(tokens, width),
        coef_grad,
        n,
    )
    grads, owned = attention_back(
        context_grad, qkv, d_in, d_out, d_o, segment_ids, cosine, sine, n, nf
    )
    low, m_grad, s_q, s_k, s_v, s_in, s_out, s_o, *small = finish(
        grads,
        normed,
        hats,
        scales,
        e,
        w_qkv,
        hidden_grad,
        norm_gain,
        owned,
        (d_gain, d_bias, d_w1, d_w2, d_mb),
        mix_in.shape,
        n,
        nf,
    )
    e_grad, g_qkv, g_in, g_out, g_o = spread_back(
        low, hidden_grad, mix_in, s_q, s_k, s_v, s_in, s_out, s_o
    )
    return (
        layer_out.reshape(seqs, 2, block, width),
        coefs,
        e_grad.reshape(count, seqs, 2, block, width),
        m_grad,
        g_qkv,
        g_o,
        g_in,
        g_out,
        small[0],
        small[1],
        small[2],
        small[3],
        small[4][0],
    )


def solution(mesh):
    in_specs = (
        P(None, "fsdp", None, "ctx", None),
        P(None, None, "fsdp", None, "ctx"),
        P("fsdp", None, None),
        P("fsdp", None),
        P("fsdp", None),
        P("fsdp", None),
        P("fsdp", None),
        P(),
        P(),
        P(),
        P(),
        P(),
        P("fsdp", None, "ctx", None),
        P(None, None, "fsdp", None, "ctx"),
    )
    out_specs = (
        P("fsdp", None, "ctx", None),
        P(None, None, "fsdp", None, "ctx"),
        P(None, "fsdp", None, "ctx", None),
        P(None, None, "fsdp", None, "ctx"),
        P("fsdp", None),
        P("fsdp", None),
        P("fsdp", None),
        P("fsdp", None),
        P(),
        P(),
        P(),
        P(),
        P(),
    )
    return jax.shard_map(body, mesh=mesh, in_specs=in_specs, out_specs=out_specs, check_vma=False)
```

```python
import functools
import math

import jax
import jax.numpy as jnp
import numpy as np
from jax import lax
from jax.experimental import pallas as pl
from jax.experimental.pallas import tpu as pltpu
from jax.sharding import PartitionSpec as P

HD = 64
ROT = 16
LANES = 128
EPSILON = 1e-05
RMS_EPSILON = 1e-06
MASKED = -1e30
F32 = jnp.float32
BF16 = jnp.bfloat16
MESH = pl.DeviceIdType.MESH
MIB = 1024 * 1024

NN = (((1,), (0,)), ((), ()))
NT = (((1,), (1,)), ((), ()))
TN = (((0,), (0,)), ((), ()))

ERFC_RATE = 0.4
ERFC = (
    0.22567586600780487,
    0.22566929459571838,
    0.20784726738929749,
    0.16851142048835754,
    0.1415392905473709,
    -0.005822250619530678,
    0.16932761669158936,
    -0.18304575979709625,
    0.05029737576842308,
)


def dot(a, b, dims=NN):
    return lax.dot_general(a, b, dims, preferred_element_type=F32)


def gelu_and_slope(v):
    z = jnp.abs(v) * math.sqrt(0.5)
    bell = jnp.exp(-0.5 * v * v)
    t = 1.0 / (1.0 + ERFC_RATE * z)
    poly = jnp.full_like(t, ERFC[-1])
    for coefficient in ERFC[-2::-1]:
        poly = poly * t + coefficient
    tail = 0.5 * poly * t * bell
    phi = jnp.where(v >= 0.0, 1.0 - tail, tail)
    return v * phi, phi + v * bell * (1.0 / math.sqrt(2.0 * math.pi))


def halves(x):
    high = x.astype(BF16)
    return high, (x - high.astype(F32)).astype(BF16)


def params(limit_mib, **more):
    return pltpu.CompilerParams(vmem_limit_bytes=limit_mib * MIB, **more)


def once(shape, index):
    return pl.BlockSpec(shape, index, pipeline_mode=pl.Buffered(1))


def turn_tables(length):
    half = ROT // 2
    frequency = 10000.0 ** (-(np.arange(half) * 2.0 / ROT))
    angle = np.arange(length)[:, None] * frequency[None, :]
    lane = np.arange(LANES) % HD
    cosine = np.ones((length, LANES), np.float32)
    sine = np.zeros((length, LANES), np.float32)
    for k in range(LANES):
        if lane[k] < ROT:
            cosine[:, k] = np.cos(angle[:, lane[k] % half])
            sign = -1.0 if lane[k] < half else 1.0
            sine[:, k] = sign * np.sin(angle[:, lane[k] % half])
    return cosine, sine


def turned(x, cosine, sine):
    half = ROT // 2
    lane = lax.broadcasted_iota(jnp.int32, x.shape, 1) % HD
    other = jnp.where(
        lane < half, pltpu.roll(x, LANES - half, axis=1), pltpu.roll(x, half, axis=1)
    )
    return x * cosine + other * sine


def row_tile(length):
    return min(256, length)


def head_lanes(shape, h):
    lane = lax.broadcasted_iota(jnp.int32, shape, 1)
    return (lane >= h * HD) & (lane < (h + 1) * HD)


def only(x, h):
    return jnp.where(head_lanes(x.shape, h), x, jnp.zeros_like(x))


def coefficient_places(ref):
    outer, inner, seqs, _, block = ref.shape
    for a in range(outer):
        for seq in range(seqs):
            for h in range(2):
                first = (2 * seq + h) * block
                yield a, seq, h, slice(a * inner, (a + 1) * inner), slice(first, first + block)


def feed_kernel(
    res_ref,
    ctx_ref,
    wo_ref,
    win_ref,
    wout_ref,
    g_ref,
    b_ref,
    w1_ref,
    w2_ref,
    mb_ref,
    og_ref,
    cg_ref,
    out_ref,
    coef_ref,
    dwin_ref,
    dwout_ref,
    dwo_ref,
    cgrad_ref,
    hgrad_ref,
    dgain_ref,
    dbias_ref,
    dw1_ref,
    dw2_ref,
    dmb_ref,
    hidden,
    normed,
    total,
    active,
    slope,
    branch,
    r_high,
    r_rest,
    cotangent,
    *,
    tiles,
    strip,
):
    step = pl.program_id(0)
    tokens, width = res_ref.shape
    cut = win_ref.shape[1]
    inv = 1.0 / width

    @pl.when(step == 0)
    def _():
        hidden[...] = dot(ctx_ref[...], wo_ref[...])

        @pl.loop(0, tokens // strip)
        def _(i):
            rows = pl.ds(pl.multiple_of(i * strip, strip), strip)
            v = hidden[rows] + res_ref[rows]
            hidden[rows] = v
            center = v - jnp.sum(v, axis=-1, keepdims=True) * inv
            spread = jnp.sum(center * center, axis=-1, keepdims=True) * inv
            hat = center * lax.rsqrt(spread + EPSILON)
            normed[rows] = (hat * g_ref[3:4] + b_ref[3:4]).astype(BF16)
            total[rows] = v

    @pl.when(step < tiles)
    def _():
        value, rate = gelu_and_slope(dot(normed[...], win_ref[...]))
        low = value.astype(BF16)
        active[step] = low
        slope[step] = rate
        total[...] += dot(low, wout_ref[...])

    @pl.when(step == tiles - 1)
    def _():
        w1 = w1_ref[...]
        w2 = w2_ref[...]

        @pl.loop(0, tokens // strip)
        def _(i):
            rows = pl.ds(pl.multiple_of(i * strip, strip), strip)
            v = total[rows]
            out_ref[rows] = v.astype(BF16)
            scale = lax.rsqrt(jnp.sum(v * v, axis=-1, keepdims=True) * inv + RMS_EPSILON)
            r = v * scale
            high = r.astype(BF16)
            r_high[rows] = high
            r_rest[rows] = (r - high.astype(F32)).astype(BF16)

        high, rest = r_high[...], r_rest[...]
        for a, seq, h, rows, cols in coefficient_places(cg_ref):
            cotangent[rows, cols] = cg_ref[a, :, seq, h, :]
        z = dot(w1, high, NT) + dot(w1, rest, NT)
        value, rate = gelu_and_slope(z)
        v_high, v_rest = halves(value)
        ones = jnp.ones((1, tokens), BF16)
        mb_high, mb_rest = halves(mb_ref[...])
        mb_last = (mb_ref[...] - mb_high.astype(F32) - mb_rest.astype(F32)).astype(BF16)
        shift = dot(mb_high, ones, TN) + dot(mb_rest, ones, TN) + dot(mb_last, ones, TN)
        coefs = dot(w2, v_high, TN) + dot(w2, v_rest, TN) + shift
        for a, seq, h, rows, cols in coefficient_places(coef_ref):
            coef_ref[a, :, seq, h, :] = coefs[rows, cols]
        c_high, c_rest = halves(cotangent[...])
        dmb_ref[...] = dot(ones, c_high, NT) + dot(ones, c_rest, NT)
        dw2_ref[...] = dot(v_high, c_high, NT) + dot(v_rest, c_high, NT) + dot(v_high, c_rest, NT)
        z_high, z_rest = halves((dot(w2, c_high) + dot(w2, c_rest)) * rate)
        dw1_ref[...] = dot(z_high, high) + dot(z_high, rest) + dot(z_rest, high)
        hgrad_ref[...] = dot(z_high, w1, TN) + dot(z_rest, w1, TN)

        @pl.loop(0, tokens // strip)
        def _(i):
            rows = pl.ds(pl.multiple_of(i * strip, strip), strip)
            v = total[rows]
            scale = lax.rsqrt(jnp.sum(v * v, axis=-1, keepdims=True) * inv + RMS_EPSILON)
            dr = hgrad_ref[rows]
            r = v * scale
            mean = jnp.sum(dr * r, axis=-1, keepdims=True) * inv
            grad = scale * (dr - r * mean) + og_ref[rows].astype(F32)
            hgrad_ref[rows] = grad
            branch[rows] = grad.astype(BF16)
            total[rows] = jnp.zeros_like(v)

    @pl.when(step >= tiles)
    def _():
        j = step - tiles
        low = (dot(branch[...], wout_ref[...], NT) * slope[j]).astype(BF16)
        total[...] += dot(low, win_ref[...], NT)
        dwin_ref[...] = dot(normed[...], low, TN).astype(BF16)
        dwout_ref[...] = dot(active[j], branch[...], TN).astype(BF16)

    @pl.when(step == 2 * tiles - 1)
    def _():
        dgain_ref[...] = jnp.zeros_like(dgain_ref)
        dbias_ref[...] = jnp.zeros_like(dbias_ref)

        @pl.loop(0, tokens // strip)
        def _(i):
            rows = pl.ds(pl.multiple_of(i * strip, strip), strip)
            v = hidden[rows]
            dy = total[rows]
            center = v - jnp.sum(v, axis=-1, keepdims=True) * inv
            spread = jnp.sum(center * center, axis=-1, keepdims=True) * inv
            scale = lax.rsqrt(spread + EPSILON)
            hat = center * scale
            dgain_ref[...] += jnp.sum(dy * hat, axis=0, keepdims=True)
            dbias_ref[...] += jnp.sum(dy, axis=0, keepdims=True)
            dh = dy * g_ref[3:4]
            first = jnp.sum(dh, axis=-1, keepdims=True) * inv
            second = jnp.sum(dh * hat, axis=-1, keepdims=True) * inv
            grad = hgrad_ref[rows] + scale * (dh - first - hat * second)
            hgrad_ref[rows] = grad
            branch[rows] = grad.astype(BF16)

        dwo_ref[...] = dot(ctx_ref[...], branch[...], TN).astype(BF16)
        groups, _, group = cgrad_ref.shape
        for i in range(groups):
            rows = slice(i * group, (i + 1) * group)
            cgrad_ref[i] = dot(branch[...], wo_ref[rows], NT).astype(BF16)


def feed(res, ctx, wo, win, wout, gain, bias, w1, w2, mb, og, cg, groups):
    tokens, width = res.shape
    hidden_units = win.shape[1]
    cut = 1024
    tiles = hidden_units // cut
    small, coefs = w1.shape[0], w2.shape[1]

    def whole(x):
        zeros = (0,) * x.ndim
        return once(x.shape, lambda i: zeros)

    def result(shape, dtype=F32):
        zeros = (0,) * len(shape)
        return once(shape, lambda i: zeros), jax.ShapeDtypeStruct(shape, dtype)

    def back(i):
        return jnp.maximum(i - tiles, 0)

    outs = [
        result((tokens, width), BF16),
        result(cg.shape),
        (
            pl.BlockSpec((width, cut), lambda i: (0, back(i))),
            jax.ShapeDtypeStruct((width, hidden_units), BF16),
        ),
        (
            pl.BlockSpec((cut, width), lambda i: (back(i), 0)),
            jax.ShapeDtypeStruct((hidden_units, width), BF16),
        ),
        result((width, width), BF16),
        result((groups, tokens, width // groups), BF16),
        result((tokens, width)),
        result((1, width)),
        result((1, width)),
        result((small, width)),
        result((small, coefs)),
        result((1, coefs)),
    ]
    return pl.pallas_call(
        functools.partial(feed_kernel, tiles=tiles, strip=min(512, tokens)),
        grid=(2 * tiles,),
        in_specs=[
            whole(res),
            whole(ctx),
            whole(wo),
            pl.BlockSpec((width, cut), lambda i: (0, lax.rem(i, tiles))),
            pl.BlockSpec((cut, width), lambda i: (lax.rem(i, tiles), 0)),
            whole(gain),
            whole(bias),
            whole(w1),
            whole(w2),
            whole(mb),
            whole(og),
            whole(cg),
        ],
        out_specs=[spec for spec, _ in outs],
        out_shape=[shape for _, shape in outs],
        scratch_shapes=[
            pltpu.VMEM((tokens, width), F32),
            pltpu.VMEM((tokens, width), BF16),
            pltpu.VMEM((tokens, width), F32),
            pltpu.VMEM((tiles, tokens, cut), BF16),
            pltpu.VMEM((tiles, tokens, cut), F32),
            pltpu.VMEM((tokens, width), BF16),
            pltpu.VMEM((tokens, width), BF16),
            pltpu.VMEM((tokens, width), BF16),
            pltpu.VMEM((coefs, tokens), F32),
        ],
        compiler_params=params(58),
        cost_estimate=pl.CostEstimate(
            flops=12 * tokens * width * hidden_units + 6 * tokens * width * width,
            bytes_accessed=12 * width * hidden_units + 4 * width * width + 20 * tokens * width,
            transcendentals=2 * tokens * hidden_units,
        ),
        name="feed",
    )(res, ctx, wo, win, wout, gain, bias, w1, w2, mb, og, cg)


def flipped(v, mask):
    bit = 1
    while bit <= mask:
        if mask & bit:
            v = v + bit - 2 * bit * lax.rem(v // bit, 2)
        bit *= 2
    return v


def added(out_ref, refs, rows, strip=32):
    strip = min(strip, rows)

    @pl.loop(0, rows // strip)
    def _(i):
        at = pl.ds(pl.multiple_of(i * strip, strip), strip)
        total = refs[0][at].astype(F32)
        for ref in refs[1:]:
            total = total + ref[at].astype(F32)
        out_ref[at] = total.astype(out_ref.dtype)


class Remote:
    def __init__(self, send, recv):
        self.send, self.recv, self.used = send, recv, 0

    def start(self, src, dst, where):
        copy = self.make(src, dst, where)
        copy.start()
        return copy

    def make(self, src, dst, where):
        copy = pltpu.make_async_remote_copy(
            src_ref=src,
            dst_ref=dst,
            send_sem=self.send.at[self.used],
            recv_sem=self.recv.at[self.used],
            device_id=where,
            device_id_type=MESH,
        )
        self.used += 1
        return copy


class Chain:
    def __init__(self, remote, n):
        self.remote, self.n = remote, n
        self.me = lax.axis_index("ctx")
        place = lax.rem(self.me, 4)
        self.outer = jnp.logical_or(place == 0, place == 3)
        self.inner = jnp.logical_not(self.outer)
        self.pieces = []
        self.started = 0

    def add(self, work, out, land, own, crosses):
        there = {"ctx": flipped(self.me, 1)}
        up = self.remote.make(work, land, there)
        masks = [3]
        bit = 4
        while bit < self.n:
            masks.append(bit)
            bit *= 2
        across = [
            self.remote.make(own.at[i], crosses.at[i], {"ctx": flipped(self.me, mask)})
            for i, mask in enumerate(masks)
        ]
        down = self.remote.make(out, out, there)
        self.pieces.append((work, out, land, own, crosses, up, across, down))

    def start(self):
        if self.started < len(self.pieces):
            up = self.pieces[self.started][5]

            @pl.when(self.outer)
            def _():
                up.start()

        self.started += 1

    def step(self, c):
        work, _, land, own, _, up, across, _ = self.pieces[c]

        @pl.when(self.outer)
        def _():
            up.wait_send()

        self.start()

        @pl.when(self.inner)
        def _():
            up.wait_recv()
            added(own.at[0], [work, land], work.shape[0])
            across[0].start()

        if c >= 2:
            self.leave(c - 2)

    def leave(self, c):
        _, out, _, own, crosses, _, across, down = self.pieces[c]

        @pl.when(self.inner)
        def _():
            for i, copy in enumerate(across):
                copy.wait()
                last = i + 1 == len(across)
                to = out if last else own.at[i + 1]
                added(to, [own.at[i], crosses.at[i]], out.shape[0])
                if not last:
                    across[i + 1].start()
            down.start()

    def end(self, c):
        down = self.pieces[c][7]

        @pl.when(self.outer)
        def _():
            down.wait_recv()

        @pl.when(self.inner)
        def _():
            down.wait_send()

    @staticmethod
    def levels(n):
        return max(1, n.bit_length() - 2)


def chain_scratch(n, rows, cols):
    levels = Chain.levels(n)
    return [
        pltpu.VMEM((rows, cols), BF16),
        pltpu.VMEM((levels, rows, cols), BF16),
        pltpu.VMEM((levels, rows, cols), BF16),
    ]


class ChipSum:
    def __init__(self, remote, nf, terms, keep, got, part):
        self.remote, self.nf, self.terms = remote, nf, terms
        self.keep, self.got, self.part = keep, got, part
        self.f = lax.axis_index("fsdp")
        self.chip, self.core = self.f // 2, lax.rem(self.f, 2)
        self.rows = got.shape[1]
        self.half = self.rows // 2
        bits = []
        bit = 1
        while bit < nf // 2:
            bits.append(bit)
            bit *= 2
        self.orders = (bits, bits[::-1])
        self.level = len(bits) - 1
        self.slots = 0

    def cores(self):
        self.copy = self.remote.start(
            self.terms.at[:, 1 - self.core], self.got, {"fsdp": flipped(self.f, 1)}
        )

    def masks(self, which, level):
        found = [0]
        for bit in self.orders[which][:level]:
            found += [mask + bit for mask in found]
        return found

    def piece(self, which, chip):
        return self.got.at[chip, pl.ds(which * self.half, self.half)]

    def launch(self):
        self.flying = []
        for which in range(2):
            bit = self.orders[which][self.level]
            to = 2 * flipped(self.chip, bit) + self.core
            for mask in self.masks(which, self.level):
                landing = self.part.at[self.slots]
                self.slots += 1
                copy = self.remote.start(
                    self.piece(which, flipped(self.chip, mask + bit)), landing, {"fsdp": to}
                )
                self.flying.append((copy, which, mask, landing))

    def cross(self):
        self.copy.wait()
        for k in range(self.nf // 2):
            added(self.got.at[k], [self.keep.at[k], self.got.at[k]], self.rows)
        self.launch()

    def relay(self):
        while self.level > 0:
            for copy, which, mask, landing in self.flying:
                copy.wait()
                here = self.piece(which, flipped(self.chip, mask))
                added(here, [here, landing], self.half)
            self.level -= 1
            self.launch()

    def total(self, out):
        for copy, which, _, landing in self.flying:
            copy.wait()
            added(
                out.at[pl.ds(which * self.half, self.half)],
                [self.piece(which, self.chip), landing],
                self.half,
            )

    @staticmethod
    def count(nf):
        return 1 + 2 * (nf // 2 - 1)


def chip_scratch(nf, rows, cols):
    chips = nf // 2
    return [
        pltpu.VMEM((chips, rows, cols), BF16),
        pltpu.VMEM((chips, rows, cols), BF16),
        pltpu.VMEM((2 * chips - 2, rows // 2, cols), BF16),
    ]


def greet_all(n, nf):
    z, f = lax.axis_index("ctx"), lax.axis_index("fsdp")
    barrier = pltpu.get_barrier_semaphore()
    for k in range(1, nf):
        pl.semaphore_signal(
            barrier, inc=1, device_id={"fsdp": lax.rem(f + k, nf)}, device_id_type=MESH
        )
    for k in range(1, n):
        pl.semaphore_signal(
            barrier, inc=1, device_id={"ctx": lax.rem(z + k, n)}, device_id_type=MESH
        )
    pl.semaphore_wait(barrier, nf + n - 2)


def place_segments(ids_ref, row, column, block):
    seqs, _, half = ids_ref.shape
    n = half // block
    for s in range(seqs):
        row[s, :, 0:half] = ids_ref[s, 0:1].astype(F32)
        for b in range(n):
            at = slice((n - 1 - b) * block, (n - b) * block)
            to = slice(half + b * block, half + (b + 1) * block)
            row[s, :, to] = ids_ref[s, 1:2, at].astype(F32)
        column[s] = jnp.broadcast_to(row[s], (8, 2 * half)).T


def mix_columns(mix_ref, mixes, t):
    block = mix_ref.shape[4]
    tile = mixes.shape[0]
    per = tile // block
    parts = []
    for i in range(t * per, (t + 1) * per):
        rows = [mix_ref[a, :, i // 2, i % 2, :] for a in range(mix_ref.shape[0])]
        parts.append(jnp.concatenate(rows, axis=0))
    mixes[...] = (parts[0] if per == 1 else jnp.concatenate(parts, axis=1)).T


class PlaneGather:
    def __init__(self, remote, nf, src, out):
        self.remote, self.nf, self.src, self.out = remote, nf, src, out
        self.f = lax.axis_index("fsdp")
        self.half = src.shape[0] // 2
        bits = []
        bit = 2
        while bit < nf:
            bits.append(bit)
            bit *= 2
        self.orders = (bits, bits[::-1])
        self.levels = len(bits)
        self.flying = {}
        self.inner = []

    def masks(self, which, level):
        found = [0]
        for bit in self.orders[which][:level]:
            found += [mask + bit for mask in found]
        return found

    def place(self, which, shard):
        return self.out.at[shard, pl.ds(which * self.half, self.half)]

    def launch(self, which, level, mask):
        shard = flipped(self.f, mask)
        here = self.src.at[pl.ds(which * self.half, self.half)]
        if mask:
            here = self.place(which, shard)
        to = flipped(self.f, self.orders[which][level])
        self.flying[which, level, mask] = self.remote.start(
            here, self.place(which, shard), {"fsdp": to}
        )

    def begin(self, sem):
        for level in range(self.levels):
            for which in range(2):
                self.launch(which, level, 0)
        self.inner.append(
            self.remote.start(self.src, self.out.at[self.f], {"fsdp": flipped(self.f, 1)})
        )
        self.own = pltpu.make_async_copy(self.src, self.out.at[self.f], sem)
        self.own.start()

    def relay(self, level):
        for which in range(2):
            order = self.orders[which]
            for mask in self.masks(which, level):
                self.flying[which, level, mask].wait()
                arrived = mask + order[level]
                for later in range(level + 1, self.levels):
                    self.launch(which, later, arrived)
                place = self.place(which, flipped(self.f, arrived))
                self.inner.append(self.remote.start(place, place, {"fsdp": flipped(self.f, 1)}))

    def end(self):
        self.own.wait()
        for copy in self.inner:
            copy.wait()

    @staticmethod
    def count(nf):
        return 2 * (nf // 2 - 1) + 2 * (nf // 2 - 1) + 1


def front_tile(e, mixes, st, g_ref, b_ref, normed, hats, scales, res, first, strip=16):
    count, tile, width = e.shape
    inv = 1.0 / width

    @pl.loop(0, tile // strip)
    def _(i):
        rows = pl.ds(pl.multiple_of(i * strip, strip), strip)
        mix = mixes[rows]
        for pair in ((0, 1), (2, 3)):
            totals = [None, None]
            for j in range(count):
                part = e[j, rows].astype(F32)
                for slot, s in enumerate(pair):
                    term = part * mix[:, s * count + j : s * count + j + 1]
                    totals[slot] = term if j == 0 else totals[slot] + term
            for slot, s in enumerate(pair):
                st[s, rows] = totals[slot]

    to = slice(first, first + tile)
    lane = lax.broadcasted_iota(jnp.int32, (tile, LANES), 1)
    kept = jnp.zeros((tile, LANES), F32)
    for s in range(3):
        v = st[s]
        center = v - jnp.sum(v, axis=-1, keepdims=True) * inv
        spread = jnp.sum(center * center, axis=-1, keepdims=True) * inv
        scale = lax.rsqrt(spread + EPSILON)
        hat = center * scale
        hats[s, to] = hat.astype(BF16)
        normed[s, to] = (hat * g_ref[s : s + 1] + b_ref[s : s + 1]).astype(BF16)
        kept = jnp.where(lane == s, scale, kept)
    scales[to] = kept
    res[to] = st[3]


def attend_pair(qkv, out, column_ref, row_ref, seq, lanes):
    blocks, block = out.shape[1], out.shape[2]
    length = blocks * block
    rows = row_tile(length)
    per = rows // block

    def load(kind, first, last):
        return qkv[kind, seq, first:last, :, lanes].reshape(-1, LANES)

    for i in range(length // rows):
        first, until = i * rows, (i + 1) * rows
        b0, b1 = i * per, (i + 1) * per
        query = first + lax.broadcasted_iota(jnp.int32, (rows, until), 0)
        key = lax.broadcasted_iota(jnp.int32, (rows, until), 1)
        same = column_ref[seq, first:until, 0:1] == row_ref[seq, 0:1, 0:until]
        allowed = same & (key <= query)
        q = load(0, b0, b1) * BF16(HD**-0.5)
        k = load(1, 0, b1)
        v = load(2, 0, b1)
        total = None
        for h in range(LANES // HD):
            scores = jnp.where(allowed, dot(only(q, h), k, NT), MASKED)
            peak = jnp.max(scores, axis=-1, keepdims=True)
            raised = jnp.exp(scores - peak)
            mass = jnp.sum(raised, axis=-1, keepdims=True)
            probs = (raised * (1.0 / mass)).astype(BF16)
            part = dot(probs, v)
            part = jnp.where(head_lanes(part.shape, h), part, 0.0)
            total = part if total is None else total + part
        out[seq, b0:b1, :, lanes] = total.astype(BF16).reshape(per, block, LANES)


def forward_kernel(
    n,
    nf,
    e_ref,
    wqkv_ref,
    wo_ref,
    win_ref,
    wout_ref,
    mix_ref,
    gain_ref,
    bias_ref,
    c_ref,
    s_ref,
    ids_ref,
    normed_ref,
    hats_ref,
    scales_ref,
    res_ref,
    gqkv_ref,
    go_ref,
    gin_ref,
    gout_ref,
    qkv_ref,
    ctx_ref,
    e,
    mixes,
    st,
    normed,
    hats,
    scales,
    res,
    w,
    raw,
    shares,
    qkv,
    heads,
    row,
    column,
    send,
    recv,
    local,
    e_sem,
):
    f, z = lax.axis_index("fsdp"), lax.axis_index("ctx")
    count, tokens, width = e_ref.shape
    tile = e.shape[2]
    tiles = tokens // tile
    seqs, _, block, cols = heads.shape
    seq_rows = 2 * block
    cut = raw.shape[1]
    remote = Remote(send, recv)
    spots = (z, 2 * n - 1 - z)
    mine = pl.ds(pl.multiple_of(z * cols, LANES), cols)

    def fetch(t):
        return pltpu.make_async_copy(
            e_ref.at[:, t * tile : (t + 1) * tile], e.at[t % 2], e_sem.at[t % 2]
        )

    fetch(0).start()
    greet_all(n, nf)

    def columns(ref, i):
        at = pl.ds(i * width, width)
        return ref.at[:, at] if len(ref.shape) == 2 else ref.at[:, :, at]

    parts = [
        PlaneGather(remote, nf, columns(wqkv_ref, i), columns(w, i)) for i in range(3)
    ]
    others = [
        PlaneGather(remote, nf, win_ref, gin_ref),
        PlaneGather(remote, nf, wout_ref, gout_ref),
        PlaneGather(remote, nf, wo_ref, go_ref),
    ]
    levels = parts[0].levels
    parts[0].begin(local.at[0])
    parts[1].begin(local.at[1])

    def do_tile(t):
        fetch(t).wait()
        if t + 1 < tiles:
            fetch(t + 1).start()
        mix_columns(mix_ref, mixes, t)
        front_tile(
            e.at[t % 2], mixes, st, gain_ref, bias_ref, normed, hats, scales, res, t * tile
        )

    do_tile(0)
    parts[0].relay(0)
    parts[2].begin(local.at[2])
    do_tile(1)
    parts[1].relay(0)
    for t in range(2, tiles - 1):
        do_tile(t)
    parts[2].relay(0)
    for level in range(1, levels):
        parts[0].relay(level)
    if tiles > 2:
        do_tile(tiles - 1)
    others[0].begin(local.at[3])
    own_tables = []
    for table in (c_ref, s_ref):
        early = table[pl.ds(pl.multiple_of(z * block, block), block)]
        late = table[pl.ds(pl.multiple_of((2 * n - 1 - z) * block, block), block)]
        own_tables.append((early, late))

    def project(i):
        @pl.loop(0, width // cut)
        def _(j):
            at = pl.ds(pl.multiple_of(i * width + j * cut, cut), cut)
            raw[...] = dot(normed[i], w[:, :, at].reshape(width, cut))
            for s in range(seqs):
                for h in range(2):
                    first = s * seq_rows + h * block
                    for c in range(cut // LANES):
                        x = raw[first : first + block, c * LANES : (c + 1) * LANES]
                        if i < 2:
                            x = turned(x, own_tables[0][h], own_tables[1][h])
                        to = c * LANES % cols
                        group = j * (cut // cols) + c * LANES // cols
                        shares[i, group, s, h, :, to : to + LANES] = x.astype(BF16)

    pairs = cols // LANES
    units = [(0, None)] + [(s, p) for s in range(1, seqs) for p in range(pairs)]
    arriving = {unit: [] for unit in units}
    kept = []

    def give(kind, unit):
        s, p = unit
        lanes = slice(None) if p is None else slice(p * LANES, (p + 1) * LANES)
        for k in range(1, n):
            to = lax.rem(z + k, n)
            for h in range(2):
                arriving[unit].append(
                    remote.start(
                        shares.at[kind, to, s, h, :, lanes],
                        qkv.at[kind, s, spots[h], :, lanes],
                        {"ctx": to},
                    )
                )

    for i in range(3):
        parts[i].end()
        project(i)
        give(i, units[0])
        if i < 2:
            for level in range(1, levels):
                parts[i + 1].relay(level)
    for h in range(2):
        copy = pltpu.make_async_copy(
            shares.at[:, z, :, h], qkv.at[:, :, spots[h]], local.at[8 + h]
        )
        copy.start()
        kept.append(copy)
    for unit in units[1:]:
        give(slice(None), unit)
    others[1].begin(local.at[4])
    others[2].begin(local.at[5])
    out_copies = [
        pltpu.make_async_copy(w, gqkv_ref, local.at[10]),
        pltpu.make_async_copy(normed, normed_ref, local.at[6]),
        pltpu.make_async_copy(res, res_ref, local.at[7]),
        pltpu.make_async_copy(hats, hats_ref, local.at[12]),
        pltpu.make_async_copy(scales, scales_ref, local.at[13]),
    ]
    for copy in out_copies:
        copy.start()
    place_segments(ids_ref, row, column, block)

    others[0].relay(0)
    for copy in kept:
        copy.wait()
    leaving = []
    stored = 14
    for index, unit in enumerate(units):
        for copy in arriving[unit]:
            copy.wait()
        s, p = unit
        if p is None:

            @pl.loop(0, pairs)
            def _(p):
                lanes = pl.ds(pl.multiple_of(p * LANES, LANES), LANES)
                attend_pair(qkv, heads, column, row, s, lanes)

            there, here = mine, slice(None)
        else:
            here = slice(p * LANES, (p + 1) * LANES)
            attend_pair(qkv, heads, column, row, s, here)
            there = pl.ds(pl.multiple_of(z * cols + p * LANES, LANES), LANES)
        for k in range(1, n):
            to = lax.rem(z + k, n)
            for h in range(2):
                spot = to if h == 0 else 2 * n - 1 - to
                leaving.append(
                    remote.start(
                        heads.at[s, spot, :, here], ctx_ref.at[s, h, :, there], {"ctx": to}
                    )
                )
        for h in range(2):
            copy = pltpu.make_async_copy(
                heads.at[s, spots[h], :, here], ctx_ref.at[s, h, :, there], local.at[stored]
            )
            stored += 1
            copy.start()
            out_copies.append(copy)
        if index == 0:
            others[1].relay(0)
            others[2].relay(0)
            for level in range(1, levels):
                others[0].relay(level)
    copy = pltpu.make_async_copy(qkv, qkv_ref, local.at[11])
    copy.start()
    out_copies.append(copy)
    for level in range(1, levels):
        others[1].relay(level)
        others[2].relay(level)
    for gather in others:
        gather.end()
    for copy in out_copies + leaving:
        copy.wait()


def forward(e, mix, w_qkv, w_o, w_in, w_out, gain, bias, cosine, sine, ids, n, nf):
    count, tokens, width = e.shape
    seqs, block = mix.shape[2], mix.shape[4]
    length = 2 * n * block
    cols = width // n
    spots = 2 * n
    tile = 128
    cut = max(cols, 512)
    rows = width // nf
    units = 1 + (seqs - 1) * (cols // LANES)
    copies = 6 * PlaneGather.count(nf) + (2 + 2 * units) * 2 * (n - 1)
    vmem = pl.BlockSpec(memory_space=pltpu.VMEM)
    hbm = pl.BlockSpec(memory_space=pltpu.HBM)

    def gathered(x):
        return jax.ShapeDtypeStruct((nf,) + x.shape, x.dtype)

    normed, hats, scales, res, g_qkv, g_o, g_in, g_out, qkv, ctx = pl.pallas_call(
        functools.partial(forward_kernel, n, nf),
        in_specs=[hbm] * 5 + [vmem] * 6,
        out_specs=[hbm] * 10,
        out_shape=[
            jax.ShapeDtypeStruct((3, tokens, width), BF16),
            jax.ShapeDtypeStruct((3, tokens, width), BF16),
            jax.ShapeDtypeStruct((tokens, LANES), F32),
            jax.ShapeDtypeStruct((tokens, width), F32),
            gathered(w_qkv),
            gathered(w_o),
            gathered(w_in),
            gathered(w_out),
            jax.ShapeDtypeStruct((3, seqs, spots, block, cols), BF16),
            jax.ShapeDtypeStruct((seqs, 2, block, width), BF16),
        ],
        scratch_shapes=[
            pltpu.VMEM((2, count, tile, width), BF16),
            pltpu.VMEM((tile, 4 * count), F32),
            pltpu.VMEM((4, tile, width), F32),
            pltpu.VMEM((3, tokens, width), BF16),
            pltpu.VMEM((3, tokens, width), BF16),
            pltpu.VMEM((tokens, LANES), F32),
            pltpu.VMEM((tokens, width), F32),
            pltpu.VMEM((nf, rows, 3 * width), BF16),
            pltpu.VMEM((tokens, cut), F32),
            pltpu.VMEM((3, n, seqs, 2, block, cols), BF16),
            pltpu.VMEM((3, seqs, spots, block, cols), BF16),
            pltpu.VMEM((seqs, spots, block, cols), BF16),
            pltpu.VMEM((seqs, 1, length), F32),
            pltpu.VMEM((seqs, length, 8), F32),
            pltpu.SemaphoreType.DMA((copies,)),
            pltpu.SemaphoreType.DMA((copies,)),
            pltpu.SemaphoreType.DMA((14 + 2 * units,)),
            pltpu.SemaphoreType.DMA((2,)),
        ],
        compiler_params=params(58, collective_id=0, has_side_effects=True),
        name="forward",
    )(e, w_qkv, w_o, w_in, w_out, mix, gain, bias, cosine, sine, ids)

    def whole(x):
        return x.reshape(x.shape[0] * x.shape[1], x.shape[2])

    weights = [whole(g) for g in (g_qkv, g_o, g_in, g_out)]
    return normed, hats, scales, res, *weights, qkv, ctx.reshape(tokens, width)


def attend_back_pair(qkv, grad, out, dk, dv, column_ref, row_ref, c_ref, s_ref, seq, lanes):
    blocks, block = grad.shape[1], grad.shape[2]
    length = blocks * block
    rows = row_tile(length)
    per = rows // block
    factor = HD**-0.5

    def load(ref, at, first, last):
        return ref[(*at, slice(first, last), slice(None), lanes)].reshape(-1, LANES)

    for i in range(length // rows):
        here = slice(i * rows, (i + 1) * rows)
        dk[here] = jnp.zeros((rows, LANES), F32)
        dv[here] = jnp.zeros((rows, LANES), F32)
    for i in range(length // rows):
        first, until = i * rows, (i + 1) * rows
        b0, b1 = i * per, (i + 1) * per
        query = first + lax.broadcasted_iota(jnp.int32, (rows, until), 0)
        key = lax.broadcasted_iota(jnp.int32, (rows, until), 1)
        same = column_ref[seq, first:until, 0:1] == row_ref[seq, 0:1, 0:until]
        allowed = same & (key <= query)
        q = load(qkv, (0, seq), b0, b1) * BF16(factor)
        g = load(grad, (seq,), b0, b1)
        k = load(qkv, (1, seq), 0, b1)
        v = load(qkv, (2, seq), 0, b1)
        total = None
        for h in range(LANES // HD):
            q_h = only(q, h)
            g_h = only(g, h)
            scores = jnp.where(allowed, dot(q_h, k, NT), MASKED)
            peak = jnp.max(scores, axis=-1, keepdims=True)
            raised = jnp.exp(scores - peak)
            mass = jnp.sum(raised, axis=-1, keepdims=True)
            probs = raised * (1.0 / mass)
            dots = dot(g_h, v, NT)
            center = jnp.sum(probs * dots, axis=-1, keepdims=True)
            slope = (probs * (dots - center)).astype(BF16)
            part = dot(slope, k)
            part = jnp.where(head_lanes(part.shape, h), part, 0.0)
            total = part if total is None else total + part
            dk[0:until] += dot(slope, q_h, TN)
            dv[0:until] += dot(probs.astype(BF16), g_h, TN)
        cosine, sine = c_ref[first:until], s_ref[first:until]
        low = turned(total * factor, cosine, -sine).astype(BF16)
        out[0, seq, b0:b1, :, lanes] = low.reshape(per, block, LANES)
    for i in range(length // rows):
        here = slice(i * rows, (i + 1) * rows)
        b0, b1 = i * per, (i + 1) * per
        low = turned(dk[here], c_ref[here], -s_ref[here]).astype(BF16)
        out[1, seq, b0:b1, :, lanes] = low.reshape(per, block, LANES)
        out[2, seq, b0:b1, :, lanes] = dv[here].astype(BF16).reshape(per, block, LANES)


def back_kernel(
    n,
    nf,
    cg_ref,
    qkv_ref,
    in_ref,
    out_ref,
    o_ref,
    ids_ref,
    c_ref,
    s_ref,
    grads_ref,
    in_sum,
    out_sum,
    o_sum,
    qkv,
    grad,
    back,
    dk,
    dv,
    in_keep,
    in_got,
    in_part,
    out_keep,
    out_got,
    out_part,
    o_keep,
    o_got,
    o_part,
    row,
    column,
    send,
    recv,
    local,
):
    f, z = lax.axis_index("fsdp"), lax.axis_index("ctx")
    core = lax.rem(f, 2)
    seqs, _, block, cols = grad.shape
    remote = Remote(send, recv)
    sums = [
        ChipSum(remote, nf, in_ref, in_keep, in_got, in_part),
        ChipSum(remote, nf, out_ref, out_keep, out_got, out_part),
        ChipSum(remote, nf, o_ref, o_keep, o_got, o_part),
    ]
    spots = (z, 2 * n - 1 - z)
    mine = pl.ds(pl.multiple_of(z * cols, LANES), cols)

    loads = [pltpu.make_async_copy(qkv_ref, qkv, local.at[0])]
    for i, (ref, keep) in enumerate([(in_ref, in_keep), (out_ref, out_keep), (o_ref, o_keep)]):
        loads.append(pltpu.make_async_copy(ref.at[:, core], keep, local.at[1 + i]))
    for h in range(2):
        loads.append(
            pltpu.make_async_copy(cg_ref.at[z, :, h], grad.at[:, spots[h]], local.at[4 + h])
        )
    for load in loads:
        load.start()

    greet_all(n, nf)

    arriving = []
    for s in range(seqs):
        copies = []
        for k in range(1, n):
            to = lax.rem(z + k, n)
            for h in range(2):
                copies.append(
                    remote.start(cg_ref.at[to, s, h], grad.at[s, spots[h]], {"ctx": to})
                )
        arriving.append(copies)
    for chip_sum in sums:
        chip_sum.cores()
    place_segments(ids_ref, row, column, block)
    for load in loads:
        load.wait()
    sums[0].cross()

    leaving = []
    kept = []
    for s in range(seqs):
        for copy in arriving[s]:
            copy.wait()

        @pl.loop(0, cols // LANES)
        def _(p):
            lanes = pl.ds(pl.multiple_of(p * LANES, LANES), LANES)
            attend_back_pair(qkv, grad, back, dk, dv, column, row, c_ref, s_ref, s, lanes)

        for k in range(1, n):
            to = lax.rem(z + k, n)
            for h in range(2):
                spot = to if h == 0 else 2 * n - 1 - to
                leaving.append(
                    remote.start(
                        back.at[:, s, spot], grads_ref.at[:, s, h, :, mine], {"ctx": to}
                    )
                )
        for h in range(2):
            copy = pltpu.make_async_copy(
                back.at[:, s, spots[h]], grads_ref.at[:, s, h, :, mine], local.at[6 + 2 * s + h]
            )
            copy.start()
            kept.append(copy)
        if s == 0:
            sums[1].cross()
            sums[2].cross()
            sums[0].relay()

    sums[1].relay()
    sums[2].relay()
    for chip_sum, out in zip(sums, (in_sum, out_sum, o_sum)):
        chip_sum.total(out)
    for copy in kept + leaving:
        copy.wait()


def attention_back(context_grad, qkv, d_in, d_out, d_o, ids, cosine, sine, n, nf):
    _, seqs, spots, block, cols = qkv.shape
    length = spots * block
    width = d_o.shape[1]
    chips = nf // 2

    def by_owner(x):
        return x.reshape(chips, 2, x.shape[0] // nf, x.shape[1])

    terms = [by_owner(d_in), by_owner(d_out), by_owner(d_o)]
    copies = seqs * 4 * (n - 1) + 3 * ChipSum.count(nf)
    vmem = pl.BlockSpec(memory_space=pltpu.VMEM)
    hbm = pl.BlockSpec(memory_space=pltpu.HBM)
    scratch = []
    for term in terms:
        scratch += chip_scratch(nf, term.shape[2], term.shape[3])
    grads, *owned = pl.pallas_call(
        functools.partial(back_kernel, n, nf),
        in_specs=[hbm] * 5 + [vmem] * 3,
        out_specs=[hbm, vmem, vmem, vmem],
        out_shape=[jax.ShapeDtypeStruct((3, seqs, 2, block, width), BF16)]
        + [jax.ShapeDtypeStruct(term.shape[2:], BF16) for term in terms],
        scratch_shapes=[
            pltpu.VMEM((3, seqs, spots, block, cols), BF16),
            pltpu.VMEM((seqs, spots, block, cols), BF16),
            pltpu.VMEM((3, seqs, spots, block, cols), BF16),
            pltpu.VMEM((length, LANES), F32),
            pltpu.VMEM((length, LANES), F32),
            *scratch,
            pltpu.VMEM((seqs, 1, length), F32),
            pltpu.VMEM((seqs, length, 8), F32),
            pltpu.SemaphoreType.DMA((copies,)),
            pltpu.SemaphoreType.DMA((copies,)),
            pltpu.SemaphoreType.DMA((6 + 2 * seqs,)),
        ],
        compiler_params=params(56, collective_id=2, has_side_effects=True),
        name="attention_back",
    )(
        context_grad.reshape(n, seqs, 2, block, cols),
        qkv,
        *terms,
        ids,
        cosine,
        sine,
    )
    return grads.reshape(3, seqs * 2 * block, width), owned


def norm_back_tile(hats, scales, ng, st, e, mg, mg_ref, g_ref, h, low, dgain, dbias, selector, t, strip=16):
    count, tile, width = e.shape
    inv = 1.0 / width
    to = slice(t * tile, (t + 1) * tile)
    for s in range(3):
        dy = ng[s]
        hat = hats[s, to].astype(F32)
        scale = scales[to, s : s + 1]
        dgain[s : s + 1] += jnp.sum(dy * hat, axis=0, keepdims=True)
        dbias[s : s + 1] += jnp.sum(dy, axis=0, keepdims=True)
        dh = dy * g_ref[s : s + 1]
        mean = jnp.sum(dh, axis=-1, keepdims=True) * inv
        along = jnp.sum(dh * hat, axis=-1, keepdims=True) * inv
        out = (scale * (dh - mean - hat * along)).astype(BF16)
        low[s, to] = out
        st[s] = out
    st[3] = h[to].astype(BF16)

    shape = (4 * strip, count * strip)
    same = lax.rem(lax.broadcasted_iota(jnp.int32, shape, 0), strip) == lax.rem(
        lax.broadcasted_iota(jnp.int32, shape, 1), strip
    )
    for i in range(tile // strip):
        rows = slice(i * strip, (i + 1) * strip)
        grads = st[:, rows].reshape(4 * strip, width)
        inputs = e[:, rows].reshape(count * strip, width)
        products = jnp.where(same, dot(grads, inputs, NT), 0.0)
        wide = jnp.concatenate(
            [products[s * strip : (s + 1) * strip] for s in range(4)], axis=1
        )
        high, rest = halves(wide)
        mg[rows] = dot(high, selector[...]) + dot(rest, selector[...])
    turned_mg = mg[...].T
    block = mg_ref.shape[4]
    per = tile // block
    for i in range(per):
        place = t * per + i
        for a in range(4):
            mg_ref[a, :, place // 2, place % 2, :] = turned_mg[
                a * count : (a + 1) * count, i * block : (i + 1) * block
            ]


def small_squares(rows, cols):
    first = 8 + rows
    places = []
    for g in range(-(-rows // 8)):
        size = min(8, rows - 8 * g)
        places.append(
            (
                slice(first, first + size),
                slice(g * LANES, g * LANES + cols),
                slice(8 * g, 8 * g + size),
            )
        )
    return places


def small_line_at(rows, cols):
    groups = -(-rows // 8)
    return slice(groups * LANES, groups * LANES + cols)


def end_kernel(
    n,
    nf,
    grads_ref,
    normed_ref,
    hats_ref,
    scales_ref,
    e_ref,
    w_ref,
    h_ref,
    gain_ref,
    in_ref,
    out_ref,
    o_ref,
    sgain_ref,
    sbias_ref,
    sw1_ref,
    sw2_ref,
    smb_ref,
    low_ref,
    mg_ref,
    q_sum,
    k_sum,
    v_sum,
    in_sum,
    out_sum,
    o_sum,
    small_sum,
    grads,
    normed,
    hats,
    scales,
    w,
    h,
    e,
    ng,
    st,
    low,
    mg,
    selector,
    dgain,
    dbias,
    small_work,
    small_in,
    small_line,
    send,
    recv,
    local,
    e_sem,
    *more,
):
    f, z = lax.axis_index("fsdp"), lax.axis_index("ctx")
    core = lax.rem(f, 2)
    count, tokens, width = e_ref.shape
    tile = e.shape[2]
    tiles = tokens // tile
    remote = Remote(send, recv)
    chip_sets = [more[4 * i : 4 * i + 4] for i in range(3)]
    rest = more[12:]
    shard = chip_sets[0][1].shape[1]

    def fetch(t):
        return pltpu.make_async_copy(
            e_ref.at[:, t * tile : (t + 1) * tile], e.at[t % 2], e_sem.at[t % 2]
        )

    loads = [
        pltpu.make_async_copy(src, dst, local.at[i])
        for i, (src, dst) in enumerate(
            [
                (grads_ref, grads),
                (normed_ref, normed),
                (w_ref, w),
                (hats_ref, hats),
                (scales_ref, scales),
                (h_ref, h),
            ]
        )
    ]
    for load in loads:
        load.start()
    fetch(0).start()

    greet_all(n, nf)

    chain = Chain(remote, n)
    planned = [(in_ref, in_sum, 4), (out_ref, out_sum, 4), (o_ref, o_sum, 1)]
    planned += [
        (chip_set[3], out, 1) for chip_set, out in zip(chip_sets, (q_sum, k_sum, v_sum))
    ]
    for work, out, count_of in planned:
        size = work.shape[0] // count_of
        for i in range(count_of):
            at = pl.ds(i * size, size)
            chain.add(work.at[at], out.at[at], *rest[:3])
            rest = rest[3:]
    chain.start()
    chain.start()

    loads[0].wait()
    loads[1].wait()
    cut = 256
    per = cut // (2 * shard)
    sums = []
    for i in range(3):
        terms, got, part, own = chip_sets[i]
        for c in range(width // cut):
            value = dot(normed[i, :, c * cut : (c + 1) * cut], grads[i], TN).astype(BF16)
            terms[c * per : (c + 1) * per] = value.reshape(per, 2, shard, width)
        chip_sum = ChipSum(remote, nf, terms, terms.at[:, core], got, part)
        chip_sum.cores()
        sums.append(chip_sum)
    dgain[...] = jnp.zeros_like(dgain)
    dbias[...] = jnp.zeros_like(dbias)
    size = selector.shape
    group = lax.broadcasted_iota(jnp.int32, size, 0) // 16
    selector[...] = jnp.where(
        group == lax.broadcasted_iota(jnp.int32, size, 1), 1.0, 0.0
    ).astype(BF16)
    for load in loads[2:]:
        load.wait()

    def do_tile(t):
        fetch(t).wait()
        if t + 1 < tiles:
            fetch(t + 1).start()
        rows = slice(t * tile, (t + 1) * tile)
        for i in range(3):
            ng[i] = dot(grads[i, rows], w[:, i * width : (i + 1) * width], NT)
        norm_back_tile(
            hats, scales, ng, st, e.at[t % 2], mg, mg_ref, gain_ref, h, low, dgain, dbias, selector, t
        )

    todo = list(range(tiles))

    def some():
        if todo:
            do_tile(todo.pop(0))

    chain.step(0)
    for chip_sum in sums:
        chip_sum.cross()
    chain.step(1)
    some()
    chain.step(2)
    some()
    chain.step(3)
    chain.step(4)
    for chip_sum in sums:
        chip_sum.relay()
    some()
    chain.step(5)
    while todo:
        some()
    keep = pltpu.make_async_copy(low, low_ref, local.at[6])
    keep.start()
    for chip_sum, chip_set in zip(sums, chip_sets):
        chip_sum.total(chip_set[3])
    chain.step(6)

    thin = small_in.shape[1]
    hidden_count, coef_count = sw2_ref.shape
    first = 8 + hidden_count
    squares = small_squares(hidden_count, coef_count)
    line_at = small_line_at(hidden_count, coef_count)
    small_work[...] = jnp.zeros_like(small_work)
    small_work[0:3] = dgain[...]
    small_work[3:4] = sgain_ref[...]
    small_work[4:7] = dbias[...]
    small_work[7:8] = sbias_ref[...]
    small_work[8:first] = sw1_ref[...]
    for rows, lanes, which in squares:
        small_work[rows, lanes] = sw2_ref[which]
    small_work[first : first + 1, line_at] = smb_ref[...]
    here = pl.ds(pl.multiple_of(f * thin, thin), thin)
    small_in[0] = small_work[here]
    slices = []
    for k in range(1, nf):
        to = lax.rem(f + k, nf)
        slices.append(
            remote.start(
                small_work.at[pl.ds(pl.multiple_of(to * thin, thin), thin)],
                small_in.at[k],
                {"fsdp": to},
            )
        )

    chain.step(7)
    for copy in slices:
        copy.wait()
    total = small_in[0]
    for k in range(1, nf):
        total = total + small_in[k]
    small_line[z] = total
    across = []
    for k in range(1, n):
        across.append(
            remote.start(small_line.at[z], small_line.at[z], {"ctx": lax.rem(z + k, n)})
        )
    chain.step(8)
    chain.step(9)
    for copy in across:
        copy.wait()
    total = small_line[0]
    for k in range(1, n):
        total = total + small_line[k]
    small_sum[here] = total
    spread = []
    for k in range(1, nf):
        spread.append(
            remote.start(small_sum.at[here], small_sum.at[here], {"fsdp": lax.rem(f + k, nf)})
        )
    chain.step(10)
    chain.step(11)
    chain.leave(10)
    chain.leave(11)
    for copy in spread:
        copy.wait()
    for c in range(12):
        chain.end(c)
    keep.wait()


def finish(grads, normed, hats, scales, e, w, hgrad, gain, owned, small, mix_shape, n, nf):
    count, tokens, width = e.shape
    tile = 128
    chips = nf // 2
    shard = width // nf
    rows = 8 + small[2].shape[0] + 8
    thin = 8 * -(-rows // (8 * nf))
    m_in, m_out, m_o = owned
    lines, chip_sums = [], []
    for x, count_of in ((m_in, 4), (m_out, 4), (m_o, 1)):
        for _ in range(count_of):
            lines += chain_scratch(n, x.shape[0] // count_of, x.shape[1])
    for _ in range(3):
        lines += chain_scratch(n, shard, width)
        chip_sums += [
            pltpu.VMEM((chips, 2, shard, width), BF16),
            *chip_scratch(nf, shard, width)[1:],
            pltpu.VMEM((shard, width), BF16),
        ]
    copies = 12 * (Chain.levels(n) + 2) + 3 * ChipSum.count(nf) + 2 * (nf - 1) + (n - 1)
    vmem = pl.BlockSpec(memory_space=pltpu.VMEM)
    hbm = pl.BlockSpec(memory_space=pltpu.HBM)
    wide = jax.ShapeDtypeStruct((shard, width), BF16)
    return pl.pallas_call(
        functools.partial(end_kernel, n, nf),
        in_specs=[hbm] * 7 + [vmem] * 9,
        out_specs=[hbm] + [vmem] * 8,
        out_shape=[
            jax.ShapeDtypeStruct((3, tokens, width), BF16),
            jax.ShapeDtypeStruct(mix_shape, F32),
            wide,
            wide,
            wide,
            *[jax.ShapeDtypeStruct(x.shape, BF16) for x in owned],
            jax.ShapeDtypeStruct((nf * thin, width), F32),
        ],
        scratch_shapes=[
            pltpu.VMEM(grads.shape, BF16),
            pltpu.VMEM(normed.shape, BF16),
            pltpu.VMEM(hats.shape, BF16),
            pltpu.VMEM(scales.shape, F32),
            pltpu.VMEM(w.shape, BF16),
            pltpu.VMEM(hgrad.shape, F32),
            pltpu.VMEM((2, count, tile, width), BF16),
            pltpu.VMEM((3, tile, width), F32),
            pltpu.VMEM((4, tile, width), BF16),
            pltpu.VMEM((3, tokens, width), BF16),
            pltpu.VMEM((tile, LANES), F32),
            pltpu.VMEM((4 * count * 16, LANES), BF16),
            pltpu.VMEM((3, width), F32),
            pltpu.VMEM((3, width), F32),
            pltpu.VMEM((nf * thin, width), F32),
            pltpu.VMEM((nf, thin, width), F32),
            pltpu.VMEM((n, thin, width), F32),
            pltpu.SemaphoreType.DMA((copies,)),
            pltpu.SemaphoreType.DMA((copies,)),
            pltpu.SemaphoreType.DMA((7,)),
            pltpu.SemaphoreType.DMA((2,)),
            *chip_sums,
            *lines,
        ],
        compiler_params=params(60, collective_id=3, has_side_effects=True),
        name="finish",
    )(grads, normed, hats, scales, e, w, hgrad, gain, *owned, *small)


def tail_kernel(
    low_ref,
    h_ref,
    mix_ref,
    q_ref,
    k_ref,
    v_ref,
    in_ref,
    out_ref,
    o_ref,
    small_ref,
    mg_ref,
    eg_ref,
    qkv_ref,
    in32_ref,
    out32_ref,
    o32_ref,
    gain_ref,
    bias_ref,
    w1_ref,
    w2_ref,
    mb_ref,
    mg_out_ref,
    mixes,
    *,
    strip,
):
    count, tile, width = eg_ref.shape
    chunk = 512
    block = mix_ref.shape[4]
    tiles = mix_ref.shape[2] * 2 * block // tile
    step = pl.program_id(0)
    for t in range(tiles):

        @pl.when(step == t)
        def _():
            mix_columns(mix_ref, mixes, t)

    @pl.when(step == 0)
    def _():
        hidden_count, coef_count = w2_ref.shape
        first = 8 + hidden_count
        gain_ref[...] = small_ref[0:4]
        bias_ref[...] = small_ref[4:8]
        w1_ref[...] = small_ref[8:first]
        for rows, lanes, which in small_squares(hidden_count, coef_count):
            w2_ref[which] = small_ref[rows, lanes]
        mb_ref[...] = small_ref[first : first + 1, small_line_at(hidden_count, coef_count)]
        mg_out_ref[...] = mg_ref[...]

    def part(ref, out):
        size = out.shape[0]
        return ref[pl.ds(pl.multiple_of(step * size, 16), size)].astype(F32)

    for i, ref in enumerate((q_ref, k_ref, v_ref)):
        qkv_ref[:, i * width : (i + 1) * width] = part(ref, qkv_ref)
    in32_ref[...] = part(in_ref, in32_ref)
    out32_ref[...] = part(out_ref, out32_ref)
    o32_ref[...] = part(o_ref, o32_ref)

    @pl.loop(0, tile // strip)
    def _(i):
        rows = pl.ds(pl.multiple_of(i * strip, strip), strip)
        mix = mixes[rows]
        for c in range(width // chunk):
            cols = slice(c * chunk, (c + 1) * chunk)
            grads = [low_ref[s, rows, cols].astype(F32) for s in range(3)]
            grads.append(h_ref[rows, cols])
            for j in range(count):
                total = grads[0] * mix[:, j : j + 1]
                for s in range(1, 4):
                    total = total + grads[s] * mix[:, s * count + j : s * count + j + 1]
                eg_ref[j, rows, cols] = total.astype(BF16)


def spread_back(low, hgrad, mix, sums, small, m_grad, sizes):
    _, tokens, width = low.shape
    count = mix.shape[1]
    tile = 128
    tiles = tokens // tile
    hidden_count, coef_count = sizes

    def part(x):
        return pl.BlockSpec((x.shape[0] // tiles, x.shape[1]), lambda i: (i, 0))

    def whole(x):
        zeros = (0,) * len(x.shape)
        return once(x.shape, lambda i: zeros)

    shard = sums[0].shape[0]
    outs = [
        jax.ShapeDtypeStruct((count, tokens, width), BF16),
        jax.ShapeDtypeStruct((shard, 3 * width), F32),
        *[jax.ShapeDtypeStruct(x.shape, F32) for x in sums[3:]],
        jax.ShapeDtypeStruct((4, width), F32),
        jax.ShapeDtypeStruct((4, width), F32),
        jax.ShapeDtypeStruct((hidden_count, width), F32),
        jax.ShapeDtypeStruct((hidden_count, coef_count), F32),
        jax.ShapeDtypeStruct((1, coef_count), F32),
        jax.ShapeDtypeStruct(m_grad.shape, F32),
    ]
    vmem = pl.BlockSpec(memory_space=pltpu.VMEM)
    return pl.pallas_call(
        functools.partial(tail_kernel, strip=16),
        grid=(tiles,),
        in_specs=[
            pl.BlockSpec((3, tile, width), lambda i: (0, i, 0)),
            pl.BlockSpec((tile, width), lambda i: (i, 0)),
            whole(mix),
            *[vmem] * 8,
        ],
        out_specs=[pl.BlockSpec((count, tile, width), lambda i: (0, i, 0))]
        + [part(x) for x in outs[1:5]]
        + [whole(x) for x in outs[5:]],
        out_shape=outs,
        scratch_shapes=[pltpu.VMEM((tile, 4 * count), F32)],
        compiler_params=params(40),
        cost_estimate=pl.CostEstimate(
            flops=64 * tokens * width, bytes_accessed=40 * tokens * width, transcendentals=0
        ),
        name="spread_back",
    )(low, hgrad, mix, *sums, small, m_grad)


def body(
    earlier,
    mix_in,
    segment_ids,
    attn_qkv,
    attn_out,
    mlp_in,
    mlp_out,
    norm_gain,
    norm_bias,
    mix_w1,
    mix_w2,
    mix_bias,
    out_grad,
    coef_grad,
):
    count, seqs, _, block, width = earlier.shape
    n = lax.axis_size("ctx")
    tokens = seqs * 2 * block
    length = 2 * n * block
    me = lax.axis_index("ctx")

    nf = lax.axis_size("fsdp")
    e = earlier.reshape(count, tokens, width)
    cosine, sine = (jnp.asarray(table) for table in turn_tables(length))
    normed, hats, scales, residual, w_qkv, w_o, w_in, w_out, qkv, context = forward(
        e,
        mix_in,
        attn_qkv,
        attn_out,
        mlp_in,
        mlp_out,
        norm_gain,
        norm_bias,
        cosine,
        sine,
        segment_ids,
        n,
        nf,
    )
    (
        layer_out,
        coefs,
        d_in,
        d_out,
        d_o,
        context_grad,
        hidden_grad,
        d_gain,
        d_bias,
        d_w1,
        d_w2,
        d_mb,
    ) = feed(
        residual,
        context,
        w_o,
        w_in,
        w_out,
        norm_gain,
        norm_bias,
        mix_w1,
        mix_w2,
        mix_bias[None, :],
        out_grad.reshape(tokens, width),
        coef_grad,
        n,
    )
    grads, owned = attention_back(
        context_grad, qkv, d_in, d_out, d_o, segment_ids, cosine, sine, n, nf
    )
    low, m_grad, *sums, small = finish(
        grads,
        normed,
        hats,
        scales,
        e,
        w_qkv,
        hidden_grad,
        norm_gain,
        owned,
        (d_gain, d_bias, d_w1, d_w2, d_mb),
        mix_in.shape,
        n,
        nf,
    )
    e_grad, g_qkv, g_in, g_out, g_o, gain_sum, bias_sum, w1_sum, w2_sum, mb_sum, m_grad = (
        spread_back(low, hidden_grad, mix_in, sums, small, m_grad, mix_w2.shape)
    )
    return (
        layer_out.reshape(seqs, 2, block, width),
        coefs,
        e_grad.reshape(count, seqs, 2, block, width),
        m_grad,
        g_qkv,
        g_o,
        g_in,
        g_out,
        gain_sum,
        bias_sum,
        w1_sum,
        w2_sum,
        mb_sum[0],
    )


def solution(mesh):
    in_specs = (
        P(None, "fsdp", None, "ctx", None),
        P(None, None, "fsdp", None, "ctx"),
        P("fsdp", None, None),
        P("fsdp", None),
        P("fsdp", None),
        P("fsdp", None),
        P("fsdp", None),
        P(),
        P(),
        P(),
        P(),
        P(),
        P("fsdp", None, "ctx", None),
        P(None, None, "fsdp", None, "ctx"),
    )
    out_specs = (
        P("fsdp", None, "ctx", None),
        P(None, None, "fsdp", None, "ctx"),
        P(None, "fsdp", None, "ctx", None),
        P(None, None, "fsdp", None, "ctx"),
        P("fsdp", None),
        P("fsdp", None),
        P("fsdp", None),
        P("fsdp", None),
        P(),
        P(),
        P(),
        P(),
        P(),
    )
    return jax.shard_map(body, mesh=mesh, in_specs=in_specs, out_specs=out_specs, check_vma=False)
```

```python
import functools
import math

import jax
import jax.numpy as jnp
import numpy as np
from jax import lax
from jax.experimental import pallas as pl
from jax.experimental.pallas import tpu as pltpu
from jax.sharding import PartitionSpec as P

HD = 64
ROT = 16
LANES = 128
EPSILON = 1e-05
RMS_EPSILON = 1e-06
MASKED = -1e30
F32 = jnp.float32
BF16 = jnp.bfloat16
MESH = pl.DeviceIdType.MESH
MIB = 1024 * 1024

NN = (((1,), (0,)), ((), ()))
NT = (((1,), (1,)), ((), ()))
TN = (((0,), (0,)), ((), ()))

ERFC_RATE = 0.4
ERFC = (
    0.22567586600780487,
    0.22566929459571838,
    0.20784726738929749,
    0.16851142048835754,
    0.1415392905473709,
    -0.005822250619530678,
    0.16932761669158936,
    -0.18304575979709625,
    0.05029737576842308,
)


def dot(a, b, dims=NN):
    return lax.dot_general(a, b, dims, preferred_element_type=F32)


def gelu_and_slope(v):
    z = jnp.abs(v) * math.sqrt(0.5)
    bell = jnp.exp(-0.5 * v * v)
    t = 1.0 / (1.0 + ERFC_RATE * z)
    poly = jnp.full_like(t, ERFC[-1])
    for coefficient in ERFC[-2::-1]:
        poly = poly * t + coefficient
    tail = 0.5 * poly * t * bell
    phi = jnp.where(v >= 0.0, 1.0 - tail, tail)
    return v * phi, phi + v * bell * (1.0 / math.sqrt(2.0 * math.pi))


def halves(x):
    high = x.astype(BF16)
    return high, (x - high.astype(F32)).astype(BF16)


def params(limit_mib, **more):
    return pltpu.CompilerParams(vmem_limit_bytes=limit_mib * MIB, **more)


def once(shape, index):
    return pl.BlockSpec(shape, index, pipeline_mode=pl.Buffered(1))


def turn_tables(length):
    half = ROT // 2
    frequency = 10000.0 ** (-(np.arange(half) * 2.0 / ROT))
    angle = np.arange(length)[:, None] * frequency[None, :]
    lane = np.arange(LANES) % HD
    cosine = np.ones((length, LANES), np.float32)
    sine = np.zeros((length, LANES), np.float32)
    for k in range(LANES):
        if lane[k] < ROT:
            cosine[:, k] = np.cos(angle[:, lane[k] % half])
            sign = -1.0 if lane[k] < half else 1.0
            sine[:, k] = sign * np.sin(angle[:, lane[k] % half])
    return cosine, sine


def turned(x, cosine, sine):
    half = ROT // 2
    lane = lax.broadcasted_iota(jnp.int32, x.shape, 1) % HD
    other = jnp.where(
        lane < half, pltpu.roll(x, LANES - half, axis=1), pltpu.roll(x, half, axis=1)
    )
    return x * cosine + other * sine


def row_tile(length):
    return min(256, length)


def head_lanes(shape, h):
    lane = lax.broadcasted_iota(jnp.int32, shape, 1)
    return (lane >= h * HD) & (lane < (h + 1) * HD)


def only(x, h):
    return jnp.where(head_lanes(x.shape, h), x, jnp.zeros_like(x))


def coefficient_places(ref):
    outer, inner, seqs, _, block = ref.shape
    for a in range(outer):
        for seq in range(seqs):
            for h in range(2):
                first = (2 * seq + h) * block
                yield a, seq, h, slice(a * inner, (a + 1) * inner), slice(first, first + block)


def feed_kernel(
    res_ref,
    ctx_ref,
    wo_ref,
    win_ref,
    wout_ref,
    g_ref,
    b_ref,
    w1_ref,
    w2_ref,
    mb_ref,
    og_ref,
    cg_ref,
    out_ref,
    coef_ref,
    active,
    lowered,
    normed,
    branch,
    attention,
    cgrad_ref,
    hgrad_ref,
    dgain_ref,
    dbias_ref,
    dw1_ref,
    dw2_ref,
    dmb_ref,
    hidden,
    total,
    slope,
    r_high,
    r_rest,
    cotangent,
    *,
    tiles,
    strip,
):
    step = pl.program_id(0)
    tokens, width = res_ref.shape
    cut = win_ref.shape[1]
    inv = 1.0 / width

    @pl.when(step == 0)
    def _():
        hidden[...] = dot(ctx_ref[...], wo_ref[...])

        @pl.loop(0, tokens // strip)
        def _(i):
            rows = pl.ds(pl.multiple_of(i * strip, strip), strip)
            v = hidden[rows] + res_ref[rows]
            hidden[rows] = v
            center = v - jnp.sum(v, axis=-1, keepdims=True) * inv
            spread = jnp.sum(center * center, axis=-1, keepdims=True) * inv
            hat = center * lax.rsqrt(spread + EPSILON)
            normed[rows] = (hat * g_ref[3:4] + b_ref[3:4]).astype(BF16)
            total[rows] = v

    @pl.when(step < tiles)
    def _():
        value, rate = gelu_and_slope(dot(normed[...], win_ref[...]))
        low = value.astype(BF16)
        active[...] = low
        slope[step] = rate
        total[...] += dot(low, wout_ref[...])

    @pl.when(step == tiles - 1)
    def _():
        w1 = w1_ref[...]
        w2 = w2_ref[...]

        @pl.loop(0, tokens // strip)
        def _(i):
            rows = pl.ds(pl.multiple_of(i * strip, strip), strip)
            v = total[rows]
            out_ref[rows] = v.astype(BF16)
            scale = lax.rsqrt(jnp.sum(v * v, axis=-1, keepdims=True) * inv + RMS_EPSILON)
            r = v * scale
            high = r.astype(BF16)
            r_high[rows] = high
            r_rest[rows] = (r - high.astype(F32)).astype(BF16)

        high, rest = r_high[...], r_rest[...]
        for a, seq, h, rows, cols in coefficient_places(cg_ref):
            cotangent[rows, cols] = cg_ref[a, :, seq, h, :]
        z = dot(w1, high, NT) + dot(w1, rest, NT)
        value, rate = gelu_and_slope(z)
        v_high, v_rest = halves(value)
        ones = jnp.ones((1, tokens), BF16)
        mb_high, mb_rest = halves(mb_ref[...])
        mb_last = (mb_ref[...] - mb_high.astype(F32) - mb_rest.astype(F32)).astype(BF16)
        shift = dot(mb_high, ones, TN) + dot(mb_rest, ones, TN) + dot(mb_last, ones, TN)
        coefs = dot(w2, v_high, TN) + dot(w2, v_rest, TN) + shift
        for a, seq, h, rows, cols in coefficient_places(coef_ref):
            coef_ref[a, :, seq, h, :] = coefs[rows, cols]
        c_high, c_rest = halves(cotangent[...])
        dmb_ref[...] = dot(ones, c_high, NT) + dot(ones, c_rest, NT)
        dw2_ref[...] = dot(v_high, c_high, NT) + dot(v_rest, c_high, NT) + dot(v_high, c_rest, NT)
        z_high, z_rest = halves((dot(w2, c_high) + dot(w2, c_rest)) * rate)
        dw1_ref[...] = dot(z_high, high) + dot(z_high, rest) + dot(z_rest, high)
        hgrad_ref[...] = dot(z_high, w1, TN) + dot(z_rest, w1, TN)

        @pl.loop(0, tokens // strip)
        def _(i):
            rows = pl.ds(pl.multiple_of(i * strip, strip), strip)
            v = total[rows]
            scale = lax.rsqrt(jnp.sum(v * v, axis=-1, keepdims=True) * inv + RMS_EPSILON)
            dr = hgrad_ref[rows]
            r = v * scale
            mean = jnp.sum(dr * r, axis=-1, keepdims=True) * inv
            grad = scale * (dr - r * mean) + og_ref[rows].astype(F32)
            hgrad_ref[rows] = grad
            branch[rows] = grad.astype(BF16)
            total[rows] = jnp.zeros_like(v)

    @pl.when(step >= tiles)
    def _():
        j = step - tiles
        low = (dot(branch[...], wout_ref[...], NT) * slope[j]).astype(BF16)
        lowered[...] = low
        total[...] += dot(low, win_ref[...], NT)

    @pl.when(step == 2 * tiles - 1)
    def _():
        dgain_ref[...] = jnp.zeros_like(dgain_ref)
        dbias_ref[...] = jnp.zeros_like(dbias_ref)

        @pl.loop(0, tokens // strip)
        def _(i):
            rows = pl.ds(pl.multiple_of(i * strip, strip), strip)
            v = hidden[rows]
            dy = total[rows]
            center = v - jnp.sum(v, axis=-1, keepdims=True) * inv
            spread = jnp.sum(center * center, axis=-1, keepdims=True) * inv
            scale = lax.rsqrt(spread + EPSILON)
            hat = center * scale
            dgain_ref[...] += jnp.sum(dy * hat, axis=0, keepdims=True)
            dbias_ref[...] += jnp.sum(dy, axis=0, keepdims=True)
            dh = dy * g_ref[3:4]
            first = jnp.sum(dh, axis=-1, keepdims=True) * inv
            second = jnp.sum(dh * hat, axis=-1, keepdims=True) * inv
            grad = hgrad_ref[rows] + scale * (dh - first - hat * second)
            hgrad_ref[rows] = grad
            attention[rows] = grad.astype(BF16)

        groups, _, group = cgrad_ref.shape
        for i in range(groups):
            rows = slice(i * group, (i + 1) * group)
            cgrad_ref[i] = dot(attention[...], wo_ref[rows], NT).astype(BF16)


def feed(res, ctx, wo, win, wout, gain, bias, w1, w2, mb, og, cg, groups):
    tokens, width = res.shape
    hidden_units = win.shape[1]
    cut = 1024
    tiles = hidden_units // cut
    small, coefs = w1.shape[0], w2.shape[1]

    def whole(x):
        zeros = (0,) * x.ndim
        return once(x.shape, lambda i: zeros)

    def result(shape, dtype=F32):
        zeros = (0,) * len(shape)
        return once(shape, lambda i: zeros), jax.ShapeDtypeStruct(shape, dtype)

    def back(i):
        return jnp.maximum(i - tiles, 0)

    outs = [
        result((tokens, width), BF16),
        result(cg.shape),
        (
            pl.BlockSpec((tokens, cut), lambda i: (0, jnp.minimum(i, tiles - 1))),
            jax.ShapeDtypeStruct((tokens, hidden_units), BF16),
        ),
        (
            pl.BlockSpec((tokens, cut), lambda i: (0, back(i))),
            jax.ShapeDtypeStruct((tokens, hidden_units), BF16),
        ),
        result((tokens, width), BF16),
        result((tokens, width), BF16),
        result((tokens, width), BF16),
        result((groups, tokens, width // groups), BF16),
        result((tokens, width)),
        result((1, width)),
        result((1, width)),
        result((small, width)),
        result((small, coefs)),
        result((1, coefs)),
    ]
    return pl.pallas_call(
        functools.partial(feed_kernel, tiles=tiles, strip=min(512, tokens)),
        grid=(2 * tiles,),
        in_specs=[
            whole(res),
            whole(ctx),
            whole(wo),
            pl.BlockSpec((width, cut), lambda i: (0, lax.rem(i, tiles))),
            pl.BlockSpec((cut, width), lambda i: (lax.rem(i, tiles), 0)),
            whole(gain),
            whole(bias),
            whole(w1),
            whole(w2),
            whole(mb),
            whole(og),
            whole(cg),
        ],
        out_specs=[spec for spec, _ in outs],
        out_shape=[shape for _, shape in outs],
        scratch_shapes=[
            pltpu.VMEM((tokens, width), F32),
            pltpu.VMEM((tokens, width), F32),
            pltpu.VMEM((tiles, tokens, cut), F32),
            pltpu.VMEM((tokens, width), BF16),
            pltpu.VMEM((tokens, width), BF16),
            pltpu.VMEM((coefs, tokens), F32),
        ],
        compiler_params=params(58),
        cost_estimate=pl.CostEstimate(
            flops=8 * tokens * width * hidden_units + 4 * tokens * width * width,
            bytes_accessed=8 * width * hidden_units + 4 * width * width + 20 * tokens * width,
            transcendentals=2 * tokens * hidden_units,
        ),
        name="feed",
    )(res, ctx, wo, win, wout, gain, bias, w1, w2, mb, og, cg)


def flipped(v, mask):
    bit = 1
    while bit <= mask:
        if mask & bit:
            v = v + bit - 2 * bit * lax.rem(v // bit, 2)
        bit *= 2
    return v


def added(out_ref, refs, rows, strip=32):
    strip = min(strip, rows)

    @pl.loop(0, rows // strip)
    def _(i):
        at = pl.ds(pl.multiple_of(i * strip, strip), strip)
        total = refs[0][at].astype(F32)
        for ref in refs[1:]:
            total = total + ref[at].astype(F32)
        out_ref[at] = total.astype(out_ref.dtype)


class Remote:
    def __init__(self, send, recv):
        self.send, self.recv, self.used = send, recv, 0

    def start(self, src, dst, where):
        copy = self.make(src, dst, where)
        copy.start()
        return copy

    def make(self, src, dst, where):
        copy = pltpu.make_async_remote_copy(
            src_ref=src,
            dst_ref=dst,
            send_sem=self.send.at[self.used],
            recv_sem=self.recv.at[self.used],
            device_id=where,
            device_id_type=MESH,
        )
        self.used += 1
        return copy


class Chain:
    def __init__(self, remote, n):
        self.remote, self.n = remote, n
        self.me = lax.axis_index("ctx")
        place = lax.rem(self.me, 4)
        self.outer = jnp.logical_or(place == 0, place == 3)
        self.inner = jnp.logical_not(self.outer)
        self.pieces = []
        self.started = 0

    def add(self, work, out, land, own, crosses):
        there = {"ctx": flipped(self.me, 1)}
        up = self.remote.make(work, land, there)
        masks = [3]
        bit = 4
        while bit < self.n:
            masks.append(bit)
            bit *= 2
        across = [
            self.remote.make(own.at[i], crosses.at[i], {"ctx": flipped(self.me, mask)})
            for i, mask in enumerate(masks)
        ]
        down = self.remote.make(out, out, there)
        self.pieces.append((work, out, land, own, crosses, up, across, down))

    def start(self):
        if self.started < len(self.pieces):
            up = self.pieces[self.started][5]

            @pl.when(self.outer)
            def _():
                up.start()

        self.started += 1

    def step(self, c):
        work, _, land, own, _, up, across, _ = self.pieces[c]

        @pl.when(self.outer)
        def _():
            up.wait_send()

        self.start()

        @pl.when(self.inner)
        def _():
            up.wait_recv()
            added(own.at[0], [work, land], work.shape[0])
            across[0].start()

        if c >= 2:
            self.leave(c - 2)

    def leave(self, c):
        _, out, _, own, crosses, _, across, down = self.pieces[c]

        @pl.when(self.inner)
        def _():
            for i, copy in enumerate(across):
                copy.wait()
                last = i + 1 == len(across)
                to = out if last else own.at[i + 1]
                added(to, [own.at[i], crosses.at[i]], out.shape[0])
                if not last:
                    across[i + 1].start()
            down.start()

    def end(self, c):
        down = self.pieces[c][7]

        @pl.when(self.outer)
        def _():
            down.wait_recv()

        @pl.when(self.inner)
        def _():
            down.wait_send()

    @staticmethod
    def levels(n):
        return max(1, n.bit_length() - 2)


def chain_scratch(n, rows, cols):
    levels = Chain.levels(n)
    return [
        pltpu.VMEM((rows, cols), BF16),
        pltpu.VMEM((levels, rows, cols), BF16),
        pltpu.VMEM((levels, rows, cols), BF16),
    ]


class ChipSum:
    def __init__(self, remote, nf, terms, keep, got, part):
        self.remote, self.nf, self.terms = remote, nf, terms
        self.keep, self.got, self.part = keep, got, part
        self.f = lax.axis_index("fsdp")
        self.chip, self.core = self.f // 2, lax.rem(self.f, 2)
        self.rows = got.shape[1]
        self.half = self.rows // 2
        bits = []
        bit = 1
        while bit < nf // 2:
            bits.append(bit)
            bit *= 2
        self.orders = (bits, bits[::-1])
        self.level = len(bits) - 1
        self.slots = 0

    def cores(self):
        self.copy = self.remote.start(
            self.terms.at[:, 1 - self.core], self.got, {"fsdp": flipped(self.f, 1)}
        )

    def masks(self, which, level):
        found = [0]
        for bit in self.orders[which][:level]:
            found += [mask + bit for mask in found]
        return found

    def piece(self, which, chip):
        return self.got.at[chip, pl.ds(which * self.half, self.half)]

    def launch(self):
        self.flying = []
        for which in range(2):
            bit = self.orders[which][self.level]
            to = 2 * flipped(self.chip, bit) + self.core
            for mask in self.masks(which, self.level):
                landing = self.part.at[self.slots]
                self.slots += 1
                copy = self.remote.start(
                    self.piece(which, flipped(self.chip, mask + bit)), landing, {"fsdp": to}
                )
                self.flying.append((copy, which, mask, landing))

    def cross(self):
        self.copy.wait()
        for k in range(self.nf // 2):
            added(self.got.at[k], [self.keep.at[k], self.got.at[k]], self.rows)
        self.launch()

    def relay(self):
        while self.level > 0:
            for copy, which, mask, landing in self.flying:
                copy.wait()
                here = self.piece(which, flipped(self.chip, mask))
                added(here, [here, landing], self.half)
            self.level -= 1
            self.launch()

    def total(self, out):
        for copy, which, _, landing in self.flying:
            copy.wait()
            added(
                out.at[pl.ds(which * self.half, self.half)],
                [self.piece(which, self.chip), landing],
                self.half,
            )

    @staticmethod
    def count(nf):
        return 1 + 2 * (nf // 2 - 1)


def chip_scratch(nf, rows, cols):
    chips = nf // 2
    return [
        pltpu.VMEM((chips, rows, cols), BF16),
        pltpu.VMEM((chips, rows, cols), BF16),
        pltpu.VMEM((2 * chips - 2, rows // 2, cols), BF16),
    ]


def greet_all(n, nf):
    z, f = lax.axis_index("ctx"), lax.axis_index("fsdp")
    barrier = pltpu.get_barrier_semaphore()
    for k in range(1, nf):
        pl.semaphore_signal(
            barrier, inc=1, device_id={"fsdp": lax.rem(f + k, nf)}, device_id_type=MESH
        )
    for k in range(1, n):
        pl.semaphore_signal(
            barrier, inc=1, device_id={"ctx": lax.rem(z + k, n)}, device_id_type=MESH
        )
    pl.semaphore_wait(barrier, nf + n - 2)


def place_segments(ids_ref, row, column, block):
    seqs, _, half = ids_ref.shape
    n = half // block
    for s in range(seqs):
        row[s, :, 0:half] = ids_ref[s, 0:1].astype(F32)
        for b in range(n):
            at = slice((n - 1 - b) * block, (n - b) * block)
            to = slice(half + b * block, half + (b + 1) * block)
            row[s, :, to] = ids_ref[s, 1:2, at].astype(F32)
        column[s] = jnp.broadcast_to(row[s], (8, 2 * half)).T


def mix_columns(mix_ref, mixes, t):
    block = mix_ref.shape[4]
    tile = mixes.shape[0]
    per = tile // block
    parts = []
    for i in range(t * per, (t + 1) * per):
        rows = [mix_ref[a, :, i // 2, i % 2, :] for a in range(mix_ref.shape[0])]
        parts.append(jnp.concatenate(rows, axis=0))
    mixes[...] = (parts[0] if per == 1 else jnp.concatenate(parts, axis=1)).T


class PlaneGather:
    def __init__(self, remote, nf, src, out):
        self.remote, self.nf, self.src, self.out = remote, nf, src, out
        self.f = lax.axis_index("fsdp")
        self.half = src.shape[0] // 2
        bits = []
        bit = 2
        while bit < nf:
            bits.append(bit)
            bit *= 2
        self.orders = (bits, bits[::-1])
        self.levels = len(bits)
        self.flying = {}
        self.inner = []

    def masks(self, which, level):
        found = [0]
        for bit in self.orders[which][:level]:
            found += [mask + bit for mask in found]
        return found

    def place(self, which, shard):
        return self.out.at[shard, pl.ds(which * self.half, self.half)]

    def launch(self, which, level, mask):
        shard = flipped(self.f, mask)
        here = self.src.at[pl.ds(which * self.half, self.half)]
        if mask:
            here = self.place(which, shard)
        to = flipped(self.f, self.orders[which][level])
        self.flying[which, level, mask] = self.remote.start(
            here, self.place(which, shard), {"fsdp": to}
        )

    def begin(self, sem):
        for level in range(self.levels):
            for which in range(2):
                self.launch(which, level, 0)
        self.inner.append(
            self.remote.start(self.src, self.out.at[self.f], {"fsdp": flipped(self.f, 1)})
        )
        self.own = pltpu.make_async_copy(self.src, self.out.at[self.f], sem)
        self.own.start()

    def relay(self, level):
        for which in range(2):
            order = self.orders[which]
            for mask in self.masks(which, level):
                self.flying[which, level, mask].wait()
                arrived = mask + order[level]
                for later in range(level + 1, self.levels):
                    self.launch(which, later, arrived)
                place = self.place(which, flipped(self.f, arrived))
                self.inner.append(self.remote.start(place, place, {"fsdp": flipped(self.f, 1)}))

    def end(self):
        self.own.wait()
        for copy in self.inner:
            copy.wait()

    @staticmethod
    def count(nf):
        return 2 * (nf // 2 - 1) + 2 * (nf // 2 - 1) + 1


def front_tile(e, mixes, st, g_ref, b_ref, normed, hats, scales, res, first, strip=16):
    count, tile, width = e.shape
    inv = 1.0 / width

    @pl.loop(0, tile // strip)
    def _(i):
        rows = pl.ds(pl.multiple_of(i * strip, strip), strip)
        mix = mixes[rows]
        for pair in ((0, 1), (2, 3)):
            totals = [None, None]
            for j in range(count):
                part = e[j, rows].astype(F32)
                for slot, s in enumerate(pair):
                    term = part * mix[:, s * count + j : s * count + j + 1]
                    totals[slot] = term if j == 0 else totals[slot] + term
            for slot, s in enumerate(pair):
                st[s, rows] = totals[slot]

    to = slice(first, first + tile)
    lane = lax.broadcasted_iota(jnp.int32, (tile, LANES), 1)
    kept = jnp.zeros((tile, LANES), F32)
    for s in range(3):
        v = st[s]
        center = v - jnp.sum(v, axis=-1, keepdims=True) * inv
        spread = jnp.sum(center * center, axis=-1, keepdims=True) * inv
        scale = lax.rsqrt(spread + EPSILON)
        hat = center * scale
        hats[s, to] = hat.astype(BF16)
        normed[s, to] = (hat * g_ref[s : s + 1] + b_ref[s : s + 1]).astype(BF16)
        kept = jnp.where(lane == s, scale, kept)
    scales[to] = kept
    res[to] = st[3]


def attend_pair(qkv, out, column_ref, row_ref, seq, lanes):
    blocks, block = out.shape[1], out.shape[2]
    length = blocks * block
    rows = row_tile(length)
    per = rows // block

    def load(kind, first, last):
        return qkv[kind, seq, first:last, :, lanes].reshape(-1, LANES)

    for i in range(length // rows):
        first, until = i * rows, (i + 1) * rows
        b0, b1 = i * per, (i + 1) * per
        query = first + lax.broadcasted_iota(jnp.int32, (rows, until), 0)
        key = lax.broadcasted_iota(jnp.int32, (rows, until), 1)
        same = column_ref[seq, first:until, 0:1] == row_ref[seq, 0:1, 0:until]
        allowed = same & (key <= query)
        q = load(0, b0, b1) * BF16(HD**-0.5)
        k = load(1, 0, b1)
        v = load(2, 0, b1)
        total = None
        for h in range(LANES // HD):
            scores = jnp.where(allowed, dot(only(q, h), k, NT), MASKED)
            peak = jnp.max(scores, axis=-1, keepdims=True)
            raised = jnp.exp(scores - peak)
            mass = jnp.sum(raised, axis=-1, keepdims=True)
            probs = (raised * (1.0 / mass)).astype(BF16)
            part = dot(probs, v)
            part = jnp.where(head_lanes(part.shape, h), part, 0.0)
            total = part if total is None else total + part
        out[seq, b0:b1, :, lanes] = total.astype(BF16).reshape(per, block, LANES)


def forward_kernel(
    n,
    nf,
    e_ref,
    wqkv_ref,
    wo_ref,
    win_ref,
    wout_ref,
    mix_ref,
    gain_ref,
    bias_ref,
    c_ref,
    s_ref,
    ids_ref,
    normed_ref,
    hats_ref,
    scales_ref,
    res_ref,
    gqkv_ref,
    go_ref,
    gin_ref,
    gout_ref,
    qkv_ref,
    ctx_ref,
    e,
    mixes,
    st,
    normed,
    hats,
    scales,
    res,
    w,
    raw,
    shares,
    qkv,
    heads,
    row,
    column,
    send,
    recv,
    local,
    e_sem,
):
    f, z = lax.axis_index("fsdp"), lax.axis_index("ctx")
    count, tokens, width = e_ref.shape
    tile = e.shape[2]
    tiles = tokens // tile
    seqs, _, block, cols = heads.shape
    seq_rows = 2 * block
    cut = raw.shape[1]
    remote = Remote(send, recv)
    spots = (z, 2 * n - 1 - z)
    mine = pl.ds(pl.multiple_of(z * cols, LANES), cols)

    def fetch(t):
        return pltpu.make_async_copy(
            e_ref.at[:, t * tile : (t + 1) * tile], e.at[t % 2], e_sem.at[t % 2]
        )

    fetch(0).start()
    greet_all(n, nf)

    def columns(ref, i):
        at = pl.ds(i * width, width)
        return ref.at[:, at] if len(ref.shape) == 2 else ref.at[:, :, at]

    parts = [
        PlaneGather(remote, nf, columns(wqkv_ref, i), columns(w, i)) for i in range(3)
    ]
    others = [
        PlaneGather(remote, nf, win_ref, gin_ref),
        PlaneGather(remote, nf, wout_ref, gout_ref),
        PlaneGather(remote, nf, wo_ref, go_ref),
    ]
    levels = parts[0].levels
    parts[0].begin(local.at[0])

    def do_tile(t):
        fetch(t).wait()
        if t + 1 < tiles:
            fetch(t + 1).start()
        mix_columns(mix_ref, mixes, t)
        front_tile(
            e.at[t % 2], mixes, st, gain_ref, bias_ref, normed, hats, scales, res, t * tile
        )

    def first_hops():
        parts[0].relay(0)
        parts[1].begin(local.at[1])

    def second_hops():
        for level in range(1, levels):
            parts[0].relay(level)
        parts[1].relay(0)
        parts[2].begin(local.at[2])

    def third_hops():
        for level in range(1, levels):
            parts[1].relay(level)
        parts[2].relay(0)
        others[0].begin(local.at[3])

    hops = [first_hops, second_hops, third_hops]
    for t in range(tiles):
        do_tile(t)
        if hops:
            hops.pop(0)()
    for hop in hops:
        hop()
    own_tables = []
    for table in (c_ref, s_ref):
        early = table[pl.ds(pl.multiple_of(z * block, block), block)]
        late = table[pl.ds(pl.multiple_of((2 * n - 1 - z) * block, block), block)]
        own_tables.append((early, late))

    def project(i):
        @pl.loop(0, width // cut)
        def _(j):
            at = pl.ds(pl.multiple_of(i * width + j * cut, cut), cut)
            raw[...] = dot(normed[i], w[:, :, at].reshape(width, cut))
            for s in range(seqs):
                for h in range(2):
                    first = s * seq_rows + h * block
                    for c in range(cut // LANES):
                        x = raw[first : first + block, c * LANES : (c + 1) * LANES]
                        if i < 2:
                            x = turned(x, own_tables[0][h], own_tables[1][h])
                        to = c * LANES % cols
                        group = j * (cut // cols) + c * LANES // cols
                        shares[i, group, s, h, :, to : to + LANES] = x.astype(BF16)

    pairs = cols // LANES
    units = [(0, None)] + [(s, p) for s in range(1, seqs) for p in range(pairs)]
    arriving = {unit: [] for unit in units}
    kept = []

    def give(kind, unit):
        s, p = unit
        lanes = slice(None) if p is None else slice(p * LANES, (p + 1) * LANES)
        for k in range(1, n):
            to = lax.rem(z + k, n)
            for h in range(2):
                arriving[unit].append(
                    remote.start(
                        shares.at[kind, to, s, h, :, lanes],
                        qkv.at[kind, s, spots[h], :, lanes],
                        {"ctx": to},
                    )
                )

    for i in range(3):
        parts[i].end()
        project(i)
        give(i, units[0])
        if i == 0:
            for level in range(1, levels):
                parts[2].relay(level)
    for h in range(2):
        copy = pltpu.make_async_copy(
            shares.at[:, z, :, h], qkv.at[:, :, spots[h]], local.at[8 + h]
        )
        copy.start()
        kept.append(copy)
    for unit in units[1:2]:
        give(slice(None), unit)
    others[1].begin(local.at[4])
    others[2].begin(local.at[5])
    out_copies = [
        pltpu.make_async_copy(w, gqkv_ref, local.at[10]),
        pltpu.make_async_copy(normed, normed_ref, local.at[6]),
        pltpu.make_async_copy(res, res_ref, local.at[7]),
        pltpu.make_async_copy(hats, hats_ref, local.at[12]),
        pltpu.make_async_copy(scales, scales_ref, local.at[13]),
    ]
    for copy in out_copies:
        copy.start()
    place_segments(ids_ref, row, column, block)

    others[0].relay(0)
    for copy in kept:
        copy.wait()
    leaving = []
    stored = 14
    for index, unit in enumerate(units):
        for copy in arriving[unit]:
            copy.wait()
        for other in units[index + 2 : index + 3]:
            give(slice(None), other)
        s, p = unit
        if p is None:

            @pl.loop(0, pairs)
            def _(p):
                lanes = pl.ds(pl.multiple_of(p * LANES, LANES), LANES)
                attend_pair(qkv, heads, column, row, s, lanes)

            there, here = mine, slice(None)
        else:
            here = slice(p * LANES, (p + 1) * LANES)
            attend_pair(qkv, heads, column, row, s, here)
            there = pl.ds(pl.multiple_of(z * cols + p * LANES, LANES), LANES)
        for k in range(1, n):
            to = lax.rem(z + k, n)
            for h in range(2):
                spot = to if h == 0 else 2 * n - 1 - to
                leaving.append(
                    remote.start(
                        heads.at[s, spot, :, here], ctx_ref.at[s, h, :, there], {"ctx": to}
                    )
                )
        for h in range(2):
            copy = pltpu.make_async_copy(
                heads.at[s, spots[h], :, here], ctx_ref.at[s, h, :, there], local.at[stored]
            )
            stored += 1
            copy.start()
            out_copies.append(copy)
        if index == 0:
            others[1].relay(0)
            others[2].relay(0)
            for level in range(1, levels):
                others[0].relay(level)
    copy = pltpu.make_async_copy(qkv, qkv_ref, local.at[11])
    copy.start()
    out_copies.append(copy)
    for level in range(1, levels):
        others[1].relay(level)
        others[2].relay(level)
    for gather in others:
        gather.end()
    for copy in out_copies + leaving:
        copy.wait()


def forward(e, mix, w_qkv, w_o, w_in, w_out, gain, bias, cosine, sine, ids, n, nf):
    count, tokens, width = e.shape
    seqs, block = mix.shape[2], mix.shape[4]
    length = 2 * n * block
    cols = width // n
    spots = 2 * n
    tile = 128
    cut = max(cols, 512)
    rows = width // nf
    units = 1 + (seqs - 1) * (cols // LANES)
    copies = 6 * PlaneGather.count(nf) + (2 + 2 * units) * 2 * (n - 1)
    vmem = pl.BlockSpec(memory_space=pltpu.VMEM)
    hbm = pl.BlockSpec(memory_space=pltpu.HBM)

    def gathered(x):
        return jax.ShapeDtypeStruct((nf,) + x.shape, x.dtype)

    normed, hats, scales, res, g_qkv, g_o, g_in, g_out, qkv, ctx = pl.pallas_call(
        functools.partial(forward_kernel, n, nf),
        in_specs=[hbm] * 5 + [vmem] * 6,
        out_specs=[hbm] * 10,
        out_shape=[
            jax.ShapeDtypeStruct((3, tokens, width), BF16),
            jax.ShapeDtypeStruct((3, tokens, width), BF16),
            jax.ShapeDtypeStruct((tokens, LANES), F32),
            jax.ShapeDtypeStruct((tokens, width), F32),
            gathered(w_qkv),
            gathered(w_o),
            gathered(w_in),
            gathered(w_out),
            jax.ShapeDtypeStruct((3, seqs, spots, block, cols), BF16),
            jax.ShapeDtypeStruct((seqs, 2, block, width), BF16),
        ],
        scratch_shapes=[
            pltpu.VMEM((2, count, tile, width), BF16),
            pltpu.VMEM((tile, 4 * count), F32),
            pltpu.VMEM((4, tile, width), F32),
            pltpu.VMEM((3, tokens, width), BF16),
            pltpu.VMEM((3, tokens, width), BF16),
            pltpu.VMEM((tokens, LANES), F32),
            pltpu.VMEM((tokens, width), F32),
            pltpu.VMEM((nf, rows, 3 * width), BF16),
            pltpu.VMEM((tokens, cut), F32),
            pltpu.VMEM((3, n, seqs, 2, block, cols), BF16),
            pltpu.VMEM((3, seqs, spots, block, cols), BF16),
            pltpu.VMEM((seqs, spots, block, cols), BF16),
            pltpu.VMEM((seqs, 1, length), F32),
            pltpu.VMEM((seqs, length, 8), F32),
            pltpu.SemaphoreType.DMA((copies,)),
            pltpu.SemaphoreType.DMA((copies,)),
            pltpu.SemaphoreType.DMA((14 + 2 * units,)),
            pltpu.SemaphoreType.DMA((2,)),
        ],
        compiler_params=params(58, collective_id=0, has_side_effects=True),
        name="forward",
    )(e, w_qkv, w_o, w_in, w_out, mix, gain, bias, cosine, sine, ids)

    def whole(x):
        return x.reshape(x.shape[0] * x.shape[1], x.shape[2])

    weights = [whole(g) for g in (g_qkv, g_o, g_in, g_out)]
    return normed, hats, scales, res, *weights, qkv, ctx.reshape(tokens, width)


def attend_back_pair(qkv, grad, out, dk, dv, column_ref, row_ref, c_ref, s_ref, seq, lanes):
    blocks, block = grad.shape[1], grad.shape[2]
    length = blocks * block
    rows = row_tile(length)
    per = rows // block
    factor = HD**-0.5

    def load(ref, at, first, last):
        return ref[(*at, slice(first, last), slice(None), lanes)].reshape(-1, LANES)

    for i in range(length // rows):
        here = slice(i * rows, (i + 1) * rows)
        dk[here] = jnp.zeros((rows, LANES), F32)
        dv[here] = jnp.zeros((rows, LANES), F32)
    for i in range(length // rows):
        first, until = i * rows, (i + 1) * rows
        b0, b1 = i * per, (i + 1) * per
        query = first + lax.broadcasted_iota(jnp.int32, (rows, until), 0)
        key = lax.broadcasted_iota(jnp.int32, (rows, until), 1)
        same = column_ref[seq, first:until, 0:1] == row_ref[seq, 0:1, 0:until]
        allowed = same & (key <= query)
        q = load(qkv, (0, seq), b0, b1) * BF16(factor)
        g = load(grad, (seq,), b0, b1)
        k = load(qkv, (1, seq), 0, b1)
        v = load(qkv, (2, seq), 0, b1)
        total = None
        for h in range(LANES // HD):
            q_h = only(q, h)
            g_h = only(g, h)
            scores = jnp.where(allowed, dot(q_h, k, NT), MASKED)
            peak = jnp.max(scores, axis=-1, keepdims=True)
            raised = jnp.exp(scores - peak)
            mass = jnp.sum(raised, axis=-1, keepdims=True)
            probs = raised * (1.0 / mass)
            dots = dot(g_h, v, NT)
            center = jnp.sum(probs * dots, axis=-1, keepdims=True)
            slope = (probs * (dots - center)).astype(BF16)
            part = dot(slope, k)
            part = jnp.where(head_lanes(part.shape, h), part, 0.0)
            total = part if total is None else total + part
            dk[0:until] += dot(slope, q_h, TN)
            dv[0:until] += dot(probs.astype(BF16), g_h, TN)
        cosine, sine = c_ref[first:until], s_ref[first:until]
        low = turned(total * factor, cosine, -sine).astype(BF16)
        out[0, seq, b0:b1, :, lanes] = low.reshape(per, block, LANES)
    for i in range(length // rows):
        here = slice(i * rows, (i + 1) * rows)
        b0, b1 = i * per, (i + 1) * per
        low = turned(dk[here], c_ref[here], -s_ref[here]).astype(BF16)
        out[1, seq, b0:b1, :, lanes] = low.reshape(per, block, LANES)
        out[2, seq, b0:b1, :, lanes] = dv[here].astype(BF16).reshape(per, block, LANES)


def back_kernel(
    n,
    nf,
    cg_ref,
    qkv_ref,
    active_ref,
    lowered_ref,
    normed_ref,
    branch_ref,
    ctx_ref,
    attention_ref,
    ids_ref,
    c_ref,
    s_ref,
    grads_ref,
    in_sum,
    out_sum,
    o_sum,
    qkv,
    grad,
    back,
    dk,
    dv,
    in_terms,
    in_got,
    in_part,
    out_terms,
    out_got,
    out_part,
    o_terms,
    o_got,
    o_part,
    normed,
    branch,
    ctx,
    attention,
    low_tiles,
    active_tiles,
    row,
    column,
    tile_sem,
    send,
    recv,
    local,
):
    f, z = lax.axis_index("fsdp"), lax.axis_index("ctx")
    core = lax.rem(f, 2)
    seqs, _, block, cols = grad.shape
    remote = Remote(send, recv)
    sums = [
        ChipSum(remote, nf, in_terms, in_terms.at[:, core], in_got, in_part),
        ChipSum(remote, nf, out_terms, out_terms.at[:, core], out_got, out_part),
        ChipSum(remote, nf, o_terms, o_terms.at[:, core], o_got, o_part),
    ]
    spots = (z, 2 * n - 1 - z)
    mine = pl.ds(pl.multiple_of(z * cols, LANES), cols)

    def fetch(ref, tiles, sem, t):
        size = tiles.shape[2]
        slot = lax.rem(t, 2)
        at = pl.ds(pl.multiple_of(t * size, LANES), size)
        return pltpu.make_async_copy(ref.at[:, at], tiles.at[slot], tile_sem.at[sem + slot])

    wholes = [(normed_ref, normed), (branch_ref, branch), (ctx_ref, ctx), (attention_ref, attention)]
    loads = [
        pltpu.make_async_copy(ref, there, local.at[i]) for i, (ref, there) in enumerate(wholes)
    ]
    loads[0].start()
    fetch(lowered_ref, low_tiles, 0, 0).start()
    for load in loads[1:]:
        load.start()
    fetch(active_ref, active_tiles, 2, 0).start()
    later = [pltpu.make_async_copy(qkv_ref, qkv, local.at[6 + 2 * seqs])]
    for h in range(2):
        later.append(
            pltpu.make_async_copy(cg_ref.at[z, :, h], grad.at[:, spots[h]], local.at[4 + h])
        )
    for load in later:
        load.start()

    greet_all(n, nf)

    arriving = []

    def take(s):
        copies = []
        for k in range(1, n):
            to = lax.rem(z + k, n)
            for h in range(2):
                copies.append(
                    remote.start(cg_ref.at[to, s, h], grad.at[s, spots[h]], {"ctx": to})
                )
        arriving.append(copies)

    def each_tile(ref, tiles, sem, work):
        count = ref.shape[1] // tiles.shape[2]

        @pl.loop(0, count)
        def _(t):
            fetch(ref, tiles, sem, t).wait()

            @pl.when(t + 1 < count)
            def _():
                fetch(ref, tiles, sem, t + 1).start()

            work(t, tiles[lax.rem(t, 2)])

    def in_tile(t, low):
        chips, _, rows, _ = in_terms.shape
        size = low.shape[1]
        at = pl.ds(pl.multiple_of(t * size, LANES), size)
        value = dot(normed[...], low, TN).astype(BF16)
        in_terms[:, :, :, at] = value.reshape(chips, 2, rows, size)

    def out_tile(t, active):
        _, _, rows, width = out_terms.shape
        out_terms[t] = dot(active, branch[...], TN).astype(BF16).reshape(2, rows, width)

    take(0)
    loads[0].wait()
    each_tile(lowered_ref, low_tiles, 0, in_tile)
    sums[0].cores()
    for load in loads[1:]:
        load.wait()
    each_tile(active_ref, active_tiles, 2, out_tile)
    sums[1].cores()
    for s in range(1, seqs):
        take(s)
    o_terms[...] = dot(ctx[...], attention[...], TN).astype(BF16).reshape(o_terms.shape)
    sums[2].cores()
    place_segments(ids_ref, row, column, block)
    sums[0].cross()
    for load in later:
        load.wait()

    leaving = []
    kept = []
    for s in range(seqs):
        for copy in arriving[s]:
            copy.wait()

        @pl.loop(0, cols // LANES)
        def _(p):
            lanes = pl.ds(pl.multiple_of(p * LANES, LANES), LANES)
            attend_back_pair(qkv, grad, back, dk, dv, column, row, c_ref, s_ref, s, lanes)

        for k in range(1, n):
            to = lax.rem(z + k, n)
            for h in range(2):
                spot = to if h == 0 else 2 * n - 1 - to
                leaving.append(
                    remote.start(
                        back.at[:, s, spot], grads_ref.at[:, s, h, :, mine], {"ctx": to}
                    )
                )
        for h in range(2):
            copy = pltpu.make_async_copy(
                back.at[:, s, spots[h]], grads_ref.at[:, s, h, :, mine], local.at[6 + 2 * s + h]
            )
            copy.start()
            kept.append(copy)
        if s == 0:
            sums[1].cross()
            sums[2].cross()
            sums[0].relay()

    sums[1].relay()
    sums[2].relay()
    for chip_sum, out in zip(sums, (in_sum, out_sum, o_sum)):
        chip_sum.total(out)
    for copy in kept + leaving:
        copy.wait()


def attention_back(context_grad, qkv, saved, ids, cosine, sine, n, nf):
    _, seqs, spots, block, cols = qkv.shape
    length = spots * block
    tokens, units = saved[0].shape
    width = saved[2].shape[1]
    chips = nf // 2
    shapes = [(width // nf, units), (units // nf, width), (width // nf, width)]
    copies = seqs * 4 * (n - 1) + 3 * ChipSum.count(nf)
    vmem = pl.BlockSpec(memory_space=pltpu.VMEM)
    hbm = pl.BlockSpec(memory_space=pltpu.HBM)
    scratch = []
    for rows, wide in shapes:
        scratch.append(pltpu.VMEM((chips, 2, rows, wide), BF16))
        scratch += chip_scratch(nf, rows, wide)[1:]
    grads, *owned = pl.pallas_call(
        functools.partial(back_kernel, n, nf),
        in_specs=[hbm] * 8 + [vmem] * 3,
        out_specs=[hbm, vmem, vmem, vmem],
        out_shape=[jax.ShapeDtypeStruct((3, seqs, 2, block, width), BF16)]
        + [jax.ShapeDtypeStruct(shape, BF16) for shape in shapes],
        scratch_shapes=[
            pltpu.VMEM((3, seqs, spots, block, cols), BF16),
            pltpu.VMEM((seqs, spots, block, cols), BF16),
            pltpu.VMEM((3, seqs, spots, block, cols), BF16),
            pltpu.VMEM((length, LANES), F32),
            pltpu.VMEM((length, LANES), F32),
            *scratch,
            *[pltpu.VMEM((tokens, width), BF16)] * 4,
            pltpu.VMEM((2, tokens, 512), BF16),
            pltpu.VMEM((2, tokens, units // chips), BF16),
            pltpu.VMEM((seqs, 1, length), F32),
            pltpu.VMEM((seqs, length, 8), F32),
            pltpu.SemaphoreType.DMA((4,)),
            pltpu.SemaphoreType.DMA((copies,)),
            pltpu.SemaphoreType.DMA((copies,)),
            pltpu.SemaphoreType.DMA((7 + 2 * seqs,)),
        ],
        compiler_params=params(62, collective_id=2, has_side_effects=True),
        name="attention_back",
    )(
        context_grad.reshape(n, seqs, 2, block, cols),
        qkv,
        *saved,
        ids,
        cosine,
        sine,
    )
    return grads.reshape(3, seqs * 2 * block, width), owned


def norm_back_tile(hats, scales, ng, st, e, mg, mg_ref, g_ref, h, low, dgain, dbias, selector, t, strip=16):
    count, tile, width = e.shape
    inv = 1.0 / width
    to = slice(t * tile, (t + 1) * tile)
    for s in range(3):
        dy = ng[s]
        hat = hats[s, to].astype(F32)
        scale = scales[to, s : s + 1]
        dgain[s : s + 1] += jnp.sum(dy * hat, axis=0, keepdims=True)
        dbias[s : s + 1] += jnp.sum(dy, axis=0, keepdims=True)
        dh = dy * g_ref[s : s + 1]
        mean = jnp.sum(dh, axis=-1, keepdims=True) * inv
        along = jnp.sum(dh * hat, axis=-1, keepdims=True) * inv
        out = (scale * (dh - mean - hat * along)).astype(BF16)
        low[s, to] = out
        st[s] = out
    st[3] = h[to].astype(BF16)

    shape = (4 * strip, count * strip)
    same = lax.rem(lax.broadcasted_iota(jnp.int32, shape, 0), strip) == lax.rem(
        lax.broadcasted_iota(jnp.int32, shape, 1), strip
    )
    for i in range(tile // strip):
        rows = slice(i * strip, (i + 1) * strip)
        grads = st[:, rows].reshape(4 * strip, width)
        inputs = e[:, rows].reshape(count * strip, width)
        products = jnp.where(same, dot(grads, inputs, NT), 0.0)
        wide = jnp.concatenate(
            [products[s * strip : (s + 1) * strip] for s in range(4)], axis=1
        )
        high, rest = halves(wide)
        mg[rows] = dot(high, selector[...]) + dot(rest, selector[...])
    turned_mg = mg[...].T
    block = mg_ref.shape[4]
    per = tile // block
    for i in range(per):
        place = t * per + i
        for a in range(4):
            mg_ref[a, :, place // 2, place % 2, :] = turned_mg[
                a * count : (a + 1) * count, i * block : (i + 1) * block
            ]


def small_squares(rows, cols):
    first = 8 + rows
    places = []
    for g in range(-(-rows // 8)):
        size = min(8, rows - 8 * g)
        places.append(
            (
                slice(first, first + size),
                slice(g * LANES, g * LANES + cols),
                slice(8 * g, 8 * g + size),
            )
        )
    return places


def small_line_at(rows, cols):
    groups = -(-rows // 8)
    return slice(groups * LANES, groups * LANES + cols)


def end_kernel(
    n,
    nf,
    grads_ref,
    normed_ref,
    hats_ref,
    scales_ref,
    e_ref,
    w_ref,
    h_ref,
    gain_ref,
    in_ref,
    out_ref,
    o_ref,
    sgain_ref,
    sbias_ref,
    sw1_ref,
    sw2_ref,
    smb_ref,
    low_ref,
    mg_ref,
    q_sum,
    k_sum,
    v_sum,
    in_sum,
    out_sum,
    o_sum,
    small_sum,
    grads,
    normed,
    hats,
    scales,
    w,
    h,
    e,
    ng,
    st,
    low,
    mg,
    selector,
    dgain,
    dbias,
    small_work,
    small_in,
    small_line,
    send,
    recv,
    local,
    e_sem,
    *more,
):
    f, z = lax.axis_index("fsdp"), lax.axis_index("ctx")
    core = lax.rem(f, 2)
    count, tokens, width = e_ref.shape
    tile = e.shape[2]
    tiles = tokens // tile
    remote = Remote(send, recv)
    chip_sets = [more[4 * i : 4 * i + 4] for i in range(3)]
    rest = more[12:]
    shard = chip_sets[0][1].shape[1]

    def fetch(t):
        return pltpu.make_async_copy(
            e_ref.at[:, t * tile : (t + 1) * tile], e.at[t % 2], e_sem.at[t % 2]
        )

    loads = [
        pltpu.make_async_copy(src, dst, local.at[i])
        for i, (src, dst) in enumerate(
            [
                (grads_ref, grads),
                (normed_ref, normed),
                (w_ref, w),
                (hats_ref, hats),
                (scales_ref, scales),
                (h_ref, h),
            ]
        )
    ]
    for load in loads:
        load.start()
    fetch(0).start()

    greet_all(n, nf)

    chain = Chain(remote, n)
    planned = [(in_ref, in_sum, 4), (out_ref, out_sum, 4), (o_ref, o_sum, 1)]
    planned += [
        (chip_set[3], out, 1) for chip_set, out in zip(chip_sets, (q_sum, k_sum, v_sum))
    ]
    for work, out, count_of in planned:
        size = work.shape[0] // count_of
        for i in range(count_of):
            at = pl.ds(i * size, size)
            chain.add(work.at[at], out.at[at], *rest[:3])
            rest = rest[3:]
    chain.start()
    chain.start()

    loads[0].wait()
    loads[1].wait()
    cut = 256
    per = cut // (2 * shard)
    sums = []
    for i in range(3):
        terms, got, part, own = chip_sets[i]
        for c in range(width // cut):
            value = dot(normed[i, :, c * cut : (c + 1) * cut], grads[i], TN).astype(BF16)
            terms[c * per : (c + 1) * per] = value.reshape(per, 2, shard, width)
        chip_sum = ChipSum(remote, nf, terms, terms.at[:, core], got, part)
        chip_sum.cores()
        sums.append(chip_sum)
    dgain[...] = jnp.zeros_like(dgain)
    dbias[...] = jnp.zeros_like(dbias)
    size = selector.shape
    group = lax.broadcasted_iota(jnp.int32, size, 0) // 16
    selector[...] = jnp.where(
        group == lax.broadcasted_iota(jnp.int32, size, 1), 1.0, 0.0
    ).astype(BF16)
    for load in loads[2:]:
        load.wait()

    def do_tile(t):
        fetch(t).wait()
        if t + 1 < tiles:
            fetch(t + 1).start()
        rows = slice(t * tile, (t + 1) * tile)
        for i in range(3):
            ng[i] = dot(grads[i, rows], w[:, i * width : (i + 1) * width], NT)
        norm_back_tile(
            hats, scales, ng, st, e.at[t % 2], mg, mg_ref, gain_ref, h, low, dgain, dbias, selector, t
        )

    todo = list(range(tiles))

    def some():
        if todo:
            do_tile(todo.pop(0))

    chain.step(0)
    for chip_sum in sums:
        chip_sum.cross()
    chain.step(1)
    some()
    chain.step(2)
    some()
    chain.step(3)
    chain.step(4)
    for chip_sum in sums:
        chip_sum.relay()
    some()
    chain.step(5)
    while todo:
        some()
    keep = pltpu.make_async_copy(low, low_ref, local.at[6])
    keep.start()
    for chip_sum, chip_set in zip(sums, chip_sets):
        chip_sum.total(chip_set[3])
    chain.step(6)

    thin = small_in.shape[1]
    hidden_count, coef_count = sw2_ref.shape
    first = 8 + hidden_count
    squares = small_squares(hidden_count, coef_count)
    line_at = small_line_at(hidden_count, coef_count)
    small_work[...] = jnp.zeros_like(small_work)
    small_work[0:3] = dgain[...]
    small_work[3:4] = sgain_ref[...]
    small_work[4:7] = dbias[...]
    small_work[7:8] = sbias_ref[...]
    small_work[8:first] = sw1_ref[...]
    for rows, lanes, which in squares:
        small_work[rows, lanes] = sw2_ref[which]
    small_work[first : first + 1, line_at] = smb_ref[...]
    here = pl.ds(pl.multiple_of(f * thin, thin), thin)
    small_in[0] = small_work[here]
    slices = []
    for k in range(1, nf):
        to = lax.rem(f + k, nf)
        slices.append(
            remote.start(
                small_work.at[pl.ds(pl.multiple_of(to * thin, thin), thin)],
                small_in.at[k],
                {"fsdp": to},
            )
        )

    chain.step(7)
    for copy in slices:
        copy.wait()
    total = small_in[0]
    for k in range(1, nf):
        total = total + small_in[k]
    small_line[z] = total
    across = []
    for k in range(1, n):
        across.append(
            remote.start(small_line.at[z], small_line.at[z], {"ctx": lax.rem(z + k, n)})
        )
    chain.step(8)
    chain.step(9)
    for copy in across:
        copy.wait()
    total = small_line[0]
    for k in range(1, n):
        total = total + small_line[k]
    small_sum[here] = total
    spread = []
    for k in range(1, nf):
        spread.append(
            remote.start(small_sum.at[here], small_sum.at[here], {"fsdp": lax.rem(f + k, nf)})
        )
    chain.step(10)
    chain.step(11)
    chain.leave(10)
    chain.leave(11)
    for copy in spread:
        copy.wait()
    for c in range(12):
        chain.end(c)
    keep.wait()


def finish(grads, normed, hats, scales, e, w, hgrad, gain, owned, small, mix_shape, n, nf):
    count, tokens, width = e.shape
    tile = 128
    chips = nf // 2
    shard = width // nf
    rows = 8 + small[2].shape[0] + 8
    thin = 8 * -(-rows // (8 * nf))
    m_in, m_out, m_o = owned
    lines, chip_sums = [], []
    for x, count_of in ((m_in, 4), (m_out, 4), (m_o, 1)):
        for _ in range(count_of):
            lines += chain_scratch(n, x.shape[0] // count_of, x.shape[1])
    for _ in range(3):
        lines += chain_scratch(n, shard, width)
        chip_sums += [
            pltpu.VMEM((chips, 2, shard, width), BF16),
            *chip_scratch(nf, shard, width)[1:],
            pltpu.VMEM((shard, width), BF16),
        ]
    copies = 12 * (Chain.levels(n) + 2) + 3 * ChipSum.count(nf) + 2 * (nf - 1) + (n - 1)
    vmem = pl.BlockSpec(memory_space=pltpu.VMEM)
    hbm = pl.BlockSpec(memory_space=pltpu.HBM)
    wide = jax.ShapeDtypeStruct((shard, width), BF16)
    return pl.pallas_call(
        functools.partial(end_kernel, n, nf),
        in_specs=[hbm] * 7 + [vmem] * 9,
        out_specs=[hbm] + [vmem] * 8,
        out_shape=[
            jax.ShapeDtypeStruct((3, tokens, width), BF16),
            jax.ShapeDtypeStruct(mix_shape, F32),
            wide,
            wide,
            wide,
            *[jax.ShapeDtypeStruct(x.shape, BF16) for x in owned],
            jax.ShapeDtypeStruct((nf * thin, width), F32),
        ],
        scratch_shapes=[
            pltpu.VMEM(grads.shape, BF16),
            pltpu.VMEM(normed.shape, BF16),
            pltpu.VMEM(hats.shape, BF16),
            pltpu.VMEM(scales.shape, F32),
            pltpu.VMEM(w.shape, BF16),
            pltpu.VMEM(hgrad.shape, F32),
            pltpu.VMEM((2, count, tile, width), BF16),
            pltpu.VMEM((3, tile, width), F32),
            pltpu.VMEM((4, tile, width), BF16),
            pltpu.VMEM((3, tokens, width), BF16),
            pltpu.VMEM((tile, LANES), F32),
            pltpu.VMEM((4 * count * 16, LANES), BF16),
            pltpu.VMEM((3, width), F32),
            pltpu.VMEM((3, width), F32),
            pltpu.VMEM((nf * thin, width), F32),
            pltpu.VMEM((nf, thin, width), F32),
            pltpu.VMEM((n, thin, width), F32),
            pltpu.SemaphoreType.DMA((copies,)),
            pltpu.SemaphoreType.DMA((copies,)),
            pltpu.SemaphoreType.DMA((7,)),
            pltpu.SemaphoreType.DMA((2,)),
            *chip_sums,
            *lines,
        ],
        compiler_params=params(60, collective_id=3, has_side_effects=True),
        name="finish",
    )(grads, normed, hats, scales, e, w, hgrad, gain, *owned, *small)


def tail_kernel(
    low_ref,
    h_ref,
    mix_ref,
    q_ref,
    k_ref,
    v_ref,
    in_ref,
    out_ref,
    o_ref,
    small_ref,
    mg_ref,
    eg_ref,
    qkv_ref,
    in32_ref,
    out32_ref,
    o32_ref,
    gain_ref,
    bias_ref,
    w1_ref,
    w2_ref,
    mb_ref,
    mg_out_ref,
    mixes,
    *,
    strip,
):
    count, tile, width = eg_ref.shape
    chunk = 512
    block = mix_ref.shape[4]
    tiles = mix_ref.shape[2] * 2 * block // tile
    step = pl.program_id(0)
    for t in range(tiles):

        @pl.when(step == t)
        def _():
            mix_columns(mix_ref, mixes, t)

    @pl.when(step == 0)
    def _():
        hidden_count, coef_count = w2_ref.shape
        first = 8 + hidden_count
        gain_ref[...] = small_ref[0:4]
        bias_ref[...] = small_ref[4:8]
        w1_ref[...] = small_ref[8:first]
        for rows, lanes, which in small_squares(hidden_count, coef_count):
            w2_ref[which] = small_ref[rows, lanes]
        mb_ref[...] = small_ref[first : first + 1, small_line_at(hidden_count, coef_count)]
        mg_out_ref[...] = mg_ref[...]

    for i, ref in enumerate((q_ref, k_ref, v_ref)):
        qkv_ref[:, i * width : (i + 1) * width] = ref[...].astype(F32)
    in32_ref[...] = in_ref[...].astype(F32)
    out32_ref[...] = out_ref[...].astype(F32)
    o32_ref[...] = o_ref[...].astype(F32)

    @pl.loop(0, tile // strip)
    def _(i):
        rows = pl.ds(pl.multiple_of(i * strip, strip), strip)
        mix = mixes[rows]
        for c in range(width // chunk):
            cols = slice(c * chunk, (c + 1) * chunk)
            grads = [low_ref[s, rows, cols].astype(F32) for s in range(3)]
            grads.append(h_ref[rows, cols])
            for j in range(count):
                total = grads[0] * mix[:, j : j + 1]
                for s in range(1, 4):
                    total = total + grads[s] * mix[:, s * count + j : s * count + j + 1]
                eg_ref[j, rows, cols] = total.astype(BF16)


def spread_back(low, hgrad, mix, sums, small, m_grad, sizes):
    _, tokens, width = low.shape
    count = mix.shape[1]
    tile = 128
    tiles = tokens // tile
    hidden_count, coef_count = sizes

    def part(x):
        return pl.BlockSpec((x.shape[0] // tiles, x.shape[1]), lambda i: (i, 0))

    def whole(x):
        zeros = (0,) * len(x.shape)
        return once(x.shape, lambda i: zeros)

    shard = sums[0].shape[0]
    outs = [
        jax.ShapeDtypeStruct((count, tokens, width), BF16),
        jax.ShapeDtypeStruct((shard, 3 * width), F32),
        *[jax.ShapeDtypeStruct(x.shape, F32) for x in sums[3:]],
        jax.ShapeDtypeStruct((4, width), F32),
        jax.ShapeDtypeStruct((4, width), F32),
        jax.ShapeDtypeStruct((hidden_count, width), F32),
        jax.ShapeDtypeStruct((hidden_count, coef_count), F32),
        jax.ShapeDtypeStruct((1, coef_count), F32),
        jax.ShapeDtypeStruct(m_grad.shape, F32),
    ]
    return pl.pallas_call(
        functools.partial(tail_kernel, strip=16),
        grid=(tiles,),
        in_specs=[
            pl.BlockSpec((3, tile, width), lambda i: (0, i, 0)),
            pl.BlockSpec((tile, width), lambda i: (i, 0)),
            whole(mix),
            *[part(x) for x in sums],
            whole(small),
            whole(m_grad),
        ],
        out_specs=[pl.BlockSpec((count, tile, width), lambda i: (0, i, 0))]
        + [part(x) for x in outs[1:5]]
        + [whole(x) for x in outs[5:]],
        out_shape=outs,
        scratch_shapes=[pltpu.VMEM((tile, 4 * count), F32)],
        compiler_params=params(60),
        cost_estimate=pl.CostEstimate(
            flops=64 * tokens * width, bytes_accessed=40 * tokens * width, transcendentals=0
        ),
        name="spread_back",
    )(low, hgrad, mix, *sums, small, m_grad)


def body(
    earlier,
    mix_in,
    segment_ids,
    attn_qkv,
    attn_out,
    mlp_in,
    mlp_out,
    norm_gain,
    norm_bias,
    mix_w1,
    mix_w2,
    mix_bias,
    out_grad,
    coef_grad,
):
    count, seqs, _, block, width = earlier.shape
    n = lax.axis_size("ctx")
    tokens = seqs * 2 * block
    length = 2 * n * block
    me = lax.axis_index("ctx")

    nf = lax.axis_size("fsdp")
    e = earlier.reshape(count, tokens, width)
    cosine, sine = (jnp.asarray(table) for table in turn_tables(length))
    normed, hats, scales, residual, w_qkv, w_o, w_in, w_out, qkv, context = forward(
        e,
        mix_in,
        attn_qkv,
        attn_out,
        mlp_in,
        mlp_out,
        norm_gain,
        norm_bias,
        cosine,
        sine,
        segment_ids,
        n,
        nf,
    )
    (
        layer_out,
        coefs,
        active,
        lowered,
        normed_mlp,
        branch,
        attention_grad,
        context_grad,
        hidden_grad,
        d_gain,
        d_bias,
        d_w1,
        d_w2,
        d_mb,
    ) = feed(
        residual,
        context,
        w_o,
        w_in,
        w_out,
        norm_gain,
        norm_bias,
        mix_w1,
        mix_w2,
        mix_bias[None, :],
        out_grad.reshape(tokens, width),
        coef_grad,
        n,
    )
    saved = (active, lowered, normed_mlp, branch, context, attention_grad)
    grads, owned = attention_back(
        context_grad, qkv, saved, segment_ids, cosine, sine, n, nf
    )
    low, m_grad, *sums, small = finish(
        grads,
        normed,
        hats,
        scales,
        e,
        w_qkv,
        hidden_grad,
        norm_gain,
        owned,
        (d_gain, d_bias, d_w1, d_w2, d_mb),
        mix_in.shape,
        n,
        nf,
    )
    e_grad, g_qkv, g_in, g_out, g_o, gain_sum, bias_sum, w1_sum, w2_sum, mb_sum, m_grad = (
        spread_back(low, hidden_grad, mix_in, sums, small, m_grad, mix_w2.shape)
    )
    return (
        layer_out.reshape(seqs, 2, block, width),
        coefs,
        e_grad.reshape(count, seqs, 2, block, width),
        m_grad,
        g_qkv,
        g_o,
        g_in,
        g_out,
        gain_sum,
        bias_sum,
        w1_sum,
        w2_sum,
        mb_sum[0],
    )


def solution(mesh):
    in_specs = (
        P(None, "fsdp", None, "ctx", None),
        P(None, None, "fsdp", None, "ctx"),
        P("fsdp", None, None),
        P("fsdp", None),
        P("fsdp", None),
        P("fsdp", None),
        P("fsdp", None),
        P(),
        P(),
        P(),
        P(),
        P(),
        P("fsdp", None, "ctx", None),
        P(None, None, "fsdp", None, "ctx"),
    )
    out_specs = (
        P("fsdp", None, "ctx", None),
        P(None, None, "fsdp", None, "ctx"),
        P(None, "fsdp", None, "ctx", None),
        P(None, None, "fsdp", None, "ctx"),
        P("fsdp", None),
        P("fsdp", None),
        P("fsdp", None),
        P("fsdp", None),
        P(),
        P(),
        P(),
        P(),
        P(),
    )
    return jax.shard_map(body, mesh=mesh, in_specs=in_specs, out_specs=out_specs, check_vma=False)
```

```python
import functools
import math

import jax
import jax.numpy as jnp
import numpy as np
from jax import lax
from jax.experimental import pallas as pl
from jax.experimental.pallas import tpu as pltpu
from jax.sharding import PartitionSpec as P

HD = 64
ROT = 16
LANES = 128
EPSILON = 1e-05
RMS_EPSILON = 1e-06
MASKED = -1e30
F32 = jnp.float32
BF16 = jnp.bfloat16
MESH = pl.DeviceIdType.MESH
MIB = 1024 * 1024

NN = (((1,), (0,)), ((), ()))
NT = (((1,), (1,)), ((), ()))
TN = (((0,), (0,)), ((), ()))

ERFC_RATE = 0.4
ERFC = (
    0.22567586600780487,
    0.22566929459571838,
    0.20784726738929749,
    0.16851142048835754,
    0.1415392905473709,
    -0.005822250619530678,
    0.16932761669158936,
    -0.18304575979709625,
    0.05029737576842308,
)


def dot(a, b, dims=NN):
    return lax.dot_general(a, b, dims, preferred_element_type=F32)


def gelu_and_slope(v):
    bell = jnp.exp(-0.5 * (v * v))
    t = 1.0 / (1.0 + (ERFC_RATE * math.sqrt(0.5)) * jnp.abs(v))
    poly = 0.5 * ERFC[-1] * t + 0.5 * ERFC[-2]
    for coefficient in ERFC[-3::-1]:
        poly = poly * t + 0.5 * coefficient
    tail = poly * t * bell
    phi = jnp.where(v >= 0.0, 1.0 - tail, tail)
    return v * phi, phi + v * bell * (1.0 / math.sqrt(2.0 * math.pi))


def halves(x):
    high = x.astype(BF16)
    return high, (x - high.astype(F32)).astype(BF16)


def params(limit_mib, **more):
    return pltpu.CompilerParams(vmem_limit_bytes=limit_mib * MIB, **more)


def once(shape, index):
    return pl.BlockSpec(shape, index, pipeline_mode=pl.Buffered(1))


def turn_tables(length):
    half = ROT // 2
    frequency = 10000.0 ** (-(np.arange(half) * 2.0 / ROT))
    angle = np.arange(length)[:, None] * frequency[None, :]
    lane = np.arange(LANES) % HD
    cosine = np.ones((length, LANES), np.float32)
    sine = np.zeros((length, LANES), np.float32)
    for k in range(LANES):
        if lane[k] < ROT:
            cosine[:, k] = np.cos(angle[:, lane[k] % half])
            sign = -1.0 if lane[k] < half else 1.0
            sine[:, k] = sign * np.sin(angle[:, lane[k] % half])
    return cosine, sine


def turned(x, cosine, sine):
    half = ROT // 2
    lane = lax.broadcasted_iota(jnp.int32, x.shape, 1) % HD
    other = jnp.where(
        lane < half, pltpu.roll(x, LANES - half, axis=1), pltpu.roll(x, half, axis=1)
    )
    return x * cosine + other * sine


def row_tile(length):
    return min(256, length)


def head_lanes(shape, h):
    lane = lax.broadcasted_iota(jnp.int32, shape, 1)
    return (lane >= h * HD) & (lane < (h + 1) * HD)


def only(x, h):
    return jnp.where(head_lanes(x.shape, h), x, jnp.zeros_like(x))


def coefficient_places(ref):
    outer, inner, seqs, _, block = ref.shape
    for a in range(outer):
        for seq in range(seqs):
            for h in range(2):
                first = (2 * seq + h) * block
                yield a, seq, h, slice(a * inner, (a + 1) * inner), slice(first, first + block)


def feed_kernel(
    res_ref,
    ctx_ref,
    wo_ref,
    win_ref,
    wout_ref,
    g_ref,
    b_ref,
    w1_ref,
    w2_ref,
    mb_ref,
    og_ref,
    cg_ref,
    out_ref,
    coef_ref,
    active,
    lowered,
    normed,
    branch,
    attention,
    cgrad_ref,
    hgrad_ref,
    dgain_ref,
    dbias_ref,
    dw1_ref,
    dw2_ref,
    dmb_ref,
    hidden,
    total,
    slope,
    r_high,
    r_rest,
    cotangent,
    *,
    tiles,
    strip,
):
    step = pl.program_id(0)
    tokens, width = res_ref.shape
    cut = win_ref.shape[1]
    inv = 1.0 / width

    @pl.when(step == 0)
    def _():
        hidden[...] = dot(ctx_ref[...], wo_ref[...])

        @pl.loop(0, tokens // strip)
        def _(i):
            rows = pl.ds(pl.multiple_of(i * strip, strip), strip)
            v = hidden[rows] + res_ref[rows]
            hidden[rows] = v
            center = v - jnp.sum(v, axis=-1, keepdims=True) * inv
            spread = jnp.sum(center * center, axis=-1, keepdims=True) * inv
            hat = center * lax.rsqrt(spread + EPSILON)
            normed[rows] = (hat * g_ref[3:4] + b_ref[3:4]).astype(BF16)
            total[rows] = v

    @pl.when(step < tiles)
    def _():
        half = tokens // 2
        parts = [slice(i * half, (i + 1) * half) for i in range(2)]
        ups = [dot(normed[rows], win_ref[...]) for rows in parts]
        for rows, up in zip(parts, ups):
            value, rate = gelu_and_slope(up)
            low = value.astype(BF16)
            active[rows] = low
            slope[step, rows] = rate
            total[rows] += dot(low, wout_ref[...])

    @pl.when(step == tiles - 1)
    def _():
        w1 = w1_ref[...]
        w2 = w2_ref[...]

        @pl.loop(0, tokens // strip)
        def _(i):
            rows = pl.ds(pl.multiple_of(i * strip, strip), strip)
            v = total[rows]
            out_ref[rows] = v.astype(BF16)
            scale = lax.rsqrt(jnp.sum(v * v, axis=-1, keepdims=True) * inv + RMS_EPSILON)
            r = v * scale
            high = r.astype(BF16)
            r_high[rows] = high
            r_rest[rows] = (r - high.astype(F32)).astype(BF16)

        high, rest = r_high[...], r_rest[...]
        for a, seq, h, rows, cols in coefficient_places(cg_ref):
            cotangent[rows, cols] = cg_ref[a, :, seq, h, :]
        z = dot(w1, high, NT) + dot(w1, rest, NT)
        value, rate = gelu_and_slope(z)
        v_high, v_rest = halves(value)
        ones = jnp.ones((1, tokens), BF16)
        mb_high, mb_rest = halves(mb_ref[...])
        mb_last = (mb_ref[...] - mb_high.astype(F32) - mb_rest.astype(F32)).astype(BF16)
        shift = dot(mb_high, ones, TN) + dot(mb_rest, ones, TN) + dot(mb_last, ones, TN)
        coefs = dot(w2, v_high, TN) + dot(w2, v_rest, TN) + shift
        for a, seq, h, rows, cols in coefficient_places(coef_ref):
            coef_ref[a, :, seq, h, :] = coefs[rows, cols]
        c_high, c_rest = halves(cotangent[...])
        dmb_ref[...] = dot(ones, c_high, NT) + dot(ones, c_rest, NT)
        dw2_ref[...] = dot(v_high, c_high, NT) + dot(v_rest, c_high, NT) + dot(v_high, c_rest, NT)
        z_high, z_rest = halves((dot(w2, c_high) + dot(w2, c_rest)) * rate)
        dw1_ref[...] = dot(z_high, high) + dot(z_high, rest) + dot(z_rest, high)
        hgrad_ref[...] = dot(z_high, w1, TN) + dot(z_rest, w1, TN)

        @pl.loop(0, tokens // strip)
        def _(i):
            rows = pl.ds(pl.multiple_of(i * strip, strip), strip)
            v = total[rows]
            scale = lax.rsqrt(jnp.sum(v * v, axis=-1, keepdims=True) * inv + RMS_EPSILON)
            dr = hgrad_ref[rows]
            r = v * scale
            mean = jnp.sum(dr * r, axis=-1, keepdims=True) * inv
            grad = scale * (dr - r * mean) + og_ref[rows].astype(F32)
            hgrad_ref[rows] = grad
            branch[rows] = grad.astype(BF16)
            total[rows] = jnp.zeros_like(v)

    @pl.when(step >= tiles)
    def _():
        j = step - tiles
        low = (dot(branch[...], wout_ref[...], NT) * slope[j]).astype(BF16)
        lowered[...] = low
        total[...] += dot(low, win_ref[...], NT)

    @pl.when(step == 2 * tiles - 1)
    def _():
        dgain_ref[...] = jnp.zeros_like(dgain_ref)
        dbias_ref[...] = jnp.zeros_like(dbias_ref)

        @pl.loop(0, tokens // strip)
        def _(i):
            rows = pl.ds(pl.multiple_of(i * strip, strip), strip)
            v = hidden[rows]
            dy = total[rows]
            center = v - jnp.sum(v, axis=-1, keepdims=True) * inv
            spread = jnp.sum(center * center, axis=-1, keepdims=True) * inv
            scale = lax.rsqrt(spread + EPSILON)
            hat = center * scale
            dgain_ref[...] += jnp.sum(dy * hat, axis=0, keepdims=True)
            dbias_ref[...] += jnp.sum(dy, axis=0, keepdims=True)
            dh = dy * g_ref[3:4]
            first = jnp.sum(dh, axis=-1, keepdims=True) * inv
            second = jnp.sum(dh * hat, axis=-1, keepdims=True) * inv
            grad = hgrad_ref[rows] + scale * (dh - first - hat * second)
            hgrad_ref[rows] = grad
            attention[rows] = grad.astype(BF16)

        groups, _, group = cgrad_ref.shape
        back = dot(attention[...], wo_ref[...], NT).astype(BF16)
        for i in range(groups):
            cgrad_ref[i] = back[:, i * group : (i + 1) * group]


def feed(res, ctx, wo, win, wout, gain, bias, w1, w2, mb, og, cg, groups):
    tokens, width = res.shape
    hidden_units = win.shape[1]
    cut = 1024
    tiles = hidden_units // cut
    small, coefs = w1.shape[0], w2.shape[1]

    def whole(x):
        zeros = (0,) * x.ndim
        return once(x.shape, lambda i: zeros)

    def result(shape, dtype=F32):
        zeros = (0,) * len(shape)
        return once(shape, lambda i: zeros), jax.ShapeDtypeStruct(shape, dtype)

    def back(i):
        return jnp.maximum(i - tiles, 0)

    outs = [
        result((tokens, width), BF16),
        result(cg.shape),
        (
            pl.BlockSpec((tokens, cut), lambda i: (0, jnp.minimum(i, tiles - 1))),
            jax.ShapeDtypeStruct((tokens, hidden_units), BF16),
        ),
        (
            pl.BlockSpec((tokens, cut), lambda i: (0, back(i))),
            jax.ShapeDtypeStruct((tokens, hidden_units), BF16),
        ),
        result((tokens, width), BF16),
        result((tokens, width), BF16),
        result((tokens, width), BF16),
        result((groups, tokens, width // groups), BF16),
        result((tokens, width)),
        result((1, width)),
        result((1, width)),
        result((small, width)),
        result((small, coefs)),
        result((1, coefs)),
    ]
    return pl.pallas_call(
        functools.partial(feed_kernel, tiles=tiles, strip=min(512, tokens)),
        grid=(2 * tiles,),
        in_specs=[
            whole(res),
            whole(ctx),
            whole(wo),
            pl.BlockSpec((width, cut), lambda i: (0, lax.rem(i, tiles))),
            pl.BlockSpec((cut, width), lambda i: (lax.rem(i, tiles), 0)),
            whole(gain),
            whole(bias),
            whole(w1),
            whole(w2),
            whole(mb),
            whole(og),
            whole(cg),
        ],
        out_specs=[spec for spec, _ in outs],
        out_shape=[shape for _, shape in outs],
        scratch_shapes=[
            pltpu.VMEM((tokens, width), F32),
            pltpu.VMEM((tokens, width), F32),
            pltpu.VMEM((tiles, tokens, cut), F32),
            pltpu.VMEM((tokens, width), BF16),
            pltpu.VMEM((tokens, width), BF16),
            pltpu.VMEM((coefs, tokens), F32),
        ],
        compiler_params=params(58),
        cost_estimate=pl.CostEstimate(
            flops=8 * tokens * width * hidden_units + 4 * tokens * width * width,
            bytes_accessed=8 * width * hidden_units + 4 * width * width + 20 * tokens * width,
            transcendentals=2 * tokens * hidden_units,
        ),
        name="feed",
    )(res, ctx, wo, win, wout, gain, bias, w1, w2, mb, og, cg)


def flipped(v, mask):
    bit = 1
    while bit <= mask:
        if mask & bit:
            v = v + bit - 2 * bit * lax.rem(v // bit, 2)
        bit *= 2
    return v


def added(out_ref, refs, rows, strip=32):
    strip = min(strip, rows)

    @pl.loop(0, rows // strip)
    def _(i):
        at = pl.ds(pl.multiple_of(i * strip, strip), strip)
        total = refs[0][at].astype(F32)
        for ref in refs[1:]:
            total = total + ref[at].astype(F32)
        out_ref[at] = total.astype(out_ref.dtype)


class Remote:
    def __init__(self, send, recv):
        self.send, self.recv, self.used = send, recv, 0

    def start(self, src, dst, where):
        copy = self.make(src, dst, where)
        copy.start()
        return copy

    def make(self, src, dst, where):
        copy = pltpu.make_async_remote_copy(
            src_ref=src,
            dst_ref=dst,
            send_sem=self.send.at[self.used],
            recv_sem=self.recv.at[self.used],
            device_id=where,
            device_id_type=MESH,
        )
        self.used += 1
        return copy


class Chain:
    def __init__(self, remote, n):
        self.remote, self.n = remote, n
        self.me = lax.axis_index("ctx")
        place = lax.rem(self.me, 4)
        self.outer = jnp.logical_or(place == 0, place == 3)
        self.inner = jnp.logical_not(self.outer)
        self.pieces = []
        self.started = 0

    def add(self, work, out, land, own, crosses):
        there = {"ctx": flipped(self.me, 1)}
        up = self.remote.make(work, land, there)
        masks = [3]
        bit = 4
        while bit < self.n:
            masks.append(bit)
            bit *= 2
        across = [
            self.remote.make(own.at[i], crosses.at[i], {"ctx": flipped(self.me, mask)})
            for i, mask in enumerate(masks)
        ]
        down = self.remote.make(out, out, there)
        self.pieces.append((work, out, land, own, crosses, up, across, down))

    def start(self):
        if self.started < len(self.pieces):
            up = self.pieces[self.started][5]

            @pl.when(self.outer)
            def _():
                up.start()

        self.started += 1

    def step(self, c):
        work, _, land, own, _, up, across, _ = self.pieces[c]

        @pl.when(self.outer)
        def _():
            up.wait_send()

        self.start()

        @pl.when(self.inner)
        def _():
            up.wait_recv()
            added(own.at[0], [work, land], work.shape[0])
            across[0].start()

        if c >= 1:
            self.leave(c - 1)

    def leave(self, c):
        _, out, _, own, crosses, _, across, down = self.pieces[c]

        @pl.when(self.inner)
        def _():
            for i, copy in enumerate(across):
                copy.wait()
                last = i + 1 == len(across)
                to = out if last else own.at[i + 1]
                added(to, [own.at[i], crosses.at[i]], out.shape[0])
                if not last:
                    across[i + 1].start()
            down.start()

    def end(self, c):
        down = self.pieces[c][7]

        @pl.when(self.outer)
        def _():
            down.wait_recv()

        @pl.when(self.inner)
        def _():
            down.wait_send()

    @staticmethod
    def levels(n):
        return max(1, n.bit_length() - 2)


def chain_scratch(n, rows, cols):
    levels = Chain.levels(n)
    return [
        pltpu.VMEM((rows, cols), BF16),
        pltpu.VMEM((levels, rows, cols), BF16),
        pltpu.VMEM((levels, rows, cols), BF16),
    ]


class ChipSum:
    def __init__(self, remote, nf, terms, keep, got, part):
        self.remote, self.nf, self.terms = remote, nf, terms
        self.keep, self.got, self.part = keep, got, part
        self.f = lax.axis_index("fsdp")
        self.chip, self.core = self.f // 2, lax.rem(self.f, 2)
        self.rows = got.shape[1]
        self.half = self.rows // 2
        bits = []
        bit = 1
        while bit < nf // 2:
            bits.append(bit)
            bit *= 2
        self.orders = (bits, bits[::-1])
        self.level = len(bits) - 1
        self.slots = 0

    def cores(self):
        self.copy = self.remote.start(
            self.terms.at[:, 1 - self.core], self.got, {"fsdp": flipped(self.f, 1)}
        )

    def masks(self, which, level):
        found = [0]
        for bit in self.orders[which][:level]:
            found += [mask + bit for mask in found]
        return found

    def piece(self, which, chip):
        return self.got.at[chip, pl.ds(which * self.half, self.half)]

    def launch(self):
        self.flying = []
        for which in range(2):
            bit = self.orders[which][self.level]
            to = 2 * flipped(self.chip, bit) + self.core
            for mask in self.masks(which, self.level):
                landing = self.part.at[self.slots]
                self.slots += 1
                copy = self.remote.start(
                    self.piece(which, flipped(self.chip, mask + bit)), landing, {"fsdp": to}
                )
                self.flying.append((copy, which, mask, landing))

    def cross(self):
        self.copy.wait()
        for k in range(self.nf // 2):
            added(self.got.at[k], [self.keep.at[k], self.got.at[k]], self.rows)
        self.launch()

    def relay(self):
        while self.level > 0:
            for copy, which, mask, landing in self.flying:
                copy.wait()
                here = self.piece(which, flipped(self.chip, mask))
                added(here, [here, landing], self.half)
            self.level -= 1
            self.launch()

    def total(self, out):
        for copy, which, _, landing in self.flying:
            copy.wait()
            added(
                out.at[pl.ds(which * self.half, self.half)],
                [self.piece(which, self.chip), landing],
                self.half,
            )

    @staticmethod
    def count(nf):
        return 1 + 2 * (nf // 2 - 1)


def chip_scratch(nf, rows, cols):
    chips = nf // 2
    return [
        pltpu.VMEM((chips, rows, cols), BF16),
        pltpu.VMEM((chips, rows, cols), BF16),
        pltpu.VMEM((2 * chips - 2, rows // 2, cols), BF16),
    ]


def greet_all(n, nf):
    z, f = lax.axis_index("ctx"), lax.axis_index("fsdp")
    barrier = pltpu.get_barrier_semaphore()
    for k in range(1, nf):
        pl.semaphore_signal(
            barrier, inc=1, device_id={"fsdp": lax.rem(f + k, nf)}, device_id_type=MESH
        )
    for k in range(1, n):
        pl.semaphore_signal(
            barrier, inc=1, device_id={"ctx": lax.rem(z + k, n)}, device_id_type=MESH
        )
    pl.semaphore_wait(barrier, nf + n - 2)


def place_segments(ids_ref, row, column, block):
    seqs, _, half = ids_ref.shape
    n = half // block
    for s in range(seqs):
        row[s, :, 0:half] = ids_ref[s, 0:1].astype(F32)
        for b in range(n):
            at = slice((n - 1 - b) * block, (n - b) * block)
            to = slice(half + b * block, half + (b + 1) * block)
            row[s, :, to] = ids_ref[s, 1:2, at].astype(F32)
        column[s] = jnp.broadcast_to(row[s], (8, 2 * half)).T


def mix_columns(mix_ref, mixes, t):
    block = mix_ref.shape[4]
    tile = mixes.shape[0]
    per = tile // block
    parts = []
    for i in range(t * per, (t + 1) * per):
        rows = [mix_ref[a, :, i // 2, i % 2, :] for a in range(mix_ref.shape[0])]
        parts.append(jnp.concatenate(rows, axis=0))
    mixes[...] = (parts[0] if per == 1 else jnp.concatenate(parts, axis=1)).T


class PlaneGather:
    def __init__(self, remote, nf, src, out):
        self.remote, self.nf, self.src, self.out = remote, nf, src, out
        self.f = lax.axis_index("fsdp")
        self.half = src.shape[0] // 2
        bits = []
        bit = 2
        while bit < nf:
            bits.append(bit)
            bit *= 2
        self.orders = (bits, bits[::-1])
        self.levels = len(bits)
        self.flying = {}
        self.inner = []

    def masks(self, which, level):
        found = [0]
        for bit in self.orders[which][:level]:
            found += [mask + bit for mask in found]
        return found

    def place(self, which, shard):
        return self.out.at[shard, pl.ds(which * self.half, self.half)]

    def launch(self, which, level, mask):
        shard = flipped(self.f, mask)
        here = self.src.at[pl.ds(which * self.half, self.half)]
        if mask:
            here = self.place(which, shard)
        to = flipped(self.f, self.orders[which][level])
        self.flying[which, level, mask] = self.remote.start(
            here, self.place(which, shard), {"fsdp": to}
        )

    def begin(self, sem):
        for level in range(self.levels):
            for which in range(2):
                self.launch(which, level, 0)
        self.inner.append(
            self.remote.start(self.src, self.out.at[self.f], {"fsdp": flipped(self.f, 1)})
        )
        self.own = pltpu.make_async_copy(self.src, self.out.at[self.f], sem)
        self.own.start()

    def relay(self, level):
        for which in range(2):
            order = self.orders[which]
            for mask in self.masks(which, level):
                self.flying[which, level, mask].wait()
                arrived = mask + order[level]
                for later in range(level + 1, self.levels):
                    self.launch(which, later, arrived)
                place = self.place(which, flipped(self.f, arrived))
                self.inner.append(self.remote.start(place, place, {"fsdp": flipped(self.f, 1)}))

    def end(self):
        self.own.wait()
        for copy in self.inner:
            copy.wait()

    @staticmethod
    def count(nf):
        return 2 * (nf // 2 - 1) + 2 * (nf // 2 - 1) + 1


def front_tile(e, mixes, st, g_ref, b_ref, normed, hats, scales, res, first, strip=16):
    count, tile, width = e.shape
    inv = 1.0 / width

    @pl.loop(0, tile // strip)
    def _(i):
        rows = pl.ds(pl.multiple_of(i * strip, strip), strip)
        mix = mixes[rows]
        for pair in ((0, 1), (2, 3)):
            totals = [None, None]
            for j in range(count):
                part = e[j, rows].astype(F32)
                for slot, s in enumerate(pair):
                    term = part * mix[:, s * count + j : s * count + j + 1]
                    totals[slot] = term if j == 0 else totals[slot] + term
            for slot, s in enumerate(pair):
                st[s, rows] = totals[slot]

    to = slice(first, first + tile)
    lane = lax.broadcasted_iota(jnp.int32, (tile, LANES), 1)
    kept = jnp.zeros((tile, LANES), F32)
    for s in range(3):
        v = st[s]
        center = v - jnp.sum(v, axis=-1, keepdims=True) * inv
        spread = jnp.sum(center * center, axis=-1, keepdims=True) * inv
        scale = lax.rsqrt(spread + EPSILON)
        hat = center * scale
        hats[s, to] = hat.astype(BF16)
        normed[s, to] = (hat * g_ref[s : s + 1] + b_ref[s : s + 1]).astype(BF16)
        kept = jnp.where(lane == s, scale, kept)
    scales[to] = kept
    res[to] = st[3]


def attend_pair(qkv, out, column_ref, row_ref, seq, lanes):
    blocks, block = out.shape[1], out.shape[2]
    length = blocks * block
    rows = row_tile(length)
    per = rows // block

    def load(kind, first, last):
        return qkv[kind, seq, first:last, :, lanes].reshape(-1, LANES)

    for i in range(length // rows):
        first, until = i * rows, (i + 1) * rows
        b0, b1 = i * per, (i + 1) * per
        query = first + lax.broadcasted_iota(jnp.int32, (rows, until), 0)
        key = lax.broadcasted_iota(jnp.int32, (rows, until), 1)
        same = column_ref[seq, first:until, 0:1] == row_ref[seq, 0:1, 0:until]
        allowed = same & (key <= query)
        q = load(0, b0, b1) * BF16(HD**-0.5)
        k = load(1, 0, b1)
        v = load(2, 0, b1)
        total = None
        for h in range(LANES // HD):
            scores = jnp.where(allowed, dot(only(q, h), k, NT), MASKED)
            peak = jnp.max(scores, axis=-1, keepdims=True)
            raised = jnp.exp(scores - peak)
            mass = jnp.sum(raised, axis=-1, keepdims=True)
            probs = (raised * (1.0 / mass)).astype(BF16)
            part = dot(probs, v)
            part = jnp.where(head_lanes(part.shape, h), part, 0.0)
            total = part if total is None else total + part
        out[seq, b0:b1, :, lanes] = total.astype(BF16).reshape(per, block, LANES)


def forward_kernel(
    n,
    nf,
    e_ref,
    wqkv_ref,
    wo_ref,
    win_ref,
    wout_ref,
    mix_ref,
    gain_ref,
    bias_ref,
    c_ref,
    s_ref,
    ids_ref,
    normed_ref,
    hats_ref,
    scales_ref,
    res_ref,
    gqkv_ref,
    go_ref,
    gin_ref,
    gout_ref,
    qkv_ref,
    ctx_ref,
    e,
    mixes,
    st,
    normed,
    hats,
    scales,
    res,
    w,
    raw,
    shares,
    qkv,
    heads,
    row,
    column,
    send,
    recv,
    local,
    e_sem,
):
    f, z = lax.axis_index("fsdp"), lax.axis_index("ctx")
    count, tokens, width = e_ref.shape
    tile = e.shape[2]
    tiles = tokens // tile
    seqs, _, block, cols = heads.shape
    seq_rows = 2 * block
    cut = raw.shape[1]
    remote = Remote(send, recv)
    spots = (z, 2 * n - 1 - z)
    mine = pl.ds(pl.multiple_of(z * cols, LANES), cols)

    def fetch(t):
        return pltpu.make_async_copy(
            e_ref.at[:, t * tile : (t + 1) * tile], e.at[t % 2], e_sem.at[t % 2]
        )

    fetch(0).start()
    greet_all(n, nf)

    def columns(ref, i):
        at = pl.ds(i * width, width)
        return ref.at[:, at] if len(ref.shape) == 2 else ref.at[:, :, at]

    parts = [
        PlaneGather(remote, nf, columns(wqkv_ref, i), columns(w, i)) for i in range(3)
    ]
    others = [
        PlaneGather(remote, nf, win_ref, gin_ref),
        PlaneGather(remote, nf, wout_ref, gout_ref),
        PlaneGather(remote, nf, wo_ref, go_ref),
    ]
    levels = parts[0].levels
    parts[0].begin(local.at[0])

    def do_tile(t):
        fetch(t).wait()
        if t + 1 < tiles:
            fetch(t + 1).start()
        mix_columns(mix_ref, mixes, t)
        front_tile(
            e.at[t % 2], mixes, st, gain_ref, bias_ref, normed, hats, scales, res, t * tile
        )

    def first_hops():
        parts[0].relay(0)
        parts[1].begin(local.at[1])

    def second_hops():
        for level in range(1, levels):
            parts[0].relay(level)

    hops = [first_hops, second_hops]
    for t in range(tiles):
        do_tile(t)
        if hops:
            hops.pop(0)()
    for hop in hops:
        hop()
    own_tables = []
    for table in (c_ref, s_ref):
        early = table[pl.ds(pl.multiple_of(z * block, block), block)]
        late = table[pl.ds(pl.multiple_of((2 * n - 1 - z) * block, block), block)]
        own_tables.append((early, late))

    def project(i):
        @pl.loop(0, width // cut)
        def _(j):
            at = pl.ds(pl.multiple_of(i * width + j * cut, cut), cut)
            raw[...] = dot(normed[i], w[:, :, at].reshape(width, cut))
            for s in range(seqs):
                for h in range(2):
                    first = s * seq_rows + h * block
                    for c in range(cut // LANES):
                        x = raw[first : first + block, c * LANES : (c + 1) * LANES]
                        if i < 2:
                            x = turned(x, own_tables[0][h], own_tables[1][h])
                        to = c * LANES % cols
                        group = j * (cut // cols) + c * LANES // cols
                        shares[i, group, s, h, :, to : to + LANES] = x.astype(BF16)

    pairs = cols // LANES
    units = [(0, None)] + [(s, p) for s in range(1, seqs) for p in range(pairs)]
    arriving = {unit: [] for unit in units}
    kept = []

    def give(kind, unit):
        s, p = unit
        lanes = slice(None) if p is None else slice(p * LANES, (p + 1) * LANES)
        for k in range(1, n):
            to = lax.rem(z + k, n)
            for h in range(2):
                arriving[unit].append(
                    remote.start(
                        shares.at[kind, to, s, h, :, lanes],
                        qkv.at[kind, s, spots[h], :, lanes],
                        {"ctx": to},
                    )
                )

    upcoming = [(parts[2], 2), (others[0], 3)]

    def begin_next():
        gather, sem = upcoming.pop(0)
        gather.begin(local.at[sem])

    for i in range(3):
        parts[i].end()
        project(i)
        give(i, units[0])
        if i < 2:
            for level in range(levels):
                parts[i + 1].relay(level)
                if level == 0:
                    begin_next()
    for h in range(2):
        copy = pltpu.make_async_copy(
            shares.at[:, z, :, h], qkv.at[:, :, spots[h]], local.at[8 + h]
        )
        copy.start()
        kept.append(copy)
    for unit in units[1:2]:
        give(slice(None), unit)
    others[1].begin(local.at[4])
    others[2].begin(local.at[5])
    out_copies = [
        pltpu.make_async_copy(w, gqkv_ref, local.at[10]),
        pltpu.make_async_copy(normed, normed_ref, local.at[6]),
        pltpu.make_async_copy(res, res_ref, local.at[7]),
        pltpu.make_async_copy(hats, hats_ref, local.at[12]),
        pltpu.make_async_copy(scales, scales_ref, local.at[13]),
    ]
    for copy in out_copies:
        copy.start()
    place_segments(ids_ref, row, column, block)

    others[0].relay(0)
    for copy in kept:
        copy.wait()
    leaving = []
    stored = 14
    for index, unit in enumerate(units):
        for copy in arriving[unit]:
            copy.wait()
        for other in units[index + 2 : index + 3]:
            give(slice(None), other)
        s, p = unit
        if p is None:

            @pl.loop(0, pairs)
            def _(p):
                lanes = pl.ds(pl.multiple_of(p * LANES, LANES), LANES)
                attend_pair(qkv, heads, column, row, s, lanes)

            there, here = mine, slice(None)
        else:
            here = slice(p * LANES, (p + 1) * LANES)
            attend_pair(qkv, heads, column, row, s, here)
            there = pl.ds(pl.multiple_of(z * cols + p * LANES, LANES), LANES)
        for k in range(1, n):
            to = lax.rem(z + k, n)
            for h in range(2):
                spot = to if h == 0 else 2 * n - 1 - to
                leaving.append(
                    remote.start(
                        heads.at[s, spot, :, here], ctx_ref.at[s, h, :, there], {"ctx": to}
                    )
                )
        for h in range(2):
            copy = pltpu.make_async_copy(
                heads.at[s, spots[h], :, here], ctx_ref.at[s, h, :, there], local.at[stored]
            )
            stored += 1
            copy.start()
            out_copies.append(copy)
        if index == 0:
            others[1].relay(0)
            others[2].relay(0)
            for level in range(1, levels):
                others[0].relay(level)
    copy = pltpu.make_async_copy(qkv, qkv_ref, local.at[11])
    copy.start()
    out_copies.append(copy)
    for level in range(1, levels):
        others[1].relay(level)
        others[2].relay(level)
    for gather in others:
        gather.end()
    for copy in out_copies + leaving:
        copy.wait()


def forward(e, mix, w_qkv, w_o, w_in, w_out, gain, bias, cosine, sine, ids, n, nf):
    count, tokens, width = e.shape
    seqs, block = mix.shape[2], mix.shape[4]
    length = 2 * n * block
    cols = width // n
    spots = 2 * n
    tile = 128
    cut = max(cols, 512)
    rows = width // nf
    units = 1 + (seqs - 1) * (cols // LANES)
    copies = 6 * PlaneGather.count(nf) + (2 + 2 * units) * 2 * (n - 1)
    vmem = pl.BlockSpec(memory_space=pltpu.VMEM)
    hbm = pl.BlockSpec(memory_space=pltpu.HBM)

    def gathered(x):
        return jax.ShapeDtypeStruct((nf,) + x.shape, x.dtype)

    normed, hats, scales, res, g_qkv, g_o, g_in, g_out, qkv, ctx = pl.pallas_call(
        functools.partial(forward_kernel, n, nf),
        in_specs=[hbm] * 5 + [vmem] * 6,
        out_specs=[hbm] * 10,
        out_shape=[
            jax.ShapeDtypeStruct((3, tokens, width), BF16),
            jax.ShapeDtypeStruct((3, tokens, width), BF16),
            jax.ShapeDtypeStruct((tokens, LANES), F32),
            jax.ShapeDtypeStruct((tokens, width), F32),
            gathered(w_qkv),
            gathered(w_o),
            gathered(w_in),
            gathered(w_out),
            jax.ShapeDtypeStruct((3, seqs, spots, block, cols), BF16),
            jax.ShapeDtypeStruct((seqs, 2, block, width), BF16),
        ],
        scratch_shapes=[
            pltpu.VMEM((2, count, tile, width), BF16),
            pltpu.VMEM((tile, 4 * count), F32),
            pltpu.VMEM((4, tile, width), F32),
            pltpu.VMEM((3, tokens, width), BF16),
            pltpu.VMEM((3, tokens, width), BF16),
            pltpu.VMEM((tokens, LANES), F32),
            pltpu.VMEM((tokens, width), F32),
            pltpu.VMEM((nf, rows, 3 * width), BF16),
            pltpu.VMEM((tokens, cut), F32),
            pltpu.VMEM((3, n, seqs, 2, block, cols), BF16),
            pltpu.VMEM((3, seqs, spots, block, cols), BF16),
            pltpu.VMEM((seqs, spots, block, cols), BF16),
            pltpu.VMEM((seqs, 1, length), F32),
            pltpu.VMEM((seqs, length, 8), F32),
            pltpu.SemaphoreType.DMA((copies,)),
            pltpu.SemaphoreType.DMA((copies,)),
            pltpu.SemaphoreType.DMA((14 + 2 * units,)),
            pltpu.SemaphoreType.DMA((2,)),
        ],
        compiler_params=params(58, collective_id=0, has_side_effects=True),
        name="forward",
    )(e, w_qkv, w_o, w_in, w_out, mix, gain, bias, cosine, sine, ids)

    def whole(x):
        return x.reshape(x.shape[0] * x.shape[1], x.shape[2])

    weights = [whole(g) for g in (g_qkv, g_o, g_in, g_out)]
    return normed, hats, scales, res, *weights, qkv, ctx.reshape(tokens, width)


def attend_back_pair(qkv, grad, out, dk, dv, column_ref, row_ref, c_ref, s_ref, seq, lanes):
    blocks, block = grad.shape[1], grad.shape[2]
    length = blocks * block
    rows = row_tile(length)
    per = rows // block
    factor = HD**-0.5

    def load(ref, at, first, last):
        return ref[(*at, slice(first, last), slice(None), lanes)].reshape(-1, LANES)

    for i in range(length // rows):
        here = slice(i * rows, (i + 1) * rows)
        dk[here] = jnp.zeros((rows, LANES), F32)
        dv[here] = jnp.zeros((rows, LANES), F32)
    for i in range(length // rows):
        first, until = i * rows, (i + 1) * rows
        b0, b1 = i * per, (i + 1) * per
        query = first + lax.broadcasted_iota(jnp.int32, (rows, until), 0)
        key = lax.broadcasted_iota(jnp.int32, (rows, until), 1)
        same = column_ref[seq, first:until, 0:1] == row_ref[seq, 0:1, 0:until]
        allowed = same & (key <= query)
        q = load(qkv, (0, seq), b0, b1) * BF16(factor)
        g = load(grad, (seq,), b0, b1)
        k = load(qkv, (1, seq), 0, b1)
        v = load(qkv, (2, seq), 0, b1)
        total = None
        for h in range(LANES // HD):
            q_h = only(q, h)
            g_h = only(g, h)
            scores = jnp.where(allowed, dot(q_h, k, NT), MASKED)
            peak = jnp.max(scores, axis=-1, keepdims=True)
            raised = jnp.exp(scores - peak)
            mass = jnp.sum(raised, axis=-1, keepdims=True)
            probs = raised * (1.0 / mass)
            dots = dot(g_h, v, NT)
            center = jnp.sum(probs * dots, axis=-1, keepdims=True)
            slope = (probs * (dots - center)).astype(BF16)
            part = dot(slope, k)
            part = jnp.where(head_lanes(part.shape, h), part, 0.0)
            total = part if total is None else total + part
            dk[0:until] += dot(slope, q_h, TN)
            dv[0:until] += dot(probs.astype(BF16), g_h, TN)
        cosine, sine = c_ref[first:until], s_ref[first:until]
        low = turned(total * factor, cosine, -sine).astype(BF16)
        out[0, seq, b0:b1, :, lanes] = low.reshape(per, block, LANES)
    for i in range(length // rows):
        here = slice(i * rows, (i + 1) * rows)
        b0, b1 = i * per, (i + 1) * per
        low = turned(dk[here], c_ref[here], -s_ref[here]).astype(BF16)
        out[1, seq, b0:b1, :, lanes] = low.reshape(per, block, LANES)
        out[2, seq, b0:b1, :, lanes] = dv[here].astype(BF16).reshape(per, block, LANES)


def back_kernel(
    n,
    nf,
    cg_ref,
    qkv_ref,
    active_ref,
    lowered_ref,
    normed_ref,
    branch_ref,
    ctx_ref,
    attention_ref,
    ids_ref,
    c_ref,
    s_ref,
    grads_ref,
    in_sum,
    out_sum,
    o_sum,
    qkv,
    grad,
    back,
    dk,
    dv,
    in_terms,
    in_got,
    in_part,
    out_terms,
    out_got,
    out_part,
    o_terms,
    o_got,
    o_part,
    normed,
    branch,
    ctx,
    attention,
    low_tiles,
    active_tiles,
    row,
    column,
    tile_sem,
    send,
    recv,
    local,
):
    f, z = lax.axis_index("fsdp"), lax.axis_index("ctx")
    core = lax.rem(f, 2)
    seqs, _, block, cols = grad.shape
    remote = Remote(send, recv)
    sums = [
        ChipSum(remote, nf, in_terms, in_terms.at[:, core], in_got, in_part),
        ChipSum(remote, nf, out_terms, out_terms.at[:, core], out_got, out_part),
        ChipSum(remote, nf, o_terms, o_terms.at[:, core], o_got, o_part),
    ]
    spots = (z, 2 * n - 1 - z)
    mine = pl.ds(pl.multiple_of(z * cols, LANES), cols)

    def fetch(ref, tiles, sem, t):
        size = tiles.shape[2]
        slot = lax.rem(t, 2)
        at = pl.ds(pl.multiple_of(t * size, LANES), size)
        return pltpu.make_async_copy(ref.at[:, at], tiles.at[slot], tile_sem.at[sem + slot])

    wholes = [(normed_ref, normed), (branch_ref, branch), (ctx_ref, ctx), (attention_ref, attention)]
    loads = [
        pltpu.make_async_copy(ref, there, local.at[i]) for i, (ref, there) in enumerate(wholes)
    ]
    loads[0].start()
    fetch(lowered_ref, low_tiles, 0, 0).start()
    for load in loads[1:]:
        load.start()
    fetch(active_ref, active_tiles, 2, 0).start()
    later = [pltpu.make_async_copy(qkv_ref, qkv, local.at[6 + 2 * seqs])]
    for h in range(2):
        later.append(
            pltpu.make_async_copy(cg_ref.at[z, :, h], grad.at[:, spots[h]], local.at[4 + h])
        )
    for load in later:
        load.start()

    greet_all(n, nf)

    arriving = []

    def take(s):
        copies = []
        for k in range(1, n):
            to = lax.rem(z + k, n)
            for h in range(2):
                copies.append(
                    remote.start(cg_ref.at[to, s, h], grad.at[s, spots[h]], {"ctx": to})
                )
        arriving.append(copies)

    def each_tile(ref, tiles, sem, work):
        count = ref.shape[1] // tiles.shape[2]

        @pl.loop(0, count)
        def _(t):
            fetch(ref, tiles, sem, t).wait()

            @pl.when(t + 1 < count)
            def _():
                fetch(ref, tiles, sem, t + 1).start()

            work(t, tiles[lax.rem(t, 2)])

    def in_tile(t, low):
        chips, _, rows, _ = in_terms.shape
        size = low.shape[1]
        at = pl.ds(pl.multiple_of(t * size, LANES), size)
        value = dot(normed[...], low, TN).astype(BF16)
        in_terms[:, :, :, at] = value.reshape(chips, 2, rows, size)

    def out_tile(t, active):
        _, _, rows, width = out_terms.shape
        out_terms[t] = dot(active, branch[...], TN).astype(BF16).reshape(2, rows, width)

    take(0)
    loads[0].wait()
    each_tile(lowered_ref, low_tiles, 0, in_tile)
    sums[0].cores()
    for load in loads[1:]:
        load.wait()
    each_tile(active_ref, active_tiles, 2, out_tile)
    sums[1].cores()
    for s in range(1, seqs):
        take(s)
    o_terms[...] = dot(ctx[...], attention[...], TN).astype(BF16).reshape(o_terms.shape)
    sums[2].cores()
    place_segments(ids_ref, row, column, block)
    sums[0].cross()
    for load in later:
        load.wait()

    leaving = []
    kept = []
    for s in range(seqs):
        for copy in arriving[s]:
            copy.wait()

        @pl.loop(0, cols // LANES)
        def _(p):
            lanes = pl.ds(pl.multiple_of(p * LANES, LANES), LANES)
            attend_back_pair(qkv, grad, back, dk, dv, column, row, c_ref, s_ref, s, lanes)

        for k in range(1, n):
            to = lax.rem(z + k, n)
            for h in range(2):
                spot = to if h == 0 else 2 * n - 1 - to
                leaving.append(
                    remote.start(
                        back.at[:, s, spot], grads_ref.at[:, s, h, :, mine], {"ctx": to}
                    )
                )
        for h in range(2):
            copy = pltpu.make_async_copy(
                back.at[:, s, spots[h]], grads_ref.at[:, s, h, :, mine], local.at[6 + 2 * s + h]
            )
            copy.start()
            kept.append(copy)
        if s == 0:
            sums[1].cross()
            sums[2].cross()
            sums[0].relay()

    sums[1].relay()
    sums[2].relay()
    for chip_sum, out in zip(sums, (in_sum, out_sum, o_sum)):
        chip_sum.total(out)
    for copy in kept + leaving:
        copy.wait()


def attention_back(context_grad, qkv, saved, ids, cosine, sine, n, nf):
    _, seqs, spots, block, cols = qkv.shape
    length = spots * block
    tokens, units = saved[0].shape
    width = saved[2].shape[1]
    chips = nf // 2
    shapes = [(width // nf, units), (units // nf, width), (width // nf, width)]
    copies = seqs * 4 * (n - 1) + 3 * ChipSum.count(nf)
    vmem = pl.BlockSpec(memory_space=pltpu.VMEM)
    hbm = pl.BlockSpec(memory_space=pltpu.HBM)
    scratch = []
    for rows, wide in shapes:
        scratch.append(pltpu.VMEM((chips, 2, rows, wide), BF16))
        scratch += chip_scratch(nf, rows, wide)[1:]
    grads, *owned = pl.pallas_call(
        functools.partial(back_kernel, n, nf),
        in_specs=[hbm] * 8 + [vmem] * 3,
        out_specs=[hbm, vmem, vmem, vmem],
        out_shape=[jax.ShapeDtypeStruct((3, seqs, 2, block, width), BF16)]
        + [jax.ShapeDtypeStruct(shape, BF16) for shape in shapes],
        scratch_shapes=[
            pltpu.VMEM((3, seqs, spots, block, cols), BF16),
            pltpu.VMEM((seqs, spots, block, cols), BF16),
            pltpu.VMEM((3, seqs, spots, block, cols), BF16),
            pltpu.VMEM((length, LANES), F32),
            pltpu.VMEM((length, LANES), F32),
            *scratch,
            *[pltpu.VMEM((tokens, width), BF16)] * 4,
            pltpu.VMEM((2, tokens, 512), BF16),
            pltpu.VMEM((2, tokens, units // chips), BF16),
            pltpu.VMEM((seqs, 1, length), F32),
            pltpu.VMEM((seqs, length, 8), F32),
            pltpu.SemaphoreType.DMA((4,)),
            pltpu.SemaphoreType.DMA((copies,)),
            pltpu.SemaphoreType.DMA((copies,)),
            pltpu.SemaphoreType.DMA((7 + 2 * seqs,)),
        ],
        compiler_params=params(62, collective_id=2, has_side_effects=True),
        name="attention_back",
    )(
        context_grad.reshape(n, seqs, 2, block, cols),
        qkv,
        *saved,
        ids,
        cosine,
        sine,
    )
    return grads.reshape(3, seqs * 2 * block, width), owned


def norm_back_tile(hats, scales, ng, st, e, mg, mg_ref, g_ref, h, low, dgain, dbias, selector, t, strip=16):
    count, tile, width = e.shape
    inv = 1.0 / width
    to = slice(t * tile, (t + 1) * tile)
    for s in range(3):
        dy = ng[s]
        hat = hats[s, to].astype(F32)
        scale = scales[to, s : s + 1]
        dgain[s : s + 1] += jnp.sum(dy * hat, axis=0, keepdims=True)
        dbias[s : s + 1] += jnp.sum(dy, axis=0, keepdims=True)
        dh = dy * g_ref[s : s + 1]
        mean = jnp.sum(dh, axis=-1, keepdims=True) * inv
        along = jnp.sum(dh * hat, axis=-1, keepdims=True) * inv
        out = (scale * (dh - mean - hat * along)).astype(BF16)
        low[s, to] = out
        st[s] = out
    st[3] = h[to].astype(BF16)

    shape = (4 * strip, count * strip)
    same = lax.rem(lax.broadcasted_iota(jnp.int32, shape, 0), strip) == lax.rem(
        lax.broadcasted_iota(jnp.int32, shape, 1), strip
    )
    for i in range(tile // strip):
        rows = slice(i * strip, (i + 1) * strip)
        grads = st[:, rows].reshape(4 * strip, width)
        inputs = e[:, rows].reshape(count * strip, width)
        products = jnp.where(same, dot(grads, inputs, NT), 0.0)
        wide = jnp.concatenate(
            [products[s * strip : (s + 1) * strip] for s in range(4)], axis=1
        )
        high, rest = halves(wide)
        mg[rows] = dot(high, selector[...]) + dot(rest, selector[...])
    turned_mg = mg[...].T
    block = mg_ref.shape[4]
    per = tile // block
    for i in range(per):
        place = t * per + i
        for a in range(4):
            mg_ref[a, :, place // 2, place % 2, :] = turned_mg[
                a * count : (a + 1) * count, i * block : (i + 1) * block
            ]


def small_squares(rows, cols):
    first = 8 + rows
    places = []
    for g in range(-(-rows // 8)):
        size = min(8, rows - 8 * g)
        places.append(
            (
                slice(first, first + size),
                slice(g * LANES, g * LANES + cols),
                slice(8 * g, 8 * g + size),
            )
        )
    return places


def small_line_at(rows, cols):
    groups = -(-rows // 8)
    return slice(groups * LANES, groups * LANES + cols)


def end_kernel(
    n,
    nf,
    grads_ref,
    normed_ref,
    hats_ref,
    scales_ref,
    e_ref,
    w_ref,
    h_ref,
    gain_ref,
    in_ref,
    out_ref,
    o_ref,
    sgain_ref,
    sbias_ref,
    sw1_ref,
    sw2_ref,
    smb_ref,
    low_ref,
    mg_ref,
    q_sum,
    k_sum,
    v_sum,
    in_sum,
    out_sum,
    o_sum,
    small_sum,
    grads,
    normed,
    hats,
    scales,
    w,
    h,
    e,
    ng,
    st,
    low,
    mg,
    selector,
    dgain,
    dbias,
    small_work,
    small_in,
    small_line,
    send,
    recv,
    local,
    e_sem,
    *more,
):
    f, z = lax.axis_index("fsdp"), lax.axis_index("ctx")
    core = lax.rem(f, 2)
    count, tokens, width = e_ref.shape
    tile = e.shape[2]
    tiles = tokens // tile
    remote = Remote(send, recv)
    chip_sets = [more[4 * i : 4 * i + 4] for i in range(3)]
    rest = more[12:]
    shard = chip_sets[0][1].shape[1]

    def fetch(t):
        return pltpu.make_async_copy(
            e_ref.at[:, t * tile : (t + 1) * tile], e.at[t % 2], e_sem.at[t % 2]
        )

    loads = [
        pltpu.make_async_copy(src, dst, local.at[i])
        for i, (src, dst) in enumerate(
            [
                (grads_ref, grads),
                (normed_ref, normed),
                (w_ref, w),
                (hats_ref, hats),
                (scales_ref, scales),
                (h_ref, h),
            ]
        )
    ]
    for load in loads:
        load.start()
    fetch(0).start()

    greet_all(n, nf)

    chain = Chain(remote, n)
    planned = [(in_ref, in_sum, 4), (out_ref, out_sum, 4), (o_ref, o_sum, 1)]
    planned += [
        (chip_set[3], out, 1) for chip_set, out in zip(chip_sets, (q_sum, k_sum, v_sum))
    ]
    for work, out, count_of in planned:
        size = work.shape[0] // count_of
        for i in range(count_of):
            at = pl.ds(i * size, size)
            chain.add(work.at[at], out.at[at], *rest[:3])
            rest = rest[3:]
    chain.start()
    chain.start()

    loads[0].wait()
    loads[1].wait()
    cut = 256
    per = cut // (2 * shard)
    sums = []
    for i in range(3):
        terms, got, part, own = chip_sets[i]
        for c in range(width // cut):
            value = dot(normed[i, :, c * cut : (c + 1) * cut], grads[i], TN).astype(BF16)
            terms[c * per : (c + 1) * per] = value.reshape(per, 2, shard, width)
        chip_sum = ChipSum(remote, nf, terms, terms.at[:, core], got, part)
        chip_sum.cores()
        sums.append(chip_sum)
    dgain[...] = jnp.zeros_like(dgain)
    dbias[...] = jnp.zeros_like(dbias)
    size = selector.shape
    group = lax.broadcasted_iota(jnp.int32, size, 0) // 16
    selector[...] = jnp.where(
        group == lax.broadcasted_iota(jnp.int32, size, 1), 1.0, 0.0
    ).astype(BF16)
    for load in loads[2:]:
        load.wait()

    def do_tile(t):
        fetch(t).wait()
        if t + 1 < tiles:
            fetch(t + 1).start()
        rows = slice(t * tile, (t + 1) * tile)
        for i in range(3):
            ng[i] = dot(grads[i, rows], w[:, i * width : (i + 1) * width], NT)
        norm_back_tile(
            hats, scales, ng, st, e.at[t % 2], mg, mg_ref, gain_ref, h, low, dgain, dbias, selector, t
        )

    todo = list(range(tiles))

    def some():
        if todo:
            do_tile(todo.pop(0))

    chain.step(0)
    for chip_sum in sums:
        chip_sum.cross()
    chain.step(1)
    some()
    chain.step(2)
    some()
    chain.step(3)
    chain.step(4)
    for chip_sum in sums:
        chip_sum.relay()
    some()
    chain.step(5)
    while todo:
        some()
    keep = pltpu.make_async_copy(low, low_ref, local.at[6])
    keep.start()
    for chip_sum, chip_set in zip(sums, chip_sets):
        chip_sum.total(chip_set[3])
    chain.step(6)

    thin = small_in.shape[1]
    hidden_count, coef_count = sw2_ref.shape
    first = 8 + hidden_count
    squares = small_squares(hidden_count, coef_count)
    line_at = small_line_at(hidden_count, coef_count)
    small_work[...] = jnp.zeros_like(small_work)
    small_work[0:3] = dgain[...]
    small_work[3:4] = sgain_ref[...]
    small_work[4:7] = dbias[...]
    small_work[7:8] = sbias_ref[...]
    small_work[8:first] = sw1_ref[...]
    for rows, lanes, which in squares:
        small_work[rows, lanes] = sw2_ref[which]
    small_work[first : first + 1, line_at] = smb_ref[...]
    here = pl.ds(pl.multiple_of(f * thin, thin), thin)
    small_in[0] = small_work[here]
    slices = []
    for k in range(1, nf):
        to = lax.rem(f + k, nf)
        slices.append(
            remote.start(
                small_work.at[pl.ds(pl.multiple_of(to * thin, thin), thin)],
                small_in.at[k],
                {"fsdp": to},
            )
        )

    chain.step(7)
    for copy in slices:
        copy.wait()
    total = small_in[0]
    for k in range(1, nf):
        total = total + small_in[k]
    small_line[z] = total
    across = []
    for k in range(1, n):
        across.append(
            remote.start(small_line.at[z], small_line.at[z], {"ctx": lax.rem(z + k, n)})
        )
    chain.step(8)
    chain.step(9)
    for copy in across:
        copy.wait()
    total = small_line[0]
    for k in range(1, n):
        total = total + small_line[k]
    small_sum[here] = total
    spread = []
    for k in range(1, nf):
        spread.append(
            remote.start(small_sum.at[here], small_sum.at[here], {"fsdp": lax.rem(f + k, nf)})
        )
    chain.step(10)
    chain.step(11)
    chain.leave(11)
    for copy in spread:
        copy.wait()
    for c in range(12):
        chain.end(c)
    keep.wait()


def finish(grads, normed, hats, scales, e, w, hgrad, gain, owned, small, mix_shape, n, nf):
    count, tokens, width = e.shape
    tile = 128
    chips = nf // 2
    shard = width // nf
    rows = 8 + small[2].shape[0] + 8
    thin = 8 * -(-rows // (8 * nf))
    m_in, m_out, m_o = owned
    lines, chip_sums = [], []
    for x, count_of in ((m_in, 4), (m_out, 4), (m_o, 1)):
        for _ in range(count_of):
            lines += chain_scratch(n, x.shape[0] // count_of, x.shape[1])
    for _ in range(3):
        lines += chain_scratch(n, shard, width)
        chip_sums += [
            pltpu.VMEM((chips, 2, shard, width), BF16),
            *chip_scratch(nf, shard, width)[1:],
            pltpu.VMEM((shard, width), BF16),
        ]
    copies = 12 * (Chain.levels(n) + 2) + 3 * ChipSum.count(nf) + 2 * (nf - 1) + (n - 1)
    vmem = pl.BlockSpec(memory_space=pltpu.VMEM)
    hbm = pl.BlockSpec(memory_space=pltpu.HBM)
    wide = jax.ShapeDtypeStruct((shard, width), BF16)
    return pl.pallas_call(
        functools.partial(end_kernel, n, nf),
        in_specs=[hbm] * 7 + [vmem] * 9,
        out_specs=[hbm] + [vmem] * 8,
        out_shape=[
            jax.ShapeDtypeStruct((3, tokens, width), BF16),
            jax.ShapeDtypeStruct(mix_shape, F32),
            wide,
            wide,
            wide,
            *[jax.ShapeDtypeStruct(x.shape, BF16) for x in owned],
            jax.ShapeDtypeStruct((nf * thin, width), F32),
        ],
        scratch_shapes=[
            pltpu.VMEM(grads.shape, BF16),
            pltpu.VMEM(normed.shape, BF16),
            pltpu.VMEM(hats.shape, BF16),
            pltpu.VMEM(scales.shape, F32),
            pltpu.VMEM(w.shape, BF16),
            pltpu.VMEM(hgrad.shape, F32),
            pltpu.VMEM((2, count, tile, width), BF16),
            pltpu.VMEM((3, tile, width), F32),
            pltpu.VMEM((4, tile, width), BF16),
            pltpu.VMEM((3, tokens, width), BF16),
            pltpu.VMEM((tile, LANES), F32),
            pltpu.VMEM((4 * count * 16, LANES), BF16),
            pltpu.VMEM((3, width), F32),
            pltpu.VMEM((3, width), F32),
            pltpu.VMEM((nf * thin, width), F32),
            pltpu.VMEM((nf, thin, width), F32),
            pltpu.VMEM((n, thin, width), F32),
            pltpu.SemaphoreType.DMA((copies,)),
            pltpu.SemaphoreType.DMA((copies,)),
            pltpu.SemaphoreType.DMA((7,)),
            pltpu.SemaphoreType.DMA((2,)),
            *chip_sums,
            *lines,
        ],
        compiler_params=params(60, collective_id=3, has_side_effects=True),
        name="finish",
    )(grads, normed, hats, scales, e, w, hgrad, gain, *owned, *small)


def tail_kernel(
    low_ref,
    h_ref,
    mix_ref,
    q_ref,
    k_ref,
    v_ref,
    in_ref,
    out_ref,
    o_ref,
    small_ref,
    mg_ref,
    eg_ref,
    qkv_ref,
    in32_ref,
    out32_ref,
    o32_ref,
    gain_ref,
    bias_ref,
    w1_ref,
    w2_ref,
    mb_ref,
    mg_out_ref,
    mixes,
    *,
    strip,
):
    count, tile, width = eg_ref.shape
    chunk = 256
    block = mix_ref.shape[4]
    tiles = mix_ref.shape[2] * 2 * block // tile
    step = pl.program_id(0)
    for t in range(tiles):

        @pl.when(step == t)
        def _():
            mix_columns(mix_ref, mixes, t)

    @pl.when(step == 0)
    def _():
        hidden_count, coef_count = w2_ref.shape
        first = 8 + hidden_count
        gain_ref[...] = small_ref[0:4]
        bias_ref[...] = small_ref[4:8]
        w1_ref[...] = small_ref[8:first]
        for rows, lanes, which in small_squares(hidden_count, coef_count):
            w2_ref[which] = small_ref[rows, lanes]
        mb_ref[...] = small_ref[first : first + 1, small_line_at(hidden_count, coef_count)]
        mg_out_ref[...] = mg_ref[...]

    for i, ref in enumerate((q_ref, k_ref, v_ref)):
        qkv_ref[:, i * width : (i + 1) * width] = ref[...].astype(F32)
    in32_ref[...] = in_ref[...].astype(F32)
    out32_ref[...] = out_ref[...].astype(F32)
    o32_ref[...] = o_ref[...].astype(F32)

    @pl.loop(0, tile // strip)
    def _(i):
        rows = pl.ds(pl.multiple_of(i * strip, strip), strip)
        mix = mixes[rows]
        for c in range(width // chunk):
            cols = slice(c * chunk, (c + 1) * chunk)
            grads = [low_ref[s, rows, cols].astype(F32) for s in range(3)]
            grads.append(h_ref[rows, cols])
            for j in range(count):
                total = grads[0] * mix[:, j : j + 1]
                for s in range(1, 4):
                    total = total + grads[s] * mix[:, s * count + j : s * count + j + 1]
                eg_ref[j, rows, cols] = total.astype(BF16)


def spread_back(low, hgrad, mix, sums, small, m_grad, sizes):
    _, tokens, width = low.shape
    count = mix.shape[1]
    tile = 128
    tiles = tokens // tile
    hidden_count, coef_count = sizes

    def part(x):
        return pl.BlockSpec((x.shape[0] // tiles, x.shape[1]), lambda i: (i, 0))

    def whole(x):
        zeros = (0,) * len(x.shape)
        return once(x.shape, lambda i: zeros)

    shard = sums[0].shape[0]
    outs = [
        jax.ShapeDtypeStruct((count, tokens, width), BF16),
        jax.ShapeDtypeStruct((shard, 3 * width), F32),
        *[jax.ShapeDtypeStruct(x.shape, F32) for x in sums[3:]],
        jax.ShapeDtypeStruct((4, width), F32),
        jax.ShapeDtypeStruct((4, width), F32),
        jax.ShapeDtypeStruct((hidden_count, width), F32),
        jax.ShapeDtypeStruct((hidden_count, coef_count), F32),
        jax.ShapeDtypeStruct((1, coef_count), F32),
        jax.ShapeDtypeStruct(m_grad.shape, F32),
    ]
    return pl.pallas_call(
        functools.partial(tail_kernel, strip=32),
        grid=(tiles,),
        in_specs=[
            pl.BlockSpec((3, tile, width), lambda i: (0, i, 0)),
            pl.BlockSpec((tile, width), lambda i: (i, 0)),
            whole(mix),
            *[part(x) for x in sums],
            whole(small),
            whole(m_grad),
        ],
        out_specs=[pl.BlockSpec((count, tile, width), lambda i: (0, i, 0))]
        + [part(x) for x in outs[1:5]]
        + [whole(x) for x in outs[5:]],
        out_shape=outs,
        scratch_shapes=[pltpu.VMEM((tile, 4 * count), F32)],
        compiler_params=params(60),
        cost_estimate=pl.CostEstimate(
            flops=64 * tokens * width, bytes_accessed=40 * tokens * width, transcendentals=0
        ),
        name="spread_back",
    )(low, hgrad, mix, *sums, small, m_grad)


def body(
    earlier,
    mix_in,
    segment_ids,
    attn_qkv,
    attn_out,
    mlp_in,
    mlp_out,
    norm_gain,
    norm_bias,
    mix_w1,
    mix_w2,
    mix_bias,
    out_grad,
    coef_grad,
):
    count, seqs, _, block, width = earlier.shape
    n = lax.axis_size("ctx")
    tokens = seqs * 2 * block
    length = 2 * n * block
    me = lax.axis_index("ctx")

    nf = lax.axis_size("fsdp")
    e = earlier.reshape(count, tokens, width)
    cosine, sine = (jnp.asarray(table) for table in turn_tables(length))
    normed, hats, scales, residual, w_qkv, w_o, w_in, w_out, qkv, context = forward(
        e,
        mix_in,
        attn_qkv,
        attn_out,
        mlp_in,
        mlp_out,
        norm_gain,
        norm_bias,
        cosine,
        sine,
        segment_ids,
        n,
        nf,
    )
    (
        layer_out,
        coefs,
        active,
        lowered,
        normed_mlp,
        branch,
        attention_grad,
        context_grad,
        hidden_grad,
        d_gain,
        d_bias,
        d_w1,
        d_w2,
        d_mb,
    ) = feed(
        residual,
        context,
        w_o,
        w_in,
        w_out,
        norm_gain,
        norm_bias,
        mix_w1,
        mix_w2,
        mix_bias[None, :],
        out_grad.reshape(tokens, width),
        coef_grad,
        n,
    )
    saved = (active, lowered, normed_mlp, branch, context, attention_grad)
    grads, owned = attention_back(
        context_grad, qkv, saved, segment_ids, cosine, sine, n, nf
    )
    low, m_grad, *sums, small = finish(
        grads,
        normed,
        hats,
        scales,
        e,
        w_qkv,
        hidden_grad,
        norm_gain,
        owned,
        (d_gain, d_bias, d_w1, d_w2, d_mb),
        mix_in.shape,
        n,
        nf,
    )
    e_grad, g_qkv, g_in, g_out, g_o, gain_sum, bias_sum, w1_sum, w2_sum, mb_sum, m_grad = (
        spread_back(low, hidden_grad, mix_in, sums, small, m_grad, mix_w2.shape)
    )
    return (
        layer_out.reshape(seqs, 2, block, width),
        coefs,
        e_grad.reshape(count, seqs, 2, block, width),
        m_grad,
        g_qkv,
        g_o,
        g_in,
        g_out,
        gain_sum,
        bias_sum,
        w1_sum,
        w2_sum,
        mb_sum[0],
    )


def solution(mesh):
    in_specs = (
        P(None, "fsdp", None, "ctx", None),
        P(None, None, "fsdp", None, "ctx"),
        P("fsdp", None, None),
        P("fsdp", None),
        P("fsdp", None),
        P("fsdp", None),
        P("fsdp", None),
        P(),
        P(),
        P(),
        P(),
        P(),
        P("fsdp", None, "ctx", None),
        P(None, None, "fsdp", None, "ctx"),
    )
    out_specs = (
        P("fsdp", None, "ctx", None),
        P(None, None, "fsdp", None, "ctx"),
        P(None, "fsdp", None, "ctx", None),
        P(None, None, "fsdp", None, "ctx"),
        P("fsdp", None),
        P("fsdp", None),
        P("fsdp", None),
        P("fsdp", None),
        P(),
        P(),
        P(),
        P(),
        P(),
    )
    return jax.shard_map(body, mesh=mesh, in_specs=in_specs, out_specs=out_specs, check_vma=False)
```

```python
import functools
import math

import jax
import jax.numpy as jnp
import numpy as np
from jax import lax
from jax.experimental import pallas as pl
from jax.experimental.pallas import tpu as pltpu
from jax.sharding import PartitionSpec as P

HD = 64
ROT = 16
LANES = 128
EPSILON = 1e-05
RMS_EPSILON = 1e-06
MASKED = -1e30
F32 = jnp.float32
BF16 = jnp.bfloat16
MESH = pl.DeviceIdType.MESH
MIB = 1024 * 1024

NN = (((1,), (0,)), ((), ()))
NT = (((1,), (1,)), ((), ()))
TN = (((0,), (0,)), ((), ()))

ERFC_RATE = 0.4
ERFC = (
    0.22567586600780487,
    0.22566929459571838,
    0.20784726738929749,
    0.16851142048835754,
    0.1415392905473709,
    -0.005822250619530678,
    0.16932761669158936,
    -0.18304575979709625,
    0.05029737576842308,
)


def dot(a, b, dims=NN):
    return lax.dot_general(a, b, dims, preferred_element_type=F32)


def gelu_and_slope(v):
    bell = jnp.exp(-0.5 * (v * v))
    t = 1.0 / (1.0 + (ERFC_RATE * math.sqrt(0.5)) * jnp.abs(v))
    poly = 0.5 * ERFC[-1] * t + 0.5 * ERFC[-2]
    for coefficient in ERFC[-3::-1]:
        poly = poly * t + 0.5 * coefficient
    tail = poly * t * bell
    phi = jnp.where(v >= 0.0, 1.0 - tail, tail)
    return v * phi, phi + v * bell * (1.0 / math.sqrt(2.0 * math.pi))


def halves(x):
    high = x.astype(BF16)
    return high, (x - high.astype(F32)).astype(BF16)


def params(limit_mib, **more):
    return pltpu.CompilerParams(vmem_limit_bytes=limit_mib * MIB, **more)


def once(shape, index):
    return pl.BlockSpec(shape, index, pipeline_mode=pl.Buffered(1))


def turn_tables(length):
    half = ROT // 2
    frequency = 10000.0 ** (-(np.arange(half) * 2.0 / ROT))
    angle = np.arange(length)[:, None] * frequency[None, :]
    lane = np.arange(LANES) % HD
    cosine = np.ones((length, LANES), np.float32)
    sine = np.zeros((length, LANES), np.float32)
    for k in range(LANES):
        if lane[k] < ROT:
            cosine[:, k] = np.cos(angle[:, lane[k] % half])
            sign = -1.0 if lane[k] < half else 1.0
            sine[:, k] = sign * np.sin(angle[:, lane[k] % half])
    return cosine, sine


def turned(x, cosine, sine):
    half = ROT // 2
    lane = lax.broadcasted_iota(jnp.int32, x.shape, 1) % HD
    other = jnp.where(
        lane < half, pltpu.roll(x, LANES - half, axis=1), pltpu.roll(x, half, axis=1)
    )
    return x * cosine + other * sine


def row_tile(length):
    return min(256, length)


def head_lanes(shape, h):
    lane = lax.broadcasted_iota(jnp.int32, shape, 1)
    return (lane >= h * HD) & (lane < (h + 1) * HD)


def only(x, h):
    return jnp.where(head_lanes(x.shape, h), x, jnp.zeros_like(x))


def coefficient_places(ref):
    outer, inner, seqs, _, block = ref.shape
    for a in range(outer):
        for seq in range(seqs):
            for h in range(2):
                first = (2 * seq + h) * block
                yield a, seq, h, slice(a * inner, (a + 1) * inner), slice(first, first + block)


def feed_kernel(
    res_ref,
    ctx_ref,
    wo_ref,
    win_ref,
    wout_ref,
    g_ref,
    b_ref,
    w1_ref,
    w2_ref,
    mb_ref,
    og_ref,
    cg_ref,
    out_ref,
    coef_ref,
    active,
    lowered,
    normed,
    branch,
    attention,
    cgrad_ref,
    hgrad_ref,
    dgain_ref,
    dbias_ref,
    dw1_ref,
    dw2_ref,
    dmb_ref,
    hidden,
    total,
    slope,
    r_high,
    r_rest,
    cotangent,
    *,
    tiles,
    strip,
):
    step = pl.program_id(0)
    tokens, width = res_ref.shape
    cut = win_ref.shape[1]
    inv = 1.0 / width

    @pl.when(step == 0)
    def _():
        hidden[...] = dot(ctx_ref[...], wo_ref[...])

        @pl.loop(0, tokens // strip)
        def _(i):
            rows = pl.ds(pl.multiple_of(i * strip, strip), strip)
            v = hidden[rows] + res_ref[rows]
            hidden[rows] = v
            center = v - jnp.sum(v, axis=-1, keepdims=True) * inv
            spread = jnp.sum(center * center, axis=-1, keepdims=True) * inv
            hat = center * lax.rsqrt(spread + EPSILON)
            normed[rows] = (hat * g_ref[3:4] + b_ref[3:4]).astype(BF16)
            total[rows] = v

    @pl.when(step < tiles)
    def _():
        half = tokens // 2
        parts = [slice(i * half, (i + 1) * half) for i in range(2)]
        ups = [dot(normed[rows], win_ref[...]) for rows in parts]
        for rows, up in zip(parts, ups):
            value, rate = gelu_and_slope(up)
            low = value.astype(BF16)
            active[rows] = low
            slope[step, rows] = rate
            total[rows] += dot(low, wout_ref[...])

    @pl.when(step == tiles - 1)
    def _():
        w1 = w1_ref[...]
        w2 = w2_ref[...]

        @pl.loop(0, tokens // strip)
        def _(i):
            rows = pl.ds(pl.multiple_of(i * strip, strip), strip)
            v = total[rows]
            out_ref[rows] = v.astype(BF16)
            scale = lax.rsqrt(jnp.sum(v * v, axis=-1, keepdims=True) * inv + RMS_EPSILON)
            r = v * scale
            high = r.astype(BF16)
            r_high[rows] = high
            r_rest[rows] = (r - high.astype(F32)).astype(BF16)

        high, rest = r_high[...], r_rest[...]
        for a, seq, h, rows, cols in coefficient_places(cg_ref):
            cotangent[rows, cols] = cg_ref[a, :, seq, h, :]
        z = dot(w1, high, NT) + dot(w1, rest, NT)
        value, rate = gelu_and_slope(z)
        v_high, v_rest = halves(value)
        ones = jnp.ones((1, tokens), BF16)
        mb_high, mb_rest = halves(mb_ref[...])
        mb_last = (mb_ref[...] - mb_high.astype(F32) - mb_rest.astype(F32)).astype(BF16)
        shift = dot(mb_high, ones, TN) + dot(mb_rest, ones, TN) + dot(mb_last, ones, TN)
        coefs = dot(w2, v_high, TN) + dot(w2, v_rest, TN) + shift
        for a, seq, h, rows, cols in coefficient_places(coef_ref):
            coef_ref[a, :, seq, h, :] = coefs[rows, cols]
        c_high, c_rest = halves(cotangent[...])
        dmb_ref[...] = dot(ones, c_high, NT) + dot(ones, c_rest, NT)
        dw2_ref[...] = dot(v_high, c_high, NT) + dot(v_rest, c_high, NT) + dot(v_high, c_rest, NT)
        z_high, z_rest = halves((dot(w2, c_high) + dot(w2, c_rest)) * rate)
        dw1_ref[...] = dot(z_high, high) + dot(z_high, rest) + dot(z_rest, high)
        hgrad_ref[...] = dot(z_high, w1, TN) + dot(z_rest, w1, TN)

        @pl.loop(0, tokens // strip)
        def _(i):
            rows = pl.ds(pl.multiple_of(i * strip, strip), strip)
            v = total[rows]
            scale = lax.rsqrt(jnp.sum(v * v, axis=-1, keepdims=True) * inv + RMS_EPSILON)
            dr = hgrad_ref[rows]
            r = v * scale
            mean = jnp.sum(dr * r, axis=-1, keepdims=True) * inv
            grad = scale * (dr - r * mean) + og_ref[rows].astype(F32)
            hgrad_ref[rows] = grad
            branch[rows] = grad.astype(BF16)
            total[rows] = jnp.zeros_like(v)

    @pl.when(step >= tiles)
    def _():
        j = step - tiles
        low = (dot(branch[...], wout_ref[...], NT) * slope[j]).astype(BF16)
        lowered[...] = low
        total[...] += dot(low, win_ref[...], NT)

    @pl.when(step == 2 * tiles - 1)
    def _():
        dgain_ref[...] = jnp.zeros_like(dgain_ref)
        dbias_ref[...] = jnp.zeros_like(dbias_ref)

        @pl.loop(0, tokens // strip)
        def _(i):
            rows = pl.ds(pl.multiple_of(i * strip, strip), strip)
            v = hidden[rows]
            dy = total[rows]
            center = v - jnp.sum(v, axis=-1, keepdims=True) * inv
            spread = jnp.sum(center * center, axis=-1, keepdims=True) * inv
            scale = lax.rsqrt(spread + EPSILON)
            hat = center * scale
            dgain_ref[...] += jnp.sum(dy * hat, axis=0, keepdims=True)
            dbias_ref[...] += jnp.sum(dy, axis=0, keepdims=True)
            dh = dy * g_ref[3:4]
            first = jnp.sum(dh, axis=-1, keepdims=True) * inv
            second = jnp.sum(dh * hat, axis=-1, keepdims=True) * inv
            grad = hgrad_ref[rows] + scale * (dh - first - hat * second)
            hgrad_ref[rows] = grad
            attention[rows] = grad.astype(BF16)

        groups, _, group = cgrad_ref.shape
        back = dot(attention[...], wo_ref[...], NT).astype(BF16)
        for i in range(groups):
            cgrad_ref[i] = back[:, i * group : (i + 1) * group]


def feed(res, ctx, wo, win, wout, gain, bias, w1, w2, mb, og, cg, groups):
    tokens, width = res.shape
    hidden_units = win.shape[1]
    cut = 1024
    tiles = hidden_units // cut
    small, coefs = w1.shape[0], w2.shape[1]

    def whole(x):
        zeros = (0,) * x.ndim
        return once(x.shape, lambda i: zeros)

    def result(shape, dtype=F32):
        zeros = (0,) * len(shape)
        return once(shape, lambda i: zeros), jax.ShapeDtypeStruct(shape, dtype)

    def back(i):
        return jnp.maximum(i - tiles, 0)

    outs = [
        result((tokens, width), BF16),
        result(cg.shape),
        (
            pl.BlockSpec((tokens, cut), lambda i: (0, jnp.minimum(i, tiles - 1))),
            jax.ShapeDtypeStruct((tokens, hidden_units), BF16),
        ),
        (
            pl.BlockSpec((tokens, cut), lambda i: (0, back(i))),
            jax.ShapeDtypeStruct((tokens, hidden_units), BF16),
        ),
        result((tokens, width), BF16),
        result((tokens, width), BF16),
        result((tokens, width), BF16),
        result((groups, tokens, width // groups), BF16),
        result((tokens, width)),
        result((1, width)),
        result((1, width)),
        result((small, width)),
        result((small, coefs)),
        result((1, coefs)),
    ]
    return pl.pallas_call(
        functools.partial(feed_kernel, tiles=tiles, strip=min(512, tokens)),
        grid=(2 * tiles,),
        in_specs=[
            whole(res),
            whole(ctx),
            whole(wo),
            pl.BlockSpec((width, cut), lambda i: (0, lax.rem(i, tiles))),
            pl.BlockSpec((cut, width), lambda i: (lax.rem(i, tiles), 0)),
            whole(gain),
            whole(bias),
            whole(w1),
            whole(w2),
            whole(mb),
            whole(og),
            whole(cg),
        ],
        out_specs=[spec for spec, _ in outs],
        out_shape=[shape for _, shape in outs],
        scratch_shapes=[
            pltpu.VMEM((tokens, width), F32),
            pltpu.VMEM((tokens, width), F32),
            pltpu.VMEM((tiles, tokens, cut), F32),
            pltpu.VMEM((tokens, width), BF16),
            pltpu.VMEM((tokens, width), BF16),
            pltpu.VMEM((coefs, tokens), F32),
        ],
        compiler_params=params(58),
        cost_estimate=pl.CostEstimate(
            flops=8 * tokens * width * hidden_units + 4 * tokens * width * width,
            bytes_accessed=8 * width * hidden_units + 4 * width * width + 20 * tokens * width,
            transcendentals=2 * tokens * hidden_units,
        ),
        name="feed",
    )(res, ctx, wo, win, wout, gain, bias, w1, w2, mb, og, cg)


def flipped(v, mask):
    bit = 1
    while bit <= mask:
        if mask & bit:
            v = v + bit - 2 * bit * lax.rem(v // bit, 2)
        bit *= 2
    return v


def added(out_ref, refs, rows, strip=32):
    strip = math.gcd(strip, rows)

    @pl.loop(0, rows // strip)
    def _(i):
        at = pl.ds(pl.multiple_of(i * strip, strip), strip)
        total = refs[0][at].astype(F32)
        for ref in refs[1:]:
            total = total + ref[at].astype(F32)
        out_ref[at] = total.astype(out_ref.dtype)


class Remote:
    def __init__(self, send, recv):
        self.send, self.recv, self.used = send, recv, 0

    def start(self, src, dst, where):
        copy = self.make(src, dst, where)
        copy.start()
        return copy

    def make(self, src, dst, where):
        copy = pltpu.make_async_remote_copy(
            src_ref=src,
            dst_ref=dst,
            send_sem=self.send.at[self.used],
            recv_sem=self.recv.at[self.used],
            device_id=where,
            device_id_type=MESH,
        )
        self.used += 1
        return copy


class Chain:
    def __init__(self, remote, n):
        self.remote, self.n = remote, n
        self.me = lax.axis_index("ctx")
        place = lax.rem(self.me, 4)
        self.outer = jnp.logical_or(place == 0, place == 3)
        self.inner = jnp.logical_not(self.outer)
        self.pieces = []
        self.started = 0

    def add(self, work, out, land, own, crosses):
        there = {"ctx": flipped(self.me, 1)}
        up = self.remote.make(work, land, there)
        masks = [3]
        bit = 4
        while bit < self.n:
            masks.append(bit)
            bit *= 2
        across = [
            self.remote.make(own.at[i], crosses.at[i], {"ctx": flipped(self.me, mask)})
            for i, mask in enumerate(masks)
        ]
        down = self.remote.make(out, out, there)
        self.pieces.append((work, out, land, own, crosses, up, across, down))

    def start(self):
        if self.started < len(self.pieces):
            up = self.pieces[self.started][5]

            @pl.when(self.outer)
            def _():
                up.start()

        self.started += 1

    def step(self, c):
        work, _, land, own, _, up, across, _ = self.pieces[c]

        @pl.when(self.outer)
        def _():
            up.wait_send()

        self.start()

        @pl.when(self.inner)
        def _():
            up.wait_recv()
            added(own.at[0], [work, land], work.shape[0])
            across[0].start()

        if c >= 1:
            self.leave(c - 1)

    def leave(self, c):
        _, out, _, own, crosses, _, across, down = self.pieces[c]

        @pl.when(self.inner)
        def _():
            for i, copy in enumerate(across):
                copy.wait()
                last = i + 1 == len(across)
                to = out if last else own.at[i + 1]
                added(to, [own.at[i], crosses.at[i]], out.shape[0])
                if not last:
                    across[i + 1].start()
            down.start()

    def end(self, c):
        down = self.pieces[c][7]

        @pl.when(self.outer)
        def _():
            down.wait_recv()

        @pl.when(self.inner)
        def _():
            down.wait_send()

    @staticmethod
    def levels(n):
        return max(1, n.bit_length() - 2)


def piece_sizes(heights):
    return [[h // 4] * 4 for h in heights[:2]] + [[h] for h in heights[2:]]


def chain_scratch(n, rows, cols):
    levels = Chain.levels(n)
    return [
        pltpu.VMEM((rows, cols), BF16),
        pltpu.VMEM((levels, rows, cols), BF16),
        pltpu.VMEM((levels, rows, cols), BF16),
    ]


class ChipSum:
    def __init__(self, remote, nf, terms, keep, got, part):
        self.remote, self.nf, self.terms = remote, nf, terms
        self.keep, self.got, self.part = keep, got, part
        self.f = lax.axis_index("fsdp")
        self.chip, self.core = self.f // 2, lax.rem(self.f, 2)
        self.rows = got.shape[1]
        self.half = self.rows // 2
        bits = []
        bit = 1
        while bit < nf // 2:
            bits.append(bit)
            bit *= 2
        self.orders = (bits, bits[::-1])
        self.level = len(bits) - 1
        self.slots = 0

    def cores(self):
        self.copy = self.remote.start(
            self.terms.at[:, 1 - self.core], self.got, {"fsdp": flipped(self.f, 1)}
        )

    def masks(self, which, level):
        found = [0]
        for bit in self.orders[which][:level]:
            found += [mask + bit for mask in found]
        return found

    def piece(self, which, chip):
        return self.got.at[chip, pl.ds(which * self.half, self.half)]

    def launch(self):
        self.flying = []
        for which in range(2):
            bit = self.orders[which][self.level]
            to = 2 * flipped(self.chip, bit) + self.core
            for mask in self.masks(which, self.level):
                landing = self.part.at[self.slots]
                self.slots += 1
                copy = self.remote.start(
                    self.piece(which, flipped(self.chip, mask + bit)), landing, {"fsdp": to}
                )
                self.flying.append((copy, which, mask, landing))

    def cross(self):
        self.copy.wait()
        for k in range(self.nf // 2):
            added(self.got.at[k], [self.keep.at[k], self.got.at[k]], self.rows)
        self.launch()

    def relay(self):
        while self.level > 0:
            for copy, which, mask, landing in self.flying:
                copy.wait()
                here = self.piece(which, flipped(self.chip, mask))
                added(here, [here, landing], self.half)
            self.level -= 1
            self.launch()

    def total(self, out):
        for copy, which, _, landing in self.flying:
            copy.wait()
            added(
                out.at[pl.ds(which * self.half, self.half)],
                [self.piece(which, self.chip), landing],
                self.half,
            )

    @staticmethod
    def count(nf):
        return 1 + 2 * (nf // 2 - 1)


def chip_scratch(nf, rows, cols):
    chips = nf // 2
    return [
        pltpu.VMEM((chips, rows, cols), BF16),
        pltpu.VMEM((chips, rows, cols), BF16),
        pltpu.VMEM((2 * chips - 2, rows // 2, cols), BF16),
    ]


def greet_all(n, nf):
    z, f = lax.axis_index("ctx"), lax.axis_index("fsdp")
    barrier = pltpu.get_barrier_semaphore()
    for k in range(1, nf):
        pl.semaphore_signal(
            barrier, inc=1, device_id={"fsdp": lax.rem(f + k, nf)}, device_id_type=MESH
        )
    for k in range(1, n):
        pl.semaphore_signal(
            barrier, inc=1, device_id={"ctx": lax.rem(z + k, n)}, device_id_type=MESH
        )
    pl.semaphore_wait(barrier, nf + n - 2)


def place_segments(ids_ref, row, column, block):
    seqs, _, half = ids_ref.shape
    n = half // block
    for s in range(seqs):
        row[s, :, 0:half] = ids_ref[s, 0:1].astype(F32)
        for b in range(n):
            at = slice((n - 1 - b) * block, (n - b) * block)
            to = slice(half + b * block, half + (b + 1) * block)
            row[s, :, to] = ids_ref[s, 1:2, at].astype(F32)
        column[s] = jnp.broadcast_to(row[s], (8, 2 * half)).T


def mix_columns(mix_ref, mixes, t):
    block = mix_ref.shape[4]
    tile = mixes.shape[0]
    per = tile // block
    parts = []
    for i in range(t * per, (t + 1) * per):
        rows = [mix_ref[a, :, i // 2, i % 2, :] for a in range(mix_ref.shape[0])]
        parts.append(jnp.concatenate(rows, axis=0))
    mixes[...] = (parts[0] if per == 1 else jnp.concatenate(parts, axis=1)).T


class PlaneGather:
    def __init__(self, remote, nf, src, out):
        self.remote, self.nf, self.src, self.out = remote, nf, src, out
        self.f = lax.axis_index("fsdp")
        self.half = src.shape[0] // 2
        bits = []
        bit = 2
        while bit < nf:
            bits.append(bit)
            bit *= 2
        self.orders = (bits, bits[::-1])
        self.levels = len(bits)
        self.flying = {}
        self.inner = []

    def masks(self, which, level):
        found = [0]
        for bit in self.orders[which][:level]:
            found += [mask + bit for mask in found]
        return found

    def place(self, which, shard):
        return self.out.at[shard, pl.ds(which * self.half, self.half)]

    def launch(self, which, level, mask):
        shard = flipped(self.f, mask)
        here = self.src.at[pl.ds(which * self.half, self.half)]
        if mask:
            here = self.place(which, shard)
        to = flipped(self.f, self.orders[which][level])
        self.flying[which, level, mask] = self.remote.start(
            here, self.place(which, shard), {"fsdp": to}
        )

    def begin(self, sem):
        for level in range(self.levels):
            for which in range(2):
                self.launch(which, level, 0)
        self.inner.append(
            self.remote.start(self.src, self.out.at[self.f], {"fsdp": flipped(self.f, 1)})
        )
        self.own = pltpu.make_async_copy(self.src, self.out.at[self.f], sem)
        self.own.start()

    def relay(self, level):
        for which in range(2):
            order = self.orders[which]
            for mask in self.masks(which, level):
                self.flying[which, level, mask].wait()
                arrived = mask + order[level]
                for later in range(level + 1, self.levels):
                    self.launch(which, later, arrived)
                place = self.place(which, flipped(self.f, arrived))
                self.inner.append(self.remote.start(place, place, {"fsdp": flipped(self.f, 1)}))

    def end(self):
        self.own.wait()
        for copy in self.inner:
            copy.wait()

    @staticmethod
    def count(nf):
        return 2 * (nf // 2 - 1) + 2 * (nf // 2 - 1) + 1


def front_tile(e, mixes, st, g_ref, b_ref, normed, hats, scales, res, first, strip=16):
    count, tile, width = e.shape
    inv = 1.0 / width

    @pl.loop(0, tile // strip)
    def _(i):
        rows = pl.ds(pl.multiple_of(i * strip, strip), strip)
        mix = mixes[rows]
        for pair in ((0, 1), (2, 3)):
            totals = [None, None]
            for j in range(count):
                part = e[j, rows].astype(F32)
                for slot, s in enumerate(pair):
                    term = part * mix[:, s * count + j : s * count + j + 1]
                    totals[slot] = term if j == 0 else totals[slot] + term
            for slot, s in enumerate(pair):
                st[s, rows] = totals[slot]

    to = slice(first, first + tile)
    lane = lax.broadcasted_iota(jnp.int32, (tile, LANES), 1)
    kept = jnp.zeros((tile, LANES), F32)
    for s in range(3):
        v = st[s]
        center = v - jnp.sum(v, axis=-1, keepdims=True) * inv
        spread = jnp.sum(center * center, axis=-1, keepdims=True) * inv
        scale = lax.rsqrt(spread + EPSILON)
        hat = center * scale
        hats[s, to] = hat.astype(BF16)
        normed[s, to] = (hat * g_ref[s : s + 1] + b_ref[s : s + 1]).astype(BF16)
        kept = jnp.where(lane == s, scale, kept)
    scales[to] = kept
    res[to] = st[3]


def attend_pair(qkv, out, column_ref, row_ref, seq, lanes, part=None):
    blocks, block = out.shape[1], out.shape[2]
    length = blocks * block
    rows = row_tile(length)
    per = rows // block

    def load(kind, first, last):
        return qkv[kind, seq, first:last, :, lanes].reshape(-1, LANES)

    count = length // rows
    if part is None:
        which = range(count)
    else:
        which = range(part * count // 2, (part + 1) * count // 2)
    for i in which:
        first, until = i * rows, (i + 1) * rows
        b0, b1 = i * per, (i + 1) * per
        query = first + lax.broadcasted_iota(jnp.int32, (rows, until), 0)
        key = lax.broadcasted_iota(jnp.int32, (rows, until), 1)
        same = column_ref[seq, first:until, 0:1] == row_ref[seq, 0:1, 0:until]
        allowed = same & (key <= query)
        q = load(0, b0, b1) * BF16(HD**-0.5)
        k = load(1, 0, b1)
        v = load(2, 0, b1)
        total = None
        for h in range(LANES // HD):
            scores = jnp.where(allowed, dot(only(q, h), k, NT), MASKED)
            peak = jnp.max(scores, axis=-1, keepdims=True)
            raised = jnp.exp(scores - peak)
            mass = jnp.sum(raised, axis=-1, keepdims=True)
            probs = (raised * (1.0 / mass)).astype(BF16)
            part = dot(probs, v)
            part = jnp.where(head_lanes(part.shape, h), part, 0.0)
            total = part if total is None else total + part
        out[seq, b0:b1, :, lanes] = total.astype(BF16).reshape(per, block, LANES)


def forward_kernel(
    n,
    nf,
    e_ref,
    wqkv_ref,
    wo_ref,
    win_ref,
    wout_ref,
    mix_ref,
    gain_ref,
    bias_ref,
    c_ref,
    s_ref,
    ids_ref,
    normed_ref,
    hats_ref,
    scales_ref,
    res_ref,
    gqkv_ref,
    go_ref,
    gin_ref,
    gout_ref,
    qkv_ref,
    ctx_ref,
    e,
    mixes,
    st,
    normed,
    hats,
    scales,
    res,
    w,
    raw,
    shares,
    qkv,
    heads,
    row,
    column,
    send,
    recv,
    local,
    e_sem,
):
    f, z = lax.axis_index("fsdp"), lax.axis_index("ctx")
    count, tokens, width = e_ref.shape
    tile = e.shape[2]
    tiles = tokens // tile
    seqs, _, block, cols = heads.shape
    seq_rows = 2 * block
    cut = raw.shape[1]
    remote = Remote(send, recv)
    spots = (z, 2 * n - 1 - z)
    mine = pl.ds(pl.multiple_of(z * cols, LANES), cols)

    def fetch(t):
        return pltpu.make_async_copy(
            e_ref.at[:, t * tile : (t + 1) * tile], e.at[t % 2], e_sem.at[t % 2]
        )

    fetch(0).start()
    greet_all(n, nf)

    def columns(ref, i):
        at = pl.ds(i * width, width)
        return ref.at[:, at] if len(ref.shape) == 2 else ref.at[:, :, at]

    parts = [
        PlaneGather(remote, nf, columns(wqkv_ref, i), columns(w, i)) for i in range(3)
    ]
    others = [
        PlaneGather(remote, nf, win_ref, gin_ref),
        PlaneGather(remote, nf, wout_ref, gout_ref),
        PlaneGather(remote, nf, wo_ref, go_ref),
    ]
    levels = parts[0].levels
    parts[0].begin(local.at[0])

    def do_tile(t):
        fetch(t).wait()
        if t + 1 < tiles:
            fetch(t + 1).start()
        mix_columns(mix_ref, mixes, t)
        front_tile(
            e.at[t % 2], mixes, st, gain_ref, bias_ref, normed, hats, scales, res, t * tile
        )

    def first_hops():
        parts[0].relay(0)
        parts[1].begin(local.at[1])

    def second_hops():
        for level in range(1, levels):
            parts[0].relay(level)

    for t in range(tiles):
        do_tile(t)
        if t == 0:
            first_hops()
        if t == max(1, tiles - 2):
            second_hops()
    own_tables = []
    for table in (c_ref, s_ref):
        early = table[pl.ds(pl.multiple_of(z * block, block), block)]
        late = table[pl.ds(pl.multiple_of((2 * n - 1 - z) * block, block), block)]
        own_tables.append((early, late))

    def project(i):
        @pl.loop(0, width // cut)
        def _(j):
            at = pl.ds(pl.multiple_of(i * width + j * cut, cut), cut)
            raw[...] = dot(normed[i], w[:, :, at].reshape(width, cut))
            for s in range(seqs):
                for h in range(2):
                    first = s * seq_rows + h * block
                    for c in range(cut // LANES):
                        x = raw[first : first + block, c * LANES : (c + 1) * LANES]
                        if i < 2:
                            x = turned(x, own_tables[0][h], own_tables[1][h])
                        to = c * LANES % cols
                        group = j * (cut // cols) + c * LANES // cols
                        shares[i, group, s, h, :, to : to + LANES] = x.astype(BF16)

    pairs = cols // LANES
    units = [(0, None)] + [(s, p) for s in range(1, seqs) for p in range(pairs)]
    arriving = {unit: [] for unit in units}
    kept = []

    def give(kind, unit):
        s, p = unit
        lanes = slice(None) if p is None else slice(p * LANES, (p + 1) * LANES)
        for k in range(1, n):
            to = lax.rem(z + k, n)
            for h in range(2):
                arriving[unit].append(
                    remote.start(
                        shares.at[kind, to, s, h, :, lanes],
                        qkv.at[kind, s, spots[h], :, lanes],
                        {"ctx": to},
                    )
                )

    for i in range(3):
        parts[i].end()
        project(i)
        give(i, units[0])
        if i < 2:
            for level in range(levels):
                parts[i + 1].relay(level)
                if level == 0:
                    (parts[2], others[0])[i].begin(local.at[2 + i])
    for h in range(2):
        copy = pltpu.make_async_copy(
            shares.at[:, z, :, h], qkv.at[:, :, spots[h]], local.at[8 + h]
        )
        copy.start()
        kept.append(copy)
    for unit in units[1:2]:
        give(slice(None), unit)
    others[1].begin(local.at[4])
    others[2].begin(local.at[5])
    out_copies = [
        pltpu.make_async_copy(w, gqkv_ref, local.at[10]),
        pltpu.make_async_copy(normed, normed_ref, local.at[6]),
        pltpu.make_async_copy(res, res_ref, local.at[7]),
        pltpu.make_async_copy(hats, hats_ref, local.at[12]),
        pltpu.make_async_copy(scales, scales_ref, local.at[13]),
    ]
    for copy in out_copies:
        copy.start()
    place_segments(ids_ref, row, column, block)

    others[0].relay(0)
    for copy in kept:
        copy.wait()
    leaving = []
    stored = 14
    for index, unit in enumerate(units):
        for copy in arriving[unit]:
            copy.wait()
        for other in units[index + 2 : index + 3]:
            give(slice(None), other)
        s, p = unit
        if p is None:

            @pl.loop(0, pairs)
            def _(p):
                lanes = pl.ds(pl.multiple_of(p * LANES, LANES), LANES)
                attend_pair(qkv, heads, column, row, s, lanes)

            there, here = mine, slice(None)
        else:
            here = slice(p * LANES, (p + 1) * LANES)
            there = pl.ds(pl.multiple_of(z * cols + p * LANES, LANES), LANES)
        halves_apart = index + 1 == len(units) and p is not None
        if p is not None and not halves_apart:
            attend_pair(qkv, heads, column, row, s, here)
        for h in range(2):
            if halves_apart:
                attend_pair(qkv, heads, column, row, s, here, h)
            for k in range(1, n):
                to = lax.rem(z + k, n)
                spot = to if h == 0 else 2 * n - 1 - to
                leaving.append(
                    remote.start(
                        heads.at[s, spot, :, here], ctx_ref.at[s, h, :, there], {"ctx": to}
                    )
                )
        for h in range(2):
            copy = pltpu.make_async_copy(
                heads.at[s, spots[h], :, here], ctx_ref.at[s, h, :, there], local.at[stored]
            )
            stored += 1
            copy.start()
            out_copies.append(copy)
        if index == 0:
            others[1].relay(0)
            others[2].relay(0)
            for level in range(1, levels):
                others[0].relay(level)
    copy = pltpu.make_async_copy(qkv, qkv_ref, local.at[11])
    copy.start()
    out_copies.append(copy)
    for level in range(1, levels):
        others[1].relay(level)
        others[2].relay(level)
    for gather in others:
        gather.end()
    for copy in out_copies + leaving:
        copy.wait()


def forward(e, mix, w_qkv, w_o, w_in, w_out, gain, bias, cosine, sine, ids, n, nf):
    count, tokens, width = e.shape
    seqs, block = mix.shape[2], mix.shape[4]
    length = 2 * n * block
    cols = width // n
    spots = 2 * n
    tile = 128
    cut = max(cols, 512)
    rows = width // nf
    units = 1 + (seqs - 1) * (cols // LANES)
    copies = 6 * PlaneGather.count(nf) + (2 + 2 * units) * 2 * (n - 1)
    vmem = pl.BlockSpec(memory_space=pltpu.VMEM)
    hbm = pl.BlockSpec(memory_space=pltpu.HBM)

    def gathered(x):
        return jax.ShapeDtypeStruct((nf,) + x.shape, x.dtype)

    normed, hats, scales, res, g_qkv, g_o, g_in, g_out, qkv, ctx = pl.pallas_call(
        functools.partial(forward_kernel, n, nf),
        in_specs=[hbm] * 5 + [vmem] * 6,
        out_specs=[hbm] * 10,
        out_shape=[
            jax.ShapeDtypeStruct((3, tokens, width), BF16),
            jax.ShapeDtypeStruct((3, tokens, width), BF16),
            jax.ShapeDtypeStruct((tokens, LANES), F32),
            jax.ShapeDtypeStruct((tokens, width), F32),
            gathered(w_qkv),
            gathered(w_o),
            gathered(w_in),
            gathered(w_out),
            jax.ShapeDtypeStruct((3, seqs, spots, block, cols), BF16),
            jax.ShapeDtypeStruct((seqs, 2, block, width), BF16),
        ],
        scratch_shapes=[
            pltpu.VMEM((2, count, tile, width), BF16),
            pltpu.VMEM((tile, 4 * count), F32),
            pltpu.VMEM((4, tile, width), F32),
            pltpu.VMEM((3, tokens, width), BF16),
            pltpu.VMEM((3, tokens, width), BF16),
            pltpu.VMEM((tokens, LANES), F32),
            pltpu.VMEM((tokens, width), F32),
            pltpu.VMEM((nf, rows, 3 * width), BF16),
            pltpu.VMEM((tokens, cut), F32),
            pltpu.VMEM((3, n, seqs, 2, block, cols), BF16),
            pltpu.VMEM((3, seqs, spots, block, cols), BF16),
            pltpu.VMEM((seqs, spots, block, cols), BF16),
            pltpu.VMEM((seqs, 1, length), F32),
            pltpu.VMEM((seqs, length, 8), F32),
            pltpu.SemaphoreType.DMA((copies,)),
            pltpu.SemaphoreType.DMA((copies,)),
            pltpu.SemaphoreType.DMA((14 + 2 * units,)),
            pltpu.SemaphoreType.DMA((2,)),
        ],
        compiler_params=params(58, collective_id=0, has_side_effects=True),
        name="forward",
    )(e, w_qkv, w_o, w_in, w_out, mix, gain, bias, cosine, sine, ids)

    def whole(x):
        return x.reshape(x.shape[0] * x.shape[1], x.shape[2])

    weights = [whole(g) for g in (g_qkv, g_o, g_in, g_out)]
    return normed, hats, scales, res, *weights, qkv, ctx.reshape(tokens, width)


def attend_back_pair(qkv, grad, out, dk, dv, column_ref, row_ref, c_ref, s_ref, seq, lanes):
    blocks, block = grad.shape[1], grad.shape[2]
    length = blocks * block
    rows = row_tile(length)
    per = rows // block
    factor = HD**-0.5

    def load(ref, at, first, last):
        return ref[(*at, slice(first, last), slice(None), lanes)].reshape(-1, LANES)

    for i in range(length // rows):
        here = slice(i * rows, (i + 1) * rows)
        dk[here] = jnp.zeros((rows, LANES), F32)
        dv[here] = jnp.zeros((rows, LANES), F32)
    for i in range(length // rows):
        first, until = i * rows, (i + 1) * rows
        b0, b1 = i * per, (i + 1) * per
        query = first + lax.broadcasted_iota(jnp.int32, (rows, until), 0)
        key = lax.broadcasted_iota(jnp.int32, (rows, until), 1)
        same = column_ref[seq, first:until, 0:1] == row_ref[seq, 0:1, 0:until]
        allowed = same & (key <= query)
        q = load(qkv, (0, seq), b0, b1) * BF16(factor)
        g = load(grad, (seq,), b0, b1)
        k = load(qkv, (1, seq), 0, b1)
        v = load(qkv, (2, seq), 0, b1)
        total = None
        for h in range(LANES // HD):
            q_h = only(q, h)
            g_h = only(g, h)
            scores = jnp.where(allowed, dot(q_h, k, NT), MASKED)
            peak = jnp.max(scores, axis=-1, keepdims=True)
            raised = jnp.exp(scores - peak)
            mass = jnp.sum(raised, axis=-1, keepdims=True)
            probs = raised * (1.0 / mass)
            dots = dot(g_h, v, NT)
            center = jnp.sum(probs * dots, axis=-1, keepdims=True)
            slope = (probs * (dots - center)).astype(BF16)
            part = dot(slope, k)
            part = jnp.where(head_lanes(part.shape, h), part, 0.0)
            total = part if total is None else total + part
            dk[0:until] += dot(slope, q_h, TN)
            dv[0:until] += dot(probs.astype(BF16), g_h, TN)
        cosine, sine = c_ref[first:until], s_ref[first:until]
        low = turned(total * factor, cosine, -sine).astype(BF16)
        out[0, seq, b0:b1, :, lanes] = low.reshape(per, block, LANES)
    for i in range(length // rows):
        here = slice(i * rows, (i + 1) * rows)
        b0, b1 = i * per, (i + 1) * per
        low = turned(dk[here], c_ref[here], -s_ref[here]).astype(BF16)
        out[1, seq, b0:b1, :, lanes] = low.reshape(per, block, LANES)
        out[2, seq, b0:b1, :, lanes] = dv[here].astype(BF16).reshape(per, block, LANES)


def back_kernel(
    n,
    nf,
    cg_ref,
    qkv_ref,
    active_ref,
    lowered_ref,
    normed_ref,
    branch_ref,
    ctx_ref,
    attention_ref,
    ids_ref,
    c_ref,
    s_ref,
    grads_ref,
    in_sum,
    out_sum,
    o_sum,
    qkv,
    grad,
    back,
    dk,
    dv,
    in_terms,
    in_got,
    in_part,
    out_terms,
    out_got,
    out_part,
    o_terms,
    o_got,
    o_part,
    normed,
    branch,
    ctx,
    attention,
    low_tiles,
    active_tiles,
    row,
    column,
    tile_sem,
    send,
    recv,
    local,
):
    f, z = lax.axis_index("fsdp"), lax.axis_index("ctx")
    core = lax.rem(f, 2)
    seqs, _, block, cols = grad.shape
    remote = Remote(send, recv)
    sums = [
        ChipSum(remote, nf, in_terms, in_terms.at[:, core], in_got, in_part),
        ChipSum(remote, nf, out_terms, out_terms.at[:, core], out_got, out_part),
        ChipSum(remote, nf, o_terms, o_terms.at[:, core], o_got, o_part),
    ]
    spots = (z, 2 * n - 1 - z)
    mine = pl.ds(pl.multiple_of(z * cols, LANES), cols)

    def fetch(ref, tiles, sem, t):
        size = tiles.shape[2]
        slot = lax.rem(t, 2)
        at = pl.ds(pl.multiple_of(t * size, LANES), size)
        return pltpu.make_async_copy(ref.at[:, at], tiles.at[slot], tile_sem.at[sem + slot])

    wholes = [(ctx_ref, ctx), (attention_ref, attention), (normed_ref, normed), (branch_ref, branch)]
    loads = [
        pltpu.make_async_copy(ref, there, local.at[i]) for i, (ref, there) in enumerate(wholes)
    ]
    for load in loads[:3]:
        load.start()
    fetch(lowered_ref, low_tiles, 0, 0).start()
    loads[3].start()
    fetch(active_ref, active_tiles, 2, 0).start()
    later = [pltpu.make_async_copy(qkv_ref, qkv, local.at[6 + 2 * seqs])]
    for h in range(2):
        later.append(
            pltpu.make_async_copy(cg_ref.at[z, :, h], grad.at[:, spots[h]], local.at[4 + h])
        )
    for load in later:
        load.start()

    greet_all(n, nf)

    arriving = []

    def take(s):
        copies = []
        for k in range(1, n):
            to = lax.rem(z + k, n)
            for h in range(2):
                copies.append(
                    remote.start(cg_ref.at[to, s, h], grad.at[s, spots[h]], {"ctx": to})
                )
        arriving.append(copies)

    def each_tile(ref, tiles, sem, work):
        count = ref.shape[1] // tiles.shape[2]

        @pl.loop(0, count)
        def _(t):
            fetch(ref, tiles, sem, t).wait()

            @pl.when(t + 1 < count)
            def _():
                fetch(ref, tiles, sem, t + 1).start()

            work(t, tiles[lax.rem(t, 2)])

    def in_tile(t, low):
        chips, _, rows, _ = in_terms.shape
        size = low.shape[1]
        at = pl.ds(pl.multiple_of(t * size, LANES), size)
        value = dot(normed[...], low, TN).astype(BF16)
        in_terms[:, :, :, at] = value.reshape(chips, 2, rows, size)

    def out_tile(t, active):
        _, _, rows, width = out_terms.shape
        out_terms[t] = dot(active, branch[...], TN).astype(BF16).reshape(2, rows, width)

    take(0)
    loads[0].wait()
    loads[1].wait()
    o_terms[...] = dot(ctx[...], attention[...], TN).astype(BF16).reshape(o_terms.shape)
    sums[2].cores()
    loads[2].wait()
    each_tile(lowered_ref, low_tiles, 0, in_tile)
    sums[0].cores()
    sums[2].cross()
    for s in range(1, seqs):
        take(s)
    loads[3].wait()
    each_tile(active_ref, active_tiles, 2, out_tile)
    sums[1].cores()
    place_segments(ids_ref, row, column, block)
    sums[0].cross()
    for load in later:
        load.wait()

    leaving = []
    kept = []

    def hand(s, here, there):
        for k in range(1, n):
            to = lax.rem(z + k, n)
            for h in range(2):
                spot = to if h == 0 else 2 * n - 1 - to
                leaving.append(
                    remote.start(
                        back.at[:, s, spot, :, here],
                        grads_ref.at[:, s, h, :, there],
                        {"ctx": to},
                    )
                )

    for s in range(seqs):
        for copy in arriving[s]:
            copy.wait()
        if s == 0:
            for p in range(cols // LANES):
                here = slice(p * LANES, (p + 1) * LANES)
                attend_back_pair(qkv, grad, back, dk, dv, column, row, c_ref, s_ref, s, here)
                hand(s, here, pl.ds(pl.multiple_of(z * cols + p * LANES, LANES), LANES))
        else:

            @pl.loop(0, cols // LANES)
            def _(p):
                lanes = pl.ds(pl.multiple_of(p * LANES, LANES), LANES)
                attend_back_pair(qkv, grad, back, dk, dv, column, row, c_ref, s_ref, s, lanes)

            hand(s, slice(None), mine)
        for h in range(2):
            copy = pltpu.make_async_copy(
                back.at[:, s, spots[h]], grads_ref.at[:, s, h, :, mine], local.at[6 + 2 * s + h]
            )
            copy.start()
            kept.append(copy)
        if s == 0:
            sums[2].relay()
            sums[1].cross()
            sums[0].relay()

    sums[1].relay()
    for chip_sum, out in zip(sums, (in_sum, out_sum, o_sum)):
        chip_sum.total(out)
    for copy in kept + leaving:
        copy.wait()


def attention_back(context_grad, qkv, saved, ids, cosine, sine, n, nf):
    _, seqs, spots, block, cols = qkv.shape
    length = spots * block
    tokens, units = saved[0].shape
    width = saved[2].shape[1]
    chips = nf // 2
    shapes = [(width // nf, units), (units // nf, width), (width // nf, width)]
    copies = (2 * seqs + cols // LANES - 1) * 2 * (n - 1) + 3 * ChipSum.count(nf)
    copies += 2 * (n - 1)
    vmem = pl.BlockSpec(memory_space=pltpu.VMEM)
    hbm = pl.BlockSpec(memory_space=pltpu.HBM)
    scratch = []
    for rows, wide in shapes:
        scratch.append(pltpu.VMEM((chips, 2, rows, wide), BF16))
        scratch += chip_scratch(nf, rows, wide)[1:]
    grads, *owned = pl.pallas_call(
        functools.partial(back_kernel, n, nf),
        in_specs=[hbm] * 8 + [vmem] * 3,
        out_specs=[hbm, vmem, vmem, vmem],
        out_shape=[jax.ShapeDtypeStruct((3, seqs, 2, block, width), BF16)]
        + [jax.ShapeDtypeStruct(shape, BF16) for shape in shapes],
        scratch_shapes=[
            pltpu.VMEM((3, seqs, spots, block, cols), BF16),
            pltpu.VMEM((seqs, spots, block, cols), BF16),
            pltpu.VMEM((3, seqs, spots, block, cols), BF16),
            pltpu.VMEM((length, LANES), F32),
            pltpu.VMEM((length, LANES), F32),
            *scratch,
            *[pltpu.VMEM((tokens, width), BF16)] * 4,
            pltpu.VMEM((2, tokens, 512), BF16),
            pltpu.VMEM((2, tokens, units // chips), BF16),
            pltpu.VMEM((seqs, 1, length), F32),
            pltpu.VMEM((seqs, length, 8), F32),
            pltpu.SemaphoreType.DMA((4,)),
            pltpu.SemaphoreType.DMA((copies,)),
            pltpu.SemaphoreType.DMA((copies,)),
            pltpu.SemaphoreType.DMA((7 + 2 * seqs,)),
        ],
        compiler_params=params(62, collective_id=2, has_side_effects=True),
        name="attention_back",
    )(
        context_grad.reshape(n, seqs, 2, block, cols),
        qkv,
        *saved,
        ids,
        cosine,
        sine,
    )
    return grads.reshape(3, seqs * 2 * block, width), owned


def norm_back_tile(hats, scales, ng, st, e, mg, mg_ref, g_ref, h, low, dgain, dbias, selector, t, strip=16):
    count, tile, width = e.shape
    inv = 1.0 / width
    to = slice(t * tile, (t + 1) * tile)
    for s in range(3):
        dy = ng[s]
        hat = hats[s, to].astype(F32)
        scale = scales[to, s : s + 1]
        dgain[s : s + 1] += jnp.sum(dy * hat, axis=0, keepdims=True)
        dbias[s : s + 1] += jnp.sum(dy, axis=0, keepdims=True)
        dh = dy * g_ref[s : s + 1]
        mean = jnp.sum(dh, axis=-1, keepdims=True) * inv
        along = jnp.sum(dh * hat, axis=-1, keepdims=True) * inv
        out = (scale * (dh - mean - hat * along)).astype(BF16)
        low[s, to] = out
        st[s] = out
    st[3] = h[to].astype(BF16)

    shape = (4 * strip, count * strip)
    same = lax.rem(lax.broadcasted_iota(jnp.int32, shape, 0), strip) == lax.rem(
        lax.broadcasted_iota(jnp.int32, shape, 1), strip
    )
    for i in range(tile // strip):
        rows = slice(i * strip, (i + 1) * strip)
        grads = st[:, rows].reshape(4 * strip, width)
        inputs = e[:, rows].reshape(count * strip, width)
        products = jnp.where(same, dot(grads, inputs, NT), 0.0)
        wide = jnp.concatenate(
            [products[s * strip : (s + 1) * strip] for s in range(4)], axis=1
        )
        high, rest = halves(wide)
        mg[rows] = dot(high, selector[...]) + dot(rest, selector[...])
    turned_mg = mg[...].T
    block = mg_ref.shape[4]
    per = tile // block
    for i in range(per):
        place = t * per + i
        for a in range(4):
            mg_ref[a, :, place // 2, place % 2, :] = turned_mg[
                a * count : (a + 1) * count, i * block : (i + 1) * block
            ]


def small_squares(rows, cols):
    first = 8 + rows
    places = []
    for g in range(-(-rows // 8)):
        size = min(8, rows - 8 * g)
        places.append(
            (
                slice(first, first + size),
                slice(g * LANES, g * LANES + cols),
                slice(8 * g, 8 * g + size),
            )
        )
    return places


def small_line_at(rows, cols):
    groups = -(-rows // 8)
    return slice(groups * LANES, groups * LANES + cols)


def end_kernel(
    n,
    nf,
    grads_ref,
    normed_ref,
    hats_ref,
    scales_ref,
    e_ref,
    w_ref,
    h_ref,
    gain_ref,
    in_ref,
    out_ref,
    o_ref,
    sgain_ref,
    sbias_ref,
    sw1_ref,
    sw2_ref,
    smb_ref,
    low_ref,
    mg_ref,
    q_sum,
    k_sum,
    v_sum,
    in_sum,
    out_sum,
    o_sum,
    small_sum,
    grads,
    normed,
    hats,
    scales,
    w,
    h,
    e,
    ng,
    st,
    low,
    mg,
    selector,
    dgain,
    dbias,
    small_work,
    small_in,
    small_line,
    send,
    recv,
    local,
    e_sem,
    *more,
):
    f, z = lax.axis_index("fsdp"), lax.axis_index("ctx")
    core = lax.rem(f, 2)
    count, tokens, width = e_ref.shape
    tile = e.shape[2]
    tiles = tokens // tile
    remote = Remote(send, recv)
    chip_sets = [more[4 * i : 4 * i + 4] for i in range(3)]
    rest = more[12:]
    shard = chip_sets[0][1].shape[1]

    def fetch(t):
        return pltpu.make_async_copy(
            e_ref.at[:, t * tile : (t + 1) * tile], e.at[t % 2], e_sem.at[t % 2]
        )

    loads = [
        pltpu.make_async_copy(src, dst, local.at[i])
        for i, (src, dst) in enumerate(
            [
                (grads_ref, grads),
                (normed_ref, normed),
                (w_ref, w),
                (hats_ref, hats),
                (scales_ref, scales),
                (h_ref, h),
            ]
        )
    ]
    for load in loads:
        load.start()
    fetch(0).start()

    greet_all(n, nf)

    chain = Chain(remote, n)
    works = [in_ref, out_ref, o_ref] + [chip_set[3] for chip_set in chip_sets]
    results = [in_sum, out_sum, o_sum, q_sum, k_sum, v_sum]
    for work, out, sizes in zip(works, results, piece_sizes([x.shape[0] for x in works])):
        first = 0
        for size in sizes:
            at = pl.ds(first, size)
            chain.add(work.at[at], out.at[at], *rest[:3])
            rest = rest[3:]
            first += size
    total_pieces = len(chain.pieces)
    chain.start()
    chain.start()

    loads[0].wait()
    loads[1].wait()
    cut = 256
    per = cut // (2 * shard)
    sums = []
    for i in range(3):
        terms, got, part, own = chip_sets[i]
        for c in range(width // cut):
            value = dot(normed[i, :, c * cut : (c + 1) * cut], grads[i], TN).astype(BF16)
            terms[c * per : (c + 1) * per] = value.reshape(per, 2, shard, width)
        chip_sum = ChipSum(remote, nf, terms, terms.at[:, core], got, part)
        chip_sum.cores()
        sums.append(chip_sum)
    dgain[...] = jnp.zeros_like(dgain)
    dbias[...] = jnp.zeros_like(dbias)
    size = selector.shape
    group = lax.broadcasted_iota(jnp.int32, size, 0) // 16
    selector[...] = jnp.where(
        group == lax.broadcasted_iota(jnp.int32, size, 1), 1.0, 0.0
    ).astype(BF16)
    for load in loads[2:]:
        load.wait()

    def do_tile(t):
        fetch(t).wait()
        if t + 1 < tiles:
            fetch(t + 1).start()
        rows = slice(t * tile, (t + 1) * tile)
        for i in range(3):
            ng[i] = dot(grads[i, rows], w[:, i * width : (i + 1) * width], NT)
        norm_back_tile(
            hats, scales, ng, st, e.at[t % 2], mg, mg_ref, gain_ref, h, low, dgain, dbias, selector, t
        )

    todo = list(range(tiles))

    def some():
        if todo:
            do_tile(todo.pop(0))

    chain.step(0)
    for chip_sum in sums:
        chip_sum.cross()
    chain.step(1)
    some()
    chain.step(2)
    some()
    chain.step(3)
    chain.step(4)
    for chip_sum in sums:
        chip_sum.relay()
    some()
    chain.step(5)
    while todo:
        some()
    keep = pltpu.make_async_copy(low, low_ref, local.at[6])
    keep.start()
    for chip_sum, chip_set in zip(sums, chip_sets):
        chip_sum.total(chip_set[3])
    chain.step(6)

    thin = small_in.shape[1]
    hidden_count, coef_count = sw2_ref.shape
    first = 8 + hidden_count
    squares = small_squares(hidden_count, coef_count)
    line_at = small_line_at(hidden_count, coef_count)
    small_work[...] = jnp.zeros_like(small_work)
    small_work[0:3] = dgain[...]
    small_work[3:4] = sgain_ref[...]
    small_work[4:7] = dbias[...]
    small_work[7:8] = sbias_ref[...]
    small_work[8:first] = sw1_ref[...]
    for rows, lanes, which in squares:
        small_work[rows, lanes] = sw2_ref[which]
    small_work[first : first + 1, line_at] = smb_ref[...]
    here = pl.ds(pl.multiple_of(f * thin, thin), thin)
    small_in[0] = small_work[here]
    slices = []
    for k in range(1, nf):
        to = lax.rem(f + k, nf)
        slices.append(
            remote.start(
                small_work.at[pl.ds(pl.multiple_of(to * thin, thin), thin)],
                small_in.at[k],
                {"fsdp": to},
            )
        )

    chain.step(7)
    for copy in slices:
        copy.wait()
    total = small_in[0]
    for k in range(1, nf):
        total = total + small_in[k]
    small_line[z] = total
    across = []
    for k in range(1, n):
        across.append(
            remote.start(small_line.at[z], small_line.at[z], {"ctx": lax.rem(z + k, n)})
        )
    chain.step(8)
    chain.step(9)
    for copy in across:
        copy.wait()
    total = small_line[0]
    for k in range(1, n):
        total = total + small_line[k]
    small_sum[here] = total
    spread = []
    for k in range(1, nf):
        spread.append(
            remote.start(small_sum.at[here], small_sum.at[here], {"fsdp": lax.rem(f + k, nf)})
        )
    for c in range(10, total_pieces):
        chain.step(c)
    chain.leave(total_pieces - 1)
    for copy in spread:
        copy.wait()
    for c in range(total_pieces):
        chain.end(c)
    keep.wait()


def finish(grads, normed, hats, scales, e, w, hgrad, gain, owned, small, mix_shape, n, nf):
    count, tokens, width = e.shape
    tile = 128
    chips = nf // 2
    shard = width // nf
    rows = 8 + small[2].shape[0] + 8
    thin = 8 * -(-rows // (8 * nf))
    m_in, m_out, m_o = owned
    lines, chip_sums = [], []
    heights = [m_in.shape[0], m_out.shape[0], m_o.shape[0]] + [shard] * 3
    widths = [m_in.shape[1], m_out.shape[1], m_o.shape[1]] + [width] * 3
    planned = piece_sizes(heights)
    for sizes, wide_as in zip(planned, widths):
        for size in sizes:
            lines += chain_scratch(n, size, wide_as)
    pieces = sum(len(sizes) for sizes in planned)
    for _ in range(3):
        chip_sums += [
            pltpu.VMEM((chips, 2, shard, width), BF16),
            *chip_scratch(nf, shard, width)[1:],
            pltpu.VMEM((shard, width), BF16),
        ]
    copies = pieces * (Chain.levels(n) + 2) + 3 * ChipSum.count(nf) + 2 * (nf - 1) + (n - 1)
    vmem = pl.BlockSpec(memory_space=pltpu.VMEM)
    hbm = pl.BlockSpec(memory_space=pltpu.HBM)
    wide = jax.ShapeDtypeStruct((shard, width), BF16)
    return pl.pallas_call(
        functools.partial(end_kernel, n, nf),
        in_specs=[hbm] * 7 + [vmem] * 9,
        out_specs=[hbm] + [vmem] * 8,
        out_shape=[
            jax.ShapeDtypeStruct((3, tokens, width), BF16),
            jax.ShapeDtypeStruct(mix_shape, F32),
            wide,
            wide,
            wide,
            *[jax.ShapeDtypeStruct(x.shape, BF16) for x in owned],
            jax.ShapeDtypeStruct((nf * thin, width), F32),
        ],
        scratch_shapes=[
            pltpu.VMEM(grads.shape, BF16),
            pltpu.VMEM(normed.shape, BF16),
            pltpu.VMEM(hats.shape, BF16),
            pltpu.VMEM(scales.shape, F32),
            pltpu.VMEM(w.shape, BF16),
            pltpu.VMEM(hgrad.shape, F32),
            pltpu.VMEM((2, count, tile, width), BF16),
            pltpu.VMEM((3, tile, width), F32),
            pltpu.VMEM((4, tile, width), BF16),
            pltpu.VMEM((3, tokens, width), BF16),
            pltpu.VMEM((tile, LANES), F32),
            pltpu.VMEM((4 * count * 16, LANES), BF16),
            pltpu.VMEM((3, width), F32),
            pltpu.VMEM((3, width), F32),
            pltpu.VMEM((nf * thin, width), F32),
            pltpu.VMEM((nf, thin, width), F32),
            pltpu.VMEM((n, thin, width), F32),
            pltpu.SemaphoreType.DMA((copies,)),
            pltpu.SemaphoreType.DMA((copies,)),
            pltpu.SemaphoreType.DMA((7,)),
            pltpu.SemaphoreType.DMA((2,)),
            *chip_sums,
            *lines,
        ],
        compiler_params=params(60, collective_id=3, has_side_effects=True),
        name="finish",
    )(grads, normed, hats, scales, e, w, hgrad, gain, *owned, *small)


def tail_kernel(
    low_ref,
    h_ref,
    mix_ref,
    q_ref,
    k_ref,
    v_ref,
    in_ref,
    out_ref,
    o_ref,
    small_ref,
    mg_ref,
    eg_ref,
    qkv_ref,
    in32_ref,
    out32_ref,
    o32_ref,
    gain_ref,
    bias_ref,
    w1_ref,
    w2_ref,
    mb_ref,
    mg_out_ref,
    mixes,
    *,
    strip,
):
    count, tile, width = eg_ref.shape
    chunk = 256
    block = mix_ref.shape[4]
    tiles = mix_ref.shape[2] * 2 * block // tile
    step = pl.program_id(0)
    for t in range(tiles):

        @pl.when(step == t)
        def _():
            mix_columns(mix_ref, mixes, t)

    @pl.when(step == 0)
    def _():
        hidden_count, coef_count = w2_ref.shape
        first = 8 + hidden_count
        gain_ref[...] = small_ref[0:4]
        bias_ref[...] = small_ref[4:8]
        w1_ref[...] = small_ref[8:first]
        for rows, lanes, which in small_squares(hidden_count, coef_count):
            w2_ref[which] = small_ref[rows, lanes]
        mb_ref[...] = small_ref[first : first + 1, small_line_at(hidden_count, coef_count)]
        mg_out_ref[...] = mg_ref[...]

    for i, ref in enumerate((q_ref, k_ref, v_ref)):
        qkv_ref[:, i * width : (i + 1) * width] = ref[...].astype(F32)
    in32_ref[...] = in_ref[...].astype(F32)
    out32_ref[...] = out_ref[...].astype(F32)
    o32_ref[...] = o_ref[...].astype(F32)

    @pl.loop(0, tile // strip)
    def _(i):
        rows = pl.ds(pl.multiple_of(i * strip, strip), strip)
        mix = mixes[rows]
        for c in range(width // chunk):
            cols = slice(c * chunk, (c + 1) * chunk)
            grads = [low_ref[s, rows, cols].astype(F32) for s in range(3)]
            grads.append(h_ref[rows, cols])
            for j in range(count):
                total = grads[0] * mix[:, j : j + 1]
                for s in range(1, 4):
                    total = total + grads[s] * mix[:, s * count + j : s * count + j + 1]
                eg_ref[j, rows, cols] = total.astype(BF16)


def spread_back(low, hgrad, mix, sums, small, m_grad, sizes):
    _, tokens, width = low.shape
    count = mix.shape[1]
    tile = 128
    tiles = tokens // tile
    hidden_count, coef_count = sizes

    def part(x):
        return pl.BlockSpec((x.shape[0] // tiles, x.shape[1]), lambda i: (i, 0))

    def whole(x):
        zeros = (0,) * len(x.shape)
        return once(x.shape, lambda i: zeros)

    shard = sums[0].shape[0]
    outs = [
        jax.ShapeDtypeStruct((count, tokens, width), BF16),
        jax.ShapeDtypeStruct((shard, 3 * width), F32),
        *[jax.ShapeDtypeStruct(x.shape, F32) for x in sums[3:]],
        jax.ShapeDtypeStruct((4, width), F32),
        jax.ShapeDtypeStruct((4, width), F32),
        jax.ShapeDtypeStruct((hidden_count, width), F32),
        jax.ShapeDtypeStruct((hidden_count, coef_count), F32),
        jax.ShapeDtypeStruct((1, coef_count), F32),
        jax.ShapeDtypeStruct(m_grad.shape, F32),
    ]
    return pl.pallas_call(
        functools.partial(tail_kernel, strip=32),
        grid=(tiles,),
        in_specs=[
            pl.BlockSpec((3, tile, width), lambda i: (0, i, 0)),
            pl.BlockSpec((tile, width), lambda i: (i, 0)),
            whole(mix),
            *[part(x) for x in sums],
            whole(small),
            whole(m_grad),
        ],
        out_specs=[pl.BlockSpec((count, tile, width), lambda i: (0, i, 0))]
        + [part(x) for x in outs[1:5]]
        + [whole(x) for x in outs[5:]],
        out_shape=outs,
        scratch_shapes=[pltpu.VMEM((tile, 4 * count), F32)],
        compiler_params=params(60),
        cost_estimate=pl.CostEstimate(
            flops=64 * tokens * width, bytes_accessed=40 * tokens * width, transcendentals=0
        ),
        name="spread_back",
    )(low, hgrad, mix, *sums, small, m_grad)


def body(
    earlier,
    mix_in,
    segment_ids,
    attn_qkv,
    attn_out,
    mlp_in,
    mlp_out,
    norm_gain,
    norm_bias,
    mix_w1,
    mix_w2,
    mix_bias,
    out_grad,
    coef_grad,
):
    count, seqs, _, block, width = earlier.shape
    n = lax.axis_size("ctx")
    tokens = seqs * 2 * block
    length = 2 * n * block
    me = lax.axis_index("ctx")

    nf = lax.axis_size("fsdp")
    e = earlier.reshape(count, tokens, width)
    cosine, sine = (jnp.asarray(table) for table in turn_tables(length))
    normed, hats, scales, residual, w_qkv, w_o, w_in, w_out, qkv, context = forward(
        e,
        mix_in,
        attn_qkv,
        attn_out,
        mlp_in,
        mlp_out,
        norm_gain,
        norm_bias,
        cosine,
        sine,
        segment_ids,
        n,
        nf,
    )
    (
        layer_out,
        coefs,
        active,
        lowered,
        normed_mlp,
        branch,
        attention_grad,
        context_grad,
        hidden_grad,
        d_gain,
        d_bias,
        d_w1,
        d_w2,
        d_mb,
    ) = feed(
        residual,
        context,
        w_o,
        w_in,
        w_out,
        norm_gain,
        norm_bias,
        mix_w1,
        mix_w2,
        mix_bias[None, :],
        out_grad.reshape(tokens, width),
        coef_grad,
        n,
    )
    saved = (active, lowered, normed_mlp, branch, context, attention_grad)
    grads, owned = attention_back(
        context_grad, qkv, saved, segment_ids, cosine, sine, n, nf
    )
    low, m_grad, *sums, small = finish(
        grads,
        normed,
        hats,
        scales,
        e,
        w_qkv,
        hidden_grad,
        norm_gain,
        owned,
        (d_gain, d_bias, d_w1, d_w2, d_mb),
        mix_in.shape,
        n,
        nf,
    )
    e_grad, g_qkv, g_in, g_out, g_o, gain_sum, bias_sum, w1_sum, w2_sum, mb_sum, m_grad = (
        spread_back(low, hidden_grad, mix_in, sums, small, m_grad, mix_w2.shape)
    )
    return (
        layer_out.reshape(seqs, 2, block, width),
        coefs,
        e_grad.reshape(count, seqs, 2, block, width),
        m_grad,
        g_qkv,
        g_o,
        g_in,
        g_out,
        gain_sum,
        bias_sum,
        w1_sum,
        w2_sum,
        mb_sum[0],
    )


def solution(mesh):
    in_specs = (
        P(None, "fsdp", None, "ctx", None),
        P(None, None, "fsdp", None, "ctx"),
        P("fsdp", None, None),
        P("fsdp", None),
        P("fsdp", None),
        P("fsdp", None),
        P("fsdp", None),
        P(),
        P(),
        P(),
        P(),
        P(),
        P("fsdp", None, "ctx", None),
        P(None, None, "fsdp", None, "ctx"),
    )
    out_specs = (
        P("fsdp", None, "ctx", None),
        P(None, None, "fsdp", None, "ctx"),
        P(None, "fsdp", None, "ctx", None),
        P(None, None, "fsdp", None, "ctx"),
        P("fsdp", None),
        P("fsdp", None),
        P("fsdp", None),
        P("fsdp", None),
        P(),
        P(),
        P(),
        P(),
        P(),
    )
    return jax.shard_map(body, mesh=mesh, in_specs=in_specs, out_specs=out_specs, check_vma=False)
```

```python
import functools
import math

import jax
import jax.numpy as jnp
import numpy as np
from jax import lax
from jax.experimental import pallas as pl
from jax.experimental.pallas import tpu as pltpu
from jax.sharding import PartitionSpec as P

HD = 64
ROT = 16
LANES = 128
EPSILON = 1e-05
RMS_EPSILON = 1e-06
MASKED = -1e30
F32 = jnp.float32
BF16 = jnp.bfloat16
MESH = pl.DeviceIdType.MESH
MIB = 1024 * 1024

NN = (((1,), (0,)), ((), ()))
NT = (((1,), (1,)), ((), ()))
TN = (((0,), (0,)), ((), ()))

ERFC_RATE = 0.4
ERFC = (
    0.22567586600780487,
    0.22566929459571838,
    0.20784726738929749,
    0.16851142048835754,
    0.1415392905473709,
    -0.005822250619530678,
    0.16932761669158936,
    -0.18304575979709625,
    0.05029737576842308,
)


def dot(a, b, dims=NN):
    return lax.dot_general(a, b, dims, preferred_element_type=F32)


def gelu_and_slope(v):
    bell = jnp.exp(-0.5 * (v * v))
    t = 1.0 / (1.0 + (ERFC_RATE * math.sqrt(0.5)) * jnp.abs(v))
    poly = 0.5 * ERFC[-1] * t + 0.5 * ERFC[-2]
    for coefficient in ERFC[-3::-1]:
        poly = poly * t + 0.5 * coefficient
    tail = poly * t * bell
    phi = jnp.where(v >= 0.0, 1.0 - tail, tail)
    return v * phi, phi + v * bell * (1.0 / math.sqrt(2.0 * math.pi))


def halves(x):
    high = x.astype(BF16)
    return high, (x - high.astype(F32)).astype(BF16)


def params(limit_mib, **more):
    return pltpu.CompilerParams(vmem_limit_bytes=limit_mib * MIB, **more)


def once(shape, index):
    return pl.BlockSpec(shape, index, pipeline_mode=pl.Buffered(1))


def turn_tables(length):
    half = ROT // 2
    frequency = 10000.0 ** (-(np.arange(half) * 2.0 / ROT))
    angle = np.arange(length)[:, None] * frequency[None, :]
    lane = np.arange(LANES) % HD
    cosine = np.ones((length, LANES), np.float32)
    sine = np.zeros((length, LANES), np.float32)
    for k in range(LANES):
        if lane[k] < ROT:
            cosine[:, k] = np.cos(angle[:, lane[k] % half])
            sign = -1.0 if lane[k] < half else 1.0
            sine[:, k] = sign * np.sin(angle[:, lane[k] % half])
    return cosine, sine


def turned(x, cosine, sine):
    half = ROT // 2
    lane = lax.broadcasted_iota(jnp.int32, x.shape, 1) % HD
    other = jnp.where(
        lane < half, pltpu.roll(x, LANES - half, axis=1), pltpu.roll(x, half, axis=1)
    )
    return x * cosine + other * sine


def row_tile(length):
    return min(256, length)


def head_lanes(shape, h):
    lane = lax.broadcasted_iota(jnp.int32, shape, 1)
    return (lane >= h * HD) & (lane < (h + 1) * HD)


def only(x, h):
    return jnp.where(head_lanes(x.shape, h), x, jnp.zeros_like(x))


def coefficient_places(ref):
    outer, inner, seqs, _, block = ref.shape
    for a in range(outer):
        for seq in range(seqs):
            for h in range(2):
                first = (2 * seq + h) * block
                yield a, seq, h, slice(a * inner, (a + 1) * inner), slice(first, first + block)


def feed_kernel(
    res_ref,
    ctx_ref,
    wo_ref,
    win_ref,
    wout_ref,
    g_ref,
    b_ref,
    w1_ref,
    w2_ref,
    mb_ref,
    og_ref,
    cg_ref,
    out_ref,
    coef_ref,
    active,
    lowered,
    normed,
    branch,
    attention,
    cgrad_ref,
    hgrad_ref,
    dgain_ref,
    dbias_ref,
    dw1_ref,
    dw2_ref,
    dmb_ref,
    hidden,
    total,
    slope,
    r_high,
    r_rest,
    cotangent,
    *,
    tiles,
    strip,
):
    step = pl.program_id(0)
    tokens, width = res_ref.shape
    cut = win_ref.shape[1]
    inv = 1.0 / width

    @pl.when(step == 0)
    def _():
        hidden[...] = dot(ctx_ref[...], wo_ref[...])

        @pl.loop(0, tokens // strip)
        def _(i):
            rows = pl.ds(pl.multiple_of(i * strip, strip), strip)
            v = hidden[rows] + res_ref[rows]
            hidden[rows] = v
            center = v - jnp.sum(v, axis=-1, keepdims=True) * inv
            spread = jnp.sum(center * center, axis=-1, keepdims=True) * inv
            hat = center * lax.rsqrt(spread + EPSILON)
            normed[rows] = (hat * g_ref[3:4] + b_ref[3:4]).astype(BF16)
            total[rows] = v

    @pl.when(step < tiles)
    def _():
        half = tokens // 2
        parts = [slice(i * half, (i + 1) * half) for i in range(2)]
        ups = [dot(normed[rows], win_ref[...]) for rows in parts]
        for rows, up in zip(parts, ups):
            value, rate = gelu_and_slope(up)
            low = value.astype(BF16)
            active[rows] = low
            slope[step, rows] = rate
            total[rows] += dot(low, wout_ref[...])

    @pl.when(step == tiles - 1)
    def _():
        w1 = w1_ref[...]
        w2 = w2_ref[...]

        @pl.loop(0, tokens // strip)
        def _(i):
            rows = pl.ds(pl.multiple_of(i * strip, strip), strip)
            v = total[rows]
            out_ref[rows] = v.astype(BF16)
            scale = lax.rsqrt(jnp.sum(v * v, axis=-1, keepdims=True) * inv + RMS_EPSILON)
            r = v * scale
            high = r.astype(BF16)
            r_high[rows] = high
            r_rest[rows] = (r - high.astype(F32)).astype(BF16)

        high, rest = r_high[...], r_rest[...]
        for a, seq, h, rows, cols in coefficient_places(cg_ref):
            cotangent[rows, cols] = cg_ref[a, :, seq, h, :]
        z = dot(w1, high, NT) + dot(w1, rest, NT)
        value, rate = gelu_and_slope(z)
        v_high, v_rest = halves(value)
        ones = jnp.ones((1, tokens), BF16)
        mb_high, mb_rest = halves(mb_ref[...])
        mb_last = (mb_ref[...] - mb_high.astype(F32) - mb_rest.astype(F32)).astype(BF16)
        shift = dot(mb_high, ones, TN) + dot(mb_rest, ones, TN) + dot(mb_last, ones, TN)
        coefs = dot(w2, v_high, TN) + dot(w2, v_rest, TN) + shift
        for a, seq, h, rows, cols in coefficient_places(coef_ref):
            coef_ref[a, :, seq, h, :] = coefs[rows, cols]
        c_high, c_rest = halves(cotangent[...])
        dmb_ref[...] = dot(ones, c_high, NT) + dot(ones, c_rest, NT)
        dw2_ref[...] = dot(v_high, c_high, NT) + dot(v_rest, c_high, NT) + dot(v_high, c_rest, NT)
        z_high, z_rest = halves((dot(w2, c_high) + dot(w2, c_rest)) * rate)
        dw1_ref[...] = dot(z_high, high) + dot(z_high, rest) + dot(z_rest, high)
        hgrad_ref[...] = dot(z_high, w1, TN) + dot(z_rest, w1, TN)

        @pl.loop(0, tokens // strip)
        def _(i):
            rows = pl.ds(pl.multiple_of(i * strip, strip), strip)
            v = total[rows]
            scale = lax.rsqrt(jnp.sum(v * v, axis=-1, keepdims=True) * inv + RMS_EPSILON)
            dr = hgrad_ref[rows]
            r = v * scale
            mean = jnp.sum(dr * r, axis=-1, keepdims=True) * inv
            grad = scale * (dr - r * mean) + og_ref[rows].astype(F32)
            hgrad_ref[rows] = grad
            branch[rows] = grad.astype(BF16)
            total[rows] = jnp.zeros_like(v)

    @pl.when(step >= tiles)
    def _():
        j = step - tiles
        low = (dot(branch[...], wout_ref[...], NT) * slope[j]).astype(BF16)
        lowered[...] = low
        total[...] += dot(low, win_ref[...], NT)

    @pl.when(step == 2 * tiles - 1)
    def _():
        dgain_ref[...] = jnp.zeros_like(dgain_ref)
        dbias_ref[...] = jnp.zeros_like(dbias_ref)

        @pl.loop(0, tokens // strip)
        def _(i):
            rows = pl.ds(pl.multiple_of(i * strip, strip), strip)
            v = hidden[rows]
            dy = total[rows]
            center = v - jnp.sum(v, axis=-1, keepdims=True) * inv
            spread = jnp.sum(center * center, axis=-1, keepdims=True) * inv
            scale = lax.rsqrt(spread + EPSILON)
            hat = center * scale
            dgain_ref[...] += jnp.sum(dy * hat, axis=0, keepdims=True)
            dbias_ref[...] += jnp.sum(dy, axis=0, keepdims=True)
            dh = dy * g_ref[3:4]
            first = jnp.sum(dh, axis=-1, keepdims=True) * inv
            second = jnp.sum(dh * hat, axis=-1, keepdims=True) * inv
            grad = hgrad_ref[rows] + scale * (dh - first - hat * second)
            hgrad_ref[rows] = grad
            attention[rows] = grad.astype(BF16)

        groups, _, group = cgrad_ref.shape
        back = dot(attention[...], wo_ref[...], NT).astype(BF16)
        for i in range(groups):
            cgrad_ref[i] = back[:, i * group : (i + 1) * group]


def feed(res, ctx, wo, win, wout, gain, bias, w1, w2, mb, og, cg, groups):
    tokens, width = res.shape
    hidden_units = win.shape[1]
    cut = 1024
    tiles = hidden_units // cut
    small, coefs = w1.shape[0], w2.shape[1]

    def whole(x):
        zeros = (0,) * x.ndim
        return once(x.shape, lambda i: zeros)

    def result(shape, dtype=F32):
        zeros = (0,) * len(shape)
        return once(shape, lambda i: zeros), jax.ShapeDtypeStruct(shape, dtype)

    def back(i):
        return jnp.maximum(i - tiles, 0)

    outs = [
        result((tokens, width), BF16),
        result(cg.shape),
        (
            pl.BlockSpec((tokens, cut), lambda i: (0, jnp.minimum(i, tiles - 1))),
            jax.ShapeDtypeStruct((tokens, hidden_units), BF16),
        ),
        (
            pl.BlockSpec((tokens, cut), lambda i: (0, back(i))),
            jax.ShapeDtypeStruct((tokens, hidden_units), BF16),
        ),
        result((tokens, width), BF16),
        result((tokens, width), BF16),
        result((tokens, width), BF16),
        result((groups, tokens, width // groups), BF16),
        result((tokens, width)),
        result((1, width)),
        result((1, width)),
        result((small, width)),
        result((small, coefs)),
        result((1, coefs)),
    ]
    return pl.pallas_call(
        functools.partial(feed_kernel, tiles=tiles, strip=min(512, tokens)),
        grid=(2 * tiles,),
        in_specs=[
            whole(res),
            whole(ctx),
            whole(wo),
            pl.BlockSpec((width, cut), lambda i: (0, lax.rem(i, tiles))),
            pl.BlockSpec((cut, width), lambda i: (lax.rem(i, tiles), 0)),
            whole(gain),
            whole(bias),
            whole(w1),
            whole(w2),
            whole(mb),
            whole(og),
            whole(cg),
        ],
        out_specs=[spec for spec, _ in outs],
        out_shape=[shape for _, shape in outs],
        scratch_shapes=[
            pltpu.VMEM((tokens, width), F32),
            pltpu.VMEM((tokens, width), F32),
            pltpu.VMEM((tiles, tokens, cut), F32),
            pltpu.VMEM((tokens, width), BF16),
            pltpu.VMEM((tokens, width), BF16),
            pltpu.VMEM((coefs, tokens), F32),
        ],
        compiler_params=params(58),
        cost_estimate=pl.CostEstimate(
            flops=8 * tokens * width * hidden_units + 4 * tokens * width * width,
            bytes_accessed=8 * width * hidden_units + 4 * width * width + 20 * tokens * width,
            transcendentals=2 * tokens * hidden_units,
        ),
        name="feed",
    )(res, ctx, wo, win, wout, gain, bias, w1, w2, mb, og, cg)


def flipped(v, mask):
    bit = 1
    while bit <= mask:
        if mask & bit:
            v = v + bit - 2 * bit * lax.rem(v // bit, 2)
        bit *= 2
    return v


def added(out_ref, refs, rows, strip=32):
    strip = math.gcd(strip, rows)

    @pl.loop(0, rows // strip)
    def _(i):
        at = pl.ds(pl.multiple_of(i * strip, strip), strip)
        total = refs[0][at].astype(F32)
        for ref in refs[1:]:
            total = total + ref[at].astype(F32)
        out_ref[at] = total.astype(out_ref.dtype)


class Remote:
    def __init__(self, send, recv):
        self.send, self.recv, self.used = send, recv, 0

    def start(self, src, dst, where):
        copy = self.make(src, dst, where)
        copy.start()
        return copy

    def make(self, src, dst, where):
        copy = pltpu.make_async_remote_copy(
            src_ref=src,
            dst_ref=dst,
            send_sem=self.send.at[self.used],
            recv_sem=self.recv.at[self.used],
            device_id=where,
            device_id_type=MESH,
        )
        self.used += 1
        return copy


class Chain:
    def __init__(self, remote, n):
        self.remote, self.n = remote, n
        self.me = lax.axis_index("ctx")
        place = lax.rem(self.me, 4)
        self.outer = jnp.logical_or(place == 0, place == 3)
        self.inner = jnp.logical_not(self.outer)
        self.pieces = []
        self.started = 0

    def add(self, work, out, land, own, crosses):
        there = {"ctx": flipped(self.me, 1)}
        up = self.remote.make(work, land, there)
        masks = [3]
        bit = 4
        while bit < self.n:
            masks.append(bit)
            bit *= 2
        across = [
            self.remote.make(own.at[i], crosses.at[i], {"ctx": flipped(self.me, mask)})
            for i, mask in enumerate(masks)
        ]
        down = self.remote.make(out, out, there)
        self.pieces.append((work, out, land, own, crosses, up, across, down))

    def start(self):
        if self.started < len(self.pieces):
            up = self.pieces[self.started][5]

            @pl.when(self.outer)
            def _():
                up.start()

        self.started += 1

    def step(self, c):
        work, _, land, own, _, up, across, _ = self.pieces[c]

        @pl.when(self.outer)
        def _():
            up.wait_send()

        self.start()

        @pl.when(self.inner)
        def _():
            up.wait_recv()
            added(own.at[0], [work, land], work.shape[0])
            across[0].start()

        if c >= 1:
            self.leave(c - 1)

    def leave(self, c):
        _, out, _, own, crosses, _, across, down = self.pieces[c]

        @pl.when(self.inner)
        def _():
            for i, copy in enumerate(across):
                copy.wait()
                last = i + 1 == len(across)
                to = out if last else own.at[i + 1]
                added(to, [own.at[i], crosses.at[i]], out.shape[0])
                if not last:
                    across[i + 1].start()
            down.start()

    def end(self, c):
        down = self.pieces[c][7]

        @pl.when(self.outer)
        def _():
            down.wait_recv()

        @pl.when(self.inner)
        def _():
            down.wait_send()

    @staticmethod
    def levels(n):
        return max(1, n.bit_length() - 2)


def piece_sizes(heights):
    return [[h // 4] * 4 for h in heights[:2]] + [[h] for h in heights[2:]]


def chain_scratch(n, rows, cols):
    levels = Chain.levels(n)
    return [
        pltpu.VMEM((rows, cols), BF16),
        pltpu.VMEM((levels, rows, cols), BF16),
        pltpu.VMEM((levels, rows, cols), BF16),
    ]


class ChipSum:
    def __init__(self, remote, nf, terms, keep, got, part):
        self.remote, self.nf, self.terms = remote, nf, terms
        self.keep, self.got, self.part = keep, got, part
        self.f = lax.axis_index("fsdp")
        self.chip, self.core = self.f // 2, lax.rem(self.f, 2)
        self.rows = got.shape[1]
        self.half = self.rows // 2
        bits = []
        bit = 1
        while bit < nf // 2:
            bits.append(bit)
            bit *= 2
        self.orders = (bits, bits[::-1])
        self.level = len(bits) - 1
        self.slots = 0

    def cores(self):
        self.copy = self.remote.start(
            self.terms.at[:, 1 - self.core], self.got, {"fsdp": flipped(self.f, 1)}
        )

    def masks(self, which, level):
        found = [0]
        for bit in self.orders[which][:level]:
            found += [mask + bit for mask in found]
        return found

    def piece(self, which, chip):
        return self.got.at[chip, pl.ds(which * self.half, self.half)]

    def launch(self):
        self.flying = []
        for which in range(2):
            bit = self.orders[which][self.level]
            to = 2 * flipped(self.chip, bit) + self.core
            for mask in self.masks(which, self.level):
                landing = self.part.at[self.slots]
                self.slots += 1
                copy = self.remote.start(
                    self.piece(which, flipped(self.chip, mask + bit)), landing, {"fsdp": to}
                )
                self.flying.append((copy, which, mask, landing))

    def cross(self):
        self.copy.wait()
        for k in range(self.nf // 2):
            added(self.got.at[k], [self.keep.at[k], self.got.at[k]], self.rows)
        self.launch()

    def relay(self):
        while self.level > 0:
            for copy, which, mask, landing in self.flying:
                copy.wait()
                here = self.piece(which, flipped(self.chip, mask))
                added(here, [here, landing], self.half)
            self.level -= 1
            self.launch()

    def total(self, out):
        for copy, which, _, landing in self.flying:
            copy.wait()
            added(
                out.at[pl.ds(which * self.half, self.half)],
                [self.piece(which, self.chip), landing],
                self.half,
            )

    @staticmethod
    def count(nf):
        return 1 + 2 * (nf // 2 - 1)


def chip_scratch(nf, rows, cols):
    chips = nf // 2
    return [
        pltpu.VMEM((chips, rows, cols), BF16),
        pltpu.VMEM((chips, rows, cols), BF16),
        pltpu.VMEM((2 * chips - 2, rows // 2, cols), BF16),
    ]


def greet_all(n, nf):
    z, f = lax.axis_index("ctx"), lax.axis_index("fsdp")
    barrier = pltpu.get_barrier_semaphore()
    for k in range(1, nf):
        pl.semaphore_signal(
            barrier, inc=1, device_id={"fsdp": lax.rem(f + k, nf)}, device_id_type=MESH
        )
    for k in range(1, n):
        pl.semaphore_signal(
            barrier, inc=1, device_id={"ctx": lax.rem(z + k, n)}, device_id_type=MESH
        )
    pl.semaphore_wait(barrier, nf + n - 2)


def place_segments(ids_ref, row, column, block):
    seqs, _, half = ids_ref.shape
    n = half // block
    for s in range(seqs):
        row[s, :, 0:half] = ids_ref[s, 0:1].astype(F32)
        for b in range(n):
            at = slice((n - 1 - b) * block, (n - b) * block)
            to = slice(half + b * block, half + (b + 1) * block)
            row[s, :, to] = ids_ref[s, 1:2, at].astype(F32)
        column[s] = jnp.broadcast_to(row[s], (8, 2 * half)).T


def mix_columns(mix_ref, mixes, t):
    block = mix_ref.shape[4]
    tile = mixes.shape[0]
    per = tile // block
    parts = []
    for i in range(t * per, (t + 1) * per):
        rows = [mix_ref[a, :, i // 2, i % 2, :] for a in range(mix_ref.shape[0])]
        parts.append(jnp.concatenate(rows, axis=0))
    mixes[...] = (parts[0] if per == 1 else jnp.concatenate(parts, axis=1)).T


class PlaneGather:
    def __init__(self, remote, nf, src, out):
        self.remote, self.nf, self.src, self.out = remote, nf, src, out
        self.f = lax.axis_index("fsdp")
        self.half = src.shape[0] // 2
        bits = []
        bit = 2
        while bit < nf:
            bits.append(bit)
            bit *= 2
        self.orders = (bits, bits[::-1])
        self.levels = len(bits)
        self.flying = {}
        self.inner = []

    def masks(self, which, level):
        found = [0]
        for bit in self.orders[which][:level]:
            found += [mask + bit for mask in found]
        return found

    def place(self, which, shard):
        return self.out.at[shard, pl.ds(which * self.half, self.half)]

    def launch(self, which, level, mask):
        shard = flipped(self.f, mask)
        here = self.src.at[pl.ds(which * self.half, self.half)]
        if mask:
            here = self.place(which, shard)
        to = flipped(self.f, self.orders[which][level])
        self.flying[which, level, mask] = self.remote.start(
            here, self.place(which, shard), {"fsdp": to}
        )

    def begin(self, sem):
        for level in range(self.levels):
            for which in range(2):
                self.launch(which, level, 0)
        self.inner.append(
            self.remote.start(self.src, self.out.at[self.f], {"fsdp": flipped(self.f, 1)})
        )
        self.own = pltpu.make_async_copy(self.src, self.out.at[self.f], sem)
        self.own.start()

    def relay(self, level):
        for which in range(2):
            order = self.orders[which]
            for mask in self.masks(which, level):
                self.flying[which, level, mask].wait()
                arrived = mask + order[level]
                for later in range(level + 1, self.levels):
                    self.launch(which, later, arrived)
                place = self.place(which, flipped(self.f, arrived))
                self.inner.append(self.remote.start(place, place, {"fsdp": flipped(self.f, 1)}))

    def end(self):
        self.own.wait()
        for copy in self.inner:
            copy.wait()

    @staticmethod
    def count(nf):
        return 2 * (nf // 2 - 1) + 2 * (nf // 2 - 1) + 1


def front_tile(e, mixes, st, g_ref, b_ref, normed, hats, scales, res, first, strip=16):
    count, tile, width = e.shape
    inv = 1.0 / width

    @pl.loop(0, tile // strip)
    def _(i):
        rows = pl.ds(pl.multiple_of(i * strip, strip), strip)
        mix = mixes[rows]
        for pair in ((0, 1), (2, 3)):
            totals = [None, None]
            for j in range(count):
                part = e[j, rows].astype(F32)
                for slot, s in enumerate(pair):
                    term = part * mix[:, s * count + j : s * count + j + 1]
                    totals[slot] = term if j == 0 else totals[slot] + term
            for slot, s in enumerate(pair):
                st[s, rows] = totals[slot]

    to = slice(first, first + tile)
    lane = lax.broadcasted_iota(jnp.int32, (tile, LANES), 1)
    kept = jnp.zeros((tile, LANES), F32)
    for s in range(3):
        v = st[s]
        center = v - jnp.sum(v, axis=-1, keepdims=True) * inv
        spread = jnp.sum(center * center, axis=-1, keepdims=True) * inv
        scale = lax.rsqrt(spread + EPSILON)
        hat = center * scale
        hats[s, to] = hat.astype(BF16)
        normed[s, to] = (hat * g_ref[s : s + 1] + b_ref[s : s + 1]).astype(BF16)
        kept = jnp.where(lane == s, scale, kept)
    scales[to] = kept
    res[to] = st[3]


def attend_pair(qkv, out, column_ref, row_ref, seq, lanes, part=None):
    blocks, block = out.shape[1], out.shape[2]
    length = blocks * block
    rows = row_tile(length)
    per = rows // block

    def load(kind, first, last):
        return qkv[kind, seq, first:last, :, lanes].reshape(-1, LANES)

    count = length // rows
    if part is None:
        which = range(count)
    else:
        which = range(part * count // 2, (part + 1) * count // 2)
    for i in which:
        first, until = i * rows, (i + 1) * rows
        b0, b1 = i * per, (i + 1) * per
        query = first + lax.broadcasted_iota(jnp.int32, (rows, until), 0)
        key = lax.broadcasted_iota(jnp.int32, (rows, until), 1)
        same = column_ref[seq, first:until, 0:1] == row_ref[seq, 0:1, 0:until]
        allowed = same & (key <= query)
        q = load(0, b0, b1) * BF16(HD**-0.5)
        k = load(1, 0, b1)
        v = load(2, 0, b1)
        total = None
        for h in range(LANES // HD):
            scores = jnp.where(allowed, dot(only(q, h), k, NT), MASKED)
            peak = jnp.max(scores, axis=-1, keepdims=True)
            raised = jnp.exp(scores - peak)
            mass = jnp.sum(raised, axis=-1, keepdims=True)
            probs = (raised * (1.0 / mass)).astype(BF16)
            part = dot(probs, v)
            part = jnp.where(head_lanes(part.shape, h), part, 0.0)
            total = part if total is None else total + part
        out[seq, b0:b1, :, lanes] = total.astype(BF16).reshape(per, block, LANES)


def forward_kernel(
    n,
    nf,
    e_ref,
    wqkv_ref,
    wo_ref,
    win_ref,
    wout_ref,
    mix_ref,
    gain_ref,
    bias_ref,
    c_ref,
    s_ref,
    ids_ref,
    normed_ref,
    hats_ref,
    scales_ref,
    res_ref,
    gqkv_ref,
    go_ref,
    gin_ref,
    gout_ref,
    qkv_ref,
    ctx_ref,
    e,
    mixes,
    st,
    normed,
    hats,
    scales,
    res,
    w,
    raw,
    shares,
    qkv,
    heads,
    row,
    column,
    send,
    recv,
    local,
    e_sem,
):
    f, z = lax.axis_index("fsdp"), lax.axis_index("ctx")
    count, tokens, width = e_ref.shape
    tile = e.shape[2]
    tiles = tokens // tile
    seqs, _, block, cols = heads.shape
    seq_rows = 2 * block
    cut = raw.shape[1]
    remote = Remote(send, recv)
    spots = (z, 2 * n - 1 - z)
    mine = pl.ds(pl.multiple_of(z * cols, LANES), cols)

    def fetch(t):
        return pltpu.make_async_copy(
            e_ref.at[:, t * tile : (t + 1) * tile], e.at[t % 2], e_sem.at[t % 2]
        )

    fetch(0).start()
    greet_all(n, nf)

    def columns(ref, i):
        at = pl.ds(i * width, width)
        return ref.at[:, at] if len(ref.shape) == 2 else ref.at[:, :, at]

    parts = [
        PlaneGather(remote, nf, columns(wqkv_ref, i), columns(w, i)) for i in range(3)
    ]
    others = [
        PlaneGather(remote, nf, win_ref, gin_ref),
        PlaneGather(remote, nf, wout_ref, gout_ref),
        PlaneGather(remote, nf, wo_ref, go_ref),
    ]
    levels = parts[0].levels
    parts[0].begin(local.at[0])

    def do_tile(t):
        fetch(t).wait()
        if t + 1 < tiles:
            fetch(t + 1).start()
        mix_columns(mix_ref, mixes, t)
        front_tile(
            e.at[t % 2], mixes, st, gain_ref, bias_ref, normed, hats, scales, res, t * tile
        )

    def first_hops():
        parts[0].relay(0)
        parts[1].begin(local.at[1])

    def second_hops():
        for level in range(1, levels):
            parts[0].relay(level)

    for t in range(tiles):
        do_tile(t)
        if t == 0:
            first_hops()
        if t == max(1, tiles - 2):
            second_hops()
    own_tables = []
    for table in (c_ref, s_ref):
        early = table[pl.ds(pl.multiple_of(z * block, block), block)]
        late = table[pl.ds(pl.multiple_of((2 * n - 1 - z) * block, block), block)]
        own_tables.append((early, late))

    def project(i):
        @pl.loop(0, width // cut)
        def _(j):
            at = pl.ds(pl.multiple_of(i * width + j * cut, cut), cut)
            raw[...] = dot(normed[i], w[:, :, at].reshape(width, cut))
            for s in range(seqs):
                for h in range(2):
                    first = s * seq_rows + h * block
                    for c in range(cut // LANES):
                        x = raw[first : first + block, c * LANES : (c + 1) * LANES]
                        if i < 2:
                            x = turned(x, own_tables[0][h], own_tables[1][h])
                        to = c * LANES % cols
                        group = j * (cut // cols) + c * LANES // cols
                        shares[i, group, s, h, :, to : to + LANES] = x.astype(BF16)

    pairs = cols // LANES
    units = [(0, None)] + [(s, p) for s in range(1, seqs) for p in range(pairs)]
    arriving = {unit: [] for unit in units}
    kept = []

    def give(kind, unit):
        s, p = unit
        lanes = slice(None) if p is None else slice(p * LANES, (p + 1) * LANES)
        for k in range(1, n):
            to = lax.rem(z + k, n)
            for h in range(2):
                arriving[unit].append(
                    remote.start(
                        shares.at[kind, to, s, h, :, lanes],
                        qkv.at[kind, s, spots[h], :, lanes],
                        {"ctx": to},
                    )
                )

    for i in range(3):
        parts[i].end()
        project(i)
        give(i, units[0])
        if i < 2:
            for level in range(levels):
                parts[i + 1].relay(level)
                if level == 0:
                    (parts[2], others[0])[i].begin(local.at[2 + i])
    for h in range(2):
        copy = pltpu.make_async_copy(
            shares.at[:, z, :, h], qkv.at[:, :, spots[h]], local.at[8 + h]
        )
        copy.start()
        kept.append(copy)
    for unit in units[1:2]:
        give(slice(None), unit)
    others[1].begin(local.at[4])
    others[2].begin(local.at[5])
    out_copies = [
        pltpu.make_async_copy(w, gqkv_ref, local.at[10]),
        pltpu.make_async_copy(normed, normed_ref, local.at[6]),
        pltpu.make_async_copy(res, res_ref, local.at[7]),
        pltpu.make_async_copy(hats, hats_ref, local.at[12]),
        pltpu.make_async_copy(scales, scales_ref, local.at[13]),
    ]
    for copy in out_copies:
        copy.start()
    place_segments(ids_ref, row, column, block)

    others[0].relay(0)
    for copy in kept:
        copy.wait()
    leaving = []
    stored = 14
    for index, unit in enumerate(units):
        for copy in arriving[unit]:
            copy.wait()
        for other in units[index + 2 : index + 3]:
            give(slice(None), other)
        s, p = unit
        if p is None:

            @pl.loop(0, pairs)
            def _(p):
                lanes = pl.ds(pl.multiple_of(p * LANES, LANES), LANES)
                attend_pair(qkv, heads, column, row, s, lanes)

            there, here = mine, slice(None)
        else:
            here = slice(p * LANES, (p + 1) * LANES)
            there = pl.ds(pl.multiple_of(z * cols + p * LANES, LANES), LANES)
        halves_apart = index + 1 == len(units) and p is not None
        if p is not None and not halves_apart:
            attend_pair(qkv, heads, column, row, s, here)
        for h in range(2):
            if halves_apart:
                attend_pair(qkv, heads, column, row, s, here, h)
            for k in range(1, n):
                to = lax.rem(z + k, n)
                spot = to if h == 0 else 2 * n - 1 - to
                leaving.append(
                    remote.start(
                        heads.at[s, spot, :, here], ctx_ref.at[s, h, :, there], {"ctx": to}
                    )
                )
        for h in range(2):
            copy = pltpu.make_async_copy(
                heads.at[s, spots[h], :, here], ctx_ref.at[s, h, :, there], local.at[stored]
            )
            stored += 1
            copy.start()
            out_copies.append(copy)
        if index == 0:
            others[1].relay(0)
            others[2].relay(0)
            for level in range(1, levels):
                others[0].relay(level)
    copy = pltpu.make_async_copy(qkv, qkv_ref, local.at[11])
    copy.start()
    out_copies.append(copy)
    for level in range(1, levels):
        others[1].relay(level)
        others[2].relay(level)
    for gather in others:
        gather.end()
    for copy in out_copies + leaving:
        copy.wait()


def forward(e, mix, w_qkv, w_o, w_in, w_out, gain, bias, cosine, sine, ids, n, nf):
    count, tokens, width = e.shape
    seqs, block = mix.shape[2], mix.shape[4]
    length = 2 * n * block
    cols = width // n
    spots = 2 * n
    tile = 128
    cut = max(cols, 512)
    rows = width // nf
    units = 1 + (seqs - 1) * (cols // LANES)
    copies = 6 * PlaneGather.count(nf) + (2 + 2 * units) * 2 * (n - 1)
    vmem = pl.BlockSpec(memory_space=pltpu.VMEM)
    hbm = pl.BlockSpec(memory_space=pltpu.HBM)

    def gathered(x):
        return jax.ShapeDtypeStruct((nf,) + x.shape, x.dtype)

    normed, hats, scales, res, g_qkv, g_o, g_in, g_out, qkv, ctx = pl.pallas_call(
        functools.partial(forward_kernel, n, nf),
        in_specs=[hbm] * 5 + [vmem] * 6,
        out_specs=[hbm] * 10,
        out_shape=[
            jax.ShapeDtypeStruct((3, tokens, width), BF16),
            jax.ShapeDtypeStruct((3, tokens, width), BF16),
            jax.ShapeDtypeStruct((tokens, LANES), F32),
            jax.ShapeDtypeStruct((tokens, width), F32),
            gathered(w_qkv),
            gathered(w_o),
            gathered(w_in),
            gathered(w_out),
            jax.ShapeDtypeStruct((3, seqs, spots, block, cols), BF16),
            jax.ShapeDtypeStruct((seqs, 2, block, width), BF16),
        ],
        scratch_shapes=[
            pltpu.VMEM((2, count, tile, width), BF16),
            pltpu.VMEM((tile, 4 * count), F32),
            pltpu.VMEM((4, tile, width), F32),
            pltpu.VMEM((3, tokens, width), BF16),
            pltpu.VMEM((3, tokens, width), BF16),
            pltpu.VMEM((tokens, LANES), F32),
            pltpu.VMEM((tokens, width), F32),
            pltpu.VMEM((nf, rows, 3 * width), BF16),
            pltpu.VMEM((tokens, cut), F32),
            pltpu.VMEM((3, n, seqs, 2, block, cols), BF16),
            pltpu.VMEM((3, seqs, spots, block, cols), BF16),
            pltpu.VMEM((seqs, spots, block, cols), BF16),
            pltpu.VMEM((seqs, 1, length), F32),
            pltpu.VMEM((seqs, length, 8), F32),
            pltpu.SemaphoreType.DMA((copies,)),
            pltpu.SemaphoreType.DMA((copies,)),
            pltpu.SemaphoreType.DMA((14 + 2 * units,)),
            pltpu.SemaphoreType.DMA((2,)),
        ],
        compiler_params=params(58, collective_id=0, has_side_effects=True),
        name="forward",
    )(e, w_qkv, w_o, w_in, w_out, mix, gain, bias, cosine, sine, ids)

    def whole(x):
        return x.reshape(x.shape[0] * x.shape[1], x.shape[2])

    weights = [whole(g) for g in (g_qkv, g_o, g_in, g_out)]
    return normed, hats, scales, res, *weights, qkv, ctx.reshape(tokens, width)


def attend_back_pair(qkv, grad, out, dk, dv, column_ref, row_ref, c_ref, s_ref, seq, lanes):
    blocks, block = grad.shape[1], grad.shape[2]
    length = blocks * block
    rows = row_tile(length)
    per = rows // block
    factor = HD**-0.5

    def load(ref, at, first, last):
        return ref[(*at, slice(first, last), slice(None), lanes)].reshape(-1, LANES)

    for i in range(length // rows):
        here = slice(i * rows, (i + 1) * rows)
        dk[here] = jnp.zeros((rows, LANES), F32)
        dv[here] = jnp.zeros((rows, LANES), F32)
    for i in range(length // rows):
        first, until = i * rows, (i + 1) * rows
        b0, b1 = i * per, (i + 1) * per
        query = first + lax.broadcasted_iota(jnp.int32, (rows, until), 0)
        key = lax.broadcasted_iota(jnp.int32, (rows, until), 1)
        same = column_ref[seq, first:until, 0:1] == row_ref[seq, 0:1, 0:until]
        allowed = same & (key <= query)
        q = load(qkv, (0, seq), b0, b1) * BF16(factor)
        g = load(grad, (seq,), b0, b1)
        k = load(qkv, (1, seq), 0, b1)
        v = load(qkv, (2, seq), 0, b1)
        total = None
        for h in range(LANES // HD):
            q_h = only(q, h)
            g_h = only(g, h)
            scores = jnp.where(allowed, dot(q_h, k, NT), MASKED)
            peak = jnp.max(scores, axis=-1, keepdims=True)
            raised = jnp.exp(scores - peak)
            mass = jnp.sum(raised, axis=-1, keepdims=True)
            probs = raised * (1.0 / mass)
            dots = dot(g_h, v, NT)
            center = jnp.sum(probs * dots, axis=-1, keepdims=True)
            slope = (probs * (dots - center)).astype(BF16)
            part = dot(slope, k)
            part = jnp.where(head_lanes(part.shape, h), part, 0.0)
            total = part if total is None else total + part
            dk[0:until] += dot(slope, q_h, TN)
            dv[0:until] += dot(probs.astype(BF16), g_h, TN)
        cosine, sine = c_ref[first:until], s_ref[first:until]
        low = turned(total * factor, cosine, -sine).astype(BF16)
        out[0, seq, b0:b1, :, lanes] = low.reshape(per, block, LANES)
    for i in range(length // rows):
        here = slice(i * rows, (i + 1) * rows)
        b0, b1 = i * per, (i + 1) * per
        low = turned(dk[here], c_ref[here], -s_ref[here]).astype(BF16)
        out[1, seq, b0:b1, :, lanes] = low.reshape(per, block, LANES)
        out[2, seq, b0:b1, :, lanes] = dv[here].astype(BF16).reshape(per, block, LANES)


def back_kernel(
    n,
    nf,
    cg_ref,
    qkv_ref,
    active_ref,
    lowered_ref,
    normed_ref,
    branch_ref,
    ctx_ref,
    attention_ref,
    ids_ref,
    c_ref,
    s_ref,
    grads_ref,
    in_sum,
    out_sum,
    o_sum,
    qkv,
    grad,
    back,
    dk,
    dv,
    in_terms,
    in_got,
    in_part,
    out_terms,
    out_got,
    out_part,
    o_terms,
    o_got,
    o_part,
    normed,
    branch,
    ctx,
    attention,
    low_tiles,
    active_tiles,
    row,
    column,
    tile_sem,
    send,
    recv,
    local,
):
    f, z = lax.axis_index("fsdp"), lax.axis_index("ctx")
    core = lax.rem(f, 2)
    seqs, _, block, cols = grad.shape
    remote = Remote(send, recv)
    sums = [
        ChipSum(remote, nf, in_terms, in_terms.at[:, core], in_got, in_part),
        ChipSum(remote, nf, out_terms, out_terms.at[:, core], out_got, out_part),
        ChipSum(remote, nf, o_terms, o_terms.at[:, core], o_got, o_part),
    ]
    spots = (z, 2 * n - 1 - z)
    mine = pl.ds(pl.multiple_of(z * cols, LANES), cols)

    def fetch(ref, tiles, sem, t):
        size = tiles.shape[2]
        slot = lax.rem(t, 2)
        at = pl.ds(pl.multiple_of(t * size, LANES), size)
        return pltpu.make_async_copy(ref.at[:, at], tiles.at[slot], tile_sem.at[sem + slot])

    wholes = [(ctx_ref, ctx), (attention_ref, attention), (normed_ref, normed), (branch_ref, branch)]
    loads = [
        pltpu.make_async_copy(ref, there, local.at[i]) for i, (ref, there) in enumerate(wholes)
    ]
    for load in loads[:3]:
        load.start()
    fetch(lowered_ref, low_tiles, 0, 0).start()
    loads[3].start()
    fetch(active_ref, active_tiles, 2, 0).start()
    later = [pltpu.make_async_copy(qkv_ref, qkv, local.at[6 + 2 * seqs])]
    for h in range(2):
        later.append(
            pltpu.make_async_copy(cg_ref.at[z, :, h], grad.at[:, spots[h]], local.at[4 + h])
        )
    for load in later:
        load.start()

    greet_all(n, nf)

    arriving = []

    def take(s):
        copies = []
        for k in range(1, n):
            to = lax.rem(z + k, n)
            for h in range(2):
                copies.append(
                    remote.start(cg_ref.at[to, s, h], grad.at[s, spots[h]], {"ctx": to})
                )
        arriving.append(copies)

    def each_tile(ref, tiles, sem, work):
        count = ref.shape[1] // tiles.shape[2]

        @pl.loop(0, count)
        def _(t):
            fetch(ref, tiles, sem, t).wait()

            @pl.when(t + 1 < count)
            def _():
                fetch(ref, tiles, sem, t + 1).start()

            work(t, tiles[lax.rem(t, 2)])

    def in_tile(t, low):
        chips, _, rows, _ = in_terms.shape
        size = low.shape[1]
        at = pl.ds(pl.multiple_of(t * size, LANES), size)
        value = dot(normed[...], low, TN).astype(BF16)
        in_terms[:, :, :, at] = value.reshape(chips, 2, rows, size)

    def out_tile(t, active):
        _, _, rows, width = out_terms.shape
        out_terms[t] = dot(active, branch[...], TN).astype(BF16).reshape(2, rows, width)

    take(0)
    loads[0].wait()
    loads[1].wait()
    o_terms[...] = dot(ctx[...], attention[...], TN).astype(BF16).reshape(o_terms.shape)
    sums[2].cores()
    loads[2].wait()
    each_tile(lowered_ref, low_tiles, 0, in_tile)
    sums[0].cores()
    sums[2].cross()
    for s in range(1, seqs):
        take(s)
    loads[3].wait()
    each_tile(active_ref, active_tiles, 2, out_tile)
    sums[1].cores()
    place_segments(ids_ref, row, column, block)
    sums[0].cross()
    for load in later:
        load.wait()

    leaving = []
    kept = []

    def hand(s, here, there):
        for k in range(1, n):
            to = lax.rem(z + k, n)
            for h in range(2):
                spot = to if h == 0 else 2 * n - 1 - to
                leaving.append(
                    remote.start(
                        back.at[:, s, spot, :, here],
                        grads_ref.at[:, s, h, :, there],
                        {"ctx": to},
                    )
                )

    for s in range(seqs):
        for copy in arriving[s]:
            copy.wait()
        if s == 0:
            for p in range(cols // LANES):
                here = slice(p * LANES, (p + 1) * LANES)
                attend_back_pair(qkv, grad, back, dk, dv, column, row, c_ref, s_ref, s, here)
                hand(s, here, pl.ds(pl.multiple_of(z * cols + p * LANES, LANES), LANES))
        else:

            @pl.loop(0, cols // LANES)
            def _(p):
                lanes = pl.ds(pl.multiple_of(p * LANES, LANES), LANES)
                attend_back_pair(qkv, grad, back, dk, dv, column, row, c_ref, s_ref, s, lanes)

            hand(s, slice(None), mine)
        for h in range(2):
            copy = pltpu.make_async_copy(
                back.at[:, s, spots[h]], grads_ref.at[:, s, h, :, mine], local.at[6 + 2 * s + h]
            )
            copy.start()
            kept.append(copy)
        if s == 0:
            sums[2].relay()
            sums[1].cross()
            sums[0].relay()

    sums[1].relay()
    for chip_sum, out in zip(sums, (in_sum, out_sum, o_sum)):
        chip_sum.total(out)
    for copy in kept + leaving:
        copy.wait()


def attention_back(context_grad, qkv, saved, ids, cosine, sine, n, nf):
    _, seqs, spots, block, cols = qkv.shape
    length = spots * block
    tokens, units = saved[0].shape
    width = saved[2].shape[1]
    chips = nf // 2
    shapes = [(width // nf, units), (units // nf, width), (width // nf, width)]
    copies = (2 * seqs + cols // LANES - 1) * 2 * (n - 1) + 3 * ChipSum.count(nf)
    copies += 2 * (n - 1)
    vmem = pl.BlockSpec(memory_space=pltpu.VMEM)
    hbm = pl.BlockSpec(memory_space=pltpu.HBM)
    scratch = []
    for rows, wide in shapes:
        scratch.append(pltpu.VMEM((chips, 2, rows, wide), BF16))
        scratch += chip_scratch(nf, rows, wide)[1:]
    grads, *owned = pl.pallas_call(
        functools.partial(back_kernel, n, nf),
        in_specs=[hbm] * 8 + [vmem] * 3,
        out_specs=[hbm, vmem, vmem, vmem],
        out_shape=[jax.ShapeDtypeStruct((3, seqs, 2, block, width), BF16)]
        + [jax.ShapeDtypeStruct(shape, BF16) for shape in shapes],
        scratch_shapes=[
            pltpu.VMEM((3, seqs, spots, block, cols), BF16),
            pltpu.VMEM((seqs, spots, block, cols), BF16),
            pltpu.VMEM((3, seqs, spots, block, cols), BF16),
            pltpu.VMEM((length, LANES), F32),
            pltpu.VMEM((length, LANES), F32),
            *scratch,
            *[pltpu.VMEM((tokens, width), BF16)] * 4,
            pltpu.VMEM((2, tokens, 512), BF16),
            pltpu.VMEM((2, tokens, units // chips), BF16),
            pltpu.VMEM((seqs, 1, length), F32),
            pltpu.VMEM((seqs, length, 8), F32),
            pltpu.SemaphoreType.DMA((4,)),
            pltpu.SemaphoreType.DMA((copies,)),
            pltpu.SemaphoreType.DMA((copies,)),
            pltpu.SemaphoreType.DMA((7 + 2 * seqs,)),
        ],
        compiler_params=params(62, collective_id=2, has_side_effects=True),
        name="attention_back",
    )(
        context_grad.reshape(n, seqs, 2, block, cols),
        qkv,
        *saved,
        ids,
        cosine,
        sine,
    )
    return grads.reshape(3, seqs * 2 * block, width), owned


def norm_back_tile(hats, scales, ng, st, e, mg, mg_ref, g_ref, h, low, dgain, dbias, selector, t, strip=16):
    count, tile, width = e.shape
    inv = 1.0 / width
    to = slice(t * tile, (t + 1) * tile)
    for s in range(3):
        dy = ng[s]
        hat = hats[s, to].astype(F32)
        scale = scales[to, s : s + 1]
        dgain[s : s + 1] += jnp.sum(dy * hat, axis=0, keepdims=True)
        dbias[s : s + 1] += jnp.sum(dy, axis=0, keepdims=True)
        dh = dy * g_ref[s : s + 1]
        mean = jnp.sum(dh, axis=-1, keepdims=True) * inv
        along = jnp.sum(dh * hat, axis=-1, keepdims=True) * inv
        out = (scale * (dh - mean - hat * along)).astype(BF16)
        low[s, to] = out
        st[s] = out
    st[3] = h[to].astype(BF16)

    shape = (4 * strip, count * strip)
    same = lax.rem(lax.broadcasted_iota(jnp.int32, shape, 0), strip) == lax.rem(
        lax.broadcasted_iota(jnp.int32, shape, 1), strip
    )
    for i in range(tile // strip):
        rows = slice(i * strip, (i + 1) * strip)
        grads = st[:, rows].reshape(4 * strip, width)
        inputs = e[:, rows].reshape(count * strip, width)
        products = jnp.where(same, dot(grads, inputs, NT), 0.0)
        wide = jnp.concatenate(
            [products[s * strip : (s + 1) * strip] for s in range(4)], axis=1
        )
        high, rest = halves(wide)
        mg[rows] = dot(high, selector[...]) + dot(rest, selector[...])
    turned_mg = mg[...].T
    block = mg_ref.shape[4]
    per = tile // block
    for i in range(per):
        place = t * per + i
        for a in range(4):
            mg_ref[a, :, place // 2, place % 2, :] = turned_mg[
                a * count : (a + 1) * count, i * block : (i + 1) * block
            ]


def small_squares(rows, cols):
    first = 8 + rows
    places = []
    for g in range(-(-rows // 8)):
        size = min(8, rows - 8 * g)
        places.append(
            (
                slice(first, first + size),
                slice(g * LANES, g * LANES + cols),
                slice(8 * g, 8 * g + size),
            )
        )
    return places


def small_line_at(rows, cols):
    groups = -(-rows // 8)
    return slice(groups * LANES, groups * LANES + cols)


def end_kernel(
    n,
    nf,
    grads_ref,
    normed_ref,
    hats_ref,
    scales_ref,
    e_ref,
    w_ref,
    h_ref,
    gain_ref,
    in_ref,
    out_ref,
    o_ref,
    sgain_ref,
    sbias_ref,
    sw1_ref,
    sw2_ref,
    smb_ref,
    low_ref,
    mg_ref,
    q_sum,
    k_sum,
    v_sum,
    in_sum,
    out_sum,
    o_sum,
    small_sum,
    grads,
    normed,
    hats,
    scales,
    w,
    h,
    e,
    ng,
    st,
    low,
    mg,
    selector,
    dgain,
    dbias,
    small_work,
    small_in,
    small_term,
    small_land,
    small_own,
    small_cross,
    send,
    recv,
    local,
    e_sem,
    *more,
):
    f, z = lax.axis_index("fsdp"), lax.axis_index("ctx")
    core = lax.rem(f, 2)
    count, tokens, width = e_ref.shape
    tile = e.shape[2]
    tiles = tokens // tile
    remote = Remote(send, recv)
    chip_sets = [more[4 * i : 4 * i + 4] for i in range(3)]
    rest = more[12:]
    shard = chip_sets[0][1].shape[1]

    def fetch(t):
        return pltpu.make_async_copy(
            e_ref.at[:, t * tile : (t + 1) * tile], e.at[t % 2], e_sem.at[t % 2]
        )

    loads = [
        pltpu.make_async_copy(src, dst, local.at[i])
        for i, (src, dst) in enumerate(
            [
                (grads_ref, grads),
                (normed_ref, normed),
                (w_ref, w),
                (hats_ref, hats),
                (scales_ref, scales),
                (h_ref, h),
            ]
        )
    ]
    for load in loads:
        load.start()
    fetch(0).start()

    greet_all(n, nf)

    chain = Chain(remote, n)
    thin = small_in.shape[1]
    here = pl.ds(pl.multiple_of(f * thin, thin), thin)
    works = [in_ref, out_ref, o_ref] + [chip_set[3] for chip_set in chip_sets]
    results = [in_sum, out_sum, o_sum, q_sum, k_sum, v_sum]
    for work, out, sizes in zip(works, results, piece_sizes([x.shape[0] for x in works])):
        first = 0
        if work is chip_sets[0][3]:
            small_piece = len(chain.pieces)
            chain.add(small_term, small_sum.at[here], small_land, small_own, small_cross)
        for size in sizes:
            at = pl.ds(first, size)
            chain.add(work.at[at], out.at[at], *rest[:3])
            rest = rest[3:]
            first += size
    total_pieces = len(chain.pieces)
    chain.start()
    chain.start()

    loads[0].wait()
    loads[1].wait()
    cut = 256
    per = cut // (2 * shard)
    sums = []
    for i in range(3):
        terms, got, part, own = chip_sets[i]
        for c in range(width // cut):
            value = dot(normed[i, :, c * cut : (c + 1) * cut], grads[i], TN).astype(BF16)
            terms[c * per : (c + 1) * per] = value.reshape(per, 2, shard, width)
        chip_sum = ChipSum(remote, nf, terms, terms.at[:, core], got, part)
        chip_sum.cores()
        sums.append(chip_sum)
    dgain[...] = jnp.zeros_like(dgain)
    dbias[...] = jnp.zeros_like(dbias)
    size = selector.shape
    group = lax.broadcasted_iota(jnp.int32, size, 0) // 16
    selector[...] = jnp.where(
        group == lax.broadcasted_iota(jnp.int32, size, 1), 1.0, 0.0
    ).astype(BF16)
    for load in loads[2:]:
        load.wait()

    def do_tile(t):
        fetch(t).wait()
        if t + 1 < tiles:
            fetch(t + 1).start()
        rows = slice(t * tile, (t + 1) * tile)
        for i in range(3):
            ng[i] = dot(grads[i, rows], w[:, i * width : (i + 1) * width], NT)
        norm_back_tile(
            hats, scales, ng, st, e.at[t % 2], mg, mg_ref, gain_ref, h, low, dgain, dbias, selector, t
        )

    todo = list(range(tiles))

    def some():
        if todo:
            do_tile(todo.pop(0))

    chain.step(0)
    for chip_sum in sums:
        chip_sum.cross()
    chain.step(1)
    some()
    chain.step(2)
    some()
    chain.step(3)
    some()
    chain.step(4)
    while todo:
        some()
    keep = pltpu.make_async_copy(low, low_ref, local.at[6])
    keep.start()

    hidden_count, coef_count = sw2_ref.shape
    first = 8 + hidden_count
    squares = small_squares(hidden_count, coef_count)
    line_at = small_line_at(hidden_count, coef_count)
    small_work[...] = jnp.zeros_like(small_work)
    small_work[0:3] = dgain[...]
    small_work[3:4] = sgain_ref[...]
    small_work[4:7] = dbias[...]
    small_work[7:8] = sbias_ref[...]
    small_work[8:first] = sw1_ref[...]
    for rows, lanes, which in squares:
        small_work[rows, lanes] = sw2_ref[which]
    small_work[first : first + 1, line_at] = smb_ref[...]
    small_in[0] = small_work[here]
    slices = []
    for k in range(1, nf):
        to = lax.rem(f + k, nf)
        slices.append(
            remote.start(
                small_work.at[pl.ds(pl.multiple_of(to * thin, thin), thin)],
                small_in.at[k],
                {"fsdp": to},
            )
        )

    for chip_sum in sums:
        chip_sum.relay()
    chain.step(5)
    chain.step(6)
    for chip_sum, chip_set in zip(sums, chip_sets):
        chip_sum.total(chip_set[3])
    for copy in slices:
        copy.wait()
    total = small_in[0]
    for k in range(1, nf):
        total = total + small_in[k]
    small_term[...] = total
    for c in range(7, total_pieces):
        chain.step(c)
        if c == small_piece + 2:
            chain.end(small_piece)
            spread = []
            for k in range(1, nf):
                spread.append(
                    remote.start(
                        small_sum.at[here], small_sum.at[here], {"fsdp": lax.rem(f + k, nf)}
                    )
                )
    chain.leave(total_pieces - 1)
    for copy in spread:
        copy.wait()
    for c in range(total_pieces):
        if c != small_piece:
            chain.end(c)
    keep.wait()


def finish(grads, normed, hats, scales, e, w, hgrad, gain, owned, small, mix_shape, n, nf):
    count, tokens, width = e.shape
    tile = 128
    chips = nf // 2
    shard = width // nf
    rows = 8 + small[2].shape[0] + 8
    thin = 8 * -(-rows // (8 * nf))
    m_in, m_out, m_o = owned
    lines, chip_sums = [], []
    heights = [m_in.shape[0], m_out.shape[0], m_o.shape[0]] + [shard] * 3
    widths = [m_in.shape[1], m_out.shape[1], m_o.shape[1]] + [width] * 3
    planned = piece_sizes(heights)
    for sizes, wide_as in zip(planned, widths):
        for size in sizes:
            lines += chain_scratch(n, size, wide_as)
    pieces = sum(len(sizes) for sizes in planned)
    for _ in range(3):
        chip_sums += [
            pltpu.VMEM((chips, 2, shard, width), BF16),
            *chip_scratch(nf, shard, width)[1:],
            pltpu.VMEM((shard, width), BF16),
        ]
    copies = (pieces + 1) * (Chain.levels(n) + 2) + 3 * ChipSum.count(nf) + 2 * (nf - 1)
    vmem = pl.BlockSpec(memory_space=pltpu.VMEM)
    hbm = pl.BlockSpec(memory_space=pltpu.HBM)
    wide = jax.ShapeDtypeStruct((shard, width), BF16)
    return pl.pallas_call(
        functools.partial(end_kernel, n, nf),
        in_specs=[hbm] * 7 + [vmem] * 9,
        out_specs=[hbm] + [vmem] * 8,
        out_shape=[
            jax.ShapeDtypeStruct((3, tokens, width), BF16),
            jax.ShapeDtypeStruct(mix_shape, F32),
            wide,
            wide,
            wide,
            *[jax.ShapeDtypeStruct(x.shape, BF16) for x in owned],
            jax.ShapeDtypeStruct((nf * thin, width), F32),
        ],
        scratch_shapes=[
            pltpu.VMEM(grads.shape, BF16),
            pltpu.VMEM(normed.shape, BF16),
            pltpu.VMEM(hats.shape, BF16),
            pltpu.VMEM(scales.shape, F32),
            pltpu.VMEM(w.shape, BF16),
            pltpu.VMEM(hgrad.shape, F32),
            pltpu.VMEM((2, count, tile, width), BF16),
            pltpu.VMEM((3, tile, width), F32),
            pltpu.VMEM((4, tile, width), BF16),
            pltpu.VMEM((3, tokens, width), BF16),
            pltpu.VMEM((tile, LANES), F32),
            pltpu.VMEM((4 * count * 16, LANES), BF16),
            pltpu.VMEM((3, width), F32),
            pltpu.VMEM((3, width), F32),
            pltpu.VMEM((nf * thin, width), F32),
            pltpu.VMEM((nf, thin, width), F32),
            *[pltpu.VMEM((thin, width), F32)] * 2,
            *[pltpu.VMEM((Chain.levels(n), thin, width), F32)] * 2,
            pltpu.SemaphoreType.DMA((copies,)),
            pltpu.SemaphoreType.DMA((copies,)),
            pltpu.SemaphoreType.DMA((7,)),
            pltpu.SemaphoreType.DMA((2,)),
            *chip_sums,
            *lines,
        ],
        compiler_params=params(60, collective_id=3, has_side_effects=True),
        name="finish",
    )(grads, normed, hats, scales, e, w, hgrad, gain, *owned, *small)


def tail_kernel(
    low_ref,
    h_ref,
    mix_ref,
    q_ref,
    k_ref,
    v_ref,
    in_ref,
    out_ref,
    o_ref,
    small_ref,
    mg_ref,
    eg_ref,
    qkv_ref,
    in32_ref,
    out32_ref,
    o32_ref,
    gain_ref,
    bias_ref,
    w1_ref,
    w2_ref,
    mb_ref,
    mg_out_ref,
    mixes,
    *,
    strip,
):
    count, tile, width = eg_ref.shape
    chunk = 256
    block = mix_ref.shape[4]
    tiles = mix_ref.shape[2] * 2 * block // tile
    step = pl.program_id(0)
    for t in range(tiles):

        @pl.when(step == t)
        def _():
            mix_columns(mix_ref, mixes, t)

    @pl.when(step == 0)
    def _():
        hidden_count, coef_count = w2_ref.shape
        first = 8 + hidden_count
        gain_ref[...] = small_ref[0:4]
        bias_ref[...] = small_ref[4:8]
        w1_ref[...] = small_ref[8:first]
        for rows, lanes, which in small_squares(hidden_count, coef_count):
            w2_ref[which] = small_ref[rows, lanes]
        mb_ref[...] = small_ref[first : first + 1, small_line_at(hidden_count, coef_count)]
        mg_out_ref[...] = mg_ref[...]

    for i, ref in enumerate((q_ref, k_ref, v_ref)):
        qkv_ref[:, i * width : (i + 1) * width] = ref[...].astype(F32)
    in32_ref[...] = in_ref[...].astype(F32)
    out32_ref[...] = out_ref[...].astype(F32)
    o32_ref[...] = o_ref[...].astype(F32)

    @pl.loop(0, tile // strip)
    def _(i):
        rows = pl.ds(pl.multiple_of(i * strip, strip), strip)
        mix = mixes[rows]
        for c in range(width // chunk):
            cols = slice(c * chunk, (c + 1) * chunk)
            grads = [low_ref[s, rows, cols].astype(F32) for s in range(3)]
            grads.append(h_ref[rows, cols])
            for j in range(count):
                total = grads[0] * mix[:, j : j + 1]
                for s in range(1, 4):
                    total = total + grads[s] * mix[:, s * count + j : s * count + j + 1]
                eg_ref[j, rows, cols] = total.astype(BF16)


def spread_back(low, hgrad, mix, sums, small, m_grad, sizes):
    _, tokens, width = low.shape
    count = mix.shape[1]
    tile = 128
    tiles = tokens // tile
    hidden_count, coef_count = sizes

    def part(x):
        return pl.BlockSpec((x.shape[0] // tiles, x.shape[1]), lambda i: (i, 0))

    def whole(x):
        zeros = (0,) * len(x.shape)
        return once(x.shape, lambda i: zeros)

    shard = sums[0].shape[0]
    outs = [
        jax.ShapeDtypeStruct((count, tokens, width), BF16),
        jax.ShapeDtypeStruct((shard, 3 * width), F32),
        *[jax.ShapeDtypeStruct(x.shape, F32) for x in sums[3:]],
        jax.ShapeDtypeStruct((4, width), F32),
        jax.ShapeDtypeStruct((4, width), F32),
        jax.ShapeDtypeStruct((hidden_count, width), F32),
        jax.ShapeDtypeStruct((hidden_count, coef_count), F32),
        jax.ShapeDtypeStruct((1, coef_count), F32),
        jax.ShapeDtypeStruct(m_grad.shape, F32),
    ]
    return pl.pallas_call(
        functools.partial(tail_kernel, strip=32),
        grid=(tiles,),
        in_specs=[
            pl.BlockSpec((3, tile, width), lambda i: (0, i, 0)),
            pl.BlockSpec((tile, width), lambda i: (i, 0)),
            whole(mix),
            *[part(x) for x in sums],
            whole(small),
            whole(m_grad),
        ],
        out_specs=[pl.BlockSpec((count, tile, width), lambda i: (0, i, 0))]
        + [part(x) for x in outs[1:5]]
        + [whole(x) for x in outs[5:]],
        out_shape=outs,
        scratch_shapes=[pltpu.VMEM((tile, 4 * count), F32)],
        compiler_params=params(60),
        cost_estimate=pl.CostEstimate(
            flops=64 * tokens * width, bytes_accessed=40 * tokens * width, transcendentals=0
        ),
        name="spread_back",
    )(low, hgrad, mix, *sums, small, m_grad)


def body(
    earlier,
    mix_in,
    segment_ids,
    attn_qkv,
    attn_out,
    mlp_in,
    mlp_out,
    norm_gain,
    norm_bias,
    mix_w1,
    mix_w2,
    mix_bias,
    out_grad,
    coef_grad,
):
    count, seqs, _, block, width = earlier.shape
    n = lax.axis_size("ctx")
    tokens = seqs * 2 * block
    length = 2 * n * block
    me = lax.axis_index("ctx")

    nf = lax.axis_size("fsdp")
    e = earlier.reshape(count, tokens, width)
    cosine, sine = (jnp.asarray(table) for table in turn_tables(length))
    normed, hats, scales, residual, w_qkv, w_o, w_in, w_out, qkv, context = forward(
        e,
        mix_in,
        attn_qkv,
        attn_out,
        mlp_in,
        mlp_out,
        norm_gain,
        norm_bias,
        cosine,
        sine,
        segment_ids,
        n,
        nf,
    )
    (
        layer_out,
        coefs,
        active,
        lowered,
        normed_mlp,
        branch,
        attention_grad,
        context_grad,
        hidden_grad,
        d_gain,
        d_bias,
        d_w1,
        d_w2,
        d_mb,
    ) = feed(
        residual,
        context,
        w_o,
        w_in,
        w_out,
        norm_gain,
        norm_bias,
        mix_w1,
        mix_w2,
        mix_bias[None, :],
        out_grad.reshape(tokens, width),
        coef_grad,
        n,
    )
    saved = (active, lowered, normed_mlp, branch, context, attention_grad)
    grads, owned = attention_back(
        context_grad, qkv, saved, segment_ids, cosine, sine, n, nf
    )
    low, m_grad, *sums, small = finish(
        grads,
        normed,
        hats,
        scales,
        e,
        w_qkv,
        hidden_grad,
        norm_gain,
        owned,
        (d_gain, d_bias, d_w1, d_w2, d_mb),
        mix_in.shape,
        n,
        nf,
    )
    e_grad, g_qkv, g_in, g_out, g_o, gain_sum, bias_sum, w1_sum, w2_sum, mb_sum, m_grad = (
        spread_back(low, hidden_grad, mix_in, sums, small, m_grad, mix_w2.shape)
    )
    return (
        layer_out.reshape(seqs, 2, block, width),
        coefs,
        e_grad.reshape(count, seqs, 2, block, width),
        m_grad,
        g_qkv,
        g_o,
        g_in,
        g_out,
        gain_sum,
        bias_sum,
        w1_sum,
        w2_sum,
        mb_sum[0],
    )


def solution(mesh):
    in_specs = (
        P(None, "fsdp", None, "ctx", None),
        P(None, None, "fsdp", None, "ctx"),
        P("fsdp", None, None),
        P("fsdp", None),
        P("fsdp", None),
        P("fsdp", None),
        P("fsdp", None),
        P(),
        P(),
        P(),
        P(),
        P(),
        P("fsdp", None, "ctx", None),
        P(None, None, "fsdp", None, "ctx"),
    )
    out_specs = (
        P("fsdp", None, "ctx", None),
        P(None, None, "fsdp", None, "ctx"),
        P(None, "fsdp", None, "ctx", None),
        P(None, None, "fsdp", None, "ctx"),
        P("fsdp", None),
        P("fsdp", None),
        P("fsdp", None),
        P("fsdp", None),
        P(),
        P(),
        P(),
        P(),
        P(),
    )
    return jax.shard_map(body, mesh=mesh, in_specs=in_specs, out_specs=out_specs, check_vma=False)
```

```python
import functools
import math

import jax
import jax.numpy as jnp
import numpy as np
from jax import lax
from jax.experimental import pallas as pl
from jax.experimental.pallas import tpu as pltpu
from jax.sharding import PartitionSpec as P

HD = 64
ROT = 16
LANES = 128
EPSILON = 1e-05
RMS_EPSILON = 1e-06
MASKED = -1e30
F32 = jnp.float32
BF16 = jnp.bfloat16
MESH = pl.DeviceIdType.MESH
MIB = 1024 * 1024

NN = (((1,), (0,)), ((), ()))
NT = (((1,), (1,)), ((), ()))
TN = (((0,), (0,)), ((), ()))

ERFC_RATE = 0.4
ERFC = (
    0.22567586600780487,
    0.22566929459571838,
    0.20784726738929749,
    0.16851142048835754,
    0.1415392905473709,
    -0.005822250619530678,
    0.16932761669158936,
    -0.18304575979709625,
    0.05029737576842308,
)


def dot(a, b, dims=NN):
    return lax.dot_general(a, b, dims, preferred_element_type=F32)


def gelu_and_slope(v):
    bell = jnp.exp(-0.5 * (v * v))
    t = 1.0 / (1.0 + (ERFC_RATE * math.sqrt(0.5)) * jnp.abs(v))
    poly = 0.5 * ERFC[-1] * t + 0.5 * ERFC[-2]
    for coefficient in ERFC[-3::-1]:
        poly = poly * t + 0.5 * coefficient
    tail = poly * t * bell
    phi = jnp.where(v >= 0.0, 1.0 - tail, tail)
    return v * phi, phi + v * bell * (1.0 / math.sqrt(2.0 * math.pi))


def halves(x):
    high = x.astype(BF16)
    return high, (x - high.astype(F32)).astype(BF16)


def params(limit_mib, **more):
    return pltpu.CompilerParams(vmem_limit_bytes=limit_mib * MIB, **more)


def once(shape, index):
    return pl.BlockSpec(shape, index, pipeline_mode=pl.Buffered(1))


def turn_tables(length):
    half = ROT // 2
    frequency = 10000.0 ** (-(np.arange(half) * 2.0 / ROT))
    angle = np.arange(length)[:, None] * frequency[None, :]
    lane = np.arange(LANES) % HD
    cosine = np.ones((length, LANES), np.float32)
    sine = np.zeros((length, LANES), np.float32)
    for k in range(LANES):
        if lane[k] < ROT:
            cosine[:, k] = np.cos(angle[:, lane[k] % half])
            sign = -1.0 if lane[k] < half else 1.0
            sine[:, k] = sign * np.sin(angle[:, lane[k] % half])
    return cosine, sine


def turned(x, cosine, sine):
    half = ROT // 2
    lane = lax.broadcasted_iota(jnp.int32, x.shape, 1) % HD
    other = jnp.where(
        lane < half, pltpu.roll(x, LANES - half, axis=1), pltpu.roll(x, half, axis=1)
    )
    return x * cosine + other * sine


def row_tile(length):
    return min(256, length)


def head_lanes(shape, h):
    lane = lax.broadcasted_iota(jnp.int32, shape, 1)
    return (lane >= h * HD) & (lane < (h + 1) * HD)


def only(x, h):
    return jnp.where(head_lanes(x.shape, h), x, jnp.zeros_like(x))


def coefficient_places(ref):
    outer, inner, seqs, _, block = ref.shape
    for a in range(outer):
        for seq in range(seqs):
            for h in range(2):
                first = (2 * seq + h) * block
                yield a, seq, h, slice(a * inner, (a + 1) * inner), slice(first, first + block)


def feed_kernel(
    res_ref,
    ctx_ref,
    wo_ref,
    win_ref,
    wout_ref,
    g_ref,
    b_ref,
    w1_ref,
    w2_ref,
    mb_ref,
    og_ref,
    cg_ref,
    out_ref,
    coef_ref,
    active,
    lowered,
    normed,
    branch,
    attention,
    cgrad_ref,
    hgrad_ref,
    dgain_ref,
    dbias_ref,
    dw1_ref,
    dw2_ref,
    dmb_ref,
    hidden,
    total,
    slope,
    r_high,
    r_rest,
    cotangent,
    *,
    tiles,
    strip,
):
    step = pl.program_id(0)
    tokens, width = res_ref.shape
    cut = win_ref.shape[1]
    inv = 1.0 / width

    @pl.when(step == 0)
    def _():
        hidden[...] = dot(ctx_ref[...], wo_ref[...])

        @pl.loop(0, tokens // strip)
        def _(i):
            rows = pl.ds(pl.multiple_of(i * strip, strip), strip)
            v = hidden[rows] + res_ref[rows]
            hidden[rows] = v
            center = v - jnp.sum(v, axis=-1, keepdims=True) * inv
            spread = jnp.sum(center * center, axis=-1, keepdims=True) * inv
            hat = center * lax.rsqrt(spread + EPSILON)
            normed[rows] = (hat * g_ref[3:4] + b_ref[3:4]).astype(BF16)
            total[rows] = v

    @pl.when(step < tiles)
    def _():
        half = tokens // 2
        parts = [slice(i * half, (i + 1) * half) for i in range(2)]
        ups = [dot(normed[rows], win_ref[...]) for rows in parts]
        for rows, up in zip(parts, ups):
            value, rate = gelu_and_slope(up)
            low = value.astype(BF16)
            active[rows] = low
            slope[step, rows] = rate
            total[rows] += dot(low, wout_ref[...])

    @pl.when(step == tiles - 1)
    def _():
        w1 = w1_ref[...]
        w2 = w2_ref[...]

        @pl.loop(0, tokens // strip)
        def _(i):
            rows = pl.ds(pl.multiple_of(i * strip, strip), strip)
            v = total[rows]
            out_ref[rows] = v.astype(BF16)
            scale = lax.rsqrt(jnp.sum(v * v, axis=-1, keepdims=True) * inv + RMS_EPSILON)
            r = v * scale
            high = r.astype(BF16)
            r_high[rows] = high
            r_rest[rows] = (r - high.astype(F32)).astype(BF16)

        high, rest = r_high[...], r_rest[...]
        for a, seq, h, rows, cols in coefficient_places(cg_ref):
            cotangent[rows, cols] = cg_ref[a, :, seq, h, :]
        z = dot(w1, high, NT) + dot(w1, rest, NT)
        value, rate = gelu_and_slope(z)
        v_high, v_rest = halves(value)
        ones = jnp.ones((1, tokens), BF16)
        mb_high, mb_rest = halves(mb_ref[...])
        mb_last = (mb_ref[...] - mb_high.astype(F32) - mb_rest.astype(F32)).astype(BF16)
        shift = dot(mb_high, ones, TN) + dot(mb_rest, ones, TN) + dot(mb_last, ones, TN)
        coefs = dot(w2, v_high, TN) + dot(w2, v_rest, TN) + shift
        for a, seq, h, rows, cols in coefficient_places(coef_ref):
            coef_ref[a, :, seq, h, :] = coefs[rows, cols]
        c_high, c_rest = halves(cotangent[...])
        dmb_ref[...] = dot(ones, c_high, NT) + dot(ones, c_rest, NT)
        dw2_ref[...] = dot(v_high, c_high, NT) + dot(v_rest, c_high, NT) + dot(v_high, c_rest, NT)
        z_high, z_rest = halves((dot(w2, c_high) + dot(w2, c_rest)) * rate)
        dw1_ref[...] = dot(z_high, high) + dot(z_high, rest) + dot(z_rest, high)
        hgrad_ref[...] = dot(z_high, w1, TN) + dot(z_rest, w1, TN)

        @pl.loop(0, tokens // strip)
        def _(i):
            rows = pl.ds(pl.multiple_of(i * strip, strip), strip)
            v = total[rows]
            scale = lax.rsqrt(jnp.sum(v * v, axis=-1, keepdims=True) * inv + RMS_EPSILON)
            dr = hgrad_ref[rows]
            r = v * scale
            mean = jnp.sum(dr * r, axis=-1, keepdims=True) * inv
            grad = scale * (dr - r * mean) + og_ref[rows].astype(F32)
            hgrad_ref[rows] = grad
            branch[rows] = grad.astype(BF16)
            total[rows] = jnp.zeros_like(v)

    @pl.when(step >= tiles)
    def _():
        j = step - tiles
        low = (dot(branch[...], wout_ref[...], NT) * slope[j]).astype(BF16)
        lowered[...] = low
        total[...] += dot(low, win_ref[...], NT)

    @pl.when(step == 2 * tiles - 1)
    def _():
        dgain_ref[...] = jnp.zeros_like(dgain_ref)
        dbias_ref[...] = jnp.zeros_like(dbias_ref)

        @pl.loop(0, tokens // strip)
        def _(i):
            rows = pl.ds(pl.multiple_of(i * strip, strip), strip)
            v = hidden[rows]
            dy = total[rows]
            center = v - jnp.sum(v, axis=-1, keepdims=True) * inv
            spread = jnp.sum(center * center, axis=-1, keepdims=True) * inv
            scale = lax.rsqrt(spread + EPSILON)
            hat = center * scale
            dgain_ref[...] += jnp.sum(dy * hat, axis=0, keepdims=True)
            dbias_ref[...] += jnp.sum(dy, axis=0, keepdims=True)
            dh = dy * g_ref[3:4]
            first = jnp.sum(dh, axis=-1, keepdims=True) * inv
            second = jnp.sum(dh * hat, axis=-1, keepdims=True) * inv
            grad = hgrad_ref[rows] + scale * (dh - first - hat * second)
            hgrad_ref[rows] = grad
            attention[rows] = grad.astype(BF16)

        groups, _, group = cgrad_ref.shape
        back = dot(attention[...], wo_ref[...], NT).astype(BF16)
        for i in range(groups):
            cgrad_ref[i] = back[:, i * group : (i + 1) * group]


def feed(res, ctx, wo, win, wout, gain, bias, w1, w2, mb, og, cg, groups):
    tokens, width = res.shape
    hidden_units = win.shape[1]
    cut = 1024
    tiles = hidden_units // cut
    small, coefs = w1.shape[0], w2.shape[1]

    def whole(x):
        zeros = (0,) * x.ndim
        return once(x.shape, lambda i: zeros)

    def result(shape, dtype=F32):
        zeros = (0,) * len(shape)
        return once(shape, lambda i: zeros), jax.ShapeDtypeStruct(shape, dtype)

    def back(i):
        return jnp.maximum(i - tiles, 0)

    outs = [
        result((tokens, width), BF16),
        result(cg.shape),
        (
            pl.BlockSpec((tokens, cut), lambda i: (0, jnp.minimum(i, tiles - 1))),
            jax.ShapeDtypeStruct((tokens, hidden_units), BF16),
        ),
        (
            pl.BlockSpec((tokens, cut), lambda i: (0, back(i))),
            jax.ShapeDtypeStruct((tokens, hidden_units), BF16),
        ),
        result((tokens, width), BF16),
        result((tokens, width), BF16),
        result((tokens, width), BF16),
        result((groups, tokens, width // groups), BF16),
        result((tokens, width)),
        result((1, width)),
        result((1, width)),
        result((small, width)),
        result((small, coefs)),
        result((1, coefs)),
    ]
    return pl.pallas_call(
        functools.partial(feed_kernel, tiles=tiles, strip=min(512, tokens)),
        grid=(2 * tiles,),
        in_specs=[
            whole(res),
            whole(ctx),
            whole(wo),
            pl.BlockSpec((width, cut), lambda i: (0, lax.rem(i, tiles))),
            pl.BlockSpec((cut, width), lambda i: (lax.rem(i, tiles), 0)),
            whole(gain),
            whole(bias),
            whole(w1),
            whole(w2),
            whole(mb),
            whole(og),
            whole(cg),
        ],
        out_specs=[spec for spec, _ in outs],
        out_shape=[shape for _, shape in outs],
        scratch_shapes=[
            pltpu.VMEM((tokens, width), F32),
            pltpu.VMEM((tokens, width), F32),
            pltpu.VMEM((tiles, tokens, cut), F32),
            pltpu.VMEM((tokens, width), BF16),
            pltpu.VMEM((tokens, width), BF16),
            pltpu.VMEM((coefs, tokens), F32),
        ],
        compiler_params=params(58),
        cost_estimate=pl.CostEstimate(
            flops=8 * tokens * width * hidden_units + 4 * tokens * width * width,
            bytes_accessed=8 * width * hidden_units + 4 * width * width + 20 * tokens * width,
            transcendentals=2 * tokens * hidden_units,
        ),
        name="feed",
    )(res, ctx, wo, win, wout, gain, bias, w1, w2, mb, og, cg)


def flipped(v, mask):
    bit = 1
    while bit <= mask:
        if mask & bit:
            v = v + bit - 2 * bit * lax.rem(v // bit, 2)
        bit *= 2
    return v


def added(out_ref, refs, rows, strip=32):
    strip = math.gcd(strip, rows)

    @pl.loop(0, rows // strip)
    def _(i):
        at = pl.ds(pl.multiple_of(i * strip, strip), strip)
        total = refs[0][at].astype(F32)
        for ref in refs[1:]:
            total = total + ref[at].astype(F32)
        out_ref[at] = total.astype(out_ref.dtype)


class Remote:
    def __init__(self, send, recv):
        self.send, self.recv, self.used = send, recv, 0

    def start(self, src, dst, where):
        copy = self.make(src, dst, where)
        copy.start()
        return copy

    def make(self, src, dst, where):
        copy = pltpu.make_async_remote_copy(
            src_ref=src,
            dst_ref=dst,
            send_sem=self.send.at[self.used],
            recv_sem=self.recv.at[self.used],
            device_id=where,
            device_id_type=MESH,
        )
        self.used += 1
        return copy


class Chain:
    def __init__(self, remote, n):
        self.remote, self.n = remote, n
        self.me = lax.axis_index("ctx")
        place = lax.rem(self.me, 4)
        self.outer = jnp.logical_or(place == 0, place == 3)
        self.inner = jnp.logical_not(self.outer)
        self.pieces = []
        self.started = 0

    def add(self, work, out, land, own, crosses):
        there = {"ctx": flipped(self.me, 1)}
        up = self.remote.make(work, land, there)
        masks = [3]
        bit = 4
        while bit < self.n:
            masks.append(bit)
            bit *= 2
        across = [
            self.remote.make(own.at[i], crosses.at[i], {"ctx": flipped(self.me, mask)})
            for i, mask in enumerate(masks)
        ]
        down = self.remote.make(out, out, there)
        self.pieces.append((work, out, land, own, crosses, up, across, down))

    def start(self):
        if self.started < len(self.pieces):
            up = self.pieces[self.started][5]

            @pl.when(self.outer)
            def _():
                up.start()

        self.started += 1

    def step(self, c):
        work, _, land, own, _, up, across, _ = self.pieces[c]

        @pl.when(self.outer)
        def _():
            up.wait_send()

        self.start()

        @pl.when(self.inner)
        def _():
            up.wait_recv()
            added(own.at[0], [work, land], work.shape[0])
            across[0].start()

        if c >= 1:
            self.leave(c - 1)

    def leave(self, c):
        _, out, _, own, crosses, _, across, down = self.pieces[c]

        @pl.when(self.inner)
        def _():
            for i, copy in enumerate(across):
                copy.wait()
                last = i + 1 == len(across)
                to = out if last else own.at[i + 1]
                added(to, [own.at[i], crosses.at[i]], out.shape[0])
                if not last:
                    across[i + 1].start()
            down.start()

    def end(self, c):
        down = self.pieces[c][7]

        @pl.when(self.outer)
        def _():
            down.wait_recv()

        @pl.when(self.inner)
        def _():
            down.wait_send()

    @staticmethod
    def levels(n):
        return max(1, n.bit_length() - 2)


def piece_sizes(heights):
    return [[h // 4] * 4 for h in heights[:2]] + [[h] for h in heights[2:]]


def chain_scratch(n, rows, cols):
    levels = Chain.levels(n)
    return [
        pltpu.VMEM((rows, cols), BF16),
        pltpu.VMEM((levels, rows, cols), BF16),
        pltpu.VMEM((levels, rows, cols), BF16),
    ]


class ChipSum:
    def __init__(self, remote, nf, terms, keep, got, part):
        self.remote, self.nf, self.terms = remote, nf, terms
        self.keep, self.got, self.part = keep, got, part
        self.f = lax.axis_index("fsdp")
        self.chip, self.core = self.f // 2, lax.rem(self.f, 2)
        self.rows = got.shape[1]
        self.half = self.rows // 2
        bits = []
        bit = 1
        while bit < nf // 2:
            bits.append(bit)
            bit *= 2
        self.orders = (bits, bits[::-1])
        self.level = len(bits) - 1
        self.slots = 0

    def cores(self):
        self.copy = self.remote.start(
            self.terms.at[:, 1 - self.core], self.got, {"fsdp": flipped(self.f, 1)}
        )

    def masks(self, which, level):
        found = [0]
        for bit in self.orders[which][:level]:
            found += [mask + bit for mask in found]
        return found

    def piece(self, which, chip):
        return self.got.at[chip, pl.ds(which * self.half, self.half)]

    def launch(self):
        self.flying = []
        for which in range(2):
            bit = self.orders[which][self.level]
            to = 2 * flipped(self.chip, bit) + self.core
            for mask in self.masks(which, self.level):
                landing = self.part.at[self.slots]
                self.slots += 1
                copy = self.remote.start(
                    self.piece(which, flipped(self.chip, mask + bit)), landing, {"fsdp": to}
                )
                self.flying.append((copy, which, mask, landing))

    def cross(self):
        self.copy.wait()
        for k in range(self.nf // 2):
            added(self.got.at[k], [self.keep.at[k], self.got.at[k]], self.rows)
        self.launch()

    def relay(self):
        while self.level > 0:
            for copy, which, mask, landing in self.flying:
                copy.wait()
                here = self.piece(which, flipped(self.chip, mask))
                added(here, [here, landing], self.half)
            self.level -= 1
            self.launch()

    def total(self, out):
        for copy, which, _, landing in self.flying:
            copy.wait()
            added(
                out.at[pl.ds(which * self.half, self.half)],
                [self.piece(which, self.chip), landing],
                self.half,
            )

    @staticmethod
    def count(nf):
        return 1 + 2 * (nf // 2 - 1)


def chip_scratch(nf, rows, cols):
    chips = nf // 2
    return [
        pltpu.VMEM((chips, rows, cols), BF16),
        pltpu.VMEM((chips, rows, cols), BF16),
        pltpu.VMEM((2 * chips - 2, rows // 2, cols), BF16),
    ]


def greet_partners(n, nf):
    z, f = lax.axis_index("ctx"), lax.axis_index("fsdp")
    barrier = pltpu.get_barrier_semaphore()
    count = n - 1
    bit = 1
    while bit < nf:
        pl.semaphore_signal(
            barrier, inc=1, device_id={"fsdp": flipped(f, bit)}, device_id_type=MESH
        )
        count += 1
        bit *= 2
    for k in range(1, n):
        pl.semaphore_signal(
            barrier, inc=1, device_id={"ctx": lax.rem(z + k, n)}, device_id_type=MESH
        )
    pl.semaphore_wait(barrier, count)


def greet_all(n, nf):
    z, f = lax.axis_index("ctx"), lax.axis_index("fsdp")
    barrier = pltpu.get_barrier_semaphore()
    for k in range(1, nf):
        pl.semaphore_signal(
            barrier, inc=1, device_id={"fsdp": lax.rem(f + k, nf)}, device_id_type=MESH
        )
    for k in range(1, n):
        pl.semaphore_signal(
            barrier, inc=1, device_id={"ctx": lax.rem(z + k, n)}, device_id_type=MESH
        )
    pl.semaphore_wait(barrier, nf + n - 2)


def place_segments(ids_ref, row, column, block):
    seqs, _, half = ids_ref.shape
    n = half // block
    for s in range(seqs):
        row[s, :, 0:half] = ids_ref[s, 0:1].astype(F32)
        for b in range(n):
            at = slice((n - 1 - b) * block, (n - b) * block)
            to = slice(half + b * block, half + (b + 1) * block)
            row[s, :, to] = ids_ref[s, 1:2, at].astype(F32)
        column[s] = jnp.broadcast_to(row[s], (8, 2 * half)).T


def mix_columns(mix_ref, mixes, t):
    block = mix_ref.shape[4]
    tile = mixes.shape[0]
    per = tile // block
    parts = []
    for i in range(t * per, (t + 1) * per):
        rows = [mix_ref[a, :, i // 2, i % 2, :] for a in range(mix_ref.shape[0])]
        parts.append(jnp.concatenate(rows, axis=0))
    mixes[...] = (parts[0] if per == 1 else jnp.concatenate(parts, axis=1)).T


class PlaneGather:
    def __init__(self, remote, nf, src, out):
        self.remote, self.nf, self.src, self.out = remote, nf, src, out
        self.f = lax.axis_index("fsdp")
        self.half = src.shape[0] // 2
        bits = []
        bit = 2
        while bit < nf:
            bits.append(bit)
            bit *= 2
        self.orders = (bits, bits[::-1])
        self.levels = len(bits)
        self.flying = {}
        self.inner = []

    def masks(self, which, level):
        found = [0]
        for bit in self.orders[which][:level]:
            found += [mask + bit for mask in found]
        return found

    def place(self, which, shard):
        return self.out.at[shard, pl.ds(which * self.half, self.half)]

    def launch(self, which, level, mask):
        shard = flipped(self.f, mask)
        here = self.src.at[pl.ds(which * self.half, self.half)]
        if mask:
            here = self.place(which, shard)
        to = flipped(self.f, self.orders[which][level])
        self.flying[which, level, mask] = self.remote.start(
            here, self.place(which, shard), {"fsdp": to}
        )

    def begin(self, sem):
        for level in range(self.levels):
            for which in range(2):
                self.launch(which, level, 0)
        self.inner.append(
            self.remote.start(self.src, self.out.at[self.f], {"fsdp": flipped(self.f, 1)})
        )
        self.own = pltpu.make_async_copy(self.src, self.out.at[self.f], sem)
        self.own.start()

    def relay(self, level):
        for which in range(2):
            order = self.orders[which]
            for mask in self.masks(which, level):
                self.flying[which, level, mask].wait()
                arrived = mask + order[level]
                for later in range(level + 1, self.levels):
                    self.launch(which, later, arrived)
                place = self.place(which, flipped(self.f, arrived))
                self.inner.append(self.remote.start(place, place, {"fsdp": flipped(self.f, 1)}))

    def end(self):
        self.own.wait()
        for copy in self.inner:
            copy.wait()

    @staticmethod
    def count(nf):
        return 2 * (nf // 2 - 1) + 2 * (nf // 2 - 1) + 1


def front_tile(e, mixes, st, g_ref, b_ref, normed, hats, scales, res, first, strip=16):
    count, tile, width = e.shape
    inv = 1.0 / width

    @pl.loop(0, tile // strip)
    def _(i):
        rows = pl.ds(pl.multiple_of(i * strip, strip), strip)
        mix = mixes[rows]
        for pair in ((0, 1), (2, 3)):
            totals = [None, None]
            for j in range(count):
                part = e[j, rows].astype(F32)
                for slot, s in enumerate(pair):
                    term = part * mix[:, s * count + j : s * count + j + 1]
                    totals[slot] = term if j == 0 else totals[slot] + term
            for slot, s in enumerate(pair):
                st[s, rows] = totals[slot]

    to = slice(first, first + tile)
    lane = lax.broadcasted_iota(jnp.int32, (tile, LANES), 1)
    kept = jnp.zeros((tile, LANES), F32)
    for s in range(3):
        v = st[s]
        center = v - jnp.sum(v, axis=-1, keepdims=True) * inv
        spread = jnp.sum(center * center, axis=-1, keepdims=True) * inv
        scale = lax.rsqrt(spread + EPSILON)
        hat = center * scale
        hats[s, to] = hat.astype(BF16)
        normed[s, to] = (hat * g_ref[s : s + 1] + b_ref[s : s + 1]).astype(BF16)
        kept = jnp.where(lane == s, scale, kept)
    scales[to] = kept
    res[to] = st[3]


def attend_pair(qkv, out, column_ref, row_ref, seq, lanes, part=None):
    blocks, block = out.shape[1], out.shape[2]
    length = blocks * block
    rows = row_tile(length)
    per = rows // block

    def load(kind, first, last):
        return qkv[kind, seq, first:last, :, lanes].reshape(-1, LANES)

    count = length // rows
    if part is None:
        which = range(count)
    else:
        which = range(part * count // 2, (part + 1) * count // 2)
    for i in which:
        first, until = i * rows, (i + 1) * rows
        b0, b1 = i * per, (i + 1) * per
        query = first + lax.broadcasted_iota(jnp.int32, (rows, until), 0)
        key = lax.broadcasted_iota(jnp.int32, (rows, until), 1)
        same = column_ref[seq, first:until, 0:1] == row_ref[seq, 0:1, 0:until]
        allowed = same & (key <= query)
        q = load(0, b0, b1) * BF16(HD**-0.5)
        k = load(1, 0, b1)
        v = load(2, 0, b1)
        total = None
        for h in range(LANES // HD):
            scores = jnp.where(allowed, dot(only(q, h), k, NT), MASKED)
            peak = jnp.max(scores, axis=-1, keepdims=True)
            raised = jnp.exp(scores - peak)
            mass = jnp.sum(raised, axis=-1, keepdims=True)
            probs = (raised * (1.0 / mass)).astype(BF16)
            part = dot(probs, v)
            part = jnp.where(head_lanes(part.shape, h), part, 0.0)
            total = part if total is None else total + part
        out[seq, b0:b1, :, lanes] = total.astype(BF16).reshape(per, block, LANES)


def forward_kernel(
    n,
    nf,
    e_ref,
    wqkv_ref,
    wo_ref,
    win_ref,
    wout_ref,
    mix_ref,
    gain_ref,
    bias_ref,
    c_ref,
    s_ref,
    ids_ref,
    normed_ref,
    hats_ref,
    scales_ref,
    res_ref,
    gqkv_ref,
    go_ref,
    gin_ref,
    gout_ref,
    qkv_ref,
    ctx_ref,
    e,
    mixes,
    st,
    normed,
    hats,
    scales,
    res,
    w,
    raw,
    shares,
    qkv,
    heads,
    row,
    column,
    send,
    recv,
    local,
    e_sem,
):
    f, z = lax.axis_index("fsdp"), lax.axis_index("ctx")
    count, tokens, width = e_ref.shape
    tile = e.shape[2]
    tiles = tokens // tile
    seqs, _, block, cols = heads.shape
    seq_rows = 2 * block
    cut = raw.shape[1]
    remote = Remote(send, recv)
    spots = (z, 2 * n - 1 - z)
    mine = pl.ds(pl.multiple_of(z * cols, LANES), cols)

    def fetch(t):
        return pltpu.make_async_copy(
            e_ref.at[:, t * tile : (t + 1) * tile], e.at[t % 2], e_sem.at[t % 2]
        )

    fetch(0).start()
    greet_partners(n, nf)

    def columns(ref, i):
        at = pl.ds(i * width, width)
        return ref.at[:, at] if len(ref.shape) == 2 else ref.at[:, :, at]

    parts = [
        PlaneGather(remote, nf, columns(wqkv_ref, i), columns(w, i)) for i in range(3)
    ]
    others = [
        PlaneGather(remote, nf, win_ref, gin_ref),
        PlaneGather(remote, nf, wout_ref, gout_ref),
        PlaneGather(remote, nf, wo_ref, go_ref),
    ]
    levels = parts[0].levels
    parts[0].begin(local.at[0])

    def do_tile(t):
        fetch(t).wait()
        if t + 1 < tiles:
            fetch(t + 1).start()
        mix_columns(mix_ref, mixes, t)
        front_tile(
            e.at[t % 2], mixes, st, gain_ref, bias_ref, normed, hats, scales, res, t * tile
        )

    def first_hops():
        parts[0].relay(0)
        parts[1].begin(local.at[1])

    def second_hops():
        for level in range(1, levels):
            parts[0].relay(level)

    for t in range(tiles):
        do_tile(t)
        if t == 0:
            first_hops()
        if t == max(1, tiles - 2):
            second_hops()
    own_tables = []
    for table in (c_ref, s_ref):
        early = table[pl.ds(pl.multiple_of(z * block, block), block)]
        late = table[pl.ds(pl.multiple_of((2 * n - 1 - z) * block, block), block)]
        own_tables.append((early, late))

    def project(i):
        @pl.loop(0, width // cut)
        def _(j):
            at = pl.ds(pl.multiple_of(i * width + j * cut, cut), cut)
            raw[...] = dot(normed[i], w[:, :, at].reshape(width, cut))
            for s in range(seqs):
                for h in range(2):
                    first = s * seq_rows + h * block
                    for c in range(cut // LANES):
                        x = raw[first : first + block, c * LANES : (c + 1) * LANES]
                        if i < 2:
                            x = turned(x, own_tables[0][h], own_tables[1][h])
                        to = c * LANES % cols
                        group = j * (cut // cols) + c * LANES // cols
                        shares[i, group, s, h, :, to : to + LANES] = x.astype(BF16)

    pairs = cols // LANES
    units = [(0, None)] + [(s, p) for s in range(1, seqs) for p in range(pairs)]
    arriving = {unit: [] for unit in units}
    kept = []

    def give(kind, unit):
        s, p = unit
        lanes = slice(None) if p is None else slice(p * LANES, (p + 1) * LANES)
        for k in range(1, n):
            to = lax.rem(z + k, n)
            for h in range(2):
                arriving[unit].append(
                    remote.start(
                        shares.at[kind, to, s, h, :, lanes],
                        qkv.at[kind, s, spots[h], :, lanes],
                        {"ctx": to},
                    )
                )

    for i in range(3):
        parts[i].end()
        project(i)
        give(i, units[0])
        if i < 2:
            for level in range(levels):
                parts[i + 1].relay(level)
                if level == 0:
                    (parts[2], others[0])[i].begin(local.at[2 + i])
    for h in range(2):
        copy = pltpu.make_async_copy(
            shares.at[:, z, :, h], qkv.at[:, :, spots[h]], local.at[8 + h]
        )
        copy.start()
        kept.append(copy)
    for unit in units[1:2]:
        give(slice(None), unit)
    others[1].begin(local.at[4])
    others[2].begin(local.at[5])
    out_copies = [
        pltpu.make_async_copy(w, gqkv_ref, local.at[10]),
        pltpu.make_async_copy(normed, normed_ref, local.at[6]),
        pltpu.make_async_copy(res, res_ref, local.at[7]),
        pltpu.make_async_copy(hats, hats_ref, local.at[12]),
        pltpu.make_async_copy(scales, scales_ref, local.at[13]),
    ]
    for copy in out_copies:
        copy.start()
    place_segments(ids_ref, row, column, block)

    others[0].relay(0)
    for copy in kept:
        copy.wait()
    leaving = []
    stored = 14
    for index, unit in enumerate(units):
        for copy in arriving[unit]:
            copy.wait()
        for other in units[index + 2 : index + 3]:
            give(slice(None), other)
        s, p = unit
        if p is None:

            @pl.loop(0, pairs)
            def _(p):
                lanes = pl.ds(pl.multiple_of(p * LANES, LANES), LANES)
                attend_pair(qkv, heads, column, row, s, lanes)

            there, here = mine, slice(None)
        else:
            here = slice(p * LANES, (p + 1) * LANES)
            there = pl.ds(pl.multiple_of(z * cols + p * LANES, LANES), LANES)
        halves_apart = index + 1 == len(units) and p is not None
        if p is not None and not halves_apart:
            attend_pair(qkv, heads, column, row, s, here)
        for h in range(2):
            if halves_apart:
                attend_pair(qkv, heads, column, row, s, here, h)
            for k in range(1, n):
                to = lax.rem(z + k, n)
                spot = to if h == 0 else 2 * n - 1 - to
                leaving.append(
                    remote.start(
                        heads.at[s, spot, :, here], ctx_ref.at[s, h, :, there], {"ctx": to}
                    )
                )
        for h in range(2):
            copy = pltpu.make_async_copy(
                heads.at[s, spots[h], :, here], ctx_ref.at[s, h, :, there], local.at[stored]
            )
            stored += 1
            copy.start()
            out_copies.append(copy)
        if index == 0:
            others[1].relay(0)
            others[2].relay(0)
            for level in range(1, levels):
                others[0].relay(level)
    copy = pltpu.make_async_copy(qkv, qkv_ref, local.at[11])
    copy.start()
    out_copies.append(copy)
    for level in range(1, levels):
        others[1].relay(level)
        others[2].relay(level)
    for gather in others:
        gather.end()
    for copy in out_copies + leaving:
        copy.wait()


def forward(e, mix, w_qkv, w_o, w_in, w_out, gain, bias, cosine, sine, ids, n, nf):
    count, tokens, width = e.shape
    seqs, block = mix.shape[2], mix.shape[4]
    length = 2 * n * block
    cols = width // n
    spots = 2 * n
    tile = 128
    cut = max(cols, 512)
    rows = width // nf
    units = 1 + (seqs - 1) * (cols // LANES)
    copies = 6 * PlaneGather.count(nf) + (2 + 2 * units) * 2 * (n - 1)
    vmem = pl.BlockSpec(memory_space=pltpu.VMEM)
    hbm = pl.BlockSpec(memory_space=pltpu.HBM)

    def gathered(x):
        return jax.ShapeDtypeStruct((nf,) + x.shape, x.dtype)

    normed, hats, scales, res, g_qkv, g_o, g_in, g_out, qkv, ctx = pl.pallas_call(
        functools.partial(forward_kernel, n, nf),
        in_specs=[hbm] * 5 + [vmem] * 6,
        out_specs=[hbm] * 10,
        out_shape=[
            jax.ShapeDtypeStruct((3, tokens, width), BF16),
            jax.ShapeDtypeStruct((3, tokens, width), BF16),
            jax.ShapeDtypeStruct((tokens, LANES), F32),
            jax.ShapeDtypeStruct((tokens, width), F32),
            gathered(w_qkv),
            gathered(w_o),
            gathered(w_in),
            gathered(w_out),
            jax.ShapeDtypeStruct((3, seqs, spots, block, cols), BF16),
            jax.ShapeDtypeStruct((seqs, 2, block, width), BF16),
        ],
        scratch_shapes=[
            pltpu.VMEM((2, count, tile, width), BF16),
            pltpu.VMEM((tile, 4 * count), F32),
            pltpu.VMEM((4, tile, width), F32),
            pltpu.VMEM((3, tokens, width), BF16),
            pltpu.VMEM((3, tokens, width), BF16),
            pltpu.VMEM((tokens, LANES), F32),
            pltpu.VMEM((tokens, width), F32),
            pltpu.VMEM((nf, rows, 3 * width), BF16),
            pltpu.VMEM((tokens, cut), F32),
            pltpu.VMEM((3, n, seqs, 2, block, cols), BF16),
            pltpu.VMEM((3, seqs, spots, block, cols), BF16),
            pltpu.VMEM((seqs, spots, block, cols), BF16),
            pltpu.VMEM((seqs, 1, length), F32),
            pltpu.VMEM((seqs, length, 8), F32),
            pltpu.SemaphoreType.DMA((copies,)),
            pltpu.SemaphoreType.DMA((copies,)),
            pltpu.SemaphoreType.DMA((14 + 2 * units,)),
            pltpu.SemaphoreType.DMA((2,)),
        ],
        compiler_params=params(58, collective_id=0, has_side_effects=True),
        name="forward",
    )(e, w_qkv, w_o, w_in, w_out, mix, gain, bias, cosine, sine, ids)

    def whole(x):
        return x.reshape(x.shape[0] * x.shape[1], x.shape[2])

    weights = [whole(g) for g in (g_qkv, g_o, g_in, g_out)]
    return normed, hats, scales, res, *weights, qkv, ctx.reshape(tokens, width)


def attend_back_pair(qkv, grad, out, dk, dv, column_ref, row_ref, c_ref, s_ref, seq, lanes):
    blocks, block = grad.shape[1], grad.shape[2]
    length = blocks * block
    rows = row_tile(length)
    per = rows // block
    factor = HD**-0.5

    def load(ref, at, first, last):
        return ref[(*at, slice(first, last), slice(None), lanes)].reshape(-1, LANES)

    for i in range(length // rows):
        here = slice(i * rows, (i + 1) * rows)
        dk[here] = jnp.zeros((rows, LANES), F32)
        dv[here] = jnp.zeros((rows, LANES), F32)
    for i in range(length // rows):
        first, until = i * rows, (i + 1) * rows
        b0, b1 = i * per, (i + 1) * per
        query = first + lax.broadcasted_iota(jnp.int32, (rows, until), 0)
        key = lax.broadcasted_iota(jnp.int32, (rows, until), 1)
        same = column_ref[seq, first:until, 0:1] == row_ref[seq, 0:1, 0:until]
        allowed = same & (key <= query)
        q = load(qkv, (0, seq), b0, b1) * BF16(factor)
        g = load(grad, (seq,), b0, b1)
        k = load(qkv, (1, seq), 0, b1)
        v = load(qkv, (2, seq), 0, b1)
        total = None
        for h in range(LANES // HD):
            q_h = only(q, h)
            g_h = only(g, h)
            scores = jnp.where(allowed, dot(q_h, k, NT), MASKED)
            peak = jnp.max(scores, axis=-1, keepdims=True)
            raised = jnp.exp(scores - peak)
            mass = jnp.sum(raised, axis=-1, keepdims=True)
            probs = raised * (1.0 / mass)
            dots = dot(g_h, v, NT)
            center = jnp.sum(probs * dots, axis=-1, keepdims=True)
            slope = (probs * (dots - center)).astype(BF16)
            part = dot(slope, k)
            part = jnp.where(head_lanes(part.shape, h), part, 0.0)
            total = part if total is None else total + part
            dk[0:until] += dot(slope, q_h, TN)
            dv[0:until] += dot(probs.astype(BF16), g_h, TN)
        cosine, sine = c_ref[first:until], s_ref[first:until]
        low = turned(total * factor, cosine, -sine).astype(BF16)
        out[0, seq, b0:b1, :, lanes] = low.reshape(per, block, LANES)
    for i in range(length // rows):
        here = slice(i * rows, (i + 1) * rows)
        b0, b1 = i * per, (i + 1) * per
        low = turned(dk[here], c_ref[here], -s_ref[here]).astype(BF16)
        out[1, seq, b0:b1, :, lanes] = low.reshape(per, block, LANES)
        out[2, seq, b0:b1, :, lanes] = dv[here].astype(BF16).reshape(per, block, LANES)


def back_kernel(
    n,
    nf,
    cg_ref,
    qkv_ref,
    active_ref,
    lowered_ref,
    normed_ref,
    branch_ref,
    ctx_ref,
    attention_ref,
    ids_ref,
    c_ref,
    s_ref,
    grads_ref,
    in_sum,
    out_sum,
    o_sum,
    qkv,
    grad,
    back,
    dk,
    dv,
    in_terms,
    in_got,
    in_part,
    out_terms,
    out_got,
    out_part,
    o_terms,
    o_got,
    o_part,
    normed,
    branch,
    ctx,
    attention,
    low_tiles,
    active_tiles,
    row,
    column,
    tile_sem,
    send,
    recv,
    local,
):
    f, z = lax.axis_index("fsdp"), lax.axis_index("ctx")
    core = lax.rem(f, 2)
    seqs, _, block, cols = grad.shape
    remote = Remote(send, recv)
    sums = [
        ChipSum(remote, nf, in_terms, in_terms.at[:, core], in_got, in_part),
        ChipSum(remote, nf, out_terms, out_terms.at[:, core], out_got, out_part),
        ChipSum(remote, nf, o_terms, o_terms.at[:, core], o_got, o_part),
    ]
    spots = (z, 2 * n - 1 - z)
    mine = pl.ds(pl.multiple_of(z * cols, LANES), cols)

    def fetch(ref, tiles, sem, t):
        size = tiles.shape[2]
        slot = lax.rem(t, 2)
        at = pl.ds(pl.multiple_of(t * size, LANES), size)
        return pltpu.make_async_copy(ref.at[:, at], tiles.at[slot], tile_sem.at[sem + slot])

    wholes = [(ctx_ref, ctx), (attention_ref, attention), (normed_ref, normed), (branch_ref, branch)]
    loads = [
        pltpu.make_async_copy(ref, there, local.at[i]) for i, (ref, there) in enumerate(wholes)
    ]
    for load in loads[:3]:
        load.start()
    fetch(lowered_ref, low_tiles, 0, 0).start()
    loads[3].start()
    fetch(active_ref, active_tiles, 2, 0).start()
    later = [pltpu.make_async_copy(qkv_ref, qkv, local.at[6 + 2 * seqs])]
    for h in range(2):
        later.append(
            pltpu.make_async_copy(cg_ref.at[z, :, h], grad.at[:, spots[h]], local.at[4 + h])
        )
    for load in later:
        load.start()

    greet_partners(n, nf)

    arriving = []

    def take(s):
        copies = []
        for k in range(1, n):
            to = lax.rem(z + k, n)
            for h in range(2):
                copies.append(
                    remote.start(cg_ref.at[to, s, h], grad.at[s, spots[h]], {"ctx": to})
                )
        arriving.append(copies)

    def each_tile(ref, tiles, sem, work):
        count = ref.shape[1] // tiles.shape[2]

        @pl.loop(0, count)
        def _(t):
            fetch(ref, tiles, sem, t).wait()

            @pl.when(t + 1 < count)
            def _():
                fetch(ref, tiles, sem, t + 1).start()

            work(t, tiles[lax.rem(t, 2)])

    def in_tile(t, low):
        chips, _, rows, _ = in_terms.shape
        size = low.shape[1]
        at = pl.ds(pl.multiple_of(t * size, LANES), size)
        value = dot(normed[...], low, TN).astype(BF16)
        in_terms[:, :, :, at] = value.reshape(chips, 2, rows, size)

    def out_tile(t, active):
        _, _, rows, width = out_terms.shape
        out_terms[t] = dot(active, branch[...], TN).astype(BF16).reshape(2, rows, width)

    take(0)
    loads[0].wait()
    loads[1].wait()
    o_terms[...] = dot(ctx[...], attention[...], TN).astype(BF16).reshape(o_terms.shape)
    sums[2].cores()
    loads[2].wait()
    each_tile(lowered_ref, low_tiles, 0, in_tile)
    sums[0].cores()
    sums[2].cross()
    for s in range(1, seqs):
        take(s)
    loads[3].wait()
    each_tile(active_ref, active_tiles, 2, out_tile)
    sums[1].cores()
    place_segments(ids_ref, row, column, block)
    sums[0].cross()
    for load in later:
        load.wait()

    leaving = []
    kept = []

    def hand(s, here, there):
        for k in range(1, n):
            to = lax.rem(z + k, n)
            for h in range(2):
                spot = to if h == 0 else 2 * n - 1 - to
                leaving.append(
                    remote.start(
                        back.at[:, s, spot, :, here],
                        grads_ref.at[:, s, h, :, there],
                        {"ctx": to},
                    )
                )

    for s in range(seqs):
        for copy in arriving[s]:
            copy.wait()
        if s == 0:
            for p in range(cols // LANES):
                here = slice(p * LANES, (p + 1) * LANES)
                attend_back_pair(qkv, grad, back, dk, dv, column, row, c_ref, s_ref, s, here)
                hand(s, here, pl.ds(pl.multiple_of(z * cols + p * LANES, LANES), LANES))
        else:

            @pl.loop(0, cols // LANES)
            def _(p):
                lanes = pl.ds(pl.multiple_of(p * LANES, LANES), LANES)
                attend_back_pair(qkv, grad, back, dk, dv, column, row, c_ref, s_ref, s, lanes)

            hand(s, slice(None), mine)
        for h in range(2):
            copy = pltpu.make_async_copy(
                back.at[:, s, spots[h]], grads_ref.at[:, s, h, :, mine], local.at[6 + 2 * s + h]
            )
            copy.start()
            kept.append(copy)
        if s == 0:
            sums[2].relay()
            sums[1].cross()
            sums[0].relay()

    sums[1].relay()
    for chip_sum, out in zip(sums, (in_sum, out_sum, o_sum)):
        chip_sum.total(out)
    for copy in kept + leaving:
        copy.wait()


def attention_back(context_grad, qkv, saved, ids, cosine, sine, n, nf):
    _, seqs, spots, block, cols = qkv.shape
    length = spots * block
    tokens, units = saved[0].shape
    width = saved[2].shape[1]
    chips = nf // 2
    shapes = [(width // nf, units), (units // nf, width), (width // nf, width)]
    copies = (2 * seqs + cols // LANES - 1) * 2 * (n - 1) + 3 * ChipSum.count(nf)
    copies += 2 * (n - 1)
    vmem = pl.BlockSpec(memory_space=pltpu.VMEM)
    hbm = pl.BlockSpec(memory_space=pltpu.HBM)
    scratch = []
    for rows, wide in shapes:
        scratch.append(pltpu.VMEM((chips, 2, rows, wide), BF16))
        scratch += chip_scratch(nf, rows, wide)[1:]
    grads, *owned = pl.pallas_call(
        functools.partial(back_kernel, n, nf),
        in_specs=[hbm] * 8 + [vmem] * 3,
        out_specs=[hbm, vmem, vmem, vmem],
        out_shape=[jax.ShapeDtypeStruct((3, seqs, 2, block, width), BF16)]
        + [jax.ShapeDtypeStruct(shape, BF16) for shape in shapes],
        scratch_shapes=[
            pltpu.VMEM((3, seqs, spots, block, cols), BF16),
            pltpu.VMEM((seqs, spots, block, cols), BF16),
            pltpu.VMEM((3, seqs, spots, block, cols), BF16),
            pltpu.VMEM((length, LANES), F32),
            pltpu.VMEM((length, LANES), F32),
            *scratch,
            *[pltpu.VMEM((tokens, width), BF16)] * 4,
            pltpu.VMEM((2, tokens, 512), BF16),
            pltpu.VMEM((2, tokens, units // chips), BF16),
            pltpu.VMEM((seqs, 1, length), F32),
            pltpu.VMEM((seqs, length, 8), F32),
            pltpu.SemaphoreType.DMA((4,)),
            pltpu.SemaphoreType.DMA((copies,)),
            pltpu.SemaphoreType.DMA((copies,)),
            pltpu.SemaphoreType.DMA((7 + 2 * seqs,)),
        ],
        compiler_params=params(62, collective_id=2, has_side_effects=True),
        name="attention_back",
    )(
        context_grad.reshape(n, seqs, 2, block, cols),
        qkv,
        *saved,
        ids,
        cosine,
        sine,
    )
    return grads.reshape(3, seqs * 2 * block, width), owned


def norm_back_tile(hats, scales, ng, st, e, mg, mg_ref, g_ref, h, low, dgain, dbias, selector, t, strip=16):
    count, tile, width = e.shape
    inv = 1.0 / width
    to = slice(t * tile, (t + 1) * tile)
    for s in range(3):
        dy = ng[s]
        hat = hats[s, to].astype(F32)
        scale = scales[to, s : s + 1]
        dgain[s : s + 1] += jnp.sum(dy * hat, axis=0, keepdims=True)
        dbias[s : s + 1] += jnp.sum(dy, axis=0, keepdims=True)
        dh = dy * g_ref[s : s + 1]
        mean = jnp.sum(dh, axis=-1, keepdims=True) * inv
        along = jnp.sum(dh * hat, axis=-1, keepdims=True) * inv
        out = (scale * (dh - mean - hat * along)).astype(BF16)
        low[s, to] = out
        st[s] = out
    st[3] = h[to].astype(BF16)

    shape = (4 * strip, count * strip)
    same = lax.rem(lax.broadcasted_iota(jnp.int32, shape, 0), strip) == lax.rem(
        lax.broadcasted_iota(jnp.int32, shape, 1), strip
    )
    for i in range(tile // strip):
        rows = slice(i * strip, (i + 1) * strip)
        grads = st[:, rows].reshape(4 * strip, width)
        inputs = e[:, rows].reshape(count * strip, width)
        products = jnp.where(same, dot(grads, inputs, NT), 0.0)
        wide = jnp.concatenate(
            [products[s * strip : (s + 1) * strip] for s in range(4)], axis=1
        )
        high, rest = halves(wide)
        mg[rows] = dot(high, selector[...]) + dot(rest, selector[...])
    turned_mg = mg[...].T
    block = mg_ref.shape[4]
    per = tile // block
    for i in range(per):
        place = t * per + i
        for a in range(4):
            mg_ref[a, :, place // 2, place % 2, :] = turned_mg[
                a * count : (a + 1) * count, i * block : (i + 1) * block
            ]


def small_squares(rows, cols):
    first = 8 + rows
    places = []
    for g in range(-(-rows // 8)):
        size = min(8, rows - 8 * g)
        places.append(
            (
                slice(first, first + size),
                slice(g * LANES, g * LANES + cols),
                slice(8 * g, 8 * g + size),
            )
        )
    return places


def small_line_at(rows, cols):
    groups = -(-rows // 8)
    return slice(groups * LANES, groups * LANES + cols)


def end_kernel(
    n,
    nf,
    grads_ref,
    normed_ref,
    hats_ref,
    scales_ref,
    e_ref,
    w_ref,
    h_ref,
    gain_ref,
    in_ref,
    out_ref,
    o_ref,
    sgain_ref,
    sbias_ref,
    sw1_ref,
    sw2_ref,
    smb_ref,
    low_ref,
    mg_ref,
    q_sum,
    k_sum,
    v_sum,
    in_sum,
    out_sum,
    o_sum,
    small_sum,
    grads,
    normed,
    hats,
    scales,
    w,
    h,
    e,
    ng,
    st,
    low,
    mg,
    selector,
    dgain,
    dbias,
    small_work,
    small_in,
    small_term,
    small_land,
    small_own,
    small_cross,
    send,
    recv,
    local,
    e_sem,
    *more,
):
    f, z = lax.axis_index("fsdp"), lax.axis_index("ctx")
    core = lax.rem(f, 2)
    count, tokens, width = e_ref.shape
    tile = e.shape[2]
    tiles = tokens // tile
    remote = Remote(send, recv)
    chip_sets = [more[4 * i : 4 * i + 4] for i in range(3)]
    rest = more[12:]
    shard = chip_sets[0][1].shape[1]

    def fetch(t):
        return pltpu.make_async_copy(
            e_ref.at[:, t * tile : (t + 1) * tile], e.at[t % 2], e_sem.at[t % 2]
        )

    loads = [
        pltpu.make_async_copy(src, dst, local.at[i])
        for i, (src, dst) in enumerate(
            [
                (grads_ref, grads),
                (normed_ref, normed),
                (w_ref, w),
                (hats_ref, hats),
                (scales_ref, scales),
                (h_ref, h),
            ]
        )
    ]
    for load in loads:
        load.start()
    fetch(0).start()

    greet_all(n, nf)

    chain = Chain(remote, n)
    thin = small_in.shape[1]
    here = pl.ds(pl.multiple_of(f * thin, thin), thin)
    works = [in_ref, out_ref, o_ref] + [chip_set[3] for chip_set in chip_sets]
    results = [in_sum, out_sum, o_sum, q_sum, k_sum, v_sum]
    for work, out, sizes in zip(works, results, piece_sizes([x.shape[0] for x in works])):
        first = 0
        if work is chip_sets[0][3]:
            small_piece = len(chain.pieces)
            chain.add(small_term, small_sum.at[here], small_land, small_own, small_cross)
        for size in sizes:
            at = pl.ds(first, size)
            chain.add(work.at[at], out.at[at], *rest[:3])
            rest = rest[3:]
            first += size
    total_pieces = len(chain.pieces)
    chain.start()
    chain.start()

    loads[0].wait()
    loads[1].wait()
    cut = 256
    per = cut // (2 * shard)
    sums = []
    for i in range(3):
        terms, got, part, own = chip_sets[i]
        for c in range(width // cut):
            value = dot(normed[i, :, c * cut : (c + 1) * cut], grads[i], TN).astype(BF16)
            terms[c * per : (c + 1) * per] = value.reshape(per, 2, shard, width)
        chip_sum = ChipSum(remote, nf, terms, terms.at[:, core], got, part)
        chip_sum.cores()
        sums.append(chip_sum)
    dgain[...] = jnp.zeros_like(dgain)
    dbias[...] = jnp.zeros_like(dbias)
    size = selector.shape
    group = lax.broadcasted_iota(jnp.int32, size, 0) // 16
    selector[...] = jnp.where(
        group == lax.broadcasted_iota(jnp.int32, size, 1), 1.0, 0.0
    ).astype(BF16)
    for load in loads[2:]:
        load.wait()

    def do_tile(t):
        fetch(t).wait()
        if t + 1 < tiles:
            fetch(t + 1).start()
        rows = slice(t * tile, (t + 1) * tile)
        for i in range(3):
            ng[i] = dot(grads[i, rows], w[:, i * width : (i + 1) * width], NT)
        norm_back_tile(
            hats, scales, ng, st, e.at[t % 2], mg, mg_ref, gain_ref, h, low, dgain, dbias, selector, t
        )

    todo = list(range(tiles))

    def some():
        if todo:
            do_tile(todo.pop(0))

    chain.step(0)
    for chip_sum in sums:
        chip_sum.cross()
    chain.step(1)
    some()
    chain.step(2)
    some()
    chain.step(3)
    some()
    chain.step(4)
    while todo:
        some()
    keep = pltpu.make_async_copy(low, low_ref, local.at[6])
    keep.start()

    hidden_count, coef_count = sw2_ref.shape
    first = 8 + hidden_count
    squares = small_squares(hidden_count, coef_count)
    line_at = small_line_at(hidden_count, coef_count)
    small_work[...] = jnp.zeros_like(small_work)
    small_work[0:3] = dgain[...]
    small_work[3:4] = sgain_ref[...]
    small_work[4:7] = dbias[...]
    small_work[7:8] = sbias_ref[...]
    small_work[8:first] = sw1_ref[...]
    for rows, lanes, which in squares:
        small_work[rows, lanes] = sw2_ref[which]
    small_work[first : first + 1, line_at] = smb_ref[...]
    small_in[0] = small_work[here]
    slices = []
    for k in range(1, nf):
        to = lax.rem(f + k, nf)
        slices.append(
            remote.start(
                small_work.at[pl.ds(pl.multiple_of(to * thin, thin), thin)],
                small_in.at[k],
                {"fsdp": to},
            )
        )

    for chip_sum in sums:
        chip_sum.relay()
    chain.step(5)
    chain.step(6)
    for chip_sum, chip_set in zip(sums, chip_sets):
        chip_sum.total(chip_set[3])
    for copy in slices:
        copy.wait()
    total = small_in[0]
    for k in range(1, nf):
        total = total + small_in[k]
    small_term[...] = total
    for c in range(7, total_pieces):
        chain.step(c)
        if c == small_piece + 2:
            chain.end(small_piece)
            spread = []
            for k in range(1, nf):
                spread.append(
                    remote.start(
                        small_sum.at[here], small_sum.at[here], {"fsdp": lax.rem(f + k, nf)}
                    )
                )
    chain.leave(total_pieces - 1)
    for copy in spread:
        copy.wait()
    for c in range(total_pieces):
        if c != small_piece:
            chain.end(c)
    keep.wait()


def finish(grads, normed, hats, scales, e, w, hgrad, gain, owned, small, mix_shape, n, nf):
    count, tokens, width = e.shape
    tile = 128
    chips = nf // 2
    shard = width // nf
    rows = 8 + small[2].shape[0] + 8
    thin = 8 * -(-rows // (8 * nf))
    m_in, m_out, m_o = owned
    lines, chip_sums = [], []
    heights = [m_in.shape[0], m_out.shape[0], m_o.shape[0]] + [shard] * 3
    widths = [m_in.shape[1], m_out.shape[1], m_o.shape[1]] + [width] * 3
    planned = piece_sizes(heights)
    for sizes, wide_as in zip(planned, widths):
        for size in sizes:
            lines += chain_scratch(n, size, wide_as)
    pieces = sum(len(sizes) for sizes in planned)
    for _ in range(3):
        chip_sums += [
            pltpu.VMEM((chips, 2, shard, width), BF16),
            *chip_scratch(nf, shard, width)[1:],
            pltpu.VMEM((shard, width), BF16),
        ]
    copies = (pieces + 1) * (Chain.levels(n) + 2) + 3 * ChipSum.count(nf) + 2 * (nf - 1)
    vmem = pl.BlockSpec(memory_space=pltpu.VMEM)
    hbm = pl.BlockSpec(memory_space=pltpu.HBM)
    wide = jax.ShapeDtypeStruct((shard, width), BF16)
    return pl.pallas_call(
        functools.partial(end_kernel, n, nf),
        in_specs=[hbm] * 7 + [vmem] * 9,
        out_specs=[hbm] + [vmem] * 8,
        out_shape=[
            jax.ShapeDtypeStruct((3, tokens, width), BF16),
            jax.ShapeDtypeStruct(mix_shape, F32),
            wide,
            wide,
            wide,
            *[jax.ShapeDtypeStruct(x.shape, BF16) for x in owned],
            jax.ShapeDtypeStruct((nf * thin, width), F32),
        ],
        scratch_shapes=[
            pltpu.VMEM(grads.shape, BF16),
            pltpu.VMEM(normed.shape, BF16),
            pltpu.VMEM(hats.shape, BF16),
            pltpu.VMEM(scales.shape, F32),
            pltpu.VMEM(w.shape, BF16),
            pltpu.VMEM(hgrad.shape, F32),
            pltpu.VMEM((2, count, tile, width), BF16),
            pltpu.VMEM((3, tile, width), F32),
            pltpu.VMEM((4, tile, width), BF16),
            pltpu.VMEM((3, tokens, width), BF16),
            pltpu.VMEM((tile, LANES), F32),
            pltpu.VMEM((4 * count * 16, LANES), BF16),
            pltpu.VMEM((3, width), F32),
            pltpu.VMEM((3, width), F32),
            pltpu.VMEM((nf * thin, width), F32),
            pltpu.VMEM((nf, thin, width), F32),
            *[pltpu.VMEM((thin, width), F32)] * 2,
            *[pltpu.VMEM((Chain.levels(n), thin, width), F32)] * 2,
            pltpu.SemaphoreType.DMA((copies,)),
            pltpu.SemaphoreType.DMA((copies,)),
            pltpu.SemaphoreType.DMA((7,)),
            pltpu.SemaphoreType.DMA((2,)),
            *chip_sums,
            *lines,
        ],
        compiler_params=params(60, collective_id=3, has_side_effects=True),
        name="finish",
    )(grads, normed, hats, scales, e, w, hgrad, gain, *owned, *small)


def tail_kernel(
    low_ref,
    h_ref,
    mix_ref,
    q_ref,
    k_ref,
    v_ref,
    in_ref,
    out_ref,
    o_ref,
    small_ref,
    mg_ref,
    eg_ref,
    qkv_ref,
    in32_ref,
    out32_ref,
    o32_ref,
    gain_ref,
    bias_ref,
    w1_ref,
    w2_ref,
    mb_ref,
    mg_out_ref,
    mixes,
    *,
    strip,
):
    count, tile, width = eg_ref.shape
    chunk = 256
    block = mix_ref.shape[4]
    tiles = mix_ref.shape[2] * 2 * block // tile
    step = pl.program_id(0)
    for t in range(tiles):

        @pl.when(step == t)
        def _():
            mix_columns(mix_ref, mixes, t)

    @pl.when(step == 0)
    def _():
        hidden_count, coef_count = w2_ref.shape
        first = 8 + hidden_count
        gain_ref[...] = small_ref[0:4]
        bias_ref[...] = small_ref[4:8]
        w1_ref[...] = small_ref[8:first]
        for rows, lanes, which in small_squares(hidden_count, coef_count):
            w2_ref[which] = small_ref[rows, lanes]
        mb_ref[...] = small_ref[first : first + 1, small_line_at(hidden_count, coef_count)]
        mg_out_ref[...] = mg_ref[...]

    for i, ref in enumerate((q_ref, k_ref, v_ref)):
        qkv_ref[:, i * width : (i + 1) * width] = ref[...].astype(F32)
    in32_ref[...] = in_ref[...].astype(F32)
    out32_ref[...] = out_ref[...].astype(F32)
    o32_ref[...] = o_ref[...].astype(F32)

    @pl.loop(0, tile // strip)
    def _(i):
        rows = pl.ds(pl.multiple_of(i * strip, strip), strip)
        mix = mixes[rows]
        for c in range(width // chunk):
            cols = slice(c * chunk, (c + 1) * chunk)
            grads = [low_ref[s, rows, cols].astype(F32) for s in range(3)]
            grads.append(h_ref[rows, cols])
            for j in range(count):
                total = grads[0] * mix[:, j : j + 1]
                for s in range(1, 4):
                    total = total + grads[s] * mix[:, s * count + j : s * count + j + 1]
                eg_ref[j, rows, cols] = total.astype(BF16)


def spread_back(low, hgrad, mix, sums, small, m_grad, sizes):
    _, tokens, width = low.shape
    count = mix.shape[1]
    tile = 128
    tiles = tokens // tile
    hidden_count, coef_count = sizes

    def part(x):
        return pl.BlockSpec((x.shape[0] // tiles, x.shape[1]), lambda i: (i, 0))

    def whole(x):
        zeros = (0,) * len(x.shape)
        return once(x.shape, lambda i: zeros)

    shard = sums[0].shape[0]
    outs = [
        jax.ShapeDtypeStruct((count, tokens, width), BF16),
        jax.ShapeDtypeStruct((shard, 3 * width), F32),
        *[jax.ShapeDtypeStruct(x.shape, F32) for x in sums[3:]],
        jax.ShapeDtypeStruct((4, width), F32),
        jax.ShapeDtypeStruct((4, width), F32),
        jax.ShapeDtypeStruct((hidden_count, width), F32),
        jax.ShapeDtypeStruct((hidden_count, coef_count), F32),
        jax.ShapeDtypeStruct((1, coef_count), F32),
        jax.ShapeDtypeStruct(m_grad.shape, F32),
    ]
    return pl.pallas_call(
        functools.partial(tail_kernel, strip=32),
        grid=(tiles,),
        in_specs=[
            pl.BlockSpec((3, tile, width), lambda i: (0, i, 0)),
            pl.BlockSpec((tile, width), lambda i: (i, 0)),
            whole(mix),
            *[part(x) for x in sums],
            whole(small),
            whole(m_grad),
        ],
        out_specs=[pl.BlockSpec((count, tile, width), lambda i: (0, i, 0))]
        + [part(x) for x in outs[1:5]]
        + [whole(x) for x in outs[5:]],
        out_shape=outs,
        scratch_shapes=[pltpu.VMEM((tile, 4 * count), F32)],
        compiler_params=params(60),
        cost_estimate=pl.CostEstimate(
            flops=64 * tokens * width, bytes_accessed=40 * tokens * width, transcendentals=0
        ),
        name="spread_back",
    )(low, hgrad, mix, *sums, small, m_grad)


def body(
    earlier,
    mix_in,
    segment_ids,
    attn_qkv,
    attn_out,
    mlp_in,
    mlp_out,
    norm_gain,
    norm_bias,
    mix_w1,
    mix_w2,
    mix_bias,
    out_grad,
    coef_grad,
):
    count, seqs, _, block, width = earlier.shape
    n = lax.axis_size("ctx")
    tokens = seqs * 2 * block
    length = 2 * n * block
    me = lax.axis_index("ctx")

    nf = lax.axis_size("fsdp")
    e = earlier.reshape(count, tokens, width)
    cosine, sine = (jnp.asarray(table) for table in turn_tables(length))
    normed, hats, scales, residual, w_qkv, w_o, w_in, w_out, qkv, context = forward(
        e,
        mix_in,
        attn_qkv,
        attn_out,
        mlp_in,
        mlp_out,
        norm_gain,
        norm_bias,
        cosine,
        sine,
        segment_ids,
        n,
        nf,
    )
    (
        layer_out,
        coefs,
        active,
        lowered,
        normed_mlp,
        branch,
        attention_grad,
        context_grad,
        hidden_grad,
        d_gain,
        d_bias,
        d_w1,
        d_w2,
        d_mb,
    ) = feed(
        residual,
        context,
        w_o,
        w_in,
        w_out,
        norm_gain,
        norm_bias,
        mix_w1,
        mix_w2,
        mix_bias[None, :],
        out_grad.reshape(tokens, width),
        coef_grad,
        n,
    )
    saved = (active, lowered, normed_mlp, branch, context, attention_grad)
    grads, owned = attention_back(
        context_grad, qkv, saved, segment_ids, cosine, sine, n, nf
    )
    low, m_grad, *sums, small = finish(
        grads,
        normed,
        hats,
        scales,
        e,
        w_qkv,
        hidden_grad,
        norm_gain,
        owned,
        (d_gain, d_bias, d_w1, d_w2, d_mb),
        mix_in.shape,
        n,
        nf,
    )
    e_grad, g_qkv, g_in, g_out, g_o, gain_sum, bias_sum, w1_sum, w2_sum, mb_sum, m_grad = (
        spread_back(low, hidden_grad, mix_in, sums, small, m_grad, mix_w2.shape)
    )
    return (
        layer_out.reshape(seqs, 2, block, width),
        coefs,
        e_grad.reshape(count, seqs, 2, block, width),
        m_grad,
        g_qkv,
        g_o,
        g_in,
        g_out,
        gain_sum,
        bias_sum,
        w1_sum,
        w2_sum,
        mb_sum[0],
    )


def solution(mesh):
    in_specs = (
        P(None, "fsdp", None, "ctx", None),
        P(None, None, "fsdp", None, "ctx"),
        P("fsdp", None, None),
        P("fsdp", None),
        P("fsdp", None),
        P("fsdp", None),
        P("fsdp", None),
        P(),
        P(),
        P(),
        P(),
        P(),
        P("fsdp", None, "ctx", None),
        P(None, None, "fsdp", None, "ctx"),
    )
    out_specs = (
        P("fsdp", None, "ctx", None),
        P(None, None, "fsdp", None, "ctx"),
        P(None, "fsdp", None, "ctx", None),
        P(None, None, "fsdp", None, "ctx"),
        P("fsdp", None),
        P("fsdp", None),
        P("fsdp", None),
        P("fsdp", None),
        P(),
        P(),
        P(),
        P(),
        P(),
    )
    return jax.shard_map(body, mesh=mesh, in_specs=in_specs, out_specs=out_specs, check_vma=False)
```
